32 devices in a mesh: section: 2 (over core), dp: 4 (over z), tensor: 4 (over y, x).
Axes of the slice: x: 2, y: 2, z: 4, core: 2. Of those that a mesh axis runs over, the one named last changes fastest.
Arguments:
- tokens: bfloat16 [2, 3072, 1024], P(None, ('dp', 'tensor')), may hold values from -6 to 6
- cotangent: bfloat16 [2, 3072, 1024], P(None, ('dp', 'tensor')), may hold values from -6 to 6
- mixer_in_weight: bfloat16 [2, 1024, 4, 1024], P('section', None, None, 'tensor'), may hold values from -0.1875 to 0.1875
- mixer_out_weight: bfloat16 [2, 1024, 1024], P('section', 'tensor'), may hold values from -0.1875 to 0.1875
- feed_in_weight: bfloat16 [2, 1024, 2, 2816], P('section', None, None, 'tensor'), may hold values from -0.1875 to 0.1875
- feed_out_weight: bfloat16 [2, 2816, 1024], P('section', 'tensor'), may hold values from -0.109375 to 0.109375
- decay_rate: float32 [2, 8], P('section', 'tensor'), may hold values from 3e-05 to 0.05
- block_starts: int32 [2, 12], replicated, may hold values from 0 to 1, as said below
Outputs:
- layer_outputs: bfloat16 [2, 2, 3072, 1024], P('section', None, ('dp', 'tensor'))
- input_grads: bfloat16 [2, 2, 3072, 1024], P('section', None, ('dp', 'tensor'))
- grad_mixer_in: float32 [2, 1024, 4, 1024], P('section', None, None, 'tensor')
- grad_mixer_out: float32 [2, 1024, 1024], P('section', 'tensor')
- grad_feed_in: float32 [2, 1024, 2, 2816], P('section', None, None, 'tensor')
- grad_feed_out: float32 [2, 2816, 1024], P('section', 'tensor')
The draws below stay inside these ranges and needn't reach their ends.
Inputs may be any that keep to these rules, and one draw needn't show every extreme that they name: `block_starts`: the first block of every micro-batch is 1; every sequence spans 4 blocks or more and 12 blocks or fewer.
All inputs are finite; a program needn't handle non-finite values.
Results may differ from the reference program's by a relative error of at most 0.035.
Values may be sent and summed in bfloat16 or wider, within the bound.
A program may use at most 192 MiB of HBM per device.

```python
import math
import jax
import jax.numpy as jnp
from jax import lax

D = 1024
HEADS = 8
HEAD = 128
FF = 2816
BLOCK = 256
MB = 2
MIN_BLK = 4
LAYERS = 2
BLOCKS = 12
MOST_BLK = 12
TOKENS = 3072


def draw_block_starts(key, part):
    micro_keys = jax.random.split(key, MB)
    indices = jnp.arange(BLOCKS, dtype=jnp.int32)
    rows_out = []
    for micro_idx in range(MB):
        lengths = jax.random.randint(micro_keys[micro_idx], (BLOCKS,), MIN_BLK, MOST_BLK - MIN_BLK + 2, dtype=jnp.int32)
        finish = jnp.cumsum(lengths).astype(jnp.int32)
        hits = jnp.sum((finish[None, :] == indices[:, None]).astype(jnp.int32), axis=1)
        marked = (hits > 0) & (indices <= BLOCKS - MIN_BLK)
        rows_out.append(jnp.where((indices == 0) | marked, 1, 0).astype(jnp.int32))
    return jnp.stack(rows_out).astype(jnp.int32)


def steps_of(stream_key, extent, shards, least, top_value):
    def one(position, shards_of):
        draws = jax.random.uniform(jax.random.fold_in(jax.random.fold_in(stream_key, 6), position), (shards_of,), jnp.float32, least / len(shards), top_value / len(shards))
        return jnp.repeat(jnp.exp(draws), extent[position] // shards_of).reshape((-1,) + (1,) * (len(extent) - position - 1))

    factor_of = one(*shards[0])
    for cut in shards[1:]:
        factor_of = factor_of * one(*cut)
    return factor_of


def scatter_about(stream_key, shape, spread, reach, cuts=(), kind=jnp.bfloat16):
    values = spread * jax.random.normal(stream_key, shape, jnp.float32)
    if cuts:
        values = values * steps_of(stream_key, shape, cuts, -0.22, 0.18)
    return jnp.clip(values, -reach, reach).astype(kind)


def setup_inputs(seed: int = 0) -> dict:
    seeds = jax.random.split(jax.random.key(seed), 9)
    tokens = scatter_about(seeds[0], (MB, TOKENS, D), 1.0, 6.0, ((1, 16),))
    cotangent = scatter_about(seeds[1], (MB, TOKENS, D), 1.0, 6.0, ((1, 16),))
    mixer_in_weight = scatter_about(seeds[2], (LAYERS, D, 4, D), D ** -0.5, 0.1875, ((0, 2), (3, 4)))
    mixer_out_weight = scatter_about(seeds[3], (LAYERS, D, D), D ** -0.5, 0.1875, ((0, 2), (1, 4)))
    feed_in_weight = scatter_about(seeds[4], (LAYERS, D, 2, FF), D ** -0.5, 0.1875, ((0, 2), (3, 4)))
    feed_out_weight = scatter_about(seeds[5], (LAYERS, FF, D), FF ** -0.5, 0.109375, ((0, 2), (1, 4)))
    decay_rate = jnp.clip(jnp.exp(math.log(0.05) - 7.418581 * jax.random.uniform(seeds[6], (LAYERS, HEADS), jnp.float32) ** steps_of(seeds[6], (LAYERS, HEADS), ((0, 2), (1, 4)), -0.2, 0.2)), 2.9999999242136255e-05, 0.05)
    block_starts = draw_block_starts(jax.random.fold_in(seeds[8], 71), 0)
    return dict(tokens=tokens, cotangent=cotangent, mixer_in_weight=mixer_in_weight, mixer_out_weight=mixer_out_weight, feed_in_weight=feed_in_weight, feed_out_weight=feed_out_weight, decay_rate=decay_rate, block_starts=block_starts)


@jax.custom_vjp
def low(v):
    return lax.optimization_barrier(v.astype(jnp.bfloat16)).astype(jnp.float32)

@jax.custom_vjp
def low_back(v):
    return v

def low_keep(v):
    return (low(v), None)

def low_pass(kept, grad):
    return (grad,)

def back_keep(v):
    return (v, None)

def back_low(kept, grad):
    return (low(grad),)
low.defvjp(low_keep, low_pass)
low_back.defvjp(back_keep, back_low)
norm_eps = 1e-06
exact = lax.Precision.HIGHEST

def simple_norm(values):
    return values * lax.rsqrt(lax.optimization_barrier(jnp.mean(values * values, axis=-1, keepdims=True)) + norm_eps)

def swish_act(values):
    return values * jax.nn.sigmoid(values)

def rotate(values, cosine, sine_part):
    half_width = values.shape[-1] // 2
    first_half = values[..., :half_width]
    second = values[..., half_width:]
    cosine = cosine[:, None, :]
    sine_part = sine_part[:, None, :]
    return jnp.concatenate([first_half * cosine - second * sine_part, first_half * sine_part + second * cosine], axis=-1)

def token_places(starts):
    indices = jnp.arange(starts.shape[0], dtype=jnp.int32)
    begins = lax.cummax(jnp.where(starts > 0, indices, 0), axis=0)
    offsets = (indices - begins) * BLOCK
    return (offsets[:, None] + jnp.arange(BLOCK, dtype=jnp.int32)[None, :]).reshape(-1)

def angle_tables(places):
    frequency = 10000.0 ** (-jnp.arange(HEAD // 2, dtype=jnp.float32) / (HEAD // 2))
    angles = places.astype(jnp.float32)[:, None] * frequency[None, :]
    return (jnp.cos(angles), jnp.sin(angles))

def decay_tables(decay_rates):
    steps_in = jnp.arange(BLOCK, dtype=jnp.float32)
    distance = steps_in[:, None] - steps_in[None, :]
    decay_mask = jnp.where(distance[None] >= 0.0, jnp.exp(-decay_rates[:, None, None] * jnp.maximum(distance, 0.0)[None]), 0.0)
    query_decay = jnp.exp(-decay_rates[None, :] * (steps_in[:, None] + 1.0))
    key_decay = jnp.exp(-decay_rates[None, :] * (BLOCK - 1.0 - steps_in[:, None]))
    block_decay = jnp.exp(-decay_rates * BLOCK)
    return (decay_mask, query_decay, key_decay, block_decay)

def layer_forward(inputs, weights, decay_rates, starts):
    mixer_in, mixer_out, feed_in, feed_out = weights
    token_count = inputs.shape[0]
    hidden = low(simple_norm(inputs))
    projected = low_back(jnp.dot(hidden, mixer_in.reshape(D, 4 * D), precision=exact)).reshape(token_count, 4, HEADS, HEAD)
    cosine, sine_part = angle_tables(token_places(starts))
    queries = low(rotate(swish_act(projected[:, 0]), cosine, sine_part))
    rotated_keys = low(rotate(swish_act(projected[:, 1]), cosine, sine_part))
    value_rows = low(projected[:, 2])
    gate_vals = projected[:, 3].reshape(token_count, D)
    decay_mask, query_decay, key_decay, block_decay = decay_tables(decay_rates)

    def block_step(block_state, pieces):
        block_q, block_k, block_v, reset_flag = pieces
        block_state = block_state * (1.0 - reset_flag)
        scores = low_back(jnp.einsum('ihd,jhd->hij', block_q, block_k, precision=exact))
        block_weights = low(scores * decay_mask)
        inner_part = jnp.einsum('hij,jhd->ihd', block_weights, block_v, precision=exact)
        outer_part = jnp.einsum('ihd,hde->ihe', block_q * query_decay[:, :, None], block_state, precision=exact)
        local_state = jnp.einsum('jhd,jhe->hde', block_k * key_decay[:, :, None], block_v, precision=exact)
        return (block_decay[:, None, None] * block_state + local_state, inner_part + outer_part)
    block_shape = (starts.shape[0], BLOCK, HEADS, HEAD)
    start_state = jnp.zeros((HEADS, HEAD, HEAD), jnp.float32)
    final_state, mixed_heads = lax.scan(jax.checkpoint(block_step), start_state, (queries.reshape(block_shape), rotated_keys.reshape(block_shape), value_rows.reshape(block_shape), starts.astype(jnp.float32)))
    attended = low_back(mixed_heads.reshape(token_count, D))
    gated = low(simple_norm(attended) * gate_vals)
    branch = low_back(jnp.dot(gated, mixer_out, precision=exact))
    middle = inputs + branch
    hidden_two = low(simple_norm(middle))
    paired = low_back(jnp.dot(hidden_two, feed_in.reshape(D, 2 * FF), precision=exact)).reshape(token_count, 2, FF)
    product = low(paired[:, 0] * paired[:, 1])
    return middle + low_back(jnp.dot(product, feed_out, precision=exact))

def stack_forward(first_input, probes, weights, decay_rate, starts):
    current = first_input
    results = []
    for layer_idx in range(LAYERS):
        if layer_idx > 0:
            current = low_back(low(results[-1])) + probes[layer_idx - 1]
        layer_weights = tuple((matrix[layer_idx] for matrix in weights))
        results.append(layer_forward(current, layer_weights, decay_rate[layer_idx], starts))
    return (results[-1], tuple(results))

def reference(tokens, cotangent, mixer_in_weight, mixer_out_weight, feed_in_weight, feed_out_weight, decay_rate, block_starts):
    weights = tuple((matrix.astype(jnp.float32) for matrix in (mixer_in_weight, mixer_out_weight, feed_in_weight, feed_out_weight)))
    summed = tuple((jnp.zeros_like(matrix) for matrix in weights))
    outputs = []
    in_grads = []
    for micro_idx in range(MB):
        first_input = tokens[micro_idx].astype(jnp.float32)
        probes = tuple((jnp.zeros_like(first_input) for layer_idx in range(LAYERS - 1)))
        starts = block_starts[micro_idx]

        def forward_fn(first_input, probes, weights):
            return stack_forward(first_input, probes, weights, decay_rate, starts)
        last_out, pull_back, every_out = jax.vjp(forward_fn, first_input, probes, weights, has_aux=True)
        grad_first, grad_probes, grad_weights = pull_back(cotangent[micro_idx].astype(jnp.float32))
        summed = tuple((running + gradient for running, gradient in zip(summed, grad_weights)))
        outputs.append(jnp.stack(every_out))
        in_grads.append(jnp.stack((grad_first,) + tuple(grad_probes)))
    layer_outputs = jnp.stack(outputs, axis=1).astype(jnp.bfloat16)
    input_grads = jnp.stack(in_grads, axis=1).astype(jnp.bfloat16)
    return (layer_outputs, input_grads, summed[0], summed[1], summed[2], summed[3])
```

```python
import functools

import jax
import jax.numpy as jnp
from jax import lax
from jax.experimental import pallas as pl
from jax.experimental.pallas import tpu as pltpu
from jax.sharding import PartitionSpec as P

D = 1024
HEAD = 128
BLOCK = 256
WIDTH = 256
HEADS_HERE = WIDTH // HEAD
norm_eps = 1e-06
MESH = pl.DeviceIdType.MESH
ANY = pl.BlockSpec(memory_space=pl.ANY)
SMEM = pl.BlockSpec(memory_space=pltpu.SMEM)
bf16, f32 = jnp.bfloat16, jnp.float32
VMEM_BYTES = 60 * 1024 * 1024


def place():
    return lax.axis_index("section"), lax.axis_index("dp"), lax.axis_index("tensor")


def partner(t, k):
    return ((t // 2 + k // 2) % 2) * 2 + (t + k) % 2


class Sems:
    def __init__(self, ref):
        self.ref, self.used = ref, 0

    def take(self):
        self.used += 1
        return self.ref.at[self.used - 1]


def remote(src, dst, send, recv, dev):
    return pltpu.make_async_remote_copy(
        src_ref=src, dst_ref=dst, send_sem=send, recv_sem=recv, device_id=dev, device_id_type=MESH
    )


def nn(a, b):
    return lax.dot_general(a, b, (((1,), (0,)), ((), ())), preferred_element_type=f32)


def nt(a, b):
    return lax.dot_general(a, b, (((1,), (1,)), ((), ())), preferred_element_type=f32)


def tn(a, b):
    return lax.dot_general(a, b, (((0,), (0,)), ((), ())), preferred_element_type=f32)


def rms_scale(v):
    return lax.rsqrt(jnp.mean(v * v, axis=-1, keepdims=True) + norm_eps)


def norm_back(v, u):
    q = rms_scale(v)
    n = v * q
    return q * (u - n * jnp.mean(u * n, axis=-1, keepdims=True))


def sig(v):
    return 1.0 / (1.0 + jnp.exp(-v))


def rows_of(p, n):
    return pl.ds(pl.multiple_of(p * n, n), n)


def entry(dp, s, d, t, core=False):
    barrier = pltpu.get_barrier_semaphore()
    count = 3
    for k in (1, 2, 3):
        pl.semaphore_signal(barrier, inc=1, device_id=(s, d, partner(t, k)), device_id_type=MESH)
    if core:
        pl.semaphore_signal(barrier, inc=1, device_id=(1 - s, d, t), device_id_type=MESH)
        count += 1
    if dp > 1:

        def greet(k, c):
            pl.semaphore_signal(
                barrier, inc=1, device_id=(s, (d + k) % dp, t), device_id_type=MESH
            )
            return c

        lax.fori_loop(1, dp, greet, 0)
        count += dp - 1
    pl.semaphore_wait(barrier, count)


class Gather:
    def __init__(self, block_at, half, ssem, rsem, base, where):
        self.at, self.half, self.ssem, self.rsem, self.base = block_at, half, ssem, rsem, base
        self.where = where

    def copy(self, n, peer, half, to):
        s, d, t = self.where
        ref = self.at(partner(t, peer), half)
        k = self.base + n
        return remote(ref, ref, self.ssem.at[k], self.rsem.at[k], (s, d, partner(t, to)))

    def mine(self, n):
        peer, half, to = ((0, 0, 1), (0, 1, 1), (0, 0, 2), (0, 1, 2), (1, 0, 2), (2, 1, 1))[n]
        return self.copy(n, peer, half, to)

    def arriving(self, n):
        s, d, t = self.where
        peer, half = ((1, 0), (1, 1), (2, 0), (2, 1), (3, 0), (3, 1))[n]
        ref = self.at(partner(t, peer), half)
        k = self.base + n
        return remote(ref, ref, self.ssem.at[k], self.rsem.at[k], (s, d, t))

    def start(self):
        self.mine(0).start()
        self.mine(3).start()
        self.mine(1).start()
        self.mine(2).start()

    def forward(self):
        self.arriving(0).wait_recv()
        self.mine(4).start()
        self.arriving(3).wait_recv()
        self.mine(5).start()

    def ready(self, k):
        if k == 1:
            self.arriving(1).wait_recv()
        elif k == 2:
            self.arriving(2).wait_recv()
        else:
            self.arriving(4).wait_recv()
            self.arriving(5).wait_recv()

    def drain(self):
        for n in range(6):
            self.mine(n).wait_send()


class Scatter:
    def __init__(self, part, got, via, rows, ssem, rsem, base, where):
        self.part, self.got, self.via, self.half = part, got, via, rows // 2
        self.ssem, self.rsem, self.base, self.where = ssem, rsem, base, where

    def copy(self, n):
        s, d, t = self.where
        h = self.half
        h0, h1 = pl.ds(0, h), pl.ds(h, h)
        src, dst, to = (
            (self.part.at[2, h0], self.via.at[0], 2),
            (self.part.at[2, h1], self.via.at[1], 1),
            (self.part.at[0, h1], self.got.at[0, h1], 1),
            (self.part.at[1, h0], self.got.at[1, h0], 2),
            (self.part.at[0, h0], self.got.at[0, h0], 1),
            (self.part.at[1, h1], self.got.at[1, h1], 2),
        )[n]
        k = self.base + n
        return remote(src, dst, self.ssem.at[k], self.rsem.at[k], (s, d, partner(t, to)))

    def put(self, k, value):
        self.part[k - 1] = value.astype(bf16)
        self.send(k)

    def send(self, k):
        if k == 3:
            self.copy(0).start()
            self.copy(1).start()
        elif k == 2:
            self.copy(3).start()
        else:
            self.copy(2).start()

    def combine(self):
        h = self.half
        self.copy(0).wait_recv()
        self.part[0, 0:h] = (self.part[0, 0:h].astype(f32) + self.via[0].astype(f32)).astype(bf16)
        self.copy(4).start()
        self.copy(1).wait_recv()
        self.part[1, h:] = (self.part[1, h:].astype(f32) + self.via[1].astype(f32)).astype(bf16)
        self.copy(5).start()

    def result(self):
        for n in (2, 3, 4, 5):
            self.copy(n).wait_recv()
        return self.got[0].astype(f32) + self.got[1].astype(f32)

    def drain(self):
        for n in range(6):
            self.copy(n).wait_send()


def prep_kernel(wi, wo, wfi, wfo, all_wi, all_wo, all_wfi, all_wfo, lsem, ssem, rsem):
    s, d, t = place()
    entry(1, s, d, t, core=True)
    other = (1 - s, d, t)

    def shard(p):
        return all_wo.at[s, rows_of(p, WIDTH)]

    def theirs(p):
        return all_wo.at[1 - s, rows_of(p, WIDTH)]

    pairs = ((wi, all_wi.at[s]), (wfi, all_wfi.at[s]), (wfo, all_wfo.at[s]), (wo, shard(t)))
    hops = [remote(wo, shard(t), ssem.at[6 + k], rsem.at[6 + k], (s, d, partner(t, k))) for k in (1, 2, 3)]
    for hop in hops:
        hop.start()
    over = [remote(src, dst, ssem.at[n], rsem.at[n], other) for n, (src, dst) in enumerate(pairs)]
    own = [pltpu.make_async_copy(src, dst, lsem.at[n]) for n, (src, dst) in enumerate(pairs)]
    for copy in over + own:
        copy.start()
    passed = []
    for k in (1, 2, 3):
        p = partner(t, k)
        remote(wo, shard(p), ssem.at[6 + k], rsem.at[6 + k], other).wait_recv()
        copy = remote(shard(p), shard(p), ssem.at[3 + k], rsem.at[3 + k], other)
        copy.start()
        passed.append(copy)
    for copy in own:
        copy.wait()
    incoming = (all_wi.at[1 - s], all_wfi.at[1 - s], all_wfo.at[1 - s], theirs(t))
    for n, dst in enumerate(incoming):
        remote(dst, dst, ssem.at[n], rsem.at[n], other).wait_recv()
    for k in (1, 2, 3):
        dst = theirs(partner(t, k))
        remote(dst, dst, ssem.at[3 + k], rsem.at[3 + k], other).wait_recv()
    for copy in over + passed + hops:
        copy.wait_send()


def share_weights(wi, wo, wfi, wfo):
    fp = wfo.shape[0]
    outs = (
        jax.ShapeDtypeStruct((2, D, 4 * WIDTH), bf16),
        jax.ShapeDtypeStruct((2, D, D), bf16),
        jax.ShapeDtypeStruct((2, 2, D, fp), bf16),
        jax.ShapeDtypeStruct((2, fp, D), bf16),
    )
    return pl.pallas_call(
        prep_kernel,
        out_shape=outs,
        in_specs=[ANY] * 4,
        out_specs=(ANY,) * 4,
        scratch_shapes=[
            pltpu.SemaphoreType.DMA((4,)),
            pltpu.SemaphoreType.DMA((10,)),
            pltpu.SemaphoreType.DMA((10,)),
        ],
        compiler_params=pltpu.CompilerParams(collective_id=0, has_side_effects=True),
        name="share_weights",
    )(wi, wo, wfi, wfo)


def scalar_table(starts, rates, dp, blocks):
    d = lax.axis_index("dp")
    survive = 1.0 - starts.astype(f32).reshape(dp, blocks)
    decay = jnp.exp(-rates * BLOCK)
    factor = jnp.prod(survive, axis=1)[:, None] * (decay**blocks)[None, :]
    at = jnp.arange(dp)
    low, high = jnp.minimum(at, d), jnp.maximum(at, d)
    between = (at[None, :] > low[:, None]) & (at[None, :] < high[:, None])
    through = jnp.prod(jnp.where(between[:, :, None], factor[None], 1.0), axis=1)
    forward = jnp.where((at < d)[:, None], through, 0.0)
    backward = jnp.where((at > d)[:, None], through, 0.0)
    mine = lax.dynamic_index_in_dim(survive, d, 0, keepdims=False)
    return jnp.concatenate([mine, rates, decay, forward.reshape(-1), backward.reshape(-1)])


def decay_fill(scal, nb, mask, mask_t, qd, kd):
    for h in range(HEADS_HERE):
        r = scal[nb + h]
        i = lax.broadcasted_iota(jnp.int32, (BLOCK, BLOCK), 0).astype(f32)
        j = lax.broadcasted_iota(jnp.int32, (BLOCK, BLOCK), 1).astype(f32)
        gap = i - j
        mask[h] = jnp.where(gap >= 0.0, jnp.exp(-r * jnp.maximum(gap, 0.0)), 0.0)
        if mask_t is not None:
            mask_t[h] = jnp.where(gap <= 0.0, jnp.exp(-r * jnp.maximum(-gap, 0.0)), 0.0)
        i = lax.broadcasted_iota(jnp.int32, (BLOCK, HEAD), 0).astype(f32)
        qd[h] = jnp.exp(-r * (i + 1.0))
        kd[h] = jnp.exp(-r * (BLOCK - 1.0 - i))


def head(h):
    return slice(h * HEAD, (h + 1) * HEAD)


def send_states(dp, where, zout, zin, zs, zr, later):
    s, d, t = where

    def each(k, c):
        to = d + k if later else d - k

        @pl.when((to < dp) if later else (to >= 0))
        def _():
            remote(zout, zin.at[d], zs.at[k], zr.at[d], (s, to, t)).start()

        return c

    lax.fori_loop(1, dp, each, 0)


def sent_states(dp, where, zout, zin, zs, zr, later):
    s, d, t = where

    def each(k, c):
        to = d + k if later else d - k

        @pl.when((to < dp) if later else (to >= 0))
        def _():
            remote(zout, zin.at[d], zs.at[k], zr.at[d], (s, to, t)).wait_send()

        return c

    lax.fori_loop(1, dp, each, 0)


def take_states(dp, where, zout, zin, zs, zr, later, scal, base, run):
    s, d, t = where
    run[...] = jnp.zeros_like(run)

    def each(k, c):
        @pl.when((k < d) if later else (k > d))
        def _():
            remote(zout, zin.at[k], zs.at[0], zr.at[k], (s, d, t)).wait_recv()
            for h in range(HEADS_HERE):
                run[h] += scal[base + 2 * k + h] * zin[k, h].astype(f32)

        return c

    lax.fori_loop(0, dp, each, 0)


def forward_kernel(
    dp, layer, first, x_in, all_wi, all_wo, all_wfi, all_wfo, cos2, sin2, scal,
    y_out, hidden_o, zq_o, zk_o, gate_o, q_o, k_o, v_o, att_o, sc_o, states_o, branch_o, mid_o,
    hid2_o, pair_o,
    wi, wo, wfi, wfo, cosv, sinv, xf, hidden, zq, zk, gate, q, k, v, att, sc, states, branch, mid, hid2,
    pair, mask, qd, kd, loc, zout, zin, run, u, y, part, got, via, ssq, own, yb,
    lsem, ssem, rsem, zs, zr,
):
    where = s, d, t = place()
    rows = x_in.shape[-2]
    total = 4 * rows
    nb = total // BLOCK
    local = Sems(lsem)

    def load(src, dst):
        copy = pltpu.make_async_copy(src, dst, local.take())
        copy.start()
        return copy

    x_src = x_in.at[s] if first else x_in
    got_x = load(x_src, xf.at[rows_of(t, rows)])
    got_wi = load(all_wi.at[layer], wi)
    got_cos, got_sin = load(cos2, cosv), load(sin2, sinv)
    got_wo = load(all_wo.at[layer], wo)
    got_wfi = load(all_wfi.at[layer], wfi)
    got_wfo = load(all_wfo.at[layer], wfo)
    entry(dp, s, d, t)
    got_x.wait()

    half = rows // 2
    gx = Gather(
        lambda p, h: xf.at[pl.ds(pl.multiple_of(p * rows + h * half, half), half)],
        half, ssem, rsem, 0, where,
    )
    gx.start()
    decay_fill(scal, nb, mask, None, qd, kd)
    got_wi.wait()
    got_cos.wait()
    got_sin.wait()

    def project(i, c):
        for n in (1, 2, 3):

            @pl.when(i == n)
            def _(n=n):
                if n == 1:
                    gx.forward()
                gx.ready(n)

        r = rows_of(partner(t, i), rows)
        xv = xf[r, :].astype(f32)
        hid = (xv * rms_scale(xv)).astype(bf16)
        hidden[r, :] = hid
        cs, sn = cosv[r, :], sinv[r, :]
        for n, (pre, post) in enumerate(((zq, q), (zk, k))):
            z = nn(hid, wi[:, n * WIDTH : (n + 1) * WIDTH])
            pre[r, :] = z
            a = z * sig(z)
            for h in range(HEADS_HERE):
                ah = a[:, head(h)]
                post[r, head(h)] = (ah * cs + pltpu.roll(ah, HEAD // 2, 1) * sn).astype(bf16)
        v[r, :] = nn(hid, wi[:, 2 * WIDTH : 3 * WIDTH]).astype(bf16)
        gate[r, :] = nn(hid, wi[:, 3 * WIDTH :])
        return c

    lax.fori_loop(0, 4, project, 0)
    stores = [load(hidden, hidden_o), load(zq, zq_o), load(zk, zk_o), load(gate, gate_o)]
    stores += [load(q, q_o), load(k, k_o), load(v, v_o)]

    def local_state(b, c):
        r = rows_of(b, BLOCK)
        for h in range(HEADS_HERE):
            kdec = (k[r, head(h)].astype(f32) * kd[h]).astype(bf16)
            loc[b, h] = tn(kdec, v[r, head(h)])
        return c

    lax.fori_loop(0, nb, local_state, 0)
    for h in range(HEADS_HERE):
        carried = loc[0, h]
        for b in range(1, nb):
            carried = (scal[nb + 2 + h] * scal[b]) * carried + loc[b, h]
        zout[h] = carried.astype(bf16)
    send_states(dp, where, zout, zin, zs, zr, True)

    def inner(b, c):
        r = rows_of(b, BLOCK)
        for h in range(HEADS_HERE):
            w = (nt(q[r, head(h)], k[r, head(h)]) * mask[h]).astype(bf16)
            att[r, head(h)] = nn(w, v[r, head(h)])
        return c

    lax.fori_loop(0, nb, inner, 0)
    take_states(dp, where, zout, zin, zs, zr, True, scal, nb + 4, run)

    def outer(b, c):
        r = rows_of(b, BLOCK)
        for h in range(HEADS_HERE):
            entering = scal[b] * run[h]
            states[b, h] = entering
            run[h] = scal[nb + 2 + h] * entering + loc[b, h]
            qdec = (q[r, head(h)].astype(f32) * qd[h]).astype(bf16)
            a = att[r, head(h)] + nn(qdec, entering.astype(bf16))
            att[r, head(h)] = a
            u[t, r, head(h)] = (a * gate[r, head(h)]).astype(bf16)
        return c

    lax.fori_loop(0, nb, outer, 0)

    hu = total // 2
    gu = Gather(lambda p, h: u.at[p, pl.ds(h * hu, hu)], hu, ssem, rsem, 6, where)
    gu.start()
    for b in range(nb):
        a = att[b * BLOCK : (b + 1) * BLOCK, :]
        ssq[0, :, b * BLOCK : (b + 1) * BLOCK] = lax.dot_general(
            jnp.ones((8, WIDTH), f32), a * a, (((1,), (1,)), ((), ())),
            preferred_element_type=f32, precision=lax.Precision.HIGHEST,
        )
    sums = [
        remote(ssq.at[0], ssq.at[n], ssem.at[11 + n], rsem.at[11 + n], (s, d, partner(t, n)))
        for n in (1, 2, 3)
    ]
    for copy in sums:
        copy.start()
    stores += [load(att, att_o), load(states, states_o)]
    got_wo.wait()
    y[...] = jnp.zeros_like(y)

    def out_project(i, c):
        for n in (1, 2, 3):

            @pl.when(i == n)
            def _(n=n):
                if n == 1:
                    gu.forward()
                gu.ready(n)

        p = partner(t, i)

        def chunk(m, c):
            r = rows_of(m, rows)
            y[r, :] += nn(u[p, r, :], wo[rows_of(p, WIDTH), :])
            return c

        return lax.fori_loop(0, 4, chunk, c)

    lax.fori_loop(0, 4, out_project, 0)
    for copy in sums:
        copy.wait_recv()
    whole = ssq[0] + ssq[1] + ssq[2] + ssq[3]
    sc[...] = jnp.transpose(lax.rsqrt(whole * (1.0 / D) + norm_eps))
    got_wfi.wait()
    got_wfo.wait()
    out = Scatter(part, got, via, rows, ssem, rsem, 15, where)

    def feed(i, c):
        e = 3 - i
        r = rows_of(partner(t, e), rows)
        br = sc[r, 0:1] * y[r, :]
        branch[r, :] = br.astype(bf16)
        m = xf[r, :].astype(f32) + br
        h2 = (m * rms_scale(m)).astype(bf16)
        hid2[r, :] = h2
        p0, p1 = nn(h2, wfi[0]), nn(h2, wfi[1])
        pair[0, r, :] = p0
        pair[1, r, :] = p1
        o = nn((p0 * p1).astype(bf16), wfo[...])
        for n in (1, 2, 3):

            @pl.when(e == n)
            def _(n=n):
                out.put(n, o)

        @pl.when(e == 0)
        def _():
            mid[...] = m
            own[...] = o + m

        return c

    lax.fori_loop(0, 4, feed, 0)
    stores += [load(sc, sc_o), load(branch, branch_o), load(mid, mid_o), load(hid2, hid2_o)]
    stores += [load(pair, pair_o)]
    out.combine()
    yb[...] = (own[...] + out.result()).astype(bf16)
    stores += [load(yb, y_out)]
    gx.drain()
    gu.drain()
    out.drain()
    for copy in sums:
        copy.wait_send()
    sent_states(dp, where, zout, zin, zs, zr, True)
    for copy in stores:
        copy.wait()


def layer_forward(layer, first, x, weights, cos2, sin2, scal, dp, uid):
    rows = x.shape[-2]
    total = 4 * rows
    nb = total // BLOCK
    fp = weights[3].shape[1]
    saved = [
        ((rows, D), bf16), ((total, D), bf16), ((total, WIDTH), f32), ((total, WIDTH), f32),
        ((total, WIDTH), f32), ((total, WIDTH), bf16), ((total, WIDTH), bf16),
        ((total, WIDTH), bf16), ((total, WIDTH), f32), ((total, 8), f32),
        ((nb, HEADS_HERE, HEAD, HEAD), f32), ((total, D), bf16), ((rows, D), f32),
        ((total, D), bf16), ((2, total, fp), f32),
    ]
    scratch = [
        ((D, 4 * WIDTH), bf16), ((D, D), bf16), ((2, D, fp), bf16), ((fp, D), bf16),
        ((total, HEAD), f32), ((total, HEAD), f32), ((total, D), bf16),
    ]
    scratch += saved[1:]
    scratch += [
        ((HEADS_HERE, BLOCK, BLOCK), f32), ((HEADS_HERE, BLOCK, HEAD), f32),
        ((HEADS_HERE, BLOCK, HEAD), f32), ((nb, HEADS_HERE, HEAD, HEAD), f32),
        ((HEADS_HERE, HEAD, HEAD), bf16), ((dp, HEADS_HERE, HEAD, HEAD), bf16),
        ((HEADS_HERE, HEAD, HEAD), f32), ((4, total, WIDTH), bf16), ((total, D), f32),
        ((3, rows, D), bf16), ((2, rows, D), bf16), ((2, rows // 2, D), bf16),
        ((4, 8, total), f32), ((rows, D), f32), ((rows, D), bf16),
    ]
    flops = 2 * total * D * (4 * WIDTH + D + 3 * fp)
    return pl.pallas_call(
        functools.partial(forward_kernel, dp, layer, first),
        out_shape=tuple(jax.ShapeDtypeStruct(a, b) for a, b in saved),
        in_specs=[ANY] * 7 + [SMEM],
        out_specs=(ANY,) * len(saved),
        scratch_shapes=[pltpu.VMEM(a, b) for a, b in scratch]
        + [
            pltpu.SemaphoreType.DMA((24,)),
            pltpu.SemaphoreType.DMA((21,)),
            pltpu.SemaphoreType.DMA((21,)),
            pltpu.SemaphoreType.DMA((dp,)),
            pltpu.SemaphoreType.DMA((dp,)),
        ],
        compiler_params=pltpu.CompilerParams(
            collective_id=uid, has_side_effects=True, vmem_limit_bytes=VMEM_BYTES
        ),
        cost_estimate=pl.CostEstimate(flops=flops, bytes_accessed=20 << 20, transcendentals=0),
        name="layer_forward",
    )(x, *weights, cos2, sin2, scal)


def backward_kernel(
    dp, layer, last, first, g_in, x_in, all_wi, all_wo, all_wfi, all_wfo, cos2, sin2, scal,
    hidden_i, zq_i, zk_i, gate_i, q_i, k_i, v_i, att_i, sc_i, states_i, branch_i, mid_i, hid2_i, pair_i,
    g_out, gwi_o, gwo_o, gwfi_o, gwfo_o,
    wi, wo, wfi, wfo, cosv, sinv, gf, xr, hidden, zq, zk, gate, q, k, v, att, sc, states, branch, mid,
    hid2, pair, mask, mask_t, qd, kd, terms, zout, zin, run, gpair, prod, gb, gm, gated, gatt, dv, dk, gp,
    part, got, via, part2, got2, via2, own, own2, gwi, gwo, gwfi, gwfo, gr,
    lsem, ssem, rsem, zs, zr,
):
    where = s, d, t = place()
    rows = g_out.shape[0]
    total = 4 * rows
    nb = total // BLOCK
    local = Sems(lsem)

    def load(src, dst):
        copy = pltpu.make_async_copy(src, dst, local.take())
        copy.start()
        return copy

    got_g = load(g_in.at[s] if last else g_in, gf.at[rows_of(t, rows)])
    early = [load(all_wfo.at[layer], wfo), load(pair_i, pair), load(all_wfi.at[layer], wfi)]
    mids = [load(mid_i, mid), load(hid2_i, hid2)]
    gates = [
        load(all_wo.at[layer, rows_of(t, WIDTH)], wo), load(branch_i, branch), load(sc_i, sc),
        load(att_i, att), load(gate_i, gate),
    ]
    attn = [
        load(q_i, q), load(k_i, k), load(v_i, v), load(states_i, states), load(cos2, cosv),
        load(sin2, sinv), load(zq_i, zq), load(zk_i, zk),
    ]
    ends = [
        load(all_wi.at[layer], wi), load(hidden_i, hidden), load(x_in.at[s] if first else x_in, xr)
    ]
    entry(dp, s, d, t)
    got_g.wait()
    half = rows // 2

    def block_of(ref):
        return lambda p, h: ref.at[pl.ds(pl.multiple_of(p * rows + h * half, half), half)]

    gg = Gather(block_of(gf), half, ssem, rsem, 0, where)
    gg.start()
    decay_fill(scal, nb, mask, mask_t, qd, kd)
    for copy in early:
        copy.wait()
    sums = Scatter(part, got, via, rows, ssem, rsem, 6, where)

    def feed(i, c):
        for n in (1, 2, 3):

            @pl.when(i == n)
            def _(n=n):
                if n == 1:
                    gg.forward()
                gg.ready(n)

        r = rows_of(partner(t, i), rows)
        grad = nt(gf[r, :], wfo[...])
        p0, p1 = pair[0, r, :], pair[1, r, :]
        prod[r, :] = (p0 * p1).astype(bf16)
        g0, g1 = (grad * p1).astype(bf16), (grad * p0).astype(bf16)
        gpair[0, r, :] = g0
        gpair[1, r, :] = g1
        o = nt(g0, wfi[0]) + nt(g1, wfi[1])
        for n in (1, 2, 3):

            @pl.when(i == n)
            def _(n=n):
                sums.put(n, o)

        @pl.when(i == 0)
        def _():
            own[...] = o

        return c

    lax.fori_loop(0, 4, feed, 0)
    sums.combine()
    for copy in mids:
        copy.wait()
    fp = wfo.shape[0]

    def feed_weights(n, c):
        cols = rows_of(n, 256)
        a = hid2[:, cols]
        gwfi[0, cols, :] = tn(a, gpair[0]).astype(bf16)
        gwfi[1, cols, :] = tn(a, gpair[1]).astype(bf16)
        return c

    def out_weights(n, c):
        cols = rows_of(n, 256)
        gwfo[cols, :] = tn(prod[:, cols], gf[...]).astype(bf16)
        return c

    lax.fori_loop(0, D // 256, feed_weights, 0)
    lax.fori_loop(0, fp // 256, out_weights, 0)
    stores = [load(gwfi, gwfi_o), load(gwfo, gwfo_o)]
    me = rows_of(t, rows)
    grad_middle = gf[me, :].astype(f32) + norm_back(mid[...], own[...] + sums.result())
    gm[...] = grad_middle
    gb[me, :] = grad_middle.astype(bf16)

    gbg = Gather(block_of(gb), half, ssem, rsem, 12, where)
    gbg.start()
    for copy in gates:
        copy.wait()

    def gating(i, c):
        for n in (1, 2, 3):

            @pl.when(i == n)
            def _(n=n):
                if n == 1:
                    gbg.forward()
                gbg.ready(n)

        r = rows_of(partner(t, i), rows)
        b = gb[r, :]
        grad = nt(b, wo[...])
        dots = jnp.sum(b.astype(f32) * branch[r, :].astype(f32), axis=-1, keepdims=True) * (1.0 / D)
        scale = sc[r, 0:1]
        normed = att[r, :] * scale
        gt = gate[r, :]
        gp[r, 3 * WIDTH :] = (grad * normed).astype(bf16)
        gated[r, :] = (normed * gt).astype(bf16)
        gatt[r, :] = (scale * (grad * gt - normed * dots)).astype(bf16)
        return c

    lax.fori_loop(0, 4, gating, 0)
    for copy in attn:
        copy.wait()

    def term(b, c):
        r = rows_of(b, BLOCK)
        for h in range(HEADS_HERE):
            qdec = (q[r, head(h)].astype(f32) * qd[h]).astype(bf16)
            terms[b, h] = tn(qdec, gatt[r, head(h)])
        return c

    lax.fori_loop(0, nb, term, 0)
    for h in range(HEADS_HERE):
        carried = scal[nb - 1] * terms[nb - 1, h]
        for b in reversed(range(nb - 1)):
            carried = scal[b] * (terms[b, h] + scal[nb + 2 + h] * carried)
        zout[h] = carried.astype(bf16)
    send_states(dp, where, zout, zin, zs, zr, False)

    def unturn(pre, grad, r, h):
        back = grad * cosv[r, :] - pltpu.roll(grad, HEAD // 2, 1) * sinv[r, :]
        z = pre[r, head(h)]
        g = sig(z)
        return (back * (g * (1.0 + z * (1.0 - g)))).astype(bf16)

    def inner(b, c):
        r = rows_of(b, BLOCK)
        for h in range(HEADS_HERE):
            qh, kh, vh, gh = q[r, head(h)], k[r, head(h)], v[r, head(h)], gatt[r, head(h)]
            w_t = (nt(kh, qh) * mask_t[h]).astype(bf16)
            dv[r, head(h)] = nn(w_t, gh)
            ds = (nt(gh, vh) * mask[h]).astype(bf16)
            ds_t = (nt(vh, gh) * mask_t[h]).astype(bf16)
            dk[r, head(h)] = nn(ds_t, qh)
            dq = nn(ds, kh) + nt(gh, states[b, h].astype(bf16)) * qd[h]
            gp[r, head(h)] = unturn(zq, dq, r, h)
        return c

    lax.fori_loop(0, nb, inner, 0)
    take_states(dp, where, zout, zin, zs, zr, False, scal, nb + 4 + 2 * dp, run)

    def outer(i, c):
        b = nb - 1 - i
        r = rows_of(b, BLOCK)
        for h in range(HEADS_HERE):
            after = run[h]
            low = after.astype(bf16)
            run[h] = scal[b] * (terms[b, h] + scal[nb + 2 + h] * after)
            kdec = (k[r, head(h)].astype(f32) * kd[h]).astype(bf16)
            dkh = dk[r, head(h)] + nt(v[r, head(h)], low) * kd[h]
            k_cols = slice(WIDTH + h * HEAD, WIDTH + (h + 1) * HEAD)
            v_cols = slice(2 * WIDTH + h * HEAD, 2 * WIDTH + (h + 1) * HEAD)
            gp[r, k_cols] = unturn(zk, dkh, r, h)
            gp[r, v_cols] = (dv[r, head(h)] + nn(kdec, low)).astype(bf16)
        return c

    lax.fori_loop(0, nb, outer, 0)
    for copy in ends:
        copy.wait()
    ins = Scatter(part2, got2, via2, rows, ssem, rsem, 18, where)

    def back_in(i, c):
        e = 3 - i
        r = rows_of(partner(t, e), rows)
        o = nt(gp[r, :], wi[...])
        for n in (1, 2, 3):

            @pl.when(e == n)
            def _(n=n):
                ins.put(n, o)

        @pl.when(e == 0)
        def _():
            own2[...] = o

        return c

    lax.fori_loop(0, 4, back_in, 0)
    ins.combine()

    def in_weights(n, c):
        cols = rows_of(n, 256)
        gwi[cols, :] = tn(hidden[:, cols], gp[...]).astype(bf16)
        return c

    lax.fori_loop(0, D // 256, in_weights, 0)
    gwo[...] = tn(gated[...], gb[...]).astype(bf16)
    stores += [load(gwi, gwi_o), load(gwo, gwo_o)]
    dx = gm[...] + norm_back(xr[...].astype(f32), own2[...] + ins.result())
    gr[...] = dx.astype(bf16)
    stores += [load(gr, g_out)]
    gg.drain()
    sums.drain()
    gbg.drain()
    ins.drain()
    sent_states(dp, where, zout, zin, zs, zr, False)
    for copy in stores:
        copy.wait()


def layer_backward(layer, last, first, g, x, weights, cos2, sin2, scal, saved, dp, uid):
    rows = g.shape[-2]
    total = 4 * rows
    nb = total // BLOCK
    fp = weights[3].shape[1]
    outs = [
        ((rows, D), bf16), ((D, 4 * WIDTH), bf16), ((WIDTH, D), bf16), ((2, D, fp), bf16), ((fp, D), bf16)
    ]
    scratch = [
        ((D, 4 * WIDTH), bf16), ((WIDTH, D), bf16), ((2, D, fp), bf16), ((fp, D), bf16),
        ((total, HEAD), f32), ((total, HEAD), f32), ((total, D), bf16), ((rows, D), bf16),
    ]
    scratch += [(a.shape, a.dtype) for a in saved]
    scratch += [
        ((HEADS_HERE, BLOCK, BLOCK), f32), ((HEADS_HERE, BLOCK, BLOCK), f32),
        ((HEADS_HERE, BLOCK, HEAD), f32), ((HEADS_HERE, BLOCK, HEAD), f32),
        ((nb, HEADS_HERE, HEAD, HEAD), f32), ((HEADS_HERE, HEAD, HEAD), bf16),
        ((dp, HEADS_HERE, HEAD, HEAD), bf16), ((HEADS_HERE, HEAD, HEAD), f32),
        ((2, total, fp), bf16), ((total, fp), bf16), ((total, D), bf16), ((rows, D), f32),
        ((total, WIDTH), bf16), ((total, WIDTH), bf16), ((total, WIDTH), f32), ((total, WIDTH), f32),
        ((total, 4 * WIDTH), bf16),
        ((3, rows, D), bf16), ((2, rows, D), bf16), ((2, rows // 2, D), bf16),
        ((3, rows, D), bf16), ((2, rows, D), bf16), ((2, rows // 2, D), bf16),
        ((rows, D), f32), ((rows, D), f32),
        ((D, 4 * WIDTH), bf16), ((WIDTH, D), bf16), ((2, D, fp), bf16), ((fp, D), bf16), ((rows, D), bf16),
    ]
    flops = 4 * total * D * (4 * WIDTH + WIDTH + 3 * fp)
    return pl.pallas_call(
        functools.partial(backward_kernel, dp, layer, last, first),
        out_shape=tuple(jax.ShapeDtypeStruct(a, b) for a, b in outs),
        in_specs=[ANY] * 8 + [SMEM] + [ANY] * len(saved),
        out_specs=(ANY,) * len(outs),
        scratch_shapes=[pltpu.VMEM(a, b) for a, b in scratch]
        + [
            pltpu.SemaphoreType.DMA((30,)),
            pltpu.SemaphoreType.DMA((24,)),
            pltpu.SemaphoreType.DMA((24,)),
            pltpu.SemaphoreType.DMA((dp,)),
            pltpu.SemaphoreType.DMA((dp,)),
        ],
        compiler_params=pltpu.CompilerParams(
            collective_id=uid, has_side_effects=True, vmem_limit_bytes=VMEM_BYTES
        ),
        cost_estimate=pl.CostEstimate(flops=flops, bytes_accessed=30 << 20, transcendentals=0),
        name="layer_backward",
    )(g, x, *weights, cos2, sin2, scal, *saved)


def angle_tables(starts, blocks):
    d = lax.axis_index("dp")
    at = jnp.arange(starts.shape[0], dtype=jnp.int32)
    begins = jnp.max(
        jnp.where((at[None, :] <= at[:, None]) & (starts > 0)[None, :], at[None, :], 0), axis=1
    )
    offsets = lax.dynamic_slice_in_dim((at - begins) * BLOCK, d * blocks, blocks)
    places = (offsets[:, None] + jnp.arange(BLOCK, dtype=jnp.int32)[None, :]).reshape(-1)
    lane = jnp.arange(HEAD, dtype=jnp.int32)
    frequency = 10000.0 ** (-(lane % (HEAD // 2)).astype(f32) / (HEAD // 2))
    angles = places.astype(f32)[:, None] * frequency[None, :]
    return jnp.cos(angles), jnp.where(lane < HEAD // 2, -1.0, 1.0)[None, :] * jnp.sin(angles)


def swap(x):
    return lax.ppermute(x, "section", [(0, 1), (1, 0)])


def mine_first(s, a, b):
    return jnp.where(s == 0, a, b)


def core_halves(grads, s):
    total = []
    for g in grads:
        pieces = g.reshape((2, g.shape[0] // 2) + g.shape[1:])
        keep = lax.dynamic_index_in_dim(pieces, s, 0, keepdims=False)
        give = lax.dynamic_index_in_dim(pieces, 1 - s, 0, keepdims=False)
        total.append((keep.astype(f32) + swap(give).astype(f32)).astype(bf16))
    return lax.psum(tuple(total), "dp")


def shards(tokens, cotangent, mixer_in, mixer_out, feed_in, feed_out, decay_rate, block_starts):
    s = lax.axis_index("section")
    dp = lax.axis_size("dp")
    rows = tokens.shape[1]
    blocks = 4 * rows // BLOCK
    ff = feed_out.shape[1]
    fp = -(-ff // 256) * 256
    wi = mixer_in[0].reshape(D, 4 * WIDTH)
    wfi = jnp.pad(jnp.swapaxes(feed_in[0], 0, 1), ((0, 0), (0, 0), (0, fp - ff)))
    wfo = jnp.pad(feed_out[0], ((0, fp - ff), (0, 0)))
    weights = share_weights(wi, mixer_out[0], wfi, wfo)
    other_rates = swap(decay_rate[0])
    rates = (mine_first(s, decay_rate[0], other_rates), mine_first(s, other_rates, decay_rate[0]))
    starts = lax.dynamic_index_in_dim(block_starts, s, 0, keepdims=False)
    cos2, sin2 = angle_tables(starts, blocks)
    scal = [scalar_table(starts, r, dp, blocks) for r in rates]

    y0, *saved0 = layer_forward(0, True, tokens, weights, cos2, sin2, scal[0], dp, 1)
    y1, *saved1 = layer_forward(1, False, y0, weights, cos2, sin2, scal[1], dp, 2)
    g1, *grads1 = layer_backward(1, True, False, cotangent, y0, weights, cos2, sin2, scal[1], saved1, dp, 3)
    half1 = core_halves((grads1[0], grads1[1], grads1[2], grads1[3]), s)
    g0, *grads0 = layer_backward(0, False, True, g1, tokens, weights, cos2, sin2, scal[0], saved0, dp, 4)
    half0 = core_halves((grads0[0], grads0[1], grads0[2], grads0[3]), s)

    theirs = swap(jnp.stack([mine_first(s, y1, y0), mine_first(s, g1, g0)]))
    keep_y, keep_g = mine_first(s, y0, y1), mine_first(s, g0, g1)
    outputs = jnp.stack([mine_first(s, keep_y, theirs[0]), mine_first(s, theirs[0], keep_y)])
    in_grads = jnp.stack([mine_first(s, keep_g, theirs[1]), mine_first(s, theirs[1], keep_g)])
    full = []
    for h0, h1 in zip(half0, half1):
        got = swap(mine_first(s, h1, h0))
        kept = mine_first(s, h0, h1)
        full.append(
            jnp.stack([mine_first(s, kept, got), mine_first(s, got, kept)])
            .reshape((-1,) + h0.shape[1:])
            .astype(f32)
        )
    g_in = full[0].reshape(D, 4, WIDTH)
    g_feed_in = jnp.swapaxes(full[2].reshape(2, D, fp)[:, :, :ff], 0, 1)
    return (
        outputs[None], in_grads[None], g_in[None], full[1][None], g_feed_in[None], full[3][:ff][None]
    )


def solution(mesh):
    placed = (
        P(None, ("dp", "tensor"), None),
        P(None, ("dp", "tensor"), None),
        P("section", None, None, "tensor"),
        P("section", "tensor", None),
        P("section", None, None, "tensor"),
        P("section", "tensor", None),
        P("section", "tensor"),
        P(),
    )
    return jax.shard_map(
        shards,
        mesh=mesh,
        in_specs=placed,
        out_specs=(
            P("section", None, ("dp", "tensor"), None),
            P("section", None, ("dp", "tensor"), None),
            P("section", None, None, "tensor"),
            P("section", "tensor", None),
            P("section", None, None, "tensor"),
            P("section", "tensor", None),
        ),
        check_vma=False,
    )
```

```python
import functools

import jax
import jax.numpy as jnp
from jax import lax
from jax.experimental import pallas as pl
from jax.experimental.pallas import tpu as pltpu
from jax.sharding import PartitionSpec as P

D = 1024
HEAD = 128
BLOCK = 256
WIDTH = 256
HEADS_HERE = WIDTH // HEAD
norm_eps = 1e-06
MESH = pl.DeviceIdType.MESH
ANY = pl.BlockSpec(memory_space=pl.ANY)
SMEM = pl.BlockSpec(memory_space=pltpu.SMEM)
bf16, f32 = jnp.bfloat16, jnp.float32
VMEM_BYTES = 62 * 1024 * 1024


def place():
    return lax.axis_index("section"), lax.axis_index("dp"), lax.axis_index("tensor")


def partner(t, k):
    return ((t // 2 + k // 2) % 2) * 2 + (t + k) % 2


class Sems:
    def __init__(self, ref):
        self.ref, self.used = ref, 0

    def take(self):
        self.used += 1
        return self.ref.at[self.used - 1]


def remote(src, dst, send, recv, dev):
    return pltpu.make_async_remote_copy(
        src_ref=src, dst_ref=dst, send_sem=send, recv_sem=recv, device_id=dev, device_id_type=MESH
    )


def nn(a, b):
    return lax.dot_general(a, b, (((1,), (0,)), ((), ())), preferred_element_type=f32)


def nt(a, b):
    return lax.dot_general(a, b, (((1,), (1,)), ((), ())), preferred_element_type=f32)


def tn(a, b):
    return lax.dot_general(a, b, (((0,), (0,)), ((), ())), preferred_element_type=f32)


def rms_scale(v):
    return lax.rsqrt(jnp.mean(v * v, axis=-1, keepdims=True) + norm_eps)


def norm_back(v, u):
    q = rms_scale(v)
    n = v * q
    return q * (u - n * jnp.mean(u * n, axis=-1, keepdims=True))


def sig(v):
    return 1.0 / (1.0 + jnp.exp(-v))


def rows_of(p, n):
    return pl.ds(pl.multiple_of(p * n, n), n)


def entry(dp, s, d, t, core=False):
    barrier = pltpu.get_barrier_semaphore()
    count = 3
    for k in (1, 2, 3):
        pl.semaphore_signal(barrier, inc=1, device_id=(s, d, partner(t, k)), device_id_type=MESH)
    if core:
        pl.semaphore_signal(barrier, inc=1, device_id=(1 - s, d, t), device_id_type=MESH)
        count += 1
    if dp > 1:

        def greet(k, c):
            pl.semaphore_signal(
                barrier, inc=1, device_id=(s, (d + k) % dp, t), device_id_type=MESH
            )
            return c

        lax.fori_loop(1, dp, greet, 0)
        count += dp - 1
    pl.semaphore_wait(barrier, count)


class Gather:
    def __init__(self, block_at, half, ssem, rsem, base, where):
        self.at, self.half, self.ssem, self.rsem, self.base = block_at, half, ssem, rsem, base
        self.where = where

    def copy(self, n, peer, half, to):
        s, d, t = self.where
        ref = self.at(partner(t, peer), half)
        k = self.base + n
        return remote(ref, ref, self.ssem.at[k], self.rsem.at[k], (s, d, partner(t, to)))

    def mine(self, n):
        peer, half, to = ((0, 0, 1), (0, 1, 1), (0, 0, 2), (0, 1, 2), (1, 0, 2), (2, 1, 1))[n]
        return self.copy(n, peer, half, to)

    def arriving(self, n):
        s, d, t = self.where
        peer, half = ((1, 0), (1, 1), (2, 0), (2, 1), (3, 0), (3, 1))[n]
        ref = self.at(partner(t, peer), half)
        k = self.base + n
        return remote(ref, ref, self.ssem.at[k], self.rsem.at[k], (s, d, t))

    def start(self):
        self.mine(0).start()
        self.mine(3).start()
        self.mine(1).start()
        self.mine(2).start()

    def forward(self):
        self.arriving(0).wait_recv()
        self.mine(4).start()
        self.arriving(3).wait_recv()
        self.mine(5).start()

    def ready(self, k):
        if k == 1:
            self.arriving(1).wait_recv()
        elif k == 2:
            self.arriving(2).wait_recv()
        else:
            self.arriving(4).wait_recv()
            self.arriving(5).wait_recv()

    def drain(self):
        for n in range(6):
            self.mine(n).wait_send()


class Scatter:
    def __init__(self, part, got, via, rows, ssem, rsem, base, where):
        self.part, self.got, self.via, self.half = part, got, via, rows // 2
        self.ssem, self.rsem, self.base, self.where = ssem, rsem, base, where

    def copy(self, n):
        s, d, t = self.where
        h = self.half
        h0, h1 = pl.ds(0, h), pl.ds(h, h)
        src, dst, to = (
            (self.part.at[2, h0], self.via.at[0], 2),
            (self.part.at[2, h1], self.via.at[1], 1),
            (self.part.at[0, h1], self.got.at[0, h1], 1),
            (self.part.at[1, h0], self.got.at[1, h0], 2),
            (self.part.at[0, h0], self.got.at[0, h0], 1),
            (self.part.at[1, h1], self.got.at[1, h1], 2),
        )[n]
        k = self.base + n
        return remote(src, dst, self.ssem.at[k], self.rsem.at[k], (s, d, partner(t, to)))

    def put(self, k, value):
        self.part[k - 1] = value.astype(bf16)
        self.send(k)

    def send(self, k):
        if k == 3:
            self.copy(0).start()
            self.copy(1).start()
        elif k == 2:
            self.copy(3).start()
        else:
            self.copy(2).start()

    def combine(self):
        h = self.half
        self.copy(0).wait_recv()
        self.part[0, 0:h] = (self.part[0, 0:h].astype(f32) + self.via[0].astype(f32)).astype(bf16)
        self.copy(4).start()
        self.copy(1).wait_recv()
        self.part[1, h:] = (self.part[1, h:].astype(f32) + self.via[1].astype(f32)).astype(bf16)
        self.copy(5).start()

    def result(self):
        for n in (2, 3, 4, 5):
            self.copy(n).wait_recv()
        return self.got[0].astype(f32) + self.got[1].astype(f32)

    def drain(self):
        for n in range(6):
            self.copy(n).wait_send()


def scalar_table(starts, rates, dp, blocks):
    d = lax.axis_index("dp")
    survive = 1.0 - starts.astype(f32).reshape(dp, blocks)
    decay = jnp.exp(-rates * BLOCK)
    factor = jnp.prod(survive, axis=1)[:, None] * (decay**blocks)[None, :]
    at = jnp.arange(dp)
    low, high = jnp.minimum(at, d), jnp.maximum(at, d)
    between = (at[None, :] > low[:, None]) & (at[None, :] < high[:, None])
    through = jnp.prod(jnp.where(between[:, :, None], factor[None], 1.0), axis=1)
    forward = jnp.where((at < d)[:, None], through, 0.0)
    backward = jnp.where((at > d)[:, None], through, 0.0)
    mine = lax.dynamic_index_in_dim(survive, d, 0, keepdims=False)
    return jnp.concatenate([mine, rates, decay, forward.reshape(-1), backward.reshape(-1)])


def decay_fill(scal, base, nb, mask, mask_t, qd, kd):
    for h in range(HEADS_HERE):
        r = scal[base + nb + h]
        i = lax.broadcasted_iota(jnp.int32, (BLOCK, BLOCK), 0).astype(f32)
        j = lax.broadcasted_iota(jnp.int32, (BLOCK, BLOCK), 1).astype(f32)
        gap = i - j
        mask[h] = jnp.where(gap >= 0.0, jnp.exp(-r * jnp.maximum(gap, 0.0)), 0.0)
        if mask_t is not None:
            mask_t[h] = jnp.where(gap <= 0.0, jnp.exp(-r * jnp.maximum(-gap, 0.0)), 0.0)
        i = lax.broadcasted_iota(jnp.int32, (BLOCK, HEAD), 0).astype(f32)
        qd[h] = jnp.exp(-r * (i + 1.0))
        kd[h] = jnp.exp(-r * (BLOCK - 1.0 - i))


def head(h):
    return slice(h * HEAD, (h + 1) * HEAD)


def send_states(dp, where, zout, zin, zs, zr, later):
    s, d, t = where

    def each(k, c):
        to = d + k if later else d - k

        @pl.when((to < dp) if later else (to >= 0))
        def _():
            remote(zout, zin.at[d], zs.at[k], zr.at[d], (s, to, t)).start()

        return c

    lax.fori_loop(1, dp, each, 0)


def sent_states(dp, where, zout, zin, zs, zr, later):
    s, d, t = where

    def each(k, c):
        to = d + k if later else d - k

        @pl.when((to < dp) if later else (to >= 0))
        def _():
            remote(zout, zin.at[d], zs.at[k], zr.at[d], (s, to, t)).wait_send()

        return c

    lax.fori_loop(1, dp, each, 0)


def take_states(dp, where, zout, zin, zs, zr, later, scal, base, run):
    s, d, t = where
    run[...] = jnp.zeros_like(run)

    def each(k, c):
        @pl.when((k < d) if later else (k > d))
        def _():
            remote(zout, zin.at[k], zs.at[0], zr.at[k], (s, d, t)).wait_recv()
            for h in range(HEADS_HERE):
                run[h] += scal[base + 2 * k + h] * zin[k, h].astype(f32)

        return c

    lax.fori_loop(0, dp, each, 0)


class Fetch:
    def __init__(self, src, dst, owner, where, lsem, ssem, rsem):
        s, d, t = where
        self.owner = owner
        self.local = lambda: pltpu.make_async_copy(src, dst, lsem)
        self.far = lambda: remote(src, dst, ssem, rsem, (1 - s, d, t))

    def read(self):
        pl.when(self.owner)(lambda: self.local().start())

    def send(self):
        pl.when(self.owner)(lambda: self.far().start())

    def wait(self):
        pl.when(self.owner)(lambda: self.local().wait())
        pl.when(jnp.logical_not(self.owner))(lambda: self.far().wait_recv())

    def drain(self):
        pl.when(self.owner)(lambda: self.far().wait_send())


def to_owner(owner, where, src, own_dst, far_dst, lsem, ssem, rsem):
    s, d, t = where

    def far():
        return remote(src, far_dst, ssem, rsem, (1 - s, d, t))

    def local():
        return pltpu.make_async_copy(src, own_dst, lsem)

    def start():
        pl.when(owner)(lambda: local().start())
        pl.when(jnp.logical_not(owner))(lambda: far().start())

    def finish():
        @pl.when(owner)
        def _():
            local().wait()
            far().wait_recv()

        pl.when(jnp.logical_not(owner))(lambda: far().wait_send())

    return start, finish


def forward_kernel(
    dp, layer, first, x_in, my_wi, my_wo, my_wfi, my_wfo, cos2, sin2, scal,
    both_o, wi_o, wo_o, wfi_o, wfo_o, y_out, hidden_o, zq_o, zk_o, gate_o, q_o, k_o, v_o, att_o, sc_o, states_o, branch_o, mid_o,
    hid2_o, pair_o,
    wi, wo, wfi, wfo, cosv, sinv, xf, hidden, zq, zk, gate, q, k, v, att, sc, states, branch, mid, hid2,
    pair, mask, qd, kd, loc, zout, zin, run, u, y, part, got, via, ssq, own, yb,
    lsem, ssem, rsem, zs, zr, wl, ws, wr,
):
    where = s, d, t = place()
    rows = x_in.shape[-2]
    total = 4 * rows
    nb = total // BLOCK
    local = Sems(lsem)

    def load(src, dst):
        copy = pltpu.make_async_copy(src, dst, local.take())
        copy.start()
        return copy

    x_src = x_in.at[s] if first else x_in
    got_x = load(x_src, xf.at[rows_of(t, rows)])
    owner = s == layer
    ff = my_wfo.shape[0]
    pairs = (
        (my_wi, wi), (my_wo, wo.at[rows_of(t, WIDTH)]), (my_wfi, wfi), (my_wfo, wfo.at[pl.ds(0, ff)])
    )
    got_w = [
        Fetch(src, dst, owner, where, wl.at[n], ws.at[n], wr.at[n])
        for n, (src, dst) in enumerate(pairs)
    ]
    got_wi, got_wo, got_wfi, got_wfo = got_w
    got_wi.read()
    got_cos, got_sin = load(cos2, cosv), load(sin2, sinv)
    for fetch in got_w[1:]:
        fetch.read()
    wfo[ff:, :] = jnp.zeros_like(wfo[ff:, :])
    entry(dp, s, d, t, core=True)
    got_x.wait()

    half = rows // 2
    gx = Gather(
        lambda p, h: xf.at[pl.ds(pl.multiple_of(p * rows + h * half, half), half)],
        half, ssem, rsem, 0, where,
    )
    gx.start()
    for fetch in got_w:
        fetch.send()
    decay_fill(scal, 0, nb, mask, None, qd, kd)
    got_wi.wait()
    got_cos.wait()
    got_sin.wait()

    def project(i, c):
        for n in (1, 2, 3):

            @pl.when(i == n)
            def _(n=n):
                if n == 1:
                    gx.forward()
                gx.ready(n)

        r = rows_of(partner(t, i), rows)
        xv = xf[r, :].astype(f32)
        hid = (xv * rms_scale(xv)).astype(bf16)
        hidden[r, :] = hid
        cs, sn = cosv[r, :], sinv[r, :]
        for n, (pre, post) in enumerate(((zq, q), (zk, k))):
            z = nn(hid, wi[:, n * WIDTH : (n + 1) * WIDTH])
            pre[r, :] = z
            a = z * sig(z)
            for h in range(HEADS_HERE):
                ah = a[:, head(h)]
                post[r, head(h)] = (ah * cs + pltpu.roll(ah, HEAD // 2, 1) * sn).astype(bf16)
        v[r, :] = nn(hid, wi[:, 2 * WIDTH : 3 * WIDTH]).astype(bf16)
        gate[r, :] = nn(hid, wi[:, 3 * WIDTH :])
        return c

    lax.fori_loop(0, 4, project, 0)

    def wo_block(k, k_to, n, dev):
        ref = wo.at[rows_of(partner(t, k), WIDTH)]
        return remote(ref, ref, ws.at[n], wr.at[n], dev)

    def wo_out(k):
        return wo_block(0, k, 3 + k, (s, d, partner(t, k)))

    def wo_in(k):
        return wo_block(k, 0, 3 + k, (s, d, t))

    def wo_over(k):
        return wo_block(k, 0, 6 + k, (1 - s, d, t))

    @pl.when(owner)
    def _():
        got_wo.local().wait()
        for n in (1, 2, 3):
            wo_out(n).start()

    stores = [load(hidden, hidden_o), load(zq, zq_o), load(zk, zk_o), load(gate, gate_o)]
    stores += [load(q, q_o), load(k, k_o), load(v, v_o)]

    def local_state(b, c):
        r = rows_of(b, BLOCK)
        for h in range(HEADS_HERE):
            kdec = (k[r, head(h)].astype(f32) * kd[h]).astype(bf16)
            loc[b, h] = tn(kdec, v[r, head(h)])
        return c

    lax.fori_loop(0, nb, local_state, 0)
    for h in range(HEADS_HERE):
        carried = loc[0, h]
        for b in range(1, nb):
            carried = (scal[nb + 2 + h] * scal[b]) * carried + loc[b, h]
        zout[h] = carried.astype(bf16)
    send_states(dp, where, zout, zin, zs, zr, True)

    def inner(b, c):
        r = rows_of(b, BLOCK)
        for h in range(HEADS_HERE):
            w = (nt(q[r, head(h)], k[r, head(h)]) * mask[h]).astype(bf16)
            att[r, head(h)] = nn(w, v[r, head(h)])
        return c

    lax.fori_loop(0, nb, inner, 0)
    take_states(dp, where, zout, zin, zs, zr, True, scal, nb + 4, run)

    def outer(b, c):
        r = rows_of(b, BLOCK)
        for h in range(HEADS_HERE):
            entering = scal[b] * run[h]
            states[b, h] = entering
            run[h] = scal[nb + 2 + h] * entering + loc[b, h]
            qdec = (q[r, head(h)].astype(f32) * qd[h]).astype(bf16)
            a = att[r, head(h)] + nn(qdec, entering.astype(bf16))
            att[r, head(h)] = a
            u[t, r, head(h)] = (a * gate[r, head(h)]).astype(bf16)
        return c

    lax.fori_loop(0, nb, outer, 0)

    hu = total // 2
    gu = Gather(lambda p, h: u.at[p, pl.ds(h * hu, hu)], hu, ssem, rsem, 6, where)
    gu.start()
    for b in range(nb):
        a = att[b * BLOCK : (b + 1) * BLOCK, :]
        ssq[0, :, b * BLOCK : (b + 1) * BLOCK] = lax.dot_general(
            jnp.ones((8, WIDTH), f32), a * a, (((1,), (1,)), ((), ())),
            preferred_element_type=f32, precision=lax.Precision.HIGHEST,
        )
    sums = [
        remote(ssq.at[0], ssq.at[n], ssem.at[11 + n], rsem.at[11 + n], (s, d, partner(t, n)))
        for n in (1, 2, 3)
    ]
    for copy in sums:
        copy.start()
    stores += [load(att, att_o), load(states, states_o)]
    @pl.when(owner)
    def _():
        for n in (1, 2, 3):
            wo_in(n).wait_recv()
            wo_over(n).start()

    @pl.when(jnp.logical_not(owner))
    def _():
        got_wo.far().wait_recv()
        for n in (1, 2, 3):
            wo_over(n).wait_recv()

    y[...] = jnp.zeros_like(y)

    def out_project(i, c):
        for n in (1, 2, 3):

            @pl.when(i == n)
            def _(n=n):
                if n == 1:
                    gu.forward()
                gu.ready(n)

        p = partner(t, i)

        def chunk(m, c):
            r = rows_of(m, rows)
            y[r, :] += nn(u[p, r, :], wo[rows_of(p, WIDTH), :])
            return c

        return lax.fori_loop(0, 4, chunk, c)

    lax.fori_loop(0, 4, out_project, 0)
    for copy in sums:
        copy.wait_recv()
    whole = ssq[0] + ssq[1] + ssq[2] + ssq[3]
    sc[...] = jnp.transpose(lax.rsqrt(whole * (1.0 / D) + norm_eps))
    got_wfi.wait()
    got_wfo.wait()
    out = Scatter(part, got, via, rows, ssem, rsem, 15, where)

    def feed(i, c):
        e = 3 - i
        r = rows_of(partner(t, e), rows)
        br = sc[r, 0:1] * y[r, :]
        branch[r, :] = br.astype(bf16)
        m = xf[r, :].astype(f32) + br
        h2 = (m * rms_scale(m)).astype(bf16)
        hid2[r, :] = h2
        p0, p1 = nn(h2, wfi[0]), nn(h2, wfi[1])
        pair[0, r, :] = p0.astype(bf16)
        pair[1, r, :] = p1.astype(bf16)
        o = nn((p0 * p1).astype(bf16), wfo[...])
        for n in (1, 2, 3):

            @pl.when(e == n)
            def _(n=n):
                out.put(n, o)

        @pl.when(e == 0)
        def _():
            mid[...] = m
            own[...] = o + m

        return c

    lax.fori_loop(0, 4, feed, 0)
    stores += [load(sc, sc_o), load(branch, branch_o), load(mid, mid_o), load(hid2, hid2_o)]
    stores += [load(pair, pair_o), load(wi, wi_o), load(wo.at[rows_of(t, WIDTH)], wo_o)]
    stores += [load(wfi, wfi_o), load(wfo, wfo_o)]
    out.combine()
    yb[...] = (own[...] + out.result()).astype(bf16)
    stores += [load(yb, y_out)]
    start, finish = to_owner(
        owner, where, yb, both_o.at[s], both_o.at[s], wl.at[4], ws.at[10], wr.at[10]
    )
    start()
    for fetch in got_w:
        fetch.drain()

    @pl.when(owner)
    def _():
        for n in (1, 2, 3):
            wo_out(n).wait_send()
            wo_over(n).wait_send()

    finish()
    gx.drain()
    gu.drain()
    out.drain()
    for copy in sums:
        copy.wait_send()
    sent_states(dp, where, zout, zin, zs, zr, True)
    for copy in stores:
        copy.wait()


def layer_forward(layer, first, x, weights, cos2, sin2, scal, dp, uid):
    rows = x.shape[-2]
    total = 4 * rows
    nb = total // BLOCK
    fp = weights[2].shape[2]
    saved = [
        ((rows, D), bf16), ((total, D), bf16), ((total, WIDTH), f32), ((total, WIDTH), f32),
        ((total, WIDTH), f32), ((total, WIDTH), bf16), ((total, WIDTH), bf16),
        ((total, WIDTH), bf16), ((total, WIDTH), f32), ((total, 8), f32),
        ((nb, HEADS_HERE, HEAD, HEAD), f32), ((total, D), bf16), ((rows, D), f32),
        ((total, D), bf16), ((2, total, fp), bf16),
    ]
    scratch = [
        ((D, 4 * WIDTH), bf16), ((D, D), bf16), ((2, D, fp), bf16), ((fp, D), bf16),
        ((total, HEAD), f32), ((total, HEAD), f32), ((total, D), bf16),
    ]
    scratch += saved[1:]
    saved = [
        ((2, rows, D), bf16), ((D, 4 * WIDTH), bf16), ((WIDTH, D), bf16), ((2, D, fp), bf16),
        ((fp, D), bf16),
    ] + saved
    scratch += [
        ((HEADS_HERE, BLOCK, BLOCK), f32), ((HEADS_HERE, BLOCK, HEAD), f32),
        ((HEADS_HERE, BLOCK, HEAD), f32), ((nb, HEADS_HERE, HEAD, HEAD), f32),
        ((HEADS_HERE, HEAD, HEAD), bf16), ((dp, HEADS_HERE, HEAD, HEAD), bf16),
        ((HEADS_HERE, HEAD, HEAD), f32), ((4, total, WIDTH), bf16), ((total, D), f32),
        ((3, rows, D), bf16), ((2, rows, D), bf16), ((2, rows // 2, D), bf16),
        ((4, 8, total), f32), ((rows, D), f32), ((rows, D), bf16),
    ]
    flops = 2 * total * D * (4 * WIDTH + D + 3 * fp)
    return pl.pallas_call(
        functools.partial(forward_kernel, dp, layer, first),
        out_shape=tuple(jax.ShapeDtypeStruct(a, b) for a, b in saved),
        in_specs=[ANY] * 7 + [SMEM],
        out_specs=(ANY,) * len(saved),
        scratch_shapes=[pltpu.VMEM(a, b) for a, b in scratch]
        + [
            pltpu.SemaphoreType.DMA((24,)),
            pltpu.SemaphoreType.DMA((21,)),
            pltpu.SemaphoreType.DMA((21,)),
            pltpu.SemaphoreType.DMA((dp,)),
            pltpu.SemaphoreType.DMA((dp,)),
            pltpu.SemaphoreType.DMA((5,)),
            pltpu.SemaphoreType.DMA((11,)),
            pltpu.SemaphoreType.DMA((11,)),
        ],
        compiler_params=pltpu.CompilerParams(
            collective_id=uid, has_side_effects=True, vmem_limit_bytes=VMEM_BYTES
        ),
        cost_estimate=pl.CostEstimate(flops=flops, bytes_accessed=20 << 20, transcendentals=0),
        name="layer_forward",
    )(x, *weights, cos2, sin2, scal)


class LineSum:
    def __init__(self, dp, where, owner, arrays, sems):
        self.dp, self.where, self.owner, self.arrays = dp, where, owner, arrays
        self.core_s, self.core_r, self.rs, self.rr, self.gs, self.gr, self.ol, self.os, self.or_ = sems

    def each(self, fn):
        for n, array in enumerate(self.arrays):
            fn(n, *array)

    def own(self, halves, j):
        count = halves.shape[1] // self.dp
        return halves.at[self.where[0], rows_of(j, count)]

    def over(self, n, halves, from_core):
        s, d, t = self.where
        return remote(
            halves.at[1 - s], from_core, self.core_s.at[n], self.core_r.at[n], (1 - s, d, t)
        )

    def core_send(self):
        self.each(lambda n, halves, fc, land, res: self.over(n, halves, fc).start())

    def core_add(self):
        s = self.where[0]

        def one(n, halves, fc, land, res):
            self.over(n, halves, fc).wait()
            count = halves.shape[1] // self.dp

            def chunk(j, c):
                r = rows_of(j, count)
                halves[s, r, :] = (halves[s, r, :].astype(f32) + fc[r, :].astype(f32)).astype(bf16)
                return c

            lax.fori_loop(0, self.dp, chunk, 0)

        self.each(one)

    def partial(self, n, land, j, up):
        s, d, t = self.where
        to = d + 1 if up else d - 1
        slot = j if up else jnp.where(j == to, self.dp, j)
        return remote(land.at[j], land.at[slot], self.rs.at[n, j], self.rr.at[n, slot], (s, to, t))

    def landed(self, n, land, slot):
        s, d, t = self.where
        return remote(land.at[slot], land.at[slot], self.rs.at[n, 0], self.rr.at[n, slot], (s, d, t))

    def final(self, n, halves, j, up):
        s, d, t = self.where
        to = d + 1 if up else d - 1
        ref = self.own(halves, j)
        k = j if up else jnp.where(j == d, self.dp, j)
        return remote(ref, ref, self.gs.at[n, k], self.gr.at[n, j], (s, to, t))

    def arrived(self, n, halves, j):
        s, d, t = self.where
        ref = self.own(halves, j)
        return remote(ref, ref, self.gs.at[n, 0], self.gr.at[n, j], (s, d, t))

    def add(self, n, halves, land, slot, j, into_own):
        s = self.where[0]
        self.landed(n, land, slot).wait_recv()
        r = rows_of(j, halves.shape[1] // self.dp)
        total = (halves[s, r, :].astype(f32) + land[slot].astype(f32)).astype(bf16)
        if into_own:
            halves[s, r, :] = total
        else:
            land[slot] = total

    def step(self, k):
        dp = self.dp
        s, d, t = self.where
        if dp == 1:
            return
        if k < dp - 1:
            for up in (True, False):
                e = d if up else dp - 1 - d
                j = dp - 1 - k + d if up else k - (dp - 1 - d)

                def one(n, halves, fc, land, res, up=up, e=e, j=j):
                    @pl.when(e == 0)
                    def _():
                        land[j] = halves[s, rows_of(j, halves.shape[1] // dp), :]
                        self.partial(n, land, j, up).start()

                    @pl.when((e > 0) & (e <= k))
                    def _():
                        self.add(n, halves, land, j, j, False)
                        self.partial(n, land, j, up).start()

                self.each(one)
            return
        a = k - (dp - 1)
        if a == 0:

            def one(n, halves, fc, land, res):
                def sent(j, c):
                    pl.when(j > d)(lambda: self.partial(n, land, j, True).wait_send())
                    pl.when(j < d)(lambda: self.partial(n, land, j, False).wait_send())
                    return c

                @pl.when(d > 0)
                def _():
                    self.add(n, halves, land, d, d, True)

                @pl.when(d < dp - 1)
                def _():
                    self.add(n, halves, land, dp, d, True)

                lax.fori_loop(0, dp, sent, 0)
                pl.when(d < dp - 1)(lambda: self.final(n, halves, d, True).start())
                pl.when(d > 0)(lambda: self.final(n, halves, d, False).start())

            self.each(one)
            return

        def one(n, halves, fc, land, res):
            @pl.when(d - a >= 0)
            def _():
                self.arrived(n, halves, d - a).wait_recv()
                pl.when(d < dp - 1)(lambda: self.final(n, halves, d - a, True).start())

            @pl.when(d + a < dp)
            def _():
                self.arrived(n, halves, d + a).wait_recv()
                pl.when(d > 0)(lambda: self.final(n, halves, d + a, False).start())

        self.each(one)

    def results(self):
        out = []

        def one(n, halves, fc, land, res):
            s = self.where[0]
            out.append(
                to_owner(
                    self.owner, self.where, halves.at[s], res.at[s], res.at[s],
                    self.ol.at[n], self.os.at[n], self.or_.at[n],
                )
            )

        self.each(one)
        return out

    def finish(self):
        dp = self.dp
        s, d, t = self.where

        def one(n, halves, fc, land, res):
            def sent(j, c):
                @pl.when((j <= d) & (d < dp - 1))
                def _():
                    self.final(n, halves, j, True).wait_send()

                @pl.when((j >= d) & (d > 0))
                def _():
                    self.final(n, halves, j, False).wait_send()

                return c

            lax.fori_loop(0, dp, sent, 0)

        self.each(one)
        for start, _ in self.results():
            start()

    def close(self):
        for _, finish in self.results():
            finish()


def backward_kernel(
    dp, ct_in, y0_in, tok_in, cos2, sin2, scal,
    wi0, wo0, wfi0, wfo0, wi1, wo1, wfi1, wfo1, *refs,
):
    saved_i = (refs[0:14], refs[14:28])
    both_o, gwfi_o, gwfo_o, gmix_o = refs[28:32]
    (
        wi, wo, wfi, wfo, cosv, sinv, gf, xr, hidden, zq, zk, gate, q, k, v, att, sc, states, branch, mid,
        hid2, pair, mask, mask_t, qd, kd, terms, zout, zin, run, gpair, prod, gb, gm, dv, dk,
        gp, part, got, via, own, gr, gwfi, gwfo, gmix, c_fi, c_fo, c_mix, l_fi, l_fo, l_mix,
        lsem, ssem, rsem, zs, zr, ol, os, or_, core_s, core_r, ls, lr, fs, fr,
    ) = refs[32:]
    where = s, d, t = place()
    rows = y0_in.shape[0]
    total = 4 * rows
    nb = total // BLOCK
    fp = wfo.shape[0]
    half = rows // 2
    table = nb + 4 + 4 * dp
    local = Sems(lsem)
    me = rows_of(t, rows)
    gated, gatt = slice(0, WIDTH), slice(WIDTH, 2 * WIDTH)

    def gatt_head(h):
        return slice(WIDTH + h * HEAD, WIDTH + (h + 1) * HEAD)

    def load(src, dst):
        copy = pltpu.make_async_copy(src, dst, local.take())
        copy.start()
        return copy

    def block_of(ref):
        return lambda p, h: ref.at[pl.ds(pl.multiple_of(p * rows + h * half, half), half)]

    weights = ((wi0, wo0, wfi0, wfo0), (wi1, wo1, wfi1, wfo1))

    def load_feed(layer):
        keep = saved_i[layer]
        return [
            load(weights[layer][3], wfo), load(keep[13], pair), load(weights[layer][2], wfi),
            load(keep[11], mid), load(keep[12], hid2),
        ]

    def load_gates(layer):
        keep = saved_i[layer]
        return [
            load(weights[layer][1], wo), load(keep[10], branch), load(keep[8], sc), load(keep[7], att),
            load(keep[3], gate),
        ]

    def load_attn(layer):
        keep = saved_i[layer]
        pairs = ((4, q), (5, k), (6, v), (9, states), (1, zq), (2, zk))
        return [load(keep[n], ref) for n, ref in pairs]

    def load_ends(layer):
        x = tok_in.at[s] if layer == 0 else y0_in
        return [load(weights[layer][0], wi), load(saved_i[layer][0], hidden), load(x, xr)]

    def line(arrays, base, layer):
        n = len(arrays)
        at = pl.ds(base, n)
        sems = [ref.at[at] for ref in (core_s, core_r, ls, lr, fs, fr, ol, os, or_)]
        return LineSum(dp, where, s == layer, arrays, sems)

    feeds = [
        line(
            (
                (gwfi.at[layer], c_fi, l_fi, gwfi_o),
                (gwfo.at[layer], c_fo, l_fo, gwfo_o),
            ),
            3 * layer, layer,
        )
        for layer in (0, 1)
    ]
    mixes = [line(((gmix, c_mix, l_mix, gmix_o),), 3 * layer + 2, layer) for layer in (0, 1)]
    steps = 2 * dp - 1
    progress = {}

    def tick(piece, count=1):
        at = progress.get(id(piece), 0)
        for n in range(at, min(at + count, steps)):
            piece.step(n)
        progress[id(piece)] = at + count

    got_g = load(ct_in.at[s], gf.at[me])
    in_feed, in_tables = load_feed(1), [load(cos2, cosv), load(sin2, sinv)]
    in_gates, in_attn, in_ends = load_gates(1), load_attn(1), load_ends(1)
    entry(dp, s, d, t, core=True)
    got_g.wait()
    in_out = []

    for layer in (1, 0):
        offset = table * layer
        a_now, b_now = feeds[layer], mixes[layer]
        a_old, b_old = (feeds[1], mixes[1]) if layer == 0 else (None, None)
        base = 24 * layer
        gg = Gather(block_of(gf), half, ssem, rsem, base, where)
        gg.start()
        decay_fill(scal, offset, nb, mask, mask_t, qd, kd)
        if b_old is not None:
            b_old.core_add()
            tick(b_old)
        for copy in in_feed:
            copy.wait()
        sums = Scatter(part, got, via, rows, ssem, rsem, base + 6, where)

        def feed(i, c):
            for n in (1, 2, 3):

                @pl.when(i == n)
                def _(n=n):
                    if n == 1:
                        gg.forward()
                    gg.ready(n)

            r = rows_of(partner(t, i), rows)
            grad = nt(gf[r, :], wfo[...])
            p0, p1 = pair[0, r, :].astype(f32), pair[1, r, :].astype(f32)
            prod[r, :] = (p0 * p1).astype(bf16)
            g0, g1 = (grad * p1).astype(bf16), (grad * p0).astype(bf16)
            gpair[0, r, :] = g0
            gpair[1, r, :] = g1
            o = nt(g0, wfi[0]) + nt(g1, wfi[1])
            for n in (1, 2, 3):

                @pl.when(i == n)
                def _(n=n):
                    sums.put(n, o)

            @pl.when(i == 0)
            def _():
                own[...] = o

            return c

        lax.fori_loop(0, 4, feed, 0)
        sums.combine()
        if a_old is not None:
            tick(a_old)
            tick(b_old)

        def feed_weights(n, c):
            cols = rows_of(n, 256)
            a = hid2[:, cols]
            gwfi[layer, 0, cols, :] = tn(a, gpair[0]).astype(bf16)
            gwfi[layer, 1, cols, :] = tn(a, gpair[1]).astype(bf16)
            return c

        def out_weights(n, c):
            cols = rows_of(n, 256)
            a = prod[:, cols]
            gwfo[layer, 0, cols, :] = tn(a, gf[:, : D // 2]).astype(bf16)
            gwfo[layer, 1, cols, :] = tn(a, gf[:, D // 2 :]).astype(bf16)
            return c

        lax.fori_loop(0, D // 256, feed_weights, 0)
        lax.fori_loop(0, fp // 256, out_weights, 0)
        a_now.core_send()
        grad_middle = gf[me, :].astype(f32) + norm_back(mid[...], own[...] + sums.result())
        gm[...] = grad_middle
        gb[me, :] = grad_middle.astype(bf16)
        sums.drain()
        gg.drain()

        gbg = Gather(block_of(gb), half, ssem, rsem, base + 12, where)
        gbg.start()
        if layer == 1:
            in_feed = load_feed(0)
        if a_old is not None:
            tick(a_old, 1 if steps <= 7 else steps)
            tick(b_old)
        a_now.core_add()
        tick(a_now)
        for copy in in_gates:
            copy.wait()

        def gating(i, c):
            for n in (1, 2, 3):

                @pl.when(i == n)
                def _(n=n):
                    if n == 1:
                        gbg.forward()
                    gbg.ready(n)

            r = rows_of(partner(t, i), rows)
            b = gb[r, :]
            grad = nt(b, wo[...])
            dots = jnp.sum(b.astype(f32) * branch[r, :].astype(f32), axis=-1, keepdims=True) * (1.0 / D)
            scale = sc[r, 0:1]
            normed = att[r, :] * scale
            gt = gate[r, :]
            gp[r, 3 * WIDTH :] = (grad * normed).astype(bf16)
            prod[r, gated] = (normed * gt).astype(bf16)
            prod[r, gatt] = (scale * (grad * gt - normed * dots)).astype(bf16)
            return c

        lax.fori_loop(0, 4, gating, 0)
        if layer == 1:
            in_gates = load_gates(0)
        for copy in in_attn:
            copy.wait()
        if layer == 1:
            for copy in in_tables:
                copy.wait()

        def term(b, c):
            r = rows_of(b, BLOCK)
            for h in range(HEADS_HERE):
                qdec = (q[r, head(h)].astype(f32) * qd[h]).astype(bf16)
                terms[b, h] = tn(qdec, prod[r, gatt_head(h)])
            return c

        lax.fori_loop(0, nb, term, 0)
        for h in range(HEADS_HERE):
            carried = scal[offset + nb - 1] * terms[nb - 1, h]
            for b in reversed(range(nb - 1)):
                carried = scal[offset + b] * (terms[b, h] + scal[offset + nb + 2 + h] * carried)
            zout[layer, h] = carried.astype(bf16)
        z_args = (dp, where, zout.at[layer], zin.at[layer], zs.at[layer], zr.at[layer], False)
        send_states(*z_args)
        if a_old is not None:
            tick(b_old)
        tick(a_now)

        def unturn(pre, grad, r, h):
            back = grad * cosv[r, :] - pltpu.roll(grad, HEAD // 2, 1) * sinv[r, :]
            z = pre[r, head(h)]
            g = sig(z)
            return (back * (g * (1.0 + z * (1.0 - g)))).astype(bf16)

        def inner(b, c):
            r = rows_of(b, BLOCK)
            for h in range(HEADS_HERE):
                qh, kh, vh, gh = q[r, head(h)], k[r, head(h)], v[r, head(h)], prod[r, gatt_head(h)]
                w_t = (nt(kh, qh) * mask_t[h]).astype(bf16)
                dv[r, head(h)] = nn(w_t, gh)
                ds = (nt(gh, vh) * mask[h]).astype(bf16)
                ds_t = (nt(vh, gh) * mask_t[h]).astype(bf16)
                dk[r, head(h)] = nn(ds_t, qh)
                dq = nn(ds, kh) + nt(gh, states[b, h].astype(bf16)) * qd[h]
                gp[r, head(h)] = unturn(zq, dq, r, h)
            return c

        lax.fori_loop(0, nb, inner, 0)
        take_states(*z_args, scal, offset + nb + 4 + 2 * dp, run)

        def outer(i, c):
            b = nb - 1 - i
            r = rows_of(b, BLOCK)
            for h in range(HEADS_HERE):
                after = run[h]
                low = after.astype(bf16)
                run[h] = scal[offset + b] * (terms[b, h] + scal[offset + nb + 2 + h] * after)
                kdec = (k[r, head(h)].astype(f32) * kd[h]).astype(bf16)
                dkh = dk[r, head(h)] + nt(v[r, head(h)], low) * kd[h]
                k_cols = slice(WIDTH + h * HEAD, WIDTH + (h + 1) * HEAD)
                v_cols = slice(2 * WIDTH + h * HEAD, 2 * WIDTH + (h + 1) * HEAD)
                gp[r, k_cols] = unturn(zk, dkh, r, h)
                gp[r, v_cols] = (dv[r, head(h)] + nn(kdec, low)).astype(bf16)
            return c

        lax.fori_loop(0, nb, outer, 0)
        if layer == 1:
            in_attn = load_attn(0)
        for copy in in_ends:
            copy.wait()
        ins = Scatter(part, got, via, rows, ssem, rsem, base + 18, where)

        def back_in(i, c):
            e = 3 - i
            r = rows_of(partner(t, e), rows)
            o = nt(gp[r, :], wi[...])
            for n in (1, 2, 3):

                @pl.when(e == n)
                def _(n=n):
                    ins.put(n, o)

            @pl.when(e == 0)
            def _():
                own[...] = o

            return c

        lax.fori_loop(0, 4, back_in, 0)
        ins.combine()
        tick(a_now)
        if a_old is not None:
            tick(a_old, steps)
            tick(b_old, steps)
            a_old.finish()
            b_old.finish()
            b_old.close()

        def in_weights(n, c):
            cols = rows_of(n, 256)
            a = hidden[:, cols]
            gmix[0, cols, :] = tn(a, gp[:, : 2 * WIDTH]).astype(bf16)
            gmix[1, cols, :] = tn(a, gp[:, 2 * WIDTH :]).astype(bf16)
            return c

        lax.fori_loop(0, D // 256, in_weights, 0)
        gmix[0, D:, :] = tn(prod[:, gated], gb[:, : D // 2]).astype(bf16)
        gmix[1, D:, :] = tn(prod[:, gated], gb[:, D // 2 :]).astype(bf16)
        b_now.core_send()
        dx = gm[...] + norm_back(xr[...].astype(f32), own[...] + ins.result())
        gr[layer] = dx.astype(bf16)
        ins.drain()
        gbg.drain()
        sent_states(*z_args)
        start, finish = to_owner(
            s == layer, where, gr.at[layer], both_o.at[s], both_o.at[s],
            ol.at[6 + layer], os.at[6 + layer], or_.at[6 + layer],
        )
        start()
        in_out.append(finish)
        tick(a_now)
        if layer == 1:
            gf[me, :] = gr[layer]
            in_ends = load_ends(0)

    b_now.core_add()
    while progress.get(id(b_now), 0) < steps or progress.get(id(a_now), 0) < steps:
        tick(b_now)
        tick(a_now)
    a_now.finish()
    b_now.finish()
    feeds[1].close()
    a_now.close()
    b_now.close()
    for finish in in_out:
        finish()


def layers_backward(cotangent, y0, tokens, cos2, sin2, scal, weights, saved, dp, uid):
    rows = y0.shape[-2]
    total = 4 * rows
    nb = total // BLOCK
    fp = weights[0][3].shape[0]
    mixed = D + WIDTH
    outs = [
        ((2, rows, D), bf16), ((2, D, fp), bf16), ((2, fp, D // 2), bf16), ((2, mixed, D // 2), bf16)
    ]
    scratch = [
        ((D, 4 * WIDTH), bf16), ((WIDTH, D), bf16), ((2, D, fp), bf16), ((fp, D), bf16),
        ((total, HEAD), f32), ((total, HEAD), f32), ((total, D), bf16), ((rows, D), bf16),
    ]
    scratch += [(a.shape, a.dtype) for a in saved[0]]
    scratch += [
        ((HEADS_HERE, BLOCK, BLOCK), f32), ((HEADS_HERE, BLOCK, BLOCK), f32),
        ((HEADS_HERE, BLOCK, HEAD), f32), ((HEADS_HERE, BLOCK, HEAD), f32),
        ((nb, HEADS_HERE, HEAD, HEAD), f32), ((2, HEADS_HERE, HEAD, HEAD), bf16),
        ((2, dp, HEADS_HERE, HEAD, HEAD), bf16), ((HEADS_HERE, HEAD, HEAD), f32),
        ((2, total, fp), bf16), ((total, fp), bf16), ((total, D), bf16), ((rows, D), f32),
        ((total, WIDTH), f32), ((total, WIDTH), f32),
        ((total, 4 * WIDTH), bf16),
        ((3, rows, D), bf16), ((2, rows, D), bf16), ((2, rows // 2, D), bf16), ((rows, D), f32),
        ((2, rows, D), bf16),
        ((2, 2, D, fp), bf16), ((2, 2, fp, D // 2), bf16), ((2, mixed, D // 2), bf16),
        ((D, fp), bf16), ((fp, D // 2), bf16), ((mixed, D // 2), bf16),
        ((dp + 1, D // dp, fp), bf16), ((dp + 1, fp // dp, D // 2), bf16),
        ((dp + 1, mixed // dp, D // 2), bf16),
    ]
    dma = pltpu.SemaphoreType.DMA
    flops = 8 * total * D * (4 * WIDTH + WIDTH + 3 * fp)
    flat = [w for layer in weights for w in layer]
    kept = [a for layer in saved for a in layer]
    return pl.pallas_call(
        functools.partial(backward_kernel, dp),
        out_shape=tuple(jax.ShapeDtypeStruct(a, b) for a, b in outs),
        in_specs=[ANY] * 5 + [SMEM] + [ANY] * (len(flat) + len(kept)),
        out_specs=(ANY,) * len(outs),
        scratch_shapes=[pltpu.VMEM(a, b) for a, b in scratch]
        + [
            dma((48,)), dma((48,)), dma((48,)), dma((2, dp)), dma((2, dp)), dma((8,)), dma((8,)),
            dma((8,)), dma((6,)), dma((6,)), dma((6, dp)), dma((6, dp + 1)), dma((6, dp + 1)),
            dma((6, dp)),
        ],
        compiler_params=pltpu.CompilerParams(
            collective_id=uid, has_side_effects=True, vmem_limit_bytes=VMEM_BYTES
        ),
        cost_estimate=pl.CostEstimate(flops=flops, bytes_accessed=60 << 20, transcendentals=0),
        name="layers_backward",
    )(cotangent, y0, tokens, cos2, sin2, scal, *flat, *kept)


def angle_tables(starts, blocks):
    d = lax.axis_index("dp")
    at = jnp.arange(starts.shape[0], dtype=jnp.int32)
    begins = jnp.max(
        jnp.where((at[None, :] <= at[:, None]) & (starts > 0)[None, :], at[None, :], 0), axis=1
    )
    offsets = lax.dynamic_slice_in_dim((at - begins) * BLOCK, d * blocks, blocks)
    places = (offsets[:, None] + jnp.arange(BLOCK, dtype=jnp.int32)[None, :]).reshape(-1)
    lane = jnp.arange(HEAD, dtype=jnp.int32)
    frequency = 10000.0 ** (-(lane % (HEAD // 2)).astype(f32) / (HEAD // 2))
    angles = places.astype(f32)[:, None] * frequency[None, :]
    return jnp.cos(angles), jnp.where(lane < HEAD // 2, -1.0, 1.0)[None, :] * jnp.sin(angles)


def swap(x):
    return lax.ppermute(x, "section", [(0, 1), (1, 0)])


def mine_first(s, a, b):
    return jnp.where(s == 0, a, b)


def shards(tokens, cotangent, mixer_in, mixer_out, feed_in, feed_out, decay_rate, block_starts):
    s = lax.axis_index("section")
    dp = lax.axis_size("dp")
    rows = tokens.shape[1]
    blocks = 4 * rows // BLOCK
    ff = feed_out.shape[1]
    fp = -(-ff // 256) * 256
    wi = mixer_in[0].reshape(D, 4 * WIDTH)
    wfi = jnp.pad(jnp.swapaxes(feed_in[0], 0, 1), ((0, 0), (0, 0), (0, fp - ff)))
    mine = (wi, mixer_out[0], wfi, feed_out[0])
    other_rates = swap(decay_rate[0])
    rates = (mine_first(s, decay_rate[0], other_rates), mine_first(s, other_rates, decay_rate[0]))
    starts = lax.dynamic_index_in_dim(block_starts, s, 0, keepdims=False)
    cos2, sin2 = angle_tables(starts, blocks)
    scal = [scalar_table(starts, r, dp, blocks) for r in rates]

    both0, *out0 = layer_forward(0, True, tokens, mine, cos2, sin2, scal[0], dp, 1)
    weights0, y0, saved0 = out0[:4], out0[4], out0[5:]
    both1, *out1 = layer_forward(1, False, y0, mine, cos2, sin2, scal[1], dp, 2)
    weights1, saved1 = out1[:4], out1[5:]
    in_grads, g_fi, g_fo, g_mix = layers_backward(
        cotangent, y0, tokens, cos2, sin2, jnp.concatenate(scal), (weights0, weights1),
        (saved0, saved1), dp, 3,
    )
    outputs = mine_first(s, both0, both1)
    g_in = jnp.concatenate([g_mix[0, :D], g_mix[1, :D]], axis=1).astype(f32).reshape(D, 4, WIDTH)
    g_out = jnp.concatenate([g_mix[0, D:], g_mix[1, D:]], axis=1).astype(f32)
    g_feed_in = jnp.swapaxes(g_fi[:, :, :ff], 0, 1).astype(f32)
    g_feed_out = jnp.concatenate([g_fo[0, :ff], g_fo[1, :ff]], axis=1).astype(f32)
    return outputs[None], in_grads[None], g_in[None], g_out[None], g_feed_in[None], g_feed_out[None]


def solution(mesh):
    placed = (
        P(None, ("dp", "tensor"), None),
        P(None, ("dp", "tensor"), None),
        P("section", None, None, "tensor"),
        P("section", "tensor", None),
        P("section", None, None, "tensor"),
        P("section", "tensor", None),
        P("section", "tensor"),
        P(),
    )
    return jax.shard_map(
        shards,
        mesh=mesh,
        in_specs=placed,
        out_specs=(
            P("section", None, ("dp", "tensor"), None),
            P("section", None, ("dp", "tensor"), None),
            P("section", None, None, "tensor"),
            P("section", "tensor", None),
            P("section", None, None, "tensor"),
            P("section", "tensor", None),
        ),
        check_vma=False,
    )
```

```python
import functools

import jax
import jax.numpy as jnp
from jax import lax
from jax.experimental import pallas as pl
from jax.experimental.pallas import tpu as pltpu
from jax.sharding import PartitionSpec as P

D = 1024
HEAD = 128
BLOCK = 256
WIDTH = 256
HEADS_HERE = WIDTH // HEAD
norm_eps = 1e-06
MESH = pl.DeviceIdType.MESH
ANY = pl.BlockSpec(memory_space=pl.ANY)
SMEM = pl.BlockSpec(memory_space=pltpu.SMEM)
bf16, f32 = jnp.bfloat16, jnp.float32
PIECES = 16
VMEM_BYTES = 62 * 1024 * 1024


def place():
    return lax.axis_index("section"), lax.axis_index("dp"), lax.axis_index("tensor")


def partner(t, k):
    return ((t // 2 + k // 2) % 2) * 2 + (t + k) % 2


class Sems:
    def __init__(self, ref):
        self.ref, self.used = ref, 0

    def take(self):
        self.used += 1
        return self.ref.at[self.used - 1]


def remote(src, dst, send, recv, dev):
    return pltpu.make_async_remote_copy(
        src_ref=src, dst_ref=dst, send_sem=send, recv_sem=recv, device_id=dev, device_id_type=MESH
    )


def nn(a, b):
    return lax.dot_general(a, b, (((1,), (0,)), ((), ())), preferred_element_type=f32)


def nt(a, b):
    return lax.dot_general(a, b, (((1,), (1,)), ((), ())), preferred_element_type=f32)


def tn(a, b):
    return lax.dot_general(a, b, (((0,), (0,)), ((), ())), preferred_element_type=f32)


def rms_scale(v):
    return lax.rsqrt(jnp.mean(v * v, axis=-1, keepdims=True) + norm_eps)


def norm_back(v, u):
    q = rms_scale(v)
    n = v * q
    return q * (u - n * jnp.mean(u * n, axis=-1, keepdims=True))


def sig(v):
    return 1.0 / (1.0 + jnp.exp(-v))


def rows_of(p, n):
    return pl.ds(pl.multiple_of(p * n, n), n)


def entry(dp, s, d, t, core=False):
    barrier = pltpu.get_barrier_semaphore()
    count = 3
    for k in (1, 2, 3):
        pl.semaphore_signal(barrier, inc=1, device_id=(s, d, partner(t, k)), device_id_type=MESH)
    if core:
        pl.semaphore_signal(barrier, inc=1, device_id=(1 - s, d, t), device_id_type=MESH)
        count += 1
    if dp > 1:

        def greet(k, c):
            pl.semaphore_signal(
                barrier, inc=1, device_id=(s, (d + k) % dp, t), device_id_type=MESH
            )
            return c

        lax.fori_loop(1, dp, greet, 0)
        count += dp - 1
    pl.semaphore_wait(barrier, count)


class Gather:
    def __init__(self, block_at, half, ssem, rsem, base, where):
        self.at, self.half, self.ssem, self.rsem, self.base = block_at, half, ssem, rsem, base
        self.where = where

    def copy(self, n, peer, half, to):
        s, d, t = self.where
        ref = self.at(partner(t, peer), half)
        k = self.base + n
        return remote(ref, ref, self.ssem.at[k], self.rsem.at[k], (s, d, partner(t, to)))

    def mine(self, n):
        peer, half, to = ((0, 0, 1), (0, 1, 1), (0, 0, 2), (0, 1, 2), (1, 0, 2), (2, 1, 1))[n]
        return self.copy(n, peer, half, to)

    def arriving(self, n):
        s, d, t = self.where
        peer, half = ((1, 0), (1, 1), (2, 0), (2, 1), (3, 0), (3, 1))[n]
        ref = self.at(partner(t, peer), half)
        k = self.base + n
        return remote(ref, ref, self.ssem.at[k], self.rsem.at[k], (s, d, t))

    def start(self):
        self.mine(0).start()
        self.mine(3).start()
        self.mine(1).start()
        self.mine(2).start()

    def forward(self):
        self.arriving(0).wait_recv()
        self.mine(4).start()
        self.arriving(3).wait_recv()
        self.mine(5).start()

    def ready(self, k):
        if k == 1:
            self.arriving(1).wait_recv()
        elif k == 2:
            self.arriving(2).wait_recv()
        else:
            self.arriving(4).wait_recv()
            self.arriving(5).wait_recv()

    def drain(self):
        for n in range(6):
            self.mine(n).wait_send()


class Scatter:
    def __init__(self, part, got, via, rows, ssem, rsem, base, where):
        self.part, self.got, self.via, self.half = part, got, via, rows // 2
        self.ssem, self.rsem, self.base, self.where = ssem, rsem, base, where

    def copy(self, n):
        s, d, t = self.where
        h = self.half
        h0, h1 = pl.ds(0, h), pl.ds(h, h)
        src, dst, to = (
            (self.part.at[2, h0], self.via.at[0], 2),
            (self.part.at[2, h1], self.via.at[1], 1),
            (self.part.at[0, h1], self.got.at[0, h1], 1),
            (self.part.at[1, h0], self.got.at[1, h0], 2),
            (self.part.at[0, h0], self.got.at[0, h0], 1),
            (self.part.at[1, h1], self.got.at[1, h1], 2),
        )[n]
        k = self.base + n
        return remote(src, dst, self.ssem.at[k], self.rsem.at[k], (s, d, partner(t, to)))

    def put(self, k, value):
        self.part[k - 1] = value.astype(bf16)
        self.send(k)

    def send(self, k):
        if k == 3:
            self.copy(0).start()
            self.copy(1).start()
        elif k == 2:
            self.copy(3).start()
        else:
            self.copy(2).start()

    def combine(self):
        h = self.half
        self.copy(0).wait_recv()
        self.part[0, 0:h] = (self.part[0, 0:h].astype(f32) + self.via[0].astype(f32)).astype(bf16)
        self.copy(4).start()
        self.copy(1).wait_recv()
        self.part[1, h:] = (self.part[1, h:].astype(f32) + self.via[1].astype(f32)).astype(bf16)
        self.copy(5).start()

    def result(self):
        for n in (2, 3, 4, 5):
            self.copy(n).wait_recv()
        return self.got[0].astype(f32) + self.got[1].astype(f32)

    def drain(self):
        for n in range(6):
            self.copy(n).wait_send()


def scalar_table(starts, rates, dp, blocks):
    d = lax.axis_index("dp")
    survive = 1.0 - starts.astype(f32).reshape(dp, blocks)
    decay = jnp.exp(-rates * BLOCK)
    factor = jnp.prod(survive, axis=1)[:, None] * (decay**blocks)[None, :]
    at = jnp.arange(dp)
    low, high = jnp.minimum(at, d), jnp.maximum(at, d)
    between = (at[None, :] > low[:, None]) & (at[None, :] < high[:, None])
    through = jnp.prod(jnp.where(between[:, :, None], factor[None], 1.0), axis=1)
    forward = jnp.where((at < d)[:, None], through, 0.0)
    backward = jnp.where((at > d)[:, None], through, 0.0)
    mine = lax.dynamic_index_in_dim(survive, d, 0, keepdims=False)
    return jnp.concatenate([mine, rates, decay, forward.reshape(-1), backward.reshape(-1)])


def decay_fill(scal, base, nb, mask, mask_t, qd, kd):
    for h in range(HEADS_HERE):
        r = scal[base + nb + h]
        i = lax.broadcasted_iota(jnp.int32, (BLOCK, BLOCK), 0).astype(f32)
        j = lax.broadcasted_iota(jnp.int32, (BLOCK, BLOCK), 1).astype(f32)
        gap = i - j
        mask[h] = jnp.where(gap >= 0.0, jnp.exp(-r * jnp.maximum(gap, 0.0)), 0.0)
        if mask_t is not None:
            mask_t[h] = jnp.where(gap <= 0.0, jnp.exp(-r * jnp.maximum(-gap, 0.0)), 0.0)
        i = lax.broadcasted_iota(jnp.int32, (BLOCK, HEAD), 0).astype(f32)
        qd[h] = jnp.exp(-r * (i + 1.0))
        kd[h] = jnp.exp(-r * (BLOCK - 1.0 - i))


def head(h):
    return slice(h * HEAD, (h + 1) * HEAD)


def send_states(dp, where, zout, zin, zs, zr, later):
    s, d, t = where

    def each(k, c):
        to = d + k if later else d - k

        @pl.when((to < dp) if later else (to >= 0))
        def _():
            remote(zout, zin.at[d], zs.at[k], zr.at[d], (s, to, t)).start()

        return c

    lax.fori_loop(1, dp, each, 0)


def sent_states(dp, where, zout, zin, zs, zr, later):
    s, d, t = where

    def each(k, c):
        to = d + k if later else d - k

        @pl.when((to < dp) if later else (to >= 0))
        def _():
            remote(zout, zin.at[d], zs.at[k], zr.at[d], (s, to, t)).wait_send()

        return c

    lax.fori_loop(1, dp, each, 0)


def take_states(dp, where, zout, zin, zs, zr, later, scal, base, run):
    s, d, t = where
    run[...] = jnp.zeros_like(run)

    def each(k, c):
        @pl.when((k < d) if later else (k > d))
        def _():
            remote(zout, zin.at[k], zs.at[0], zr.at[k], (s, d, t)).wait_recv()
            for h in range(HEADS_HERE):
                run[h] += scal[base + 2 * k + h] * zin[k, h].astype(f32)

        return c

    lax.fori_loop(0, dp, each, 0)


class Fetch:
    def __init__(self, src, dst, owner, where, lsem, ssem, rsem):
        s, d, t = where
        self.owner = owner
        self.local = lambda: pltpu.make_async_copy(src, dst, lsem)
        self.far = lambda: remote(src, dst, ssem, rsem, (1 - s, d, t))

    def read(self):
        pl.when(self.owner)(lambda: self.local().start())

    def send(self):
        pl.when(self.owner)(lambda: self.far().start())

    def wait(self):
        pl.when(self.owner)(lambda: self.local().wait())
        pl.when(jnp.logical_not(self.owner))(lambda: self.far().wait_recv())

    def drain(self):
        pl.when(self.owner)(lambda: self.far().wait_send())


def to_owner(owner, where, src, own_dst, far_dst, lsem, ssem, rsem):
    s, d, t = where

    def far():
        return remote(src, far_dst, ssem, rsem, (1 - s, d, t))

    def local():
        return pltpu.make_async_copy(src, own_dst, lsem)

    def start():
        pl.when(owner)(lambda: local().start())
        pl.when(jnp.logical_not(owner))(lambda: far().start())

    def finish():
        @pl.when(owner)
        def _():
            local().wait()
            far().wait_recv()

        pl.when(jnp.logical_not(owner))(lambda: far().wait_send())

    return start, finish


def forward_kernel(
    dp, layer, first, x_in, my_wi, my_wo, my_wfi, my_wfo, cos2, sin2, scal,
    both_o, wi_o, wo_o, wfi_o, wfo_o, y_out, hidden_o, zq_o, zk_o, gate_o, q_o, k_o, v_o, att_o, sc_o, states_o, branch_o, mid_o,
    hid2_o, pair_o,
    wi, wo, wfi, wfo, cosv, sinv, xf, hidden, zq, zk, gate, q, k, v, att, sc, states, branch, mid, hid2,
    pair, mask, qd, kd, loc, zout, zin, run, u, y, part, got, via, ssq, own, yb,
    lsem, ssem, rsem, zs, zr, wl, ws, wr,
):
    where = s, d, t = place()
    rows = x_in.shape[-2]
    total = 4 * rows
    nb = total // BLOCK
    local = Sems(lsem)

    def load(src, dst):
        copy = pltpu.make_async_copy(src, dst, local.take())
        copy.start()
        return copy

    x_src = x_in.at[s] if first else x_in
    got_x = load(x_src, xf.at[rows_of(t, rows)])
    owner = s == layer
    ff = my_wfo.shape[0]
    pairs = (
        (my_wi, wi), (my_wo, wo.at[rows_of(t, WIDTH)]), (my_wfi, wfi), (my_wfo, wfo.at[pl.ds(0, ff)])
    )
    got_w = [
        Fetch(src, dst, owner, where, wl.at[n], ws.at[n], wr.at[n])
        for n, (src, dst) in enumerate(pairs)
    ]
    got_wi, got_wo, got_wfi, got_wfo = got_w
    got_wi.read()
    got_cos, got_sin = load(cos2, cosv), load(sin2, sinv)
    for fetch in got_w[1:]:
        fetch.read()
    wfo[ff:, :] = jnp.zeros_like(wfo[ff:, :])
    entry(dp, s, d, t, core=True)
    got_x.wait()

    half = rows // 2
    gx = Gather(
        lambda p, h: xf.at[pl.ds(pl.multiple_of(p * rows + h * half, half), half)],
        half, ssem, rsem, 0, where,
    )
    gx.start()
    for fetch in got_w:
        fetch.send()
    decay_fill(scal, 0, nb, mask, None, qd, kd)
    got_wi.wait()
    got_cos.wait()
    got_sin.wait()

    def project(i, c):
        for n in (1, 2, 3):

            @pl.when(i == n)
            def _(n=n):
                if n == 1:
                    gx.forward()
                gx.ready(n)

        r = rows_of(partner(t, i), rows)
        xv = xf[r, :].astype(f32)
        hid = (xv * rms_scale(xv)).astype(bf16)
        hidden[r, :] = hid
        cs, sn = cosv[r, :], sinv[r, :]
        for n, (pre, post) in enumerate(((zq, q), (zk, k))):
            z = nn(hid, wi[:, n * WIDTH : (n + 1) * WIDTH])
            pre[r, :] = z
            a = z * sig(z)
            for h in range(HEADS_HERE):
                ah = a[:, head(h)]
                post[r, head(h)] = (ah * cs + pltpu.roll(ah, HEAD // 2, 1) * sn).astype(bf16)
        v[r, :] = nn(hid, wi[:, 2 * WIDTH : 3 * WIDTH]).astype(bf16)
        gate[r, :] = nn(hid, wi[:, 3 * WIDTH :])
        return c

    lax.fori_loop(0, 4, project, 0)

    def wo_block(k, k_to, n, dev):
        ref = wo.at[rows_of(partner(t, k), WIDTH)]
        return remote(ref, ref, ws.at[n], wr.at[n], dev)

    def wo_out(k):
        return wo_block(0, k, 3 + k, (s, d, partner(t, k)))

    def wo_in(k):
        return wo_block(k, 0, 3 + k, (s, d, t))

    def wo_over(k):
        return wo_block(k, 0, 6 + k, (1 - s, d, t))

    @pl.when(owner)
    def _():
        got_wo.local().wait()
        for n in (1, 2, 3):
            wo_out(n).start()

    stores = [load(hidden, hidden_o), load(zq, zq_o), load(zk, zk_o), load(gate, gate_o)]
    stores += [load(q, q_o), load(k, k_o), load(v, v_o)]

    def local_state(b, c):
        r = rows_of(b, BLOCK)
        for h in range(HEADS_HERE):
            kdec = (k[r, head(h)].astype(f32) * kd[h]).astype(bf16)
            loc[b, h] = tn(kdec, v[r, head(h)])
        return c

    lax.fori_loop(0, nb, local_state, 0)
    for h in range(HEADS_HERE):
        carried = loc[0, h]
        for b in range(1, nb):
            carried = (scal[nb + 2 + h] * scal[b]) * carried + loc[b, h]
        zout[h] = carried.astype(bf16)
    send_states(dp, where, zout, zin, zs, zr, True)

    def inner(b, c):
        r = rows_of(b, BLOCK)
        for h in range(HEADS_HERE):
            w = (nt(q[r, head(h)], k[r, head(h)]) * mask[h]).astype(bf16)
            att[r, head(h)] = nn(w, v[r, head(h)])
        return c

    lax.fori_loop(0, nb, inner, 0)
    take_states(dp, where, zout, zin, zs, zr, True, scal, nb + 4, run)

    def outer(b, c):
        r = rows_of(b, BLOCK)
        for h in range(HEADS_HERE):
            entering = scal[b] * run[h]
            states[b, h] = entering
            run[h] = scal[nb + 2 + h] * entering + loc[b, h]
            qdec = (q[r, head(h)].astype(f32) * qd[h]).astype(bf16)
            a = att[r, head(h)] + nn(qdec, entering.astype(bf16))
            att[r, head(h)] = a
            u[t, r, head(h)] = (a * gate[r, head(h)]).astype(bf16)
        return c

    lax.fori_loop(0, nb, outer, 0)

    hu = total // 2
    gu = Gather(lambda p, h: u.at[p, pl.ds(h * hu, hu)], hu, ssem, rsem, 6, where)
    gu.start()
    for b in range(nb):
        a = att[b * BLOCK : (b + 1) * BLOCK, :]
        ssq[0, :, b * BLOCK : (b + 1) * BLOCK] = lax.dot_general(
            jnp.ones((8, WIDTH), f32), a * a, (((1,), (1,)), ((), ())),
            preferred_element_type=f32, precision=lax.Precision.HIGHEST,
        )
    sums = [
        remote(ssq.at[0], ssq.at[n], ssem.at[11 + n], rsem.at[11 + n], (s, d, partner(t, n)))
        for n in (1, 2, 3)
    ]
    for copy in sums:
        copy.start()
    stores += [load(att, att_o), load(states, states_o)]
    @pl.when(owner)
    def _():
        for n in (1, 2, 3):
            wo_in(n).wait_recv()
            wo_over(n).start()

    @pl.when(jnp.logical_not(owner))
    def _():
        got_wo.far().wait_recv()
        for n in (1, 2, 3):
            wo_over(n).wait_recv()

    y[...] = jnp.zeros_like(y)

    def out_project(i, c):
        for n in (1, 2, 3):

            @pl.when(i == n)
            def _(n=n):
                if n == 1:
                    gu.forward()
                gu.ready(n)

        p = partner(t, i)

        def chunk(m, c):
            r = rows_of(m, rows)
            y[r, :] += nn(u[p, r, :], wo[rows_of(p, WIDTH), :])
            return c

        return lax.fori_loop(0, 4, chunk, c)

    lax.fori_loop(0, 4, out_project, 0)
    for copy in sums:
        copy.wait_recv()
    whole = ssq[0] + ssq[1] + ssq[2] + ssq[3]
    sc[...] = jnp.transpose(lax.rsqrt(whole * (1.0 / D) + norm_eps))
    got_wfi.wait()
    got_wfo.wait()
    out = Scatter(part, got, via, rows, ssem, rsem, 15, where)

    def feed(i, c):
        e = 3 - i
        r = rows_of(partner(t, e), rows)
        br = sc[r, 0:1] * y[r, :]
        branch[r, :] = br.astype(bf16)
        m = xf[r, :].astype(f32) + br
        h2 = (m * rms_scale(m)).astype(bf16)
        hid2[r, :] = h2
        p0, p1 = nn(h2, wfi[0]), nn(h2, wfi[1])
        pair[0, r, :] = p0.astype(bf16)
        pair[1, r, :] = p1.astype(bf16)
        o = nn((p0 * p1).astype(bf16), wfo[...])
        for n in (1, 2, 3):

            @pl.when(e == n)
            def _(n=n):
                out.put(n, o)

        @pl.when(e == 0)
        def _():
            mid[...] = m
            own[...] = o + m

        return c

    lax.fori_loop(0, 4, feed, 0)
    stores += [load(sc, sc_o), load(branch, branch_o), load(mid, mid_o), load(hid2, hid2_o)]
    stores += [load(pair, pair_o), load(wi, wi_o), load(wo.at[rows_of(t, WIDTH)], wo_o)]
    stores += [load(wfi, wfi_o), load(wfo, wfo_o)]
    out.combine()
    yb[...] = (own[...] + out.result()).astype(bf16)
    stores += [load(yb, y_out)]
    start, finish = to_owner(
        owner, where, yb, both_o.at[s], both_o.at[s], wl.at[4], ws.at[10], wr.at[10]
    )
    start()
    for fetch in got_w:
        fetch.drain()

    @pl.when(owner)
    def _():
        for n in (1, 2, 3):
            wo_out(n).wait_send()
            wo_over(n).wait_send()

    finish()
    gx.drain()
    gu.drain()
    out.drain()
    for copy in sums:
        copy.wait_send()
    sent_states(dp, where, zout, zin, zs, zr, True)
    for copy in stores:
        copy.wait()


def layer_forward(layer, first, x, weights, cos2, sin2, scal, dp, uid):
    rows = x.shape[-2]
    total = 4 * rows
    nb = total // BLOCK
    fp = weights[2].shape[2]
    saved = [
        ((rows, D), bf16), ((total, D), bf16), ((total, WIDTH), f32), ((total, WIDTH), f32),
        ((total, WIDTH), f32), ((total, WIDTH), bf16), ((total, WIDTH), bf16),
        ((total, WIDTH), bf16), ((total, WIDTH), f32), ((total, 8), f32),
        ((nb, HEADS_HERE, HEAD, HEAD), f32), ((total, D), bf16), ((rows, D), f32),
        ((total, D), bf16), ((2, total, fp), bf16),
    ]
    scratch = [
        ((D, 4 * WIDTH), bf16), ((D, D), bf16), ((2, D, fp), bf16), ((fp, D), bf16),
        ((total, HEAD), f32), ((total, HEAD), f32), ((total, D), bf16),
    ]
    scratch += saved[1:]
    saved = [
        ((2, rows, D), bf16), ((D, 4 * WIDTH), bf16), ((WIDTH, D), bf16), ((2, D, fp), bf16),
        ((fp, D), bf16),
    ] + saved
    scratch += [
        ((HEADS_HERE, BLOCK, BLOCK), f32), ((HEADS_HERE, BLOCK, HEAD), f32),
        ((HEADS_HERE, BLOCK, HEAD), f32), ((nb, HEADS_HERE, HEAD, HEAD), f32),
        ((HEADS_HERE, HEAD, HEAD), bf16), ((dp, HEADS_HERE, HEAD, HEAD), bf16),
        ((HEADS_HERE, HEAD, HEAD), f32), ((4, total, WIDTH), bf16), ((total, D), f32),
        ((3, rows, D), bf16), ((2, rows, D), bf16), ((2, rows // 2, D), bf16),
        ((4, 8, total), f32), ((rows, D), f32), ((rows, D), bf16),
    ]
    flops = 2 * total * D * (4 * WIDTH + D + 3 * fp)
    return pl.pallas_call(
        functools.partial(forward_kernel, dp, layer, first),
        out_shape=tuple(jax.ShapeDtypeStruct(a, b) for a, b in saved),
        in_specs=[ANY] * 7 + [SMEM],
        out_specs=(ANY,) * len(saved),
        scratch_shapes=[pltpu.VMEM(a, b) for a, b in scratch]
        + [
            pltpu.SemaphoreType.DMA((24,)),
            pltpu.SemaphoreType.DMA((21,)),
            pltpu.SemaphoreType.DMA((21,)),
            pltpu.SemaphoreType.DMA((dp,)),
            pltpu.SemaphoreType.DMA((dp,)),
            pltpu.SemaphoreType.DMA((5,)),
            pltpu.SemaphoreType.DMA((11,)),
            pltpu.SemaphoreType.DMA((11,)),
        ],
        compiler_params=pltpu.CompilerParams(
            collective_id=uid, has_side_effects=True, vmem_limit_bytes=VMEM_BYTES
        ),
        cost_estimate=pl.CostEstimate(flops=flops, bytes_accessed=20 << 20, transcendentals=0),
        name="layer_forward",
    )(x, *weights, cos2, sin2, scal)


class CorePair:
    def __init__(self, where, halves, from_core, ssem, rsem):
        s, d, t = where
        self.s, self.halves, self.landed = s, halves, from_core
        self.copy = lambda: remote(halves.at[1 - s], from_core, ssem, rsem, (1 - s, d, t))

    def send(self):
        self.copy().start()

    def add(self):
        self.copy().wait()
        rows = self.landed.shape[0]
        step = 128

        def chunk(n, c):
            r = rows_of(n, step)
            mine = self.halves[self.s, r, :].astype(f32)
            self.halves[self.s, r, :] = (mine + self.landed[r, :].astype(f32)).astype(bf16)
            return c

        lax.fori_loop(0, rows // step, chunk, 0)


class LineSum:
    LAG = 2
    END = 4 * LAG

    def __init__(self, dp, where, owner, halves, first, size, land, fin, result, sems, before):
        self.dp, self.where, self.owner, self.before = dp, where, owner, before
        self.halves, self.first, self.size, self.land, self.fin = halves, first, size, land, fin
        self.result = result
        self.recv, self.sent, self.free, self.ol, self.os, self.or_ = sems
        self.age = -1
        s, d, t = where
        low = dp // 2 - 1
        self.upward = d <= low
        self.middle = (d == low) | (d == low + 1)
        self.edge = (d == 0) | (d == dp - 1)
        self.inner = (s, jnp.where(self.upward, d + 1, d - 1), t)
        self.outer = (s, jnp.where(self.upward, d - 1, d + 1), t)
        self.mine = jnp.where(self.upward, 0, 1)

    def own(self, h=None):
        return self.halves.at[self.where[0], self.rows(self.first, h)]

    def rows(self, base, h=None):
        if h is None:
            return pl.ds(base, self.size)
        half = self.size // 2
        return pl.ds(pl.multiple_of(base + h * half, 16), half)

    def final(self, h):
        return self.fin.at[self.rows(self.first, h)]

    def inward(self):
        landing = self.land.at[self.rows(self.first)]
        return remote(self.own(), landing, self.sent.at[0], self.recv.at[2], self.inner)

    def swap_part(self):
        h = 1 - self.mine
        return remote(self.own(h), self.final(h), self.sent.at[0], self.recv.at[h], self.inner)

    def swap_sum(self):
        ref = self.final(self.mine)
        return remote(ref, ref, self.sent.at[1], self.recv.at[self.mine], self.inner)

    def outward(self, h):
        ref = self.final(h)
        return remote(ref, ref, self.sent.at[2 + h], self.recv.at[h], self.outer)

    def sweep(self, base, size, fn):
        unit = 32 if size % 32 == 0 else 16

        def chunk(n, c):
            fn(pl.ds(pl.multiple_of(base + n * unit, 16), unit))
            return c

        lax.fori_loop(0, size // unit, chunk, 0)

    def start(self):
        self.age = 0
        before = self.before
        if before is not None:
            assert before.age >= self.END
            before.close()

            @pl.when(self.middle)
            def _():
                pl.semaphore_signal(
                    self.free, inc=1, device_id=self.inner, device_id_type=MESH
                )

        if self.dp > 2:
            pl.when(self.edge)(lambda: self.inward().start())

    def tick(self):
        self.age += 1
        if self.dp == 1:
            if self.age == self.END:
                self.fin[...] = self.halves[0]
            return
        s = self.where[0]
        inside = jnp.logical_not(self.edge)
        if self.age == self.LAG:

            @pl.when(inside)
            def _():
                self.inward().wait_recv()

                def fn(r):
                    total = self.halves[s, r, :].astype(f32) + self.land[r, :].astype(f32)
                    self.halves[s, r, :] = total.astype(bf16)

                self.sweep(self.first, self.size, fn)
                pl.when(jnp.logical_not(self.middle))(lambda: self.inward().start())

            @pl.when(self.middle)
            def _():
                if self.before is not None:
                    pl.semaphore_wait(self.free, 1)
                self.swap_part().start()

        if self.age == 2 * self.LAG:

            @pl.when(self.middle)
            def _():
                h = self.mine
                half = self.size // 2
                self.arrived(h)

                def fn(r):
                    total = self.halves[s, r, :].astype(f32) + self.fin[r, :].astype(f32)
                    self.fin[r, :] = total.astype(bf16)

                self.sweep(self.first + h * half, half, fn)
                self.swap_sum().start()
                pl.when(inside)(lambda: self.outward(h).start())
                self.swap_part().wait_send()

            pl.when(jnp.logical_not(self.middle))(lambda: self.inward().wait_send())

        if self.age == 3 * self.LAG:

            @pl.when(self.middle)
            def _():
                self.arrived(1 - self.mine)
                pl.when(inside)(lambda: self.outward(1 - self.mine).start())

        if self.age == self.END:

            @pl.when(jnp.logical_not(self.middle))
            def _():
                for h in (0, 1):
                    self.arrived(h)
                    pl.when(inside)(lambda h=h: self.outward(h).start())

            pl.when(self.middle)(lambda: self.swap_sum().wait_send())

            @pl.when(inside)
            def _():
                for h in (0, 1):
                    self.outward(h).wait_send()

            self.to_result()[0]()

    def arrived(self, h):
        ref = self.final(h)
        remote(ref, ref, self.sent.at[0], self.recv.at[h], self.where).wait_recv()

    def to_result(self):
        s = self.where[0]
        part = self.rows(self.first)
        target = self.result.at[s, part]
        return to_owner(
            self.owner, self.where, self.fin.at[part], target, target, self.ol, self.os, self.or_
        )

    def close(self):
        self.to_result()[1]()


class Background:
    def __init__(self):
        self.queue, self.active = [], []

    def put(self, pieces):
        self.queue += pieces

    def tick(self):
        for piece in self.active:
            piece.tick()
        self.active = [piece for piece in self.active if piece.age < piece.END]
        if self.queue:
            piece = self.queue.pop(0)
            piece.start()
            self.active.append(piece)

    def until(self, pieces, age):
        while any(piece.age < age for piece in pieces):
            self.tick()


def backward_kernel(
    dp, ct_in, y0_in, tok_in, cos2, sin2, scal,
    wi0, wo0, wfi0, wfo0, wi1, wo1, wfi1, wfo1, *refs,
):
    saved_i = (refs[0:14], refs[14:28])
    both_o, gwfi_o, gwfo_o, gmix_o = refs[28:32]
    (
        wi, wo, wfi, wfo, cosv, sinv, gf, xr, hidden, zq, zk, gate, q, k, v, att, sc, states, branch, mid,
        hid2, pair, mask, mask_t, qd, kd, terms, zout, zin, run, gpair, prod, gb, gm, dv, dk,
        gp, part, got, via, own, gr, gwfi, gwfo, gmix, c_fi, c_fo, c_mix, l_fi, l_fo, l_mix,
        f_fi, f_fo, f_mix, lsem, ssem, rsem, zs, zr, ol, os, or_, core_s, core_r, ls, lr, free,
    ) = refs[32:]
    where = s, d, t = place()
    rows = y0_in.shape[0]
    total = 4 * rows
    nb = total // BLOCK
    fp = wfo.shape[0]
    half = rows // 2
    table = nb + 4 + 4 * dp
    local = Sems(lsem)
    me = rows_of(t, rows)
    gated, gatt = slice(0, WIDTH), slice(WIDTH, 2 * WIDTH)

    def gatt_head(h):
        return slice(WIDTH + h * HEAD, WIDTH + (h + 1) * HEAD)

    def load(src, dst):
        copy = pltpu.make_async_copy(src, dst, local.take())
        copy.start()
        return copy

    def block_of(ref):
        return lambda p, h: ref.at[pl.ds(pl.multiple_of(p * rows + h * half, half), half)]

    weights = ((wi0, wo0, wfi0, wfo0), (wi1, wo1, wfi1, wfo1))

    def load_feed(layer):
        keep = saved_i[layer]
        return [
            load(weights[layer][3], wfo), load(keep[13], pair), load(weights[layer][2], wfi),
            load(keep[11], mid), load(keep[12], hid2),
        ]

    def load_gates(layer):
        keep = saved_i[layer]
        return [
            load(weights[layer][1], wo), load(keep[10], branch), load(keep[8], sc), load(keep[7], att),
            load(keep[3], gate),
        ]

    def load_attn(layer):
        keep = saved_i[layer]
        pairs = ((4, q), (5, k), (6, v), (9, states), (1, zq), (2, zk))
        return [load(keep[n], ref) for n, ref in pairs]

    def load_ends(layer):
        x = tok_in.at[s] if layer == 0 else y0_in
        return [load(weights[layer][0], wi), load(saved_i[layer][0], hidden), load(x, xr)]


    ff = l_fo.shape[0]
    pieces, pairs = {}, {}
    for layer in (1, 0):
        cuts = [(gwfo, 256 * n, min(256, ff - 256 * n), l_fo, f_fo, gwfo_o) for n in range(-(-ff // 256))]
        cuts += [(gwfi, 128 * n, 128, l_fi, f_fi, gwfi_o) for n in range(D // 128)]
        cuts += [(gmix, 256 * n, 256, l_mix, f_mix, gmix_o) for n in range((D + WIDTH) // 256)]
        made = []
        for n, cut in enumerate(cuts):
            slot = PIECES * layer + n
            sems = [ref.at[slot] for ref in (lr, ls)] + [free.at[n]]
            sems += [ref.at[slot] for ref in (ol, os, or_)]
            before = pieces[1][n] if layer == 0 else None
            made.append(LineSum(dp, where, s == layer, *cut, sems, before))
        pieces[layer] = made
        pairs[layer] = [
            CorePair(where, halves, landed, core_s.at[3 * layer + n], core_r.at[3 * layer + n])
            for n, (halves, landed) in enumerate(((gwfo, c_fo), (gwfi, c_fi), (gmix, c_mix)))
        ]
    n_out, n_feed = -(-ff // 256), -(-ff // 256) + D // 128
    work = Background()
    tick = work.tick

    got_g = load(ct_in.at[s], gf.at[me])
    in_feed, in_tables = load_feed(1), [load(cos2, cosv), load(sin2, sinv)]
    in_gates, in_attn, in_ends = load_gates(1), load_attn(1), load_ends(1)
    entry(dp, s, d, t, core=True)
    got_g.wait()
    in_out = []

    for layer in (1, 0):
        offset = table * layer
        pair_fo, pair_fi, pair_mix = pairs[layer]
        base = 24 * layer
        gg = Gather(block_of(gf), half, ssem, rsem, base, where)
        gg.start()
        decay_fill(scal, offset, nb, mask, mask_t, qd, kd)
        if layer == 0:
            pairs[1][2].add()
            work.put(pieces[1][n_feed:])
        tick()
        for copy in in_feed:
            copy.wait()
        sums = Scatter(part, got, via, rows, ssem, rsem, base + 6, where)

        def feed(i, c):
            for n in (1, 2, 3):

                @pl.when(i == n)
                def _(n=n):
                    if n == 1:
                        gg.forward()
                    if n == 3:
                        tick()
                    gg.ready(n)

            r = rows_of(partner(t, i), rows)
            grad = nt(gf[r, :], wfo[...])
            p0, p1 = pair[0, r, :].astype(f32), pair[1, r, :].astype(f32)
            prod[r, :] = (p0 * p1).astype(bf16)
            g0, g1 = (grad * p1).astype(bf16), (grad * p0).astype(bf16)
            gpair[0, r, :] = g0
            gpair[1, r, :] = g1
            o = nt(g0, wfi[0]) + nt(g1, wfi[1])
            for n in (1, 2, 3):

                @pl.when(i == n)
                def _(n=n):
                    sums.put(n, o)

            @pl.when(i == 0)
            def _():
                own[...] = o

            return c

        lax.fori_loop(0, 4, feed, 0)

        def feed_weights(n, c):
            cols = rows_of(n, 256)
            a = hid2[:, cols]
            gwfi[0, cols, :] = tn(a, gpair[0]).astype(bf16)
            gwfi[1, cols, :] = tn(a, gpair[1]).astype(bf16)
            return c

        def out_weights(n, c):
            cols = rows_of(n, 256)
            a = prod[:, cols]
            gwfo[0, cols, :] = tn(a, gf[:, : D // 2]).astype(bf16)
            gwfo[1, cols, :] = tn(a, gf[:, D // 2 :]).astype(bf16)
            return c

        if layer == 0:
            work.until(pieces[1][:n_feed], 2 * LineSum.LAG)
        lax.fori_loop(0, fp // 256, out_weights, 0)
        pair_fo.send()
        lax.fori_loop(0, D // 256, feed_weights, 0)
        pair_fi.send()
        tick()
        sums.combine()
        pair_fo.add()
        work.put(pieces[layer][:n_out])
        tick()
        pair_fi.add()
        work.put(pieces[layer][n_out:n_feed])
        grad_middle = gf[me, :].astype(f32) + norm_back(mid[...], own[...] + sums.result())
        gm[...] = grad_middle
        gb[me, :] = grad_middle.astype(bf16)
        sums.drain()
        gg.drain()

        gbg = Gather(block_of(gb), half, ssem, rsem, base + 12, where)
        gbg.start()
        if layer == 1:
            in_feed = load_feed(0)
        tick()
        for copy in in_gates:
            copy.wait()

        def gating(i, c):
            for n in (1, 2, 3):

                @pl.when(i == n)
                def _(n=n):
                    if n == 1:
                        gbg.forward()
                    if n == 3:
                        tick()
                    gbg.ready(n)

            r = rows_of(partner(t, i), rows)
            b = gb[r, :]
            grad = nt(b, wo[...])
            dots = jnp.sum(b.astype(f32) * branch[r, :].astype(f32), axis=-1, keepdims=True) * (1.0 / D)
            scale = sc[r, 0:1]
            normed = att[r, :] * scale
            gt = gate[r, :]
            gp[r, 3 * WIDTH :] = (grad * normed).astype(bf16)
            prod[r, gated] = (normed * gt).astype(bf16)
            prod[r, gatt] = (scale * (grad * gt - normed * dots)).astype(bf16)
            return c

        lax.fori_loop(0, 4, gating, 0)
        if layer == 1:
            in_gates = load_gates(0)
        for copy in in_attn:
            copy.wait()
        if layer == 1:
            for copy in in_tables:
                copy.wait()

        def term(b, c):
            r = rows_of(b, BLOCK)
            for h in range(HEADS_HERE):
                qdec = (q[r, head(h)].astype(f32) * qd[h]).astype(bf16)
                terms[b, h] = tn(qdec, prod[r, gatt_head(h)])
            return c

        lax.fori_loop(0, nb, term, 0)
        for h in range(HEADS_HERE):
            carried = scal[offset + nb - 1] * terms[nb - 1, h]
            for b in reversed(range(nb - 1)):
                carried = scal[offset + b] * (terms[b, h] + scal[offset + nb + 2 + h] * carried)
            zout[layer, h] = carried.astype(bf16)
        z_args = (dp, where, zout.at[layer], zin.at[layer], zs.at[layer], zr.at[layer], False)
        send_states(*z_args)
        tick()

        def unturn(pre, grad, r, h):
            back = grad * cosv[r, :] - pltpu.roll(grad, HEAD // 2, 1) * sinv[r, :]
            z = pre[r, head(h)]
            g = sig(z)
            return (back * (g * (1.0 + z * (1.0 - g)))).astype(bf16)

        def inner(b, c):
            r = rows_of(b, BLOCK)
            for h in range(HEADS_HERE):
                qh, kh, vh, gh = q[r, head(h)], k[r, head(h)], v[r, head(h)], prod[r, gatt_head(h)]
                w_t = (nt(kh, qh) * mask_t[h]).astype(bf16)
                dv[r, head(h)] = nn(w_t, gh)
                ds = (nt(gh, vh) * mask[h]).astype(bf16)
                ds_t = (nt(vh, gh) * mask_t[h]).astype(bf16)
                dk[r, head(h)] = nn(ds_t, qh)
                dq = nn(ds, kh) + nt(gh, states[b, h].astype(bf16)) * qd[h]
                gp[r, head(h)] = unturn(zq, dq, r, h)
            return c

        lax.fori_loop(0, nb, inner, 0)
        tick()
        take_states(*z_args, scal, offset + nb + 4 + 2 * dp, run)

        def outer(i, c):
            b = nb - 1 - i
            r = rows_of(b, BLOCK)
            for h in range(HEADS_HERE):
                after = run[h]
                low = after.astype(bf16)
                run[h] = scal[offset + b] * (terms[b, h] + scal[offset + nb + 2 + h] * after)
                kdec = (k[r, head(h)].astype(f32) * kd[h]).astype(bf16)
                dkh = dk[r, head(h)] + nt(v[r, head(h)], low) * kd[h]
                k_cols = slice(WIDTH + h * HEAD, WIDTH + (h + 1) * HEAD)
                v_cols = slice(2 * WIDTH + h * HEAD, 2 * WIDTH + (h + 1) * HEAD)
                gp[r, k_cols] = unturn(zk, dkh, r, h)
                gp[r, v_cols] = (dv[r, head(h)] + nn(kdec, low)).astype(bf16)
            return c

        lax.fori_loop(0, nb, outer, 0)
        tick()
        if layer == 1:
            in_attn = load_attn(0)
        for copy in in_ends:
            copy.wait()
        ins = Scatter(part, got, via, rows, ssem, rsem, base + 18, where)

        def back_in(i, c):
            e = 3 - i
            r = rows_of(partner(t, e), rows)
            o = nt(gp[r, :], wi[...])
            for n in (1, 2, 3):

                @pl.when(e == n)
                def _(n=n):
                    ins.put(n, o)

            @pl.when(e == 0)
            def _():
                own[...] = o

            return c

        lax.fori_loop(0, 4, back_in, 0)
        tick()
        if layer == 0:
            work.until(pieces[1], 2 * LineSum.LAG)

        def in_weights(n, c):
            cols = rows_of(n, 256)
            a = hidden[:, cols]
            gmix[0, cols, :] = tn(a, gp[:, : 2 * WIDTH]).astype(bf16)
            gmix[1, cols, :] = tn(a, gp[:, 2 * WIDTH :]).astype(bf16)
            return c

        lax.fori_loop(0, D // 256, in_weights, 0)
        gmix[0, D:, :] = tn(prod[:, gated], gb[:, : D // 2]).astype(bf16)
        gmix[1, D:, :] = tn(prod[:, gated], gb[:, D // 2 :]).astype(bf16)
        pair_mix.send()
        ins.combine()
        tick()
        dx = gm[...] + norm_back(xr[...].astype(f32), own[...] + ins.result())
        gr[layer] = dx.astype(bf16)
        ins.drain()
        gbg.drain()
        sent_states(*z_args)
        start, finish = to_owner(
            s == layer, where, gr.at[layer], both_o.at[s], both_o.at[s],
            ol.at[2 * PIECES + layer], os.at[2 * PIECES + layer], or_.at[2 * PIECES + layer],
        )
        start()
        in_out.append(finish)
        if layer == 1:
            gf[me, :] = gr[layer]
            in_ends = load_ends(0)

    pairs[0][2].add()
    work.put(pieces[0][n_feed:])
    work.until(pieces[0], LineSum.END)
    for piece in pieces[0]:
        piece.close()
    for finish in in_out:
        finish()


def layers_backward(cotangent, y0, tokens, cos2, sin2, scal, weights, saved, dp, ff, uid):
    rows = y0.shape[-2]
    total = 4 * rows
    nb = total // BLOCK
    fp = weights[0][3].shape[0]
    mixed = D + WIDTH
    outs = [
        ((2, rows, D), bf16), ((2, D, fp), bf16), ((2, fp, D // 2), bf16), ((2, mixed, D // 2), bf16)
    ]
    scratch = [
        ((D, 4 * WIDTH), bf16), ((WIDTH, D), bf16), ((2, D, fp), bf16), ((fp, D), bf16),
        ((total, HEAD), f32), ((total, HEAD), f32), ((total, D), bf16), ((rows, D), bf16),
    ]
    scratch += [(a.shape, a.dtype) for a in saved[0]]
    scratch += [
        ((HEADS_HERE, BLOCK, BLOCK), f32), ((HEADS_HERE, BLOCK, BLOCK), f32),
        ((HEADS_HERE, BLOCK, HEAD), f32), ((HEADS_HERE, BLOCK, HEAD), f32),
        ((nb, HEADS_HERE, HEAD, HEAD), f32), ((2, HEADS_HERE, HEAD, HEAD), bf16),
        ((2, dp, HEADS_HERE, HEAD, HEAD), bf16), ((HEADS_HERE, HEAD, HEAD), f32),
        ((2, total, fp), bf16), ((total, fp), bf16), ((total, D), bf16), ((rows, D), f32),
        ((total, WIDTH), f32), ((total, WIDTH), f32),
        ((total, 4 * WIDTH), bf16),
        ((3, rows, D), bf16), ((2, rows, D), bf16), ((2, rows // 2, D), bf16), ((rows, D), f32),
        ((2, rows, D), bf16),
        ((2, D, fp), bf16), ((2, fp, D // 2), bf16), ((2, mixed, D // 2), bf16),
        ((D, fp), bf16), ((fp, D // 2), bf16), ((mixed, D // 2), bf16),
        ((D, fp), bf16), ((ff, D // 2), bf16), ((mixed, D // 2), bf16),
        ((D, fp), bf16), ((ff, D // 2), bf16), ((mixed, D // 2), bf16),
    ]
    count = 2 * PIECES
    dma = pltpu.SemaphoreType.DMA
    flops = 8 * total * D * (4 * WIDTH + WIDTH + 3 * fp)
    flat = [w for layer in weights for w in layer]
    kept = [a for layer in saved for a in layer]
    return pl.pallas_call(
        functools.partial(backward_kernel, dp),
        out_shape=tuple(jax.ShapeDtypeStruct(a, b) for a, b in outs),
        in_specs=[ANY] * 5 + [SMEM] + [ANY] * (len(flat) + len(kept)),
        out_specs=(ANY,) * len(outs),
        scratch_shapes=[pltpu.VMEM(a, b) for a, b in scratch]
        + [
            dma((48,)), dma((48,)), dma((48,)), dma((2, dp)), dma((2, dp)), dma((count + 2,)),
            dma((count + 2,)), dma((count + 2,)), dma((6,)), dma((6,)), dma((count, 4)),
            dma((count, 3)), pltpu.SemaphoreType.REGULAR((PIECES,)),
        ],
        compiler_params=pltpu.CompilerParams(
            collective_id=uid, has_side_effects=True, vmem_limit_bytes=VMEM_BYTES
        ),
        cost_estimate=pl.CostEstimate(flops=flops, bytes_accessed=60 << 20, transcendentals=0),
        name="layers_backward",
    )(cotangent, y0, tokens, cos2, sin2, scal, *flat, *kept)


def angle_tables(starts, blocks):
    d = lax.axis_index("dp")
    at = jnp.arange(starts.shape[0], dtype=jnp.int32)
    begins = jnp.max(
        jnp.where((at[None, :] <= at[:, None]) & (starts > 0)[None, :], at[None, :], 0), axis=1
    )
    offsets = lax.dynamic_slice_in_dim((at - begins) * BLOCK, d * blocks, blocks)
    places = (offsets[:, None] + jnp.arange(BLOCK, dtype=jnp.int32)[None, :]).reshape(-1)
    lane = jnp.arange(HEAD, dtype=jnp.int32)
    frequency = 10000.0 ** (-(lane % (HEAD // 2)).astype(f32) / (HEAD // 2))
    angles = places.astype(f32)[:, None] * frequency[None, :]
    return jnp.cos(angles), jnp.where(lane < HEAD // 2, -1.0, 1.0)[None, :] * jnp.sin(angles)


def swap(x):
    return lax.ppermute(x, "section", [(0, 1), (1, 0)])


def mine_first(s, a, b):
    return jnp.where(s == 0, a, b)


def shards(tokens, cotangent, mixer_in, mixer_out, feed_in, feed_out, decay_rate, block_starts):
    s = lax.axis_index("section")
    dp = lax.axis_size("dp")
    rows = tokens.shape[1]
    blocks = 4 * rows // BLOCK
    ff = feed_out.shape[1]
    fp = -(-ff // 256) * 256
    wi = mixer_in[0].reshape(D, 4 * WIDTH)
    wfi = jnp.pad(jnp.swapaxes(feed_in[0], 0, 1), ((0, 0), (0, 0), (0, fp - ff)))
    mine = (wi, mixer_out[0], wfi, feed_out[0])
    other_rates = swap(decay_rate[0])
    rates = (mine_first(s, decay_rate[0], other_rates), mine_first(s, other_rates, decay_rate[0]))
    starts = lax.dynamic_index_in_dim(block_starts, s, 0, keepdims=False)
    cos2, sin2 = angle_tables(starts, blocks)
    scal = [scalar_table(starts, r, dp, blocks) for r in rates]

    both0, *out0 = layer_forward(0, True, tokens, mine, cos2, sin2, scal[0], dp, 1)
    weights0, y0, saved0 = out0[:4], out0[4], out0[5:]
    both1, *out1 = layer_forward(1, False, y0, mine, cos2, sin2, scal[1], dp, 2)
    weights1, saved1 = out1[:4], out1[5:]
    in_grads, g_fi, g_fo, g_mix = layers_backward(
        cotangent, y0, tokens, cos2, sin2, jnp.concatenate(scal), (weights0, weights1),
        (saved0, saved1), dp, ff, 3,
    )
    outputs = mine_first(s, both0, both1)
    g_in = jnp.concatenate([g_mix[0, :D], g_mix[1, :D]], axis=1).astype(f32).reshape(D, 4, WIDTH)
    g_out = jnp.concatenate([g_mix[0, D:], g_mix[1, D:]], axis=1).astype(f32)
    g_feed_in = jnp.swapaxes(g_fi[:, :, :ff], 0, 1).astype(f32)
    g_feed_out = jnp.concatenate([g_fo[0, :ff], g_fo[1, :ff]], axis=1).astype(f32)
    return outputs[None], in_grads[None], g_in[None], g_out[None], g_feed_in[None], g_feed_out[None]


def solution(mesh):
    placed = (
        P(None, ("dp", "tensor"), None),
        P(None, ("dp", "tensor"), None),
        P("section", None, None, "tensor"),
        P("section", "tensor", None),
        P("section", None, None, "tensor"),
        P("section", "tensor", None),
        P("section", "tensor"),
        P(),
    )
    return jax.shard_map(
        shards,
        mesh=mesh,
        in_specs=placed,
        out_specs=(
            P("section", None, ("dp", "tensor"), None),
            P("section", None, ("dp", "tensor"), None),
            P("section", None, None, "tensor"),
            P("section", "tensor", None),
            P("section", None, None, "tensor"),
            P("section", "tensor", None),
        ),
        check_vma=False,
    )
```

```python
import functools

import jax
import jax.numpy as jnp
from jax import lax
from jax.experimental import pallas as pl
from jax.experimental.pallas import tpu as pltpu
from jax.sharding import PartitionSpec as P

D = 1024
HEAD = 128
BLOCK = 256
WIDTH = 256
HEADS_HERE = WIDTH // HEAD
norm_eps = 1e-06
MESH = pl.DeviceIdType.MESH
ANY = pl.BlockSpec(memory_space=pl.ANY)
SMEM = pl.BlockSpec(memory_space=pltpu.SMEM)
bf16, f32 = jnp.bfloat16, jnp.float32
PIECES = 16
VMEM_BYTES = 62 * 1024 * 1024


def place():
    return lax.axis_index("section"), lax.axis_index("dp"), lax.axis_index("tensor")


def partner(t, k):
    return ((t // 2 + k // 2) % 2) * 2 + (t + k) % 2


class Sems:
    def __init__(self, ref):
        self.ref, self.used = ref, 0

    def take(self):
        self.used += 1
        return self.ref.at[self.used - 1]


def remote(src, dst, send, recv, dev):
    return pltpu.make_async_remote_copy(
        src_ref=src, dst_ref=dst, send_sem=send, recv_sem=recv, device_id=dev, device_id_type=MESH
    )


def nn(a, b):
    return lax.dot_general(a, b, (((1,), (0,)), ((), ())), preferred_element_type=f32)


def nt(a, b):
    return lax.dot_general(a, b, (((1,), (1,)), ((), ())), preferred_element_type=f32)


def tn(a, b):
    return lax.dot_general(a, b, (((0,), (0,)), ((), ())), preferred_element_type=f32)


def rms_scale(v):
    return lax.rsqrt(jnp.mean(v * v, axis=-1, keepdims=True) + norm_eps)


def norm_back(v, u):
    q = rms_scale(v)
    n = v * q
    return q * (u - n * jnp.mean(u * n, axis=-1, keepdims=True))


def sig(v):
    return 1.0 / (1.0 + jnp.exp(-v))


def rows_of(p, n):
    return pl.ds(pl.multiple_of(p * n, n), n)


def entry(dp, s, d, t, core=False):
    barrier = pltpu.get_barrier_semaphore()
    count = 3
    for k in (1, 2, 3):
        pl.semaphore_signal(barrier, inc=1, device_id=(s, d, partner(t, k)), device_id_type=MESH)
    if core:
        pl.semaphore_signal(barrier, inc=1, device_id=(1 - s, d, t), device_id_type=MESH)
        count += 1
    if dp > 1:

        def greet(k, c):
            pl.semaphore_signal(
                barrier, inc=1, device_id=(s, (d + k) % dp, t), device_id_type=MESH
            )
            return c

        lax.fori_loop(1, dp, greet, 0)
        count += dp - 1
    pl.semaphore_wait(barrier, count)


class Gather:
    def __init__(self, block_at, half, ssem, rsem, base, where):
        self.at, self.half, self.ssem, self.rsem, self.base = block_at, half, ssem, rsem, base
        self.where = where

    def copy(self, n, peer, half, to):
        s, d, t = self.where
        ref = self.at(partner(t, peer), half)
        k = self.base + n
        return remote(ref, ref, self.ssem.at[k], self.rsem.at[k], (s, d, partner(t, to)))

    def mine(self, n):
        peer, half, to = ((0, 0, 1), (0, 1, 1), (0, 0, 2), (0, 1, 2), (1, 0, 2), (2, 1, 1))[n]
        return self.copy(n, peer, half, to)

    def arriving(self, n):
        s, d, t = self.where
        peer, half = ((1, 0), (1, 1), (2, 0), (2, 1), (3, 0), (3, 1))[n]
        ref = self.at(partner(t, peer), half)
        k = self.base + n
        return remote(ref, ref, self.ssem.at[k], self.rsem.at[k], (s, d, t))

    def start(self):
        self.mine(0).start()
        self.mine(3).start()
        self.mine(1).start()
        self.mine(2).start()

    def forward(self):
        self.arriving(0).wait_recv()
        self.mine(4).start()
        self.arriving(3).wait_recv()
        self.mine(5).start()

    def ready(self, k):
        if k == 1:
            self.arriving(1).wait_recv()
        elif k == 2:
            self.arriving(2).wait_recv()
        else:
            self.arriving(4).wait_recv()
            self.arriving(5).wait_recv()

    def drain(self):
        for n in range(6):
            self.mine(n).wait_send()


class Scatter:
    def __init__(self, part, got, via, rows, ssem, rsem, base, where):
        self.part, self.got, self.via, self.half = part, got, via, rows // 2
        self.ssem, self.rsem, self.base, self.where = ssem, rsem, base, where

    def copy(self, n):
        s, d, t = self.where
        h = self.half
        h0, h1 = pl.ds(0, h), pl.ds(h, h)
        src, dst, to = (
            (self.part.at[2, h0], self.via.at[0], 2),
            (self.part.at[2, h1], self.via.at[1], 1),
            (self.part.at[0, h1], self.got.at[0, h1], 1),
            (self.part.at[1, h0], self.got.at[1, h0], 2),
            (self.part.at[0, h0], self.got.at[0, h0], 1),
            (self.part.at[1, h1], self.got.at[1, h1], 2),
        )[n]
        k = self.base + n
        return remote(src, dst, self.ssem.at[k], self.rsem.at[k], (s, d, partner(t, to)))

    def put(self, k, value):
        self.part[k - 1] = value.astype(bf16)
        self.send(k)

    def send(self, k):
        if k == 3:
            self.copy(0).start()
            self.copy(1).start()
        elif k == 2:
            self.copy(3).start()
        else:
            self.copy(2).start()

    def combine(self):
        h = self.half
        self.copy(0).wait_recv()
        self.part[0, 0:h] = (self.part[0, 0:h].astype(f32) + self.via[0].astype(f32)).astype(bf16)
        self.copy(4).start()
        self.copy(1).wait_recv()
        self.part[1, h:] = (self.part[1, h:].astype(f32) + self.via[1].astype(f32)).astype(bf16)
        self.copy(5).start()

    def result(self):
        for n in (2, 3, 4, 5):
            self.copy(n).wait_recv()
        return self.got[0].astype(f32) + self.got[1].astype(f32)

    def drain(self):
        for n in range(6):
            self.copy(n).wait_send()


def scalar_table(starts, rates, dp, blocks):
    d = lax.axis_index("dp")
    survive = 1.0 - starts.astype(f32).reshape(dp, blocks)
    decay = jnp.exp(-rates * BLOCK)
    factor = jnp.prod(survive, axis=1)[:, None] * (decay**blocks)[None, :]
    at = jnp.arange(dp)
    low, high = jnp.minimum(at, d), jnp.maximum(at, d)
    between = (at[None, :] > low[:, None]) & (at[None, :] < high[:, None])
    through = jnp.prod(jnp.where(between[:, :, None], factor[None], 1.0), axis=1)
    forward = jnp.where((at < d)[:, None], through, 0.0)
    backward = jnp.where((at > d)[:, None], through, 0.0)
    mine = lax.dynamic_index_in_dim(survive, d, 0, keepdims=False)
    return [mine, rates, decay, forward.reshape(-1), backward.reshape(-1)]


def decay_fill(scal, base, nb, mask, mask_t, qd, kd):
    for h in range(HEADS_HERE):
        r = scal[base + nb + h]
        i = lax.broadcasted_iota(jnp.int32, (BLOCK, BLOCK), 0).astype(f32)
        j = lax.broadcasted_iota(jnp.int32, (BLOCK, BLOCK), 1).astype(f32)
        gap = i - j
        mask[h] = jnp.where(gap >= 0.0, jnp.exp(-r * jnp.maximum(gap, 0.0)), 0.0)
        if mask_t is not None:
            mask_t[h] = jnp.where(gap <= 0.0, jnp.exp(-r * jnp.maximum(-gap, 0.0)), 0.0)
        i = lax.broadcasted_iota(jnp.int32, (BLOCK, HEAD), 0).astype(f32)
        qd[h] = jnp.exp(-r * (i + 1.0))
        kd[h] = jnp.exp(-r * (BLOCK - 1.0 - i))


def head(h):
    return slice(h * HEAD, (h + 1) * HEAD)


def send_states(dp, where, zout, zin, zs, zr, later):
    s, d, t = where

    def each(k, c):
        to = d + k if later else d - k

        @pl.when((to < dp) if later else (to >= 0))
        def _():
            remote(zout, zin.at[d], zs.at[k], zr.at[d], (s, to, t)).start()

        return c

    lax.fori_loop(1, dp, each, 0)


def sent_states(dp, where, zout, zin, zs, zr, later):
    s, d, t = where

    def each(k, c):
        to = d + k if later else d - k

        @pl.when((to < dp) if later else (to >= 0))
        def _():
            remote(zout, zin.at[d], zs.at[k], zr.at[d], (s, to, t)).wait_send()

        return c

    lax.fori_loop(1, dp, each, 0)


def take_states(dp, where, zout, zin, zs, zr, later, scal, base, run):
    s, d, t = where
    run[...] = jnp.zeros_like(run)

    def each(k, c):
        @pl.when((k < d) if later else (k > d))
        def _():
            remote(zout, zin.at[k], zs.at[0], zr.at[k], (s, d, t)).wait_recv()
            for h in range(HEADS_HERE):
                run[h] += scal[base + 2 * k + h] * zin[k, h].astype(f32)

        return c

    lax.fori_loop(0, dp, each, 0)


class Fetch:
    def __init__(self, src, dst, owner, where, lsem, ssem, rsem):
        s, d, t = where
        self.owner = owner
        self.local = lambda: pltpu.make_async_copy(src, dst, lsem)
        self.far = lambda: remote(src, dst, ssem, rsem, (1 - s, d, t))

    def read(self):
        pl.when(self.owner)(lambda: self.local().start())

    def send(self):
        pl.when(self.owner)(lambda: self.far().start())

    def wait(self):
        pl.when(self.owner)(lambda: self.local().wait())
        pl.when(jnp.logical_not(self.owner))(lambda: self.far().wait_recv())

    def drain(self):
        pl.when(self.owner)(lambda: self.far().wait_send())


def to_owner(owner, where, src, own_dst, far_dst, lsem, ssem, rsem):
    s, d, t = where

    def far():
        return remote(src, far_dst, ssem, rsem, (1 - s, d, t))

    def local():
        return pltpu.make_async_copy(src, own_dst, lsem)

    def start():
        pl.when(owner)(lambda: local().start())
        pl.when(jnp.logical_not(owner))(lambda: far().start())

    def finish():
        @pl.when(owner)
        def _():
            local().wait()
            far().wait_recv()

        pl.when(jnp.logical_not(owner))(lambda: far().wait_send())

    return start, finish


def forward_kernel(
    dp, layer, first, x_in, my_wi, my_wo, my_wfi, my_wfo, cos2, sin2, scal,
    both_o, wi_o, wo_o, wfi_o, wfo_o, y_out, hidden_o, zq_o, zk_o, gate_o, q_o, k_o, v_o, att_o, sc_o, states_o, branch_o, mid_o,
    hid2_o, pair_o,
    wi, wo, wfi, wfo, cosv, sinv, xf, hidden, zq, zk, gate, q, k, v, att, sc, states, branch, mid, hid2,
    pair, mask, qd, kd, loc, zout, zin, run, u, y, part, got, via, ssq, own, yb,
    lsem, ssem, rsem, zs, zr, wl, ws, wr,
):
    where = s, d, t = place()
    rows = x_in.shape[-2]
    total = 4 * rows
    nb = total // BLOCK
    at = layer * (nb + 4 + 4 * dp)
    local = Sems(lsem)

    def load(src, dst):
        copy = pltpu.make_async_copy(src, dst, local.take())
        copy.start()
        return copy

    x_src = x_in.at[s] if first else x_in
    got_x = load(x_src, xf.at[rows_of(t, rows)])
    owner = s == layer
    ff = my_wfo.shape[0]
    pairs = (
        (my_wi, wi), (my_wo, wo.at[rows_of(t, WIDTH)]), (my_wfi, wfi.at[:, pl.ds(0, ff)]),
        (my_wfo, wfo.at[pl.ds(0, ff)]),
    )
    got_w = [
        Fetch(src, dst, owner, where, wl.at[n], ws.at[n], wr.at[n])
        for n, (src, dst) in enumerate(pairs)
    ]
    got_wi, got_wo, got_wfi, got_wfo = got_w
    got_wi.read()
    got_cos, got_sin = load(cos2, cosv), load(sin2, sinv)
    for fetch in got_w[1:]:
        fetch.read()
    wfi[:, ff:, :] = jnp.zeros_like(wfi[:, ff:, :])
    wfo[ff:, :] = jnp.zeros_like(wfo[ff:, :])
    entry(dp, s, d, t, core=True)
    got_x.wait()

    half = rows // 2
    gx = Gather(
        lambda p, h: xf.at[pl.ds(pl.multiple_of(p * rows + h * half, half), half)],
        half, ssem, rsem, 0, where,
    )
    quarter = WIDTH // 2
    gw = Gather(
        lambda p, h: wo.at[pl.ds(pl.multiple_of(p * WIDTH + h * quarter, quarter), quarter)],
        quarter, ws, wr, 4, where,
    )

    def wo_over(k):
        ref = wo.at[rows_of(partner(t, k), WIDTH)]
        return remote(ref, ref, ws.at[10 + k], wr.at[10 + k], (1 - s, d, t))

    gx.start()
    for fetch in got_w:
        fetch.send()
    decay_fill(scal, at, nb, mask, None, qd, kd)
    got_wi.wait()
    got_cos.wait()
    got_sin.wait()

    def project(i, c):
        for n in (1, 2, 3):

            @pl.when(i == n)
            def _(n=n):
                if n == 1:
                    gx.forward()

                    @pl.when(owner)
                    def _():
                        got_wo.local().wait()
                        gw.start()

                gx.ready(n)

        r = rows_of(partner(t, i), rows)
        xv = xf[r, :].astype(f32)
        hid = (xv * rms_scale(xv)).astype(bf16)
        hidden[r, :] = hid
        cs, sn = cosv[r, :], sinv[r, :]
        for n, (pre, post) in enumerate(((zq, q), (zk, k))):
            z = nn(hid, wi[:, n * WIDTH : (n + 1) * WIDTH])
            pre[r, :] = z
            a = z * sig(z)
            for h in range(HEADS_HERE):
                ah = a[:, head(h)]
                post[r, head(h)] = (ah * cs + pltpu.roll(ah, HEAD // 2, 1) * sn).astype(bf16)
        v[r, :] = nn(hid, wi[:, 2 * WIDTH : 3 * WIDTH]).astype(bf16)
        gate[r, :] = nn(hid, wi[:, 3 * WIDTH :])
        return c

    lax.fori_loop(0, 4, project, 0)

    stores = [load(hidden, hidden_o), load(zq, zq_o), load(zk, zk_o), load(gate, gate_o)]
    stores += [load(q, q_o), load(k, k_o), load(v, v_o)]

    def local_state(b, c):
        r = rows_of(b, BLOCK)
        for h in range(HEADS_HERE):
            kdec = (k[r, head(h)].astype(f32) * kd[h]).astype(bf16)
            loc[b, h] = tn(kdec, v[r, head(h)])
        return c

    lax.fori_loop(0, nb, local_state, 0)
    pl.when(owner)(gw.forward)
    for h in range(HEADS_HERE):
        carried = loc[0, h]
        for b in range(1, nb):
            carried = (scal[at + nb + 2 + h] * scal[at + b]) * carried + loc[b, h]
        zout[h] = carried.astype(bf16)
    send_states(dp, where, zout, zin, zs, zr, True)

    def inner(b, c):
        r = rows_of(b, BLOCK)
        for h in range(HEADS_HERE):
            w = (nt(q[r, head(h)], k[r, head(h)]) * mask[h]).astype(bf16)
            att[r, head(h)] = nn(w, v[r, head(h)])
        return c

    lax.fori_loop(0, nb, inner, 0)
    take_states(dp, where, zout, zin, zs, zr, True, scal, at + nb + 4, run)

    def outer(b, c):
        r = rows_of(b, BLOCK)
        for h in range(HEADS_HERE):
            entering = scal[at + b] * run[h]
            states[b, h] = entering
            run[h] = scal[at + nb + 2 + h] * entering + loc[b, h]
            qdec = (q[r, head(h)].astype(f32) * qd[h]).astype(bf16)
            a = att[r, head(h)] + nn(qdec, entering.astype(bf16))
            att[r, head(h)] = a
            u[t, r, head(h)] = (a * gate[r, head(h)]).astype(bf16)
        return c

    lax.fori_loop(0, nb, outer, 0)

    hu = total // 2
    gu = Gather(lambda p, h: u.at[p, pl.ds(h * hu, hu)], hu, ssem, rsem, 6, where)
    gu.start()
    for b in range(nb):
        a = att[b * BLOCK : (b + 1) * BLOCK, :]
        ssq[0, :, b * BLOCK : (b + 1) * BLOCK] = lax.dot_general(
            jnp.ones((8, WIDTH), f32), a * a, (((1,), (1,)), ((), ())),
            preferred_element_type=f32, precision=lax.Precision.HIGHEST,
        )
    sums = [
        remote(ssq.at[0], ssq.at[n], ssem.at[11 + n], rsem.at[11 + n], (s, d, partner(t, n)))
        for n in (1, 2, 3)
    ]
    for copy in sums:
        copy.start()
    stores += [load(att, att_o), load(states, states_o)]
    @pl.when(owner)
    def _():
        for n in (1, 2, 3):
            gw.ready(n)
            wo_over(n).start()

    @pl.when(jnp.logical_not(owner))
    def _():
        got_wo.far().wait_recv()
        for n in (1, 2, 3):
            wo_over(n).wait_recv()

    y[...] = jnp.zeros_like(y)

    def out_project(i, c):
        for n in (1, 2, 3):

            @pl.when(i == n)
            def _(n=n):
                if n == 1:
                    gu.forward()
                gu.ready(n)

        p = partner(t, i)

        def chunk(m, c):
            r = rows_of(m, rows)
            y[r, :] += nn(u[p, r, :], wo[rows_of(p, WIDTH), :])
            return c

        return lax.fori_loop(0, 4, chunk, c)

    lax.fori_loop(0, 4, out_project, 0)
    for copy in sums:
        copy.wait_recv()
    whole = ssq[0] + ssq[1] + ssq[2] + ssq[3]
    sc[...] = jnp.transpose(lax.rsqrt(whole * (1.0 / D) + norm_eps))
    got_wfi.wait()
    got_wfo.wait()
    out = Scatter(part, got, via, rows, ssem, rsem, 15, where)

    def feed(i, c):
        e = 3 - i
        r = rows_of(partner(t, e), rows)
        br = sc[r, 0:1] * y[r, :]
        branch[r, :] = br.astype(bf16)
        m = xf[r, :].astype(f32) + br
        h2 = (m * rms_scale(m)).astype(bf16)
        hid2[r, :] = h2
        p0, p1 = nt(h2, wfi[0]), nt(h2, wfi[1])
        pair[0, r, :] = p0.astype(bf16)
        pair[1, r, :] = p1.astype(bf16)
        o = nn((p0 * p1).astype(bf16), wfo[...])
        for n in (1, 2, 3):

            @pl.when(e == n)
            def _(n=n):
                out.put(n, o)

        @pl.when(e == 0)
        def _():
            mid[...] = m
            own[...] = o + m

        return c

    lax.fori_loop(0, 4, feed, 0)
    stores += [load(sc, sc_o), load(branch, branch_o), load(mid, mid_o), load(hid2, hid2_o)]
    stores += [load(pair, pair_o), load(wi, wi_o), load(wo.at[rows_of(t, WIDTH)], wo_o)]
    stores += [load(wfi, wfi_o), load(wfo, wfo_o)]
    out.combine()
    yb[...] = (own[...] + out.result()).astype(bf16)
    stores += [load(yb, y_out)]
    start, finish = to_owner(
        owner, where, yb, both_o.at[s], both_o.at[s], wl.at[4], ws.at[14], wr.at[14]
    )
    start()
    for fetch in got_w:
        fetch.drain()

    @pl.when(owner)
    def _():
        for n in (1, 2, 3):
            wo_over(n).wait_send()
        gw.drain()

    finish()
    gx.drain()
    gu.drain()
    out.drain()
    for copy in sums:
        copy.wait_send()
    sent_states(dp, where, zout, zin, zs, zr, True)
    for copy in stores:
        copy.wait()


def layer_forward(layer, first, x, weights, cos2, sin2, scal, dp, uid):
    rows = x.shape[-2]
    total = 4 * rows
    nb = total // BLOCK
    fp = -(-weights[3].shape[0] // 256) * 256
    saved = [
        ((rows, D), bf16), ((total, D), bf16), ((total, WIDTH), f32), ((total, WIDTH), f32),
        ((total, WIDTH), f32), ((total, WIDTH), bf16), ((total, WIDTH), bf16),
        ((total, WIDTH), bf16), ((total, WIDTH), f32), ((total, 8), f32),
        ((nb, HEADS_HERE, HEAD, HEAD), f32), ((total, D), bf16), ((rows, D), f32),
        ((total, D), bf16), ((2, total, fp), bf16),
    ]
    scratch = [
        ((D, 4 * WIDTH), bf16), ((D, D), bf16), ((2, fp, D), bf16), ((fp, D), bf16),
        ((total, HEAD), f32), ((total, HEAD), f32), ((total, D), bf16),
    ]
    scratch += saved[1:]
    saved = [
        ((2, rows, D), bf16), ((D, 4 * WIDTH), bf16), ((WIDTH, D), bf16), ((2, fp, D), bf16),
        ((fp, D), bf16),
    ] + saved
    scratch += [
        ((HEADS_HERE, BLOCK, BLOCK), f32), ((HEADS_HERE, BLOCK, HEAD), f32),
        ((HEADS_HERE, BLOCK, HEAD), f32), ((nb, HEADS_HERE, HEAD, HEAD), f32),
        ((HEADS_HERE, HEAD, HEAD), bf16), ((dp, HEADS_HERE, HEAD, HEAD), bf16),
        ((HEADS_HERE, HEAD, HEAD), f32), ((4, total, WIDTH), bf16), ((total, D), f32),
        ((3, rows, D), bf16), ((2, rows, D), bf16), ((2, rows // 2, D), bf16),
        ((4, 8, total), f32), ((rows, D), f32), ((rows, D), bf16),
    ]
    flops = 2 * total * D * (4 * WIDTH + D + 3 * fp)
    return pl.pallas_call(
        functools.partial(forward_kernel, dp, layer, first),
        out_shape=tuple(jax.ShapeDtypeStruct(a, b) for a, b in saved),
        in_specs=[ANY] * 7 + [SMEM],
        out_specs=(ANY,) * len(saved),
        scratch_shapes=[pltpu.VMEM(a, b) for a, b in scratch]
        + [
            pltpu.SemaphoreType.DMA((24,)),
            pltpu.SemaphoreType.DMA((21,)),
            pltpu.SemaphoreType.DMA((21,)),
            pltpu.SemaphoreType.DMA((dp,)),
            pltpu.SemaphoreType.DMA((dp,)),
            pltpu.SemaphoreType.DMA((5,)),
            pltpu.SemaphoreType.DMA((15,)),
            pltpu.SemaphoreType.DMA((15,)),
        ],
        compiler_params=pltpu.CompilerParams(
            collective_id=uid, has_side_effects=True, vmem_limit_bytes=VMEM_BYTES
        ),
        cost_estimate=pl.CostEstimate(flops=flops, bytes_accessed=20 << 20, transcendentals=0),
        name="layer_forward",
    )(x, *weights, cos2, sin2, scal)


class CorePair:
    def __init__(self, where, halves, from_core, ssem, rsem):
        s, d, t = where
        self.s, self.halves, self.landed = s, halves, from_core
        self.copy = lambda: remote(halves.at[1 - s], from_core, ssem, rsem, (1 - s, d, t))

    def send(self):
        self.copy().start()

    def add(self):
        self.copy().wait()
        rows = self.landed.shape[0]
        step = 128

        def chunk(n, c):
            r = rows_of(n, step)
            mine = self.halves[self.s, r, :].astype(f32)
            self.halves[self.s, r, :] = (mine + self.landed[r, :].astype(f32)).astype(bf16)
            return c

        lax.fori_loop(0, rows // step, chunk, 0)


class LineSum:
    LAG = 2
    END = 4 * LAG

    def __init__(self, dp, where, owner, halves, first, size, land, fin, result, sems, before):
        self.dp, self.where, self.owner, self.before = dp, where, owner, before
        self.halves, self.first, self.size, self.land, self.fin = halves, first, size, land, fin
        self.result = result
        self.recv, self.sent, self.free, self.ol, self.os, self.or_ = sems
        self.age = -1
        s, d, t = where
        low = dp // 2 - 1
        self.upward = d <= low
        self.middle = (d == low) | (d == low + 1)
        self.edge = (d == 0) | (d == dp - 1)
        self.inner = (s, jnp.where(self.upward, d + 1, d - 1), t)
        self.outer = (s, jnp.where(self.upward, d - 1, d + 1), t)
        self.mine = jnp.where(self.upward, 0, 1)

    def own(self, h=None):
        return self.halves.at[self.where[0], self.rows(self.first, h)]

    def rows(self, base, h=None):
        if h is None:
            return pl.ds(base, self.size)
        half = self.size // 2
        return pl.ds(pl.multiple_of(base + h * half, 16), half)

    def final(self, h):
        return self.fin.at[self.rows(self.first, h)]

    def inward(self):
        landing = self.land.at[self.rows(self.first)]
        return remote(self.own(), landing, self.sent.at[0], self.recv.at[2], self.inner)

    def swap_part(self):
        h = 1 - self.mine
        return remote(self.own(h), self.final(h), self.sent.at[0], self.recv.at[h], self.inner)

    def swap_sum(self):
        ref = self.final(self.mine)
        return remote(ref, ref, self.sent.at[1], self.recv.at[self.mine], self.inner)

    def outward(self, h):
        ref = self.final(h)
        return remote(ref, ref, self.sent.at[2 + h], self.recv.at[h], self.outer)

    def sweep(self, base, size, fn):
        unit = 32 if size % 32 == 0 else 16

        def chunk(n, c):
            fn(pl.ds(pl.multiple_of(base + n * unit, 16), unit))
            return c

        lax.fori_loop(0, size // unit, chunk, 0)

    def start(self):
        self.age = 0
        before = self.before
        if before is not None:
            assert before.age >= self.END
            before.close()

            @pl.when(self.middle)
            def _():
                pl.semaphore_signal(
                    self.free, inc=1, device_id=self.inner, device_id_type=MESH
                )

        if self.dp > 2:
            pl.when(self.edge)(lambda: self.inward().start())

    def tick(self):
        self.age += 1
        if self.dp == 1:
            if self.age == self.END:
                self.fin[...] = self.halves[0]
            return
        s = self.where[0]
        inside = jnp.logical_not(self.edge)
        if self.age == self.LAG:

            @pl.when(inside)
            def _():
                self.inward().wait_recv()

                def fn(r):
                    total = self.halves[s, r, :].astype(f32) + self.land[r, :].astype(f32)
                    self.halves[s, r, :] = total.astype(bf16)

                self.sweep(self.first, self.size, fn)
                pl.when(jnp.logical_not(self.middle))(lambda: self.inward().start())

            @pl.when(self.middle)
            def _():
                if self.before is not None:
                    pl.semaphore_wait(self.free, 1)
                self.swap_part().start()

        if self.age == 2 * self.LAG:

            @pl.when(self.middle)
            def _():
                h = self.mine
                half = self.size // 2
                self.arrived(h)

                def fn(r):
                    total = self.halves[s, r, :].astype(f32) + self.fin[r, :].astype(f32)
                    self.fin[r, :] = total.astype(bf16)

                self.sweep(self.first + h * half, half, fn)
                self.swap_sum().start()
                pl.when(inside)(lambda: self.outward(h).start())
                self.swap_part().wait_send()

            pl.when(jnp.logical_not(self.middle))(lambda: self.inward().wait_send())

        if self.age == 3 * self.LAG:

            @pl.when(self.middle)
            def _():
                self.arrived(1 - self.mine)
                pl.when(inside)(lambda: self.outward(1 - self.mine).start())

        if self.age == self.END:

            @pl.when(jnp.logical_not(self.middle))
            def _():
                for h in (0, 1):
                    self.arrived(h)
                    pl.when(inside)(lambda h=h: self.outward(h).start())

            pl.when(self.middle)(lambda: self.swap_sum().wait_send())

            @pl.when(inside)
            def _():
                for h in (0, 1):
                    self.outward(h).wait_send()

            self.to_result()[0]()

    def arrived(self, h):
        ref = self.final(h)
        remote(ref, ref, self.sent.at[0], self.recv.at[h], self.where).wait_recv()

    def to_result(self):
        s = self.where[0]
        part = self.rows(self.first)
        target = self.result.at[s, part]
        return to_owner(
            self.owner, self.where, self.fin.at[part], target, target, self.ol, self.os, self.or_
        )

    def close(self):
        self.to_result()[1]()


class Background:
    def __init__(self):
        self.queue, self.active = [], []

    def put(self, pieces):
        self.queue += pieces

    def tick(self):
        for piece in self.active:
            piece.tick()
        self.active = [piece for piece in self.active if piece.age < piece.END]
        if self.queue:
            piece = self.queue.pop(0)
            piece.start()
            self.active.append(piece)

    def until(self, pieces, age):
        while any(piece.age < age for piece in pieces):
            self.tick()


def backward_kernel(
    dp, ct_in, y0_in, tok_in, cos2, sin2, scal,
    wi0, wo0, wfi0, wfo0, wi1, wo1, wfi1, wfo1, *refs,
):
    saved_i = (refs[0:14], refs[14:28])
    both_o, gwfi_o, gwfo_o, gmix_o = refs[28:32]
    (
        wi, wo, wfi, wfo, cosv, sinv, gf, xr, hidden, zq, zk, gate, q, k, v, att, sc, states, branch, mid,
        hid2, pair, mask, mask_t, qd, kd, terms, zout, zin, run, gpair, prod, gb, gm, dv, dk,
        gp, part, got, via, own, gr, gwfi, gwfo, gmix, c_fi, c_fo, c_mix, l_fi, l_fo, l_mix,
        f_fi, f_fo, f_mix, lsem, ssem, rsem, zs, zr, ol, os, or_, core_s, core_r, ls, lr, free,
    ) = refs[32:]
    where = s, d, t = place()
    rows = y0_in.shape[0]
    total = 4 * rows
    nb = total // BLOCK
    fp = wfo.shape[0]
    half = rows // 2
    table = nb + 4 + 4 * dp
    local = Sems(lsem)
    me = rows_of(t, rows)
    gated, gatt = slice(0, WIDTH), slice(WIDTH, 2 * WIDTH)

    def gatt_head(h):
        return slice(WIDTH + h * HEAD, WIDTH + (h + 1) * HEAD)

    def load(src, dst):
        copy = pltpu.make_async_copy(src, dst, local.take())
        copy.start()
        return copy

    def block_of(ref):
        return lambda p, h: ref.at[pl.ds(pl.multiple_of(p * rows + h * half, half), half)]

    weights = ((wi0, wo0, wfi0, wfo0), (wi1, wo1, wfi1, wfo1))

    def load_feed(layer):
        keep = saved_i[layer]
        return [
            load(weights[layer][3], wfo), load(keep[13], pair), load(weights[layer][2], wfi),
            load(keep[11], mid), load(keep[12], hid2),
        ]

    def load_gates(layer):
        keep = saved_i[layer]
        return [
            load(weights[layer][1], wo), load(keep[10], branch), load(keep[8], sc), load(keep[7], att),
            load(keep[3], gate),
        ]

    def load_attn(layer):
        keep = saved_i[layer]
        pairs = ((4, q), (5, k), (6, v), (9, states), (1, zq), (2, zk))
        return [load(keep[n], ref) for n, ref in pairs]

    def load_ends(layer):
        x = tok_in.at[s] if layer == 0 else y0_in
        return [load(weights[layer][0], wi), load(saved_i[layer][0], hidden), load(x, xr)]


    ff = l_fo.shape[0]
    pieces, pairs = {}, {}
    for layer in (1, 0):
        cuts = [(gwfo, 256 * n, min(256, ff - 256 * n), l_fo, f_fo, gwfo_o) for n in range(-(-ff // 256))]
        cuts += [(gwfi, 128 * n, min(128, ff - 128 * n), l_fi, f_fi, gwfi_o) for n in range(-(-ff // 128))]
        cuts += [(gmix, 256 * n, 256, l_mix, f_mix, gmix_o) for n in range((D + WIDTH) // 256)]
        made = []
        for n, cut in enumerate(cuts):
            slot = PIECES * layer + n
            sems = [ref.at[slot] for ref in (lr, ls)] + [free.at[n]]
            sems += [ref.at[slot] for ref in (ol, os, or_)]
            before = pieces[1][n] if layer == 0 else None
            made.append(LineSum(dp, where, s == layer, *cut, sems, before))
        pieces[layer] = made
        pairs[layer] = [
            CorePair(where, halves, landed, core_s.at[3 * layer + n], core_r.at[3 * layer + n])
            for n, (halves, landed) in enumerate(((gwfo, c_fo), (gwfi, c_fi), (gmix, c_mix)))
        ]
    n_out, n_feed = -(-ff // 256), -(-ff // 256) + -(-ff // 128)
    work = Background()
    tick = work.tick

    got_g = load(ct_in.at[s], gf.at[me])
    in_feed, in_tables = load_feed(1), [load(cos2, cosv), load(sin2, sinv)]
    in_gates, in_attn, in_ends = load_gates(1), load_attn(1), load_ends(1)
    entry(dp, s, d, t, core=True)
    got_g.wait()
    in_out = []

    for layer in (1, 0):
        offset = table * layer
        pair_fo, pair_fi, pair_mix = pairs[layer]
        base = 24 * layer
        gg = Gather(block_of(gf), half, ssem, rsem, base, where)
        gg.start()
        decay_fill(scal, offset, nb, mask, mask_t, qd, kd)
        if layer == 0:
            pairs[1][2].add()
            work.put(pieces[1][n_feed:])
        tick()
        for copy in in_feed:
            copy.wait()
        sums = Scatter(part, got, via, rows, ssem, rsem, base + 6, where)

        def feed(i, c):
            for n in (1, 2, 3):

                @pl.when(i == n)
                def _(n=n):
                    if n == 1:
                        gg.forward()
                    if n == 3:
                        tick()
                    gg.ready(n)

            r = rows_of(partner(t, i), rows)
            grad = nt(gf[r, :], wfo[...])
            p0, p1 = pair[0, r, :].astype(f32), pair[1, r, :].astype(f32)
            prod[r, :] = (p0 * p1).astype(bf16)
            g0, g1 = (grad * p1).astype(bf16), (grad * p0).astype(bf16)
            gpair[0, r, :] = g0
            gpair[1, r, :] = g1
            o = nn(g0, wfi[0]) + nn(g1, wfi[1])
            for n in (1, 2, 3):

                @pl.when(i == n)
                def _(n=n):
                    sums.put(n, o)

            @pl.when(i == 0)
            def _():
                own[...] = o

            return c

        lax.fori_loop(0, 4, feed, 0)

        def feed_weights(n, c):
            cols = rows_of(n, 256)
            for part_of in (0, 1):
                gwfi[part_of, cols, :] = tn(gpair[part_of, :, cols], hid2[...]).astype(bf16)
            return c

        def out_weights(n, c):
            cols = rows_of(n, 256)
            a = prod[:, cols]
            gwfo[0, cols, :] = tn(a, gf[:, : D // 2]).astype(bf16)
            gwfo[1, cols, :] = tn(a, gf[:, D // 2 :]).astype(bf16)
            return c

        if layer == 0:
            work.until(pieces[1][:n_feed], 2 * LineSum.LAG)
        lax.fori_loop(0, fp // 256, out_weights, 0)
        pair_fo.send()
        lax.fori_loop(0, fp // 256, feed_weights, 0)
        pair_fi.send()
        tick()
        sums.combine()
        pair_fo.add()
        work.put(pieces[layer][:n_out])
        tick()
        pair_fi.add()
        work.put(pieces[layer][n_out:n_feed])
        grad_middle = gf[me, :].astype(f32) + norm_back(mid[...], own[...] + sums.result())
        gm[...] = grad_middle
        gb[me, :] = grad_middle.astype(bf16)
        sums.drain()
        gg.drain()

        gbg = Gather(block_of(gb), half, ssem, rsem, base + 12, where)
        gbg.start()
        if layer == 1:
            in_feed = load_feed(0)
        tick()
        for copy in in_gates:
            copy.wait()

        def gating(i, c):
            for n in (1, 2, 3):

                @pl.when(i == n)
                def _(n=n):
                    if n == 1:
                        gbg.forward()
                    if n == 3:
                        tick()
                    gbg.ready(n)

            r = rows_of(partner(t, i), rows)
            b = gb[r, :]
            grad = nt(b, wo[...])
            dots = jnp.sum(b.astype(f32) * branch[r, :].astype(f32), axis=-1, keepdims=True) * (1.0 / D)
            scale = sc[r, 0:1]
            normed = att[r, :] * scale
            gt = gate[r, :]
            gp[r, 3 * WIDTH :] = (grad * normed).astype(bf16)
            prod[r, gated] = (normed * gt).astype(bf16)
            prod[r, gatt] = (scale * (grad * gt - normed * dots)).astype(bf16)
            return c

        lax.fori_loop(0, 4, gating, 0)
        if layer == 1:
            in_gates = load_gates(0)
        for copy in in_attn:
            copy.wait()
        if layer == 1:
            for copy in in_tables:
                copy.wait()

        def term(b, c):
            r = rows_of(b, BLOCK)
            for h in range(HEADS_HERE):
                qdec = (q[r, head(h)].astype(f32) * qd[h]).astype(bf16)
                terms[b, h] = tn(qdec, prod[r, gatt_head(h)])
            return c

        lax.fori_loop(0, nb, term, 0)
        for h in range(HEADS_HERE):
            carried = scal[offset + nb - 1] * terms[nb - 1, h]
            for b in reversed(range(nb - 1)):
                carried = scal[offset + b] * (terms[b, h] + scal[offset + nb + 2 + h] * carried)
            zout[layer, h] = carried.astype(bf16)
        z_args = (dp, where, zout.at[layer], zin.at[layer], zs.at[layer], zr.at[layer], False)
        send_states(*z_args)
        tick()

        def unturn(pre, grad, r, h):
            back = grad * cosv[r, :] - pltpu.roll(grad, HEAD // 2, 1) * sinv[r, :]
            z = pre[r, head(h)]
            g = sig(z)
            return (back * (g * (1.0 + z * (1.0 - g)))).astype(bf16)

        def inner(b, c):
            r = rows_of(b, BLOCK)
            for h in range(HEADS_HERE):
                qh, kh, vh, gh = q[r, head(h)], k[r, head(h)], v[r, head(h)], prod[r, gatt_head(h)]
                w_t = (nt(kh, qh) * mask_t[h]).astype(bf16)
                dv[r, head(h)] = nn(w_t, gh)
                ds = (nt(gh, vh) * mask[h]).astype(bf16)
                ds_t = (nt(vh, gh) * mask_t[h]).astype(bf16)
                dk[r, head(h)] = nn(ds_t, qh)
                dq = nn(ds, kh) + nt(gh, states[b, h].astype(bf16)) * qd[h]
                gp[r, head(h)] = unturn(zq, dq, r, h)
            return c

        lax.fori_loop(0, nb, inner, 0)
        tick()
        take_states(*z_args, scal, offset + nb + 4 + 2 * dp, run)

        def outer(i, c):
            b = nb - 1 - i
            r = rows_of(b, BLOCK)
            for h in range(HEADS_HERE):
                after = run[h]
                low = after.astype(bf16)
                run[h] = scal[offset + b] * (terms[b, h] + scal[offset + nb + 2 + h] * after)
                kdec = (k[r, head(h)].astype(f32) * kd[h]).astype(bf16)
                dkh = dk[r, head(h)] + nt(v[r, head(h)], low) * kd[h]
                k_cols = slice(WIDTH + h * HEAD, WIDTH + (h + 1) * HEAD)
                v_cols = slice(2 * WIDTH + h * HEAD, 2 * WIDTH + (h + 1) * HEAD)
                gp[r, k_cols] = unturn(zk, dkh, r, h)
                gp[r, v_cols] = (dv[r, head(h)] + nn(kdec, low)).astype(bf16)
            return c

        lax.fori_loop(0, nb, outer, 0)
        tick()
        if layer == 1:
            in_attn = load_attn(0)
        for copy in in_ends:
            copy.wait()
        ins = Scatter(part, got, via, rows, ssem, rsem, base + 18, where)

        def back_in(i, c):
            e = 3 - i
            r = rows_of(partner(t, e), rows)
            o = nt(gp[r, :], wi[...])
            for n in (1, 2, 3):

                @pl.when(e == n)
                def _(n=n):
                    ins.put(n, o)

            @pl.when(e == 0)
            def _():
                own[...] = o

            return c

        lax.fori_loop(0, 4, back_in, 0)
        tick()
        if layer == 0:
            work.until(pieces[1], 2 * LineSum.LAG)

        def in_weights(n, c):
            cols = rows_of(n, 256)
            a = hidden[:, cols]
            gmix[0, cols, :] = tn(a, gp[:, : 2 * WIDTH]).astype(bf16)
            gmix[1, cols, :] = tn(a, gp[:, 2 * WIDTH :]).astype(bf16)
            return c

        lax.fori_loop(0, D // 256, in_weights, 0)
        gmix[0, D:, :] = tn(prod[:, gated], gb[:, : D // 2]).astype(bf16)
        gmix[1, D:, :] = tn(prod[:, gated], gb[:, D // 2 :]).astype(bf16)
        pair_mix.send()
        ins.combine()
        tick()
        dx = gm[...] + norm_back(xr[...].astype(f32), own[...] + ins.result())
        gr[layer] = dx.astype(bf16)
        ins.drain()
        gbg.drain()
        sent_states(*z_args)
        start, finish = to_owner(
            s == layer, where, gr.at[layer], both_o.at[s], both_o.at[s],
            ol.at[2 * PIECES + layer], os.at[2 * PIECES + layer], or_.at[2 * PIECES + layer],
        )
        start()
        in_out.append(finish)
        if layer == 1:
            gf[me, :] = gr[layer]
            in_ends = load_ends(0)

    pairs[0][2].add()
    work.put(pieces[0][n_feed:])
    work.until(pieces[0], LineSum.END)
    for piece in pieces[0]:
        piece.close()
    for finish in in_out:
        finish()


def layers_backward(cotangent, y0, tokens, cos2, sin2, scal, weights, saved, dp, ff, uid):
    rows = y0.shape[-2]
    total = 4 * rows
    nb = total // BLOCK
    fp = weights[0][3].shape[0]
    mixed = D + WIDTH
    outs = [
        ((2, rows, D), bf16), ((2, fp, D), bf16), ((2, fp, D // 2), bf16), ((2, mixed, D // 2), bf16)
    ]
    scratch = [
        ((D, 4 * WIDTH), bf16), ((WIDTH, D), bf16), ((2, fp, D), bf16), ((fp, D), bf16),
        ((total, HEAD), f32), ((total, HEAD), f32), ((total, D), bf16), ((rows, D), bf16),
    ]
    scratch += [(a.shape, a.dtype) for a in saved[0]]
    scratch += [
        ((HEADS_HERE, BLOCK, BLOCK), f32), ((HEADS_HERE, BLOCK, BLOCK), f32),
        ((HEADS_HERE, BLOCK, HEAD), f32), ((HEADS_HERE, BLOCK, HEAD), f32),
        ((nb, HEADS_HERE, HEAD, HEAD), f32), ((2, HEADS_HERE, HEAD, HEAD), bf16),
        ((2, dp, HEADS_HERE, HEAD, HEAD), bf16), ((HEADS_HERE, HEAD, HEAD), f32),
        ((2, total, fp), bf16), ((total, fp), bf16), ((total, D), bf16), ((rows, D), f32),
        ((total, WIDTH), f32), ((total, WIDTH), f32),
        ((total, 4 * WIDTH), bf16),
        ((3, rows, D), bf16), ((2, rows, D), bf16), ((2, rows // 2, D), bf16), ((rows, D), f32),
        ((2, rows, D), bf16),
        ((2, fp, D), bf16), ((2, fp, D // 2), bf16), ((2, mixed, D // 2), bf16),
        ((fp, D), bf16), ((fp, D // 2), bf16), ((mixed, D // 2), bf16),
        ((ff, D), bf16), ((ff, D // 2), bf16), ((mixed, D // 2), bf16),
        ((ff, D), bf16), ((ff, D // 2), bf16), ((mixed, D // 2), bf16),
    ]
    count = 2 * PIECES
    dma = pltpu.SemaphoreType.DMA
    flops = 8 * total * D * (4 * WIDTH + WIDTH + 3 * fp)
    flat = [w for layer in weights for w in layer]
    kept = [a for layer in saved for a in layer]
    return pl.pallas_call(
        functools.partial(backward_kernel, dp),
        out_shape=tuple(jax.ShapeDtypeStruct(a, b) for a, b in outs),
        in_specs=[ANY] * 5 + [SMEM] + [ANY] * (len(flat) + len(kept)),
        out_specs=(ANY,) * len(outs),
        scratch_shapes=[pltpu.VMEM(a, b) for a, b in scratch]
        + [
            dma((48,)), dma((48,)), dma((48,)), dma((2, dp)), dma((2, dp)), dma((count + 2,)),
            dma((count + 2,)), dma((count + 2,)), dma((6,)), dma((6,)), dma((count, 4)),
            dma((count, 3)), pltpu.SemaphoreType.REGULAR((PIECES,)),
        ],
        compiler_params=pltpu.CompilerParams(
            collective_id=uid, has_side_effects=True, vmem_limit_bytes=VMEM_BYTES
        ),
        cost_estimate=pl.CostEstimate(flops=flops, bytes_accessed=60 << 20, transcendentals=0),
        name="layers_backward",
    )(cotangent, y0, tokens, cos2, sin2, scal, *flat, *kept)


def widen_kernel(section, fi, fo, mix, mix_out, both0, both1, g_in, g_fi, g_out, g_fo, outputs):
    for n in range(4):
        lanes = slice((n % 2) * WIDTH, (n % 2 + 1) * WIDTH)
        g_in[:, n, :] = mix[n // 2, :, lanes].astype(f32)
    for n in range(2):
        half = slice(n * (D // 2), (n + 1) * (D // 2))
        g_fi[n] = fi[n].astype(f32)
        g_out[:, half] = mix_out[n].astype(f32)
        g_fo[:, half] = fo[n].astype(f32)

    @pl.when(section[0] == 0)
    def _():
        outputs[...] = both0[...]

    @pl.when(section[0] != 0)
    def _():
        outputs[...] = both1[...]


def widen(s, g_fi, g_fo, g_mix, both0, both1, ff):
    cuts = 4
    rows = both0.shape[1]
    n = D // cuts
    ahead = D // (WIDTH // cuts)
    shapes = ((D, 4, WIDTH), (2, ff, D), (WIDTH, D), (ff, D))
    per_row = lambda *shape: pl.BlockSpec(shape, lambda i, _: (i,) + (0,) * (len(shape) - 1))
    halves = lambda *shape: pl.BlockSpec(shape, lambda i, _: (0, i, 0))
    return pl.pallas_call(
        widen_kernel,
        out_shape=tuple(jax.ShapeDtypeStruct(a, f32) for a in shapes)
        + (jax.ShapeDtypeStruct(both0.shape, bf16),),
        grid_spec=pltpu.PrefetchScalarGridSpec(
            num_scalar_prefetch=1,
            grid=(cuts,),
            in_specs=[
                halves(2, ff // cuts, D),
                halves(2, ff // cuts, D // 2),
                halves(2, n, D // 2),
                pl.BlockSpec((2, WIDTH // cuts, D // 2), lambda i, _: (0, ahead + i, 0)),
                halves(2, rows // cuts, D),
                halves(2, rows // cuts, D),
            ],
            out_specs=(
                per_row(n, 4, WIDTH), halves(2, ff // cuts, D), per_row(WIDTH // cuts, D),
                per_row(ff // cuts, D),
                halves(2, rows // cuts, D),
            ),
        ),
        compiler_params=pltpu.CompilerParams(vmem_limit_bytes=VMEM_BYTES),
        cost_estimate=pl.CostEstimate(flops=0, bytes_accessed=24 << 20, transcendentals=0),
        name="widen",
    )(s.reshape(1), g_fi, g_fo, g_mix, g_mix, both0, both1)


def angle_tables(starts, blocks):
    d = lax.axis_index("dp")
    at = jnp.arange(starts.shape[0], dtype=jnp.int32)
    begins = jnp.max(
        jnp.where((at[None, :] <= at[:, None]) & (starts > 0)[None, :], at[None, :], 0), axis=1
    )
    offsets = lax.dynamic_slice_in_dim((at - begins) * BLOCK, d * blocks, blocks)
    places = (offsets[:, None] + jnp.arange(BLOCK, dtype=jnp.int32)[None, :]).reshape(-1)
    lane = jnp.arange(HEAD, dtype=jnp.int32)
    frequency = 10000.0 ** (-(lane % (HEAD // 2)).astype(f32) / (HEAD // 2))
    angles = places.astype(f32)[:, None] * frequency[None, :]
    return jnp.cos(angles), jnp.where(lane < HEAD // 2, -1.0, 1.0)[None, :] * jnp.sin(angles)


def swap(x):
    return lax.ppermute(x, "section", [(0, 1), (1, 0)])


def mine_first(s, a, b):
    return jnp.where(s == 0, a, b)


def shards(tokens, cotangent, mixer_in, mixer_out, feed_in, feed_out, decay_rate, block_starts):
    s = lax.axis_index("section")
    dp = lax.axis_size("dp")
    rows = tokens.shape[1]
    blocks = 4 * rows // BLOCK
    ff = feed_out.shape[1]
    wi = mixer_in[0].reshape(D, 4 * WIDTH)
    wfi = jnp.transpose(feed_in[0], (1, 2, 0))
    mine = (wi, mixer_out[0], wfi, feed_out[0])
    other_rates = swap(decay_rate[0])
    rates = (mine_first(s, decay_rate[0], other_rates), mine_first(s, other_rates, decay_rate[0]))
    starts = lax.dynamic_index_in_dim(block_starts, s, 0, keepdims=False)
    cos2, sin2 = angle_tables(starts, blocks)
    scal = jnp.concatenate([row for r in rates for row in scalar_table(starts, r, dp, blocks)])

    both0, *out0 = layer_forward(0, True, tokens, mine, cos2, sin2, scal, dp, 1)
    weights0, y0, saved0 = out0[:4], out0[4], out0[5:]
    both1, *out1 = layer_forward(1, False, y0, mine, cos2, sin2, scal, dp, 2)
    weights1, saved1 = out1[:4], out1[5:]
    in_grads, g_fi, g_fo, g_mix = layers_backward(
        cotangent, y0, tokens, cos2, sin2, scal, (weights0, weights1),
        (saved0, saved1), dp, ff, 3,
    )
    g_in, g_feed_in, g_out, g_feed_out, outputs = widen(s, g_fi, g_fo, g_mix, both0, both1, ff)
    g_feed_in = jnp.transpose(g_feed_in, (2, 0, 1))
    return outputs[None], in_grads[None], g_in[None], g_out[None], g_feed_in[None], g_feed_out[None]


def solution(mesh):
    placed = (
        P(None, ("dp", "tensor"), None),
        P(None, ("dp", "tensor"), None),
        P("section", None, None, "tensor"),
        P("section", "tensor", None),
        P("section", None, None, "tensor"),
        P("section", "tensor", None),
        P("section", "tensor"),
        P(),
    )
    return jax.shard_map(
        shards,
        mesh=mesh,
        in_specs=placed,
        out_specs=(
            P("section", None, ("dp", "tensor"), None),
            P("section", None, ("dp", "tensor"), None),
            P("section", None, None, "tensor"),
            P("section", "tensor", None),
            P("section", None, None, "tensor"),
            P("section", "tensor", None),
        ),
        check_vma=False,
    )
```

```python
import functools

import jax
import jax.numpy as jnp
import numpy as np
from jax import lax
from jax.experimental import pallas as pl
from jax.experimental.pallas import tpu as pltpu
from jax.sharding import PartitionSpec as P

D = 1024
HEAD = 128
BLOCK = 256
WIDTH = 256
HEADS_HERE = WIDTH // HEAD
norm_eps = 1e-06
MESH = pl.DeviceIdType.MESH
ANY = pl.BlockSpec(memory_space=pl.ANY)
SMEM = pl.BlockSpec(memory_space=pltpu.SMEM)
bf16, f32 = jnp.bfloat16, jnp.float32
PIECES = 16
VMEM_BYTES = 62 * 1024 * 1024


def place():
    return lax.axis_index("section"), lax.axis_index("dp"), lax.axis_index("tensor")


def partner(t, k):
    return ((t // 2 + k // 2) % 2) * 2 + (t + k) % 2


class Sems:
    def __init__(self, ref):
        self.ref, self.used = ref, 0

    def take(self):
        self.used += 1
        return self.ref.at[self.used - 1]


def remote(src, dst, send, recv, dev):
    return pltpu.make_async_remote_copy(
        src_ref=src, dst_ref=dst, send_sem=send, recv_sem=recv, device_id=dev, device_id_type=MESH
    )


def nn(a, b):
    return lax.dot_general(a, b, (((1,), (0,)), ((), ())), preferred_element_type=f32)


def nt(a, b):
    return lax.dot_general(a, b, (((1,), (1,)), ((), ())), preferred_element_type=f32)


def tn(a, b):
    return lax.dot_general(a, b, (((0,), (0,)), ((), ())), preferred_element_type=f32)


def rms_scale(v):
    return lax.rsqrt(jnp.mean(v * v, axis=-1, keepdims=True) + norm_eps)


def norm_back(v, u):
    q = rms_scale(v)
    n = v * q
    return q * (u - n * jnp.mean(u * n, axis=-1, keepdims=True))


def sig(v):
    return 1.0 / (1.0 + jnp.exp(-v))


def rows_of(p, n):
    return pl.ds(pl.multiple_of(p * n, n), n)


def entry(dp, s, d, t, core=False):
    barrier = pltpu.get_barrier_semaphore()
    count = 3
    for k in (1, 2, 3):
        pl.semaphore_signal(barrier, inc=1, device_id=(s, d, partner(t, k)), device_id_type=MESH)
    if core:
        pl.semaphore_signal(barrier, inc=1, device_id=(1 - s, d, t), device_id_type=MESH)
        count += 1
    if dp > 1:

        def greet(k, c):
            pl.semaphore_signal(
                barrier, inc=1, device_id=(s, (d + k) % dp, t), device_id_type=MESH
            )
            return c

        lax.fori_loop(1, dp, greet, 0)
        count += dp - 1
    pl.semaphore_wait(barrier, count)


class Gather:
    def __init__(self, block_at, half, ssem, rsem, base, where):
        self.at, self.half, self.ssem, self.rsem, self.base = block_at, half, ssem, rsem, base
        self.where = where

    def copy(self, n, peer, half, to):
        s, d, t = self.where
        ref = self.at(partner(t, peer), half)
        k = self.base + n
        return remote(ref, ref, self.ssem.at[k], self.rsem.at[k], (s, d, partner(t, to)))

    def mine(self, n):
        peer, half, to = ((0, 0, 1), (0, 1, 1), (0, 0, 2), (0, 1, 2), (1, 0, 2), (2, 1, 1))[n]
        return self.copy(n, peer, half, to)

    def arriving(self, n):
        s, d, t = self.where
        peer, half = ((1, 0), (1, 1), (2, 0), (2, 1), (3, 0), (3, 1))[n]
        ref = self.at(partner(t, peer), half)
        k = self.base + n
        return remote(ref, ref, self.ssem.at[k], self.rsem.at[k], (s, d, t))

    def start(self):
        self.mine(0).start()
        self.mine(3).start()
        self.mine(1).start()
        self.mine(2).start()

    def forward(self):
        self.arriving(0).wait_recv()
        self.mine(4).start()
        self.arriving(3).wait_recv()
        self.mine(5).start()

    def ready(self, k):
        if k == 1:
            self.arriving(1).wait_recv()
        elif k == 2:
            self.arriving(2).wait_recv()
        else:
            self.arriving(4).wait_recv()
            self.arriving(5).wait_recv()

    def drain(self):
        for n in range(6):
            self.mine(n).wait_send()


class Scatter:
    def __init__(self, part, got, via, rows, ssem, rsem, base, where):
        self.part, self.got, self.via, self.half = part, got, via, rows // 2
        self.ssem, self.rsem, self.base, self.where = ssem, rsem, base, where

    def copy(self, n):
        s, d, t = self.where
        h = self.half
        h0, h1 = pl.ds(0, h), pl.ds(h, h)
        src, dst, to = (
            (self.part.at[2, h0], self.via.at[0], 2),
            (self.part.at[2, h1], self.via.at[1], 1),
            (self.part.at[0, h1], self.got.at[0, h1], 1),
            (self.part.at[1, h0], self.got.at[1, h0], 2),
            (self.part.at[0, h0], self.got.at[0, h0], 1),
            (self.part.at[1, h1], self.got.at[1, h1], 2),
        )[n]
        k = self.base + n
        return remote(src, dst, self.ssem.at[k], self.rsem.at[k], (s, d, partner(t, to)))

    def put(self, k, value):
        self.part[k - 1] = value.astype(bf16)
        self.send(k)

    def send(self, k):
        if k == 3:
            self.copy(0).start()
            self.copy(1).start()
        elif k == 2:
            self.copy(3).start()
        else:
            self.copy(2).start()

    def combine(self):
        h = self.half
        self.copy(0).wait_recv()
        self.part[0, 0:h] = (self.part[0, 0:h].astype(f32) + self.via[0].astype(f32)).astype(bf16)
        self.copy(4).start()
        self.copy(1).wait_recv()
        self.part[1, h:] = (self.part[1, h:].astype(f32) + self.via[1].astype(f32)).astype(bf16)
        self.copy(5).start()

    def result(self):
        for n in (2, 3, 4, 5):
            self.copy(n).wait_recv()
        return self.got[0].astype(f32) + self.got[1].astype(f32)

    def drain(self):
        for n in range(6):
            self.copy(n).wait_send()


def scalar_table(starts, rates, dp, blocks):
    d = lax.axis_index("dp")
    survive = 1.0 - starts.astype(f32).reshape(dp, blocks)
    decay = jnp.exp(-rates * BLOCK)
    factor = jnp.prod(survive, axis=1)[:, None] * (decay**blocks)[None, :]
    at = jnp.arange(dp)
    low, high = jnp.minimum(at, d), jnp.maximum(at, d)
    between = (at[None, :] > low[:, None]) & (at[None, :] < high[:, None])
    through = jnp.prod(jnp.where(between[:, :, None], factor[None], 1.0), axis=1)
    forward = jnp.where((at < d)[:, None], through, 0.0)
    backward = jnp.where((at > d)[:, None], through, 0.0)
    mine = lax.dynamic_index_in_dim(survive, d, 0, keepdims=False)
    index = jnp.arange(starts.shape[0], dtype=jnp.int32)
    begins = jnp.max(
        jnp.where((index[None, :] <= index[:, None]) & (starts > 0)[None, :], index[None, :], 0), axis=1
    )
    offsets = lax.dynamic_slice_in_dim((index - begins) * BLOCK, d * blocks, blocks).astype(f32)
    return [mine, rates, decay, forward.reshape(-1), backward.reshape(-1), offsets]


def decay_fill(scal, base, nb, mask, mask_t, qd, kd):
    for h in range(HEADS_HERE):
        r = scal[base + nb + h]
        i = lax.broadcasted_iota(jnp.int32, (BLOCK, BLOCK), 0).astype(f32)
        j = lax.broadcasted_iota(jnp.int32, (BLOCK, BLOCK), 1).astype(f32)
        gap = i - j
        mask[h] = jnp.where(gap >= 0.0, jnp.exp(-r * jnp.maximum(gap, 0.0)), 0.0)
        if mask_t is not None:
            mask_t[h] = jnp.where(gap <= 0.0, jnp.exp(-r * jnp.maximum(-gap, 0.0)), 0.0)
        i = lax.broadcasted_iota(jnp.int32, (BLOCK, HEAD), 0).astype(f32)
        qd[h] = jnp.exp(-r * (i + 1.0))
        kd[h] = jnp.exp(-r * (BLOCK - 1.0 - i))


def head(h):
    return slice(h * HEAD, (h + 1) * HEAD)


def send_states(dp, where, zout, zin, zs, zr, later):
    s, d, t = where

    def each(k, c):
        to = d + k if later else d - k

        @pl.when((to < dp) if later else (to >= 0))
        def _():
            remote(zout, zin.at[d], zs.at[k], zr.at[d], (s, to, t)).start()

        return c

    lax.fori_loop(1, dp, each, 0)


def sent_states(dp, where, zout, zin, zs, zr, later):
    s, d, t = where

    def each(k, c):
        to = d + k if later else d - k

        @pl.when((to < dp) if later else (to >= 0))
        def _():
            remote(zout, zin.at[d], zs.at[k], zr.at[d], (s, to, t)).wait_send()

        return c

    lax.fori_loop(1, dp, each, 0)


def take_states(dp, where, zout, zin, zs, zr, later, scal, base, run):
    s, d, t = where
    run[...] = jnp.zeros_like(run)

    def each(k, c):
        @pl.when((k < d) if later else (k > d))
        def _():
            remote(zout, zin.at[k], zs.at[0], zr.at[k], (s, d, t)).wait_recv()
            for h in range(HEADS_HERE):
                run[h] += scal[base + 2 * k + h] * zin[k, h].astype(f32)

        return c

    lax.fori_loop(0, dp, each, 0)


class Fetch:
    def __init__(self, src, dst, owner, where, lsem, ssem, rsem):
        s, d, t = where
        self.owner = owner
        self.local = lambda: pltpu.make_async_copy(src, dst, lsem)
        self.far = lambda: remote(src, dst, ssem, rsem, (1 - s, d, t))

    def read(self):
        pl.when(self.owner)(lambda: self.local().start())

    def send(self):
        pl.when(self.owner)(lambda: self.far().start())

    def wait(self):
        pl.when(self.owner)(lambda: self.local().wait())
        pl.when(jnp.logical_not(self.owner))(lambda: self.far().wait_recv())

    def drain(self):
        pl.when(self.owner)(lambda: self.far().wait_send())


def to_owner(owner, where, src, own_dst, far_dst, lsem, ssem, rsem):
    s, d, t = where

    def far():
        return remote(src, far_dst, ssem, rsem, (1 - s, d, t))

    def local():
        return pltpu.make_async_copy(src, own_dst, lsem)

    def start():
        pl.when(owner)(lambda: local().start())
        pl.when(jnp.logical_not(owner))(lambda: far().start())

    def finish():
        @pl.when(owner)
        def _():
            local().wait()
            far().wait_recv()

        pl.when(jnp.logical_not(owner))(lambda: far().wait_send())

    return start, finish


def forward_kernel(
    dp, layer, first, x_in, my_wi, my_wo, my_wfi, my_wfo, turn_in, scal,
    both_o, turn_o, wi_o, wo_o, wfi_o, wfo_o, y_out, hidden_o, zq_o, zk_o, gate_o, q_o, k_o, v_o, att_o, sc_o, states_o, branch_o, mid_o,
    hid2_o, pair_o,
    raw, wi, wo, wfi, wfo, turn, xf, hidden, zq, zk, gate, q, k, v, att, sc, states, branch, mid, hid2,
    pair, mask, qd, kd, loc, zout, zin, run, u, y, part, got, via, ssq, own, yb,
    lsem, ssem, rsem, zs, zr, wl, ws, wr,
):
    where = s, d, t = place()
    rows = x_in.shape[-2]
    total = 4 * rows
    nb = total // BLOCK
    at = layer * (2 * nb + 4 + 4 * dp)
    local = Sems(lsem)

    def load(src, dst):
        copy = pltpu.make_async_copy(src, dst, local.take())
        copy.start()
        return copy

    x_src = x_in.at[s] if first else x_in
    got_x = load(x_src, xf.at[rows_of(t, rows)])
    owner = s == layer
    ff = my_wfo.shape[0]
    pairs = (
        (wi, wi), (my_wo, wo.at[rows_of(t, WIDTH)]), (my_wfi, wfi.at[:, pl.ds(0, ff)]),
        (my_wfo, wfo.at[pl.ds(0, ff)]),
    )
    got_w = [
        Fetch(src, dst, owner, where, wl.at[n], ws.at[n], wr.at[n])
        for n, (src, dst) in enumerate(pairs)
    ]
    got_wi, got_wo, got_wfi, got_wfo = got_w
    got_raw = pltpu.make_async_copy(my_wi, raw, wl.at[0])
    pl.when(owner)(lambda: got_raw.start())
    got_turn = load(turn_in, turn.at[0, pl.ds(0, 8)] if first else turn)
    for fetch in got_w[1:]:
        fetch.read()
    wfi[:, ff:, :] = jnp.zeros_like(wfi[:, ff:, :])
    wfo[ff:, :] = jnp.zeros_like(wfo[ff:, :])
    entry(dp, s, d, t, core=True)
    got_x.wait()

    half = rows // 2
    gx = Gather(
        lambda p, h: xf.at[pl.ds(pl.multiple_of(p * rows + h * half, half), half)],
        half, ssem, rsem, 0, where,
    )
    quarter = WIDTH // 2
    gw = Gather(
        lambda p, h: wo.at[pl.ds(pl.multiple_of(p * WIDTH + h * quarter, quarter), quarter)],
        quarter, ws, wr, 4, where,
    )

    def wo_over(k):
        ref = wo.at[rows_of(partner(t, k), WIDTH)]
        return remote(ref, ref, ws.at[10 + k], wr.at[10 + k], (1 - s, d, t))

    gx.start()
    for fetch in got_w[1:]:
        fetch.send()

    @pl.when(owner)
    def _():
        got_raw.wait()

        def chunk(n, c):
            r = rows_of(n, 128)
            wi[r, :] = raw[r].reshape(128, 4 * WIDTH)
            return c

        lax.fori_loop(0, D // 128, chunk, 0)
        got_wi.far().start()

    got_turn.wait()
    stores = []
    if first:
        frequency = turn[0, 0:1, :]
        sign = jnp.where(lax.broadcasted_iota(jnp.int32, (1, HEAD), 1) < HEAD // 2, -1.0, 1.0)

        def angles(b, c):
            steps_in = lax.broadcasted_iota(jnp.int32, (BLOCK, HEAD), 0).astype(f32)
            angle = (scal[at + nb + 4 + 4 * dp + b] + steps_in) * frequency
            r = rows_of(b, BLOCK)
            turn[0, r, :] = jnp.cos(angle)
            turn[1, r, :] = sign * jnp.sin(angle)
            return c

        lax.fori_loop(0, nb, angles, 0)
        stores.append(load(turn, turn_o))
    decay_fill(scal, at, nb, mask, None, qd, kd)
    pl.when(jnp.logical_not(owner))(lambda: got_wi.far().wait_recv())

    def project(i, c):
        for n in (1, 2, 3):

            @pl.when(i == n)
            def _(n=n):
                if n == 1:
                    gx.forward()

                    @pl.when(owner)
                    def _():
                        got_wo.local().wait()
                        gw.start()

                gx.ready(n)

        r = rows_of(partner(t, i), rows)
        xv = xf[r, :].astype(f32)
        hid = (xv * rms_scale(xv)).astype(bf16)
        hidden[r, :] = hid
        cs, sn = turn[0, r, :], turn[1, r, :]
        for n, (pre, post) in enumerate(((zq, q), (zk, k))):
            z = nn(hid, wi[:, n * WIDTH : (n + 1) * WIDTH])
            pre[r, :] = z
            a = z * sig(z)
            for h in range(HEADS_HERE):
                ah = a[:, head(h)]
                post[r, head(h)] = (ah * cs + pltpu.roll(ah, HEAD // 2, 1) * sn).astype(bf16)
        v[r, :] = nn(hid, wi[:, 2 * WIDTH : 3 * WIDTH]).astype(bf16)
        gate[r, :] = nn(hid, wi[:, 3 * WIDTH :])
        return c

    lax.fori_loop(0, 4, project, 0)

    stores += [load(hidden, hidden_o), load(zq, zq_o), load(zk, zk_o), load(gate, gate_o)]
    stores += [load(q, q_o), load(k, k_o), load(v, v_o)]

    def local_state(b, c):
        r = rows_of(b, BLOCK)
        for h in range(HEADS_HERE):
            kdec = (k[r, head(h)].astype(f32) * kd[h]).astype(bf16)
            loc[b, h] = tn(kdec, v[r, head(h)])
        return c

    lax.fori_loop(0, nb, local_state, 0)
    pl.when(owner)(gw.forward)
    for h in range(HEADS_HERE):
        carried = loc[0, h]
        for b in range(1, nb):
            carried = (scal[at + nb + 2 + h] * scal[at + b]) * carried + loc[b, h]
        zout[h] = carried.astype(bf16)
    send_states(dp, where, zout, zin, zs, zr, True)

    def inner(b, c):
        r = rows_of(b, BLOCK)
        for h in range(HEADS_HERE):
            w = (nt(q[r, head(h)], k[r, head(h)]) * mask[h]).astype(bf16)
            att[r, head(h)] = nn(w, v[r, head(h)])
        return c

    lax.fori_loop(0, nb, inner, 0)
    take_states(dp, where, zout, zin, zs, zr, True, scal, at + nb + 4, run)

    def outer(b, c):
        r = rows_of(b, BLOCK)
        for h in range(HEADS_HERE):
            entering = scal[at + b] * run[h]
            states[b, h] = entering
            run[h] = scal[at + nb + 2 + h] * entering + loc[b, h]
            qdec = (q[r, head(h)].astype(f32) * qd[h]).astype(bf16)
            a = att[r, head(h)] + nn(qdec, entering.astype(bf16))
            att[r, head(h)] = a
            u[t, r, head(h)] = (a * gate[r, head(h)]).astype(bf16)
        return c

    lax.fori_loop(0, nb, outer, 0)

    hu = total // 2
    gu = Gather(lambda p, h: u.at[p, pl.ds(h * hu, hu)], hu, ssem, rsem, 6, where)
    gu.start()
    for b in range(nb):
        a = att[b * BLOCK : (b + 1) * BLOCK, :]
        ssq[0, :, b * BLOCK : (b + 1) * BLOCK] = lax.dot_general(
            jnp.ones((8, WIDTH), f32), a * a, (((1,), (1,)), ((), ())),
            preferred_element_type=f32, precision=lax.Precision.HIGHEST,
        )
    sums = [
        remote(ssq.at[0], ssq.at[n], ssem.at[11 + n], rsem.at[11 + n], (s, d, partner(t, n)))
        for n in (1, 2, 3)
    ]
    for copy in sums:
        copy.start()
    stores += [load(att, att_o), load(states, states_o)]
    @pl.when(owner)
    def _():
        for n in (1, 2, 3):
            gw.ready(n)
            wo_over(n).start()

    @pl.when(jnp.logical_not(owner))
    def _():
        got_wo.far().wait_recv()
        for n in (1, 2, 3):
            wo_over(n).wait_recv()

    y[...] = jnp.zeros_like(y)

    def out_project(i, c):
        for n in (1, 2, 3):

            @pl.when(i == n)
            def _(n=n):
                if n == 1:
                    gu.forward()
                gu.ready(n)

        p = partner(t, i)

        def chunk(m, c):
            r = rows_of(m, rows)
            y[r, :] += nn(u[p, r, :], wo[rows_of(p, WIDTH), :])
            return c

        return lax.fori_loop(0, 4, chunk, c)

    lax.fori_loop(0, 4, out_project, 0)
    for copy in sums:
        copy.wait_recv()
    whole = ssq[0] + ssq[1] + ssq[2] + ssq[3]
    sc[...] = jnp.transpose(lax.rsqrt(whole * (1.0 / D) + norm_eps))
    got_wfi.wait()
    got_wfo.wait()
    out = Scatter(part, got, via, rows, ssem, rsem, 15, where)

    def feed(i, c):
        e = 3 - i
        r = rows_of(partner(t, e), rows)
        br = sc[r, 0:1] * y[r, :]
        branch[r, :] = br.astype(bf16)
        m = xf[r, :].astype(f32) + br
        h2 = (m * rms_scale(m)).astype(bf16)
        hid2[r, :] = h2
        p0, p1 = nt(h2, wfi[0]), nt(h2, wfi[1])
        pair[0, r, :] = p0.astype(bf16)
        pair[1, r, :] = p1.astype(bf16)
        o = nn((p0 * p1).astype(bf16), wfo[...])
        for n in (1, 2, 3):

            @pl.when(e == n)
            def _(n=n):
                out.put(n, o)

        @pl.when(e == 0)
        def _():
            mid[...] = m
            own[...] = o + m

        return c

    lax.fori_loop(0, 4, feed, 0)
    stores += [load(sc, sc_o), load(branch, branch_o), load(mid, mid_o), load(hid2, hid2_o)]
    stores += [load(pair, pair_o), load(wi, wi_o), load(wo.at[rows_of(t, WIDTH)], wo_o)]
    stores += [load(wfi, wfi_o), load(wfo, wfo_o)]
    out.combine()
    yb[...] = (own[...] + out.result()).astype(bf16)
    stores += [load(yb, y_out)]
    start, finish = to_owner(
        owner, where, yb, both_o.at[s], both_o.at[s], wl.at[4], ws.at[14], wr.at[14]
    )
    start()
    for fetch in got_w:
        fetch.drain()

    @pl.when(owner)
    def _():
        for n in (1, 2, 3):
            wo_over(n).wait_send()
        gw.drain()

    finish()
    gx.drain()
    gu.drain()
    out.drain()
    for copy in sums:
        copy.wait_send()
    sent_states(dp, where, zout, zin, zs, zr, True)
    for copy in stores:
        copy.wait()


def layer_forward(layer, first, x, weights, turn, scal, dp, uid):
    rows = x.shape[-2]
    total = 4 * rows
    nb = total // BLOCK
    fp = -(-weights[3].shape[0] // 256) * 256
    saved = [
        ((rows, D), bf16), ((total, D), bf16), ((total, WIDTH), f32), ((total, WIDTH), f32),
        ((total, WIDTH), f32), ((total, WIDTH), bf16), ((total, WIDTH), bf16),
        ((total, WIDTH), bf16), ((total, WIDTH), f32), ((total, 8), f32),
        ((nb, HEADS_HERE, HEAD, HEAD), f32), ((total, D), bf16), ((rows, D), f32),
        ((total, D), bf16), ((2, total, fp), bf16),
    ]
    scratch = [
        ((D, 4, WIDTH), bf16), ((D, 4 * WIDTH), bf16), ((D, D), bf16), ((2, fp, D), bf16), ((fp, D), bf16),
        ((2, total, HEAD), f32), ((total, D), bf16),
    ]
    scratch += saved[1:]
    saved = [
        ((2, rows, D), bf16), ((2, total, HEAD) if first else (8, 128), f32),
        ((D, 4 * WIDTH), bf16), ((WIDTH, D), bf16), ((2, fp, D), bf16),
        ((fp, D), bf16),
    ] + saved
    scratch += [
        ((HEADS_HERE, BLOCK, BLOCK), f32), ((HEADS_HERE, BLOCK, HEAD), f32),
        ((HEADS_HERE, BLOCK, HEAD), f32), ((nb, HEADS_HERE, HEAD, HEAD), f32),
        ((HEADS_HERE, HEAD, HEAD), bf16), ((dp, HEADS_HERE, HEAD, HEAD), bf16),
        ((HEADS_HERE, HEAD, HEAD), f32), ((4, total, WIDTH), bf16), ((total, D), f32),
        ((3, rows, D), bf16), ((2, rows, D), bf16), ((2, rows // 2, D), bf16),
        ((4, 8, total), f32), ((rows, D), f32), ((rows, D), bf16),
    ]
    flops = 2 * total * D * (4 * WIDTH + D + 3 * fp)
    return pl.pallas_call(
        functools.partial(forward_kernel, dp, layer, first),
        out_shape=tuple(jax.ShapeDtypeStruct(a, b) for a, b in saved),
        in_specs=[ANY] * 6 + [SMEM],
        out_specs=(ANY,) * len(saved),
        scratch_shapes=[pltpu.VMEM(a, b) for a, b in scratch]
        + [
            pltpu.SemaphoreType.DMA((24,)),
            pltpu.SemaphoreType.DMA((21,)),
            pltpu.SemaphoreType.DMA((21,)),
            pltpu.SemaphoreType.DMA((dp,)),
            pltpu.SemaphoreType.DMA((dp,)),
            pltpu.SemaphoreType.DMA((5,)),
            pltpu.SemaphoreType.DMA((15,)),
            pltpu.SemaphoreType.DMA((15,)),
        ],
        compiler_params=pltpu.CompilerParams(
            collective_id=uid, has_side_effects=True, vmem_limit_bytes=VMEM_BYTES
        ),
        cost_estimate=pl.CostEstimate(flops=flops, bytes_accessed=20 << 20, transcendentals=0),
        name="layer_forward",
    )(x, *weights, turn, scal)


class CorePair:
    def __init__(self, where, halves, from_core, ssem, rsem):
        s, d, t = where
        self.s, self.halves, self.landed = s, halves, from_core
        self.copy = lambda: remote(halves.at[1 - s], from_core, ssem, rsem, (1 - s, d, t))

    def send(self):
        self.copy().start()

    def add(self):
        self.copy().wait()
        rows = self.landed.shape[0]
        step = 128

        def chunk(n, c):
            r = rows_of(n, step)
            mine = self.halves[self.s, r, :].astype(f32)
            self.halves[self.s, r, :] = (mine + self.landed[r, :].astype(f32)).astype(bf16)
            return c

        lax.fori_loop(0, rows // step, chunk, 0)


class LineSum:
    LAG = 2
    END = 5 * LAG

    def __init__(self, dp, where, owner, halves, first, size, land, fin, result, sems, before):
        self.dp, self.where, self.owner, self.before = dp, where, owner, before
        self.halves, self.first, self.size, self.land, self.fin = halves, first, size, land, fin
        self.result = result
        self.recv, self.sent, self.free, self.ol, self.os, self.or_ = sems
        self.age = -1
        s, d, t = where
        low = dp // 2 - 1
        self.upward = d <= low
        self.middle = (d == low) | (d == low + 1)
        self.edge = (d == 0) | (d == dp - 1)
        self.inner = (s, jnp.where(self.upward, d + 1, d - 1), t)
        self.outer = (s, jnp.where(self.upward, d - 1, d + 1), t)
        self.mine = jnp.where(self.upward, 0, 1)

    def own(self, h=None):
        return self.halves.at[self.where[0], self.rows(self.first, h)]

    def rows(self, base, h=None):
        if h is None:
            return pl.ds(base, self.size)
        half = self.size // 2
        return pl.ds(pl.multiple_of(base + h * half, 16), half)

    def final(self, h):
        return self.fin.at[self.rows(self.first, h)]

    def inward(self):
        landing = self.land.at[self.rows(self.first)]
        return remote(self.own(), landing, self.sent.at[0], self.recv.at[2], self.inner)

    def swap_part(self):
        h = 1 - self.mine
        return remote(self.own(h), self.final(h), self.sent.at[0], self.recv.at[h], self.inner)

    def swap_sum(self):
        ref = self.final(self.mine)
        return remote(ref, ref, self.sent.at[1], self.recv.at[self.mine], self.inner)

    def outward(self, h):
        ref = self.final(h)
        return remote(ref, ref, self.sent.at[2 + h], self.recv.at[h], self.outer)

    def sweep(self, base, size, fn):
        unit = 32 if size % 32 == 0 else 16

        def chunk(n, c):
            fn(pl.ds(pl.multiple_of(base + n * unit, 16), unit))
            return c

        lax.fori_loop(0, size // unit, chunk, 0)

    def start(self):
        self.age = 0
        before = self.before
        if before is not None:
            assert before.age >= self.END
            before.close()

            @pl.when(self.middle)
            def _():
                pl.semaphore_signal(
                    self.free, inc=1, device_id=self.inner, device_id_type=MESH
                )

        if self.dp > 2:
            pl.when(self.edge)(lambda: self.inward().start())

    def tick(self):
        self.age += 1
        if self.dp == 1:
            if self.age == self.END:
                self.fin[...] = self.halves[0]
            return
        s = self.where[0]
        inside = jnp.logical_not(self.edge)
        if self.age == self.LAG:

            @pl.when(inside)
            def _():
                self.inward().wait_recv()

                def fn(r):
                    total = self.halves[s, r, :].astype(f32) + self.land[r, :].astype(f32)
                    self.halves[s, r, :] = total.astype(bf16)

                self.sweep(self.first, self.size, fn)
                pl.when(jnp.logical_not(self.middle))(lambda: self.inward().start())

            @pl.when(self.middle)
            def _():
                if self.before is not None:
                    pl.semaphore_wait(self.free, 1)
                self.swap_part().start()

        if self.age == 2 * self.LAG:

            @pl.when(self.middle)
            def _():
                h = self.mine
                half = self.size // 2
                self.arrived(h)

                def fn(r):
                    total = self.halves[s, r, :].astype(f32) + self.fin[r, :].astype(f32)
                    self.fin[r, :] = total.astype(bf16)

                self.sweep(self.first + h * half, half, fn)
                self.swap_sum().start()
                pl.when(inside)(lambda: self.outward(h).start())
                self.swap_part().wait_send()

            pl.when(jnp.logical_not(self.middle))(lambda: self.inward().wait_send())

        if self.age == 3 * self.LAG:

            @pl.when(self.middle)
            def _():
                self.arrived(1 - self.mine)
                pl.when(inside)(lambda: self.outward(1 - self.mine).start())

        if self.age == self.END:

            @pl.when(jnp.logical_not(self.middle))
            def _():
                for h in (0, 1):
                    self.arrived(h)
                    pl.when(inside)(lambda h=h: self.outward(h).start())

            pl.when(self.middle)(lambda: self.swap_sum().wait_send())

            @pl.when(inside)
            def _():
                for h in (0, 1):
                    self.outward(h).wait_send()

            self.to_result()[0]()

    def arrived(self, h):
        ref = self.final(h)
        remote(ref, ref, self.sent.at[0], self.recv.at[h], self.where).wait_recv()

    def to_result(self):
        s = self.where[0]
        part = self.rows(self.first)
        target = self.result.at[s, part]
        return to_owner(
            self.owner, self.where, self.fin.at[part], target, target, self.ol, self.os, self.or_
        )

    def close(self):
        self.to_result()[1]()


class Background:
    def __init__(self):
        self.queue, self.active = [], []

    def put(self, pieces):
        self.queue += pieces

    def tick(self):
        for piece in self.active:
            piece.tick()
        self.active = [piece for piece in self.active if piece.age < piece.END]
        if self.queue:
            piece = self.queue.pop(0)
            piece.start()
            self.active.append(piece)

    def until(self, pieces, age):
        while any(piece.age < age for piece in pieces):
            self.tick()


def backward_kernel(
    dp, ct_in, y0_in, tok_in, turn_in, scal,
    wi0, wo0, wfi0, wfo0, wi1, wo1, wfi1, wfo1, *refs,
):
    saved_i = (refs[0:14], refs[14:28])
    both_o, gwfi_o, gwfo_o, gmix_o = refs[28:32]
    (
        wi, wo, wfi, wfo, turn, gf, xr, hidden, zq, zk, gate, q, k, v, att, sc, states, branch, mid,
        hid2, pair, mask, mask_t, qd, kd, terms, zout, zin, run, gpair, prod, gb, gm, dv, dk,
        gp, part, got, via, own, gr, gwfi, gwfo, gmix, c_fi, c_fo, c_mix, l_fi, l_fo, l_mix,
        f_fi, f_fo, f_mix, lsem, ssem, rsem, zs, zr, ol, os, or_, core_s, core_r, ls, lr, free,
    ) = refs[32:]
    where = s, d, t = place()
    rows = y0_in.shape[0]
    total = 4 * rows
    nb = total // BLOCK
    fp = wfo.shape[0]
    half = rows // 2
    table = 2 * nb + 4 + 4 * dp
    local = Sems(lsem)
    me = rows_of(t, rows)
    gated, gatt = slice(0, WIDTH), slice(WIDTH, 2 * WIDTH)

    def gatt_head(h):
        return slice(WIDTH + h * HEAD, WIDTH + (h + 1) * HEAD)

    def load(src, dst):
        copy = pltpu.make_async_copy(src, dst, local.take())
        copy.start()
        return copy

    def block_of(ref):
        return lambda p, h: ref.at[pl.ds(pl.multiple_of(p * rows + h * half, half), half)]

    weights = ((wi0, wo0, wfi0, wfo0), (wi1, wo1, wfi1, wfo1))

    def load_feed(layer):
        keep = saved_i[layer]
        return [
            load(weights[layer][3], wfo), load(keep[13], pair), load(weights[layer][2], wfi),
            load(keep[11], mid), load(keep[12], hid2),
        ]

    def load_gates(layer):
        keep = saved_i[layer]
        return [
            load(weights[layer][1], wo), load(keep[10], branch), load(keep[8], sc), load(keep[7], att),
            load(keep[3], gate),
        ]

    def load_attn(layer):
        keep = saved_i[layer]
        pairs = ((4, q), (5, k), (6, v), (9, states), (1, zq), (2, zk))
        return [load(keep[n], ref) for n, ref in pairs]

    def load_ends(layer):
        x = tok_in.at[s] if layer == 0 else y0_in
        return [load(weights[layer][0], wi), load(saved_i[layer][0], hidden), load(x, xr)]


    ff = l_fo.shape[0]
    pieces, pairs = {}, {}
    for layer in (1, 0):
        cuts = [(gwfo, 256 * n, min(256, ff - 256 * n), l_fo, f_fo, gwfo_o) for n in range(-(-ff // 256))]
        cuts += [(gwfi, 96 * n, min(96, ff - 96 * n), l_fi, f_fi, gwfi_o) for n in range(-(-ff // 96))]
        cuts += [(gmix, 256 * n, 256, l_mix, f_mix, gmix_o) for n in range((D + WIDTH) // 256)]
        made = []
        for n, cut in enumerate(cuts):
            slot = PIECES * layer + n
            sems = [ref.at[slot] for ref in (lr, ls)] + [free.at[n]]
            sems += [ref.at[slot] for ref in (ol, os, or_)]
            before = pieces[1][n] if layer == 0 else None
            made.append(LineSum(dp, where, s == layer, *cut, sems, before))
        pieces[layer] = made
        pairs[layer] = [
            CorePair(where, halves, landed, core_s.at[3 * layer + n], core_r.at[3 * layer + n])
            for n, (halves, landed) in enumerate(((gwfo, c_fo), (gwfi, c_fi), (gmix, c_mix)))
        ]
    n_out, n_feed = -(-ff // 256), -(-ff // 256) + -(-ff // 96)
    work = Background()
    tick = work.tick

    got_g = load(ct_in.at[s], gf.at[me])
    in_feed, in_tables = load_feed(1), [load(turn_in, turn)]
    in_gates, in_attn, in_ends = load_gates(1), load_attn(1), load_ends(1)
    entry(dp, s, d, t, core=True)
    got_g.wait()
    in_out = []

    for layer in (1, 0):
        offset = table * layer
        pair_fo, pair_fi, pair_mix = pairs[layer]
        base = 24 * layer
        gg = Gather(block_of(gf), half, ssem, rsem, base, where)
        gg.start()
        decay_fill(scal, offset, nb, mask, mask_t, qd, kd)
        tick()
        for copy in in_feed:
            copy.wait()
        sums = Scatter(part, got, via, rows, ssem, rsem, base + 6, where)

        def feed(i, c):
            for n in (1, 2, 3):

                @pl.when(i == n)
                def _(n=n):
                    if n == 1:
                        gg.forward()
                    tick()
                    gg.ready(n)

            r = rows_of(partner(t, i), rows)
            grad = nt(gf[r, :], wfo[...])
            p0, p1 = pair[0, r, :].astype(f32), pair[1, r, :].astype(f32)
            prod[r, :] = (p0 * p1).astype(bf16)
            g0, g1 = (grad * p1).astype(bf16), (grad * p0).astype(bf16)
            gpair[0, r, :] = g0
            gpair[1, r, :] = g1
            o = nn(g0, wfi[0]) + nn(g1, wfi[1])
            for n in (1, 2, 3):

                @pl.when(i == n)
                def _(n=n):
                    sums.put(n, o)

            @pl.when(i == 0)
            def _():
                own[...] = o

            return c

        lax.fori_loop(0, 4, feed, 0)
        tick()

        def feed_weights(n, c):
            cols = rows_of(n, 256)
            for part_of in (0, 1):
                gwfi[part_of, cols, :] = tn(gpair[part_of, :, cols], hid2[...]).astype(bf16)
            return c

        def out_weights(n, c):
            cols = rows_of(n, 256)
            a = prod[:, cols]
            gwfo[0, cols, :] = tn(a, gf[:, : D // 2]).astype(bf16)
            gwfo[1, cols, :] = tn(a, gf[:, D // 2 :]).astype(bf16)
            return c

        if layer == 0:
            work.until(pieces[1][:n_feed], 2 * LineSum.LAG)
        lax.fori_loop(0, fp // 256, out_weights, 0)
        pair_fo.send()
        lax.fori_loop(0, fp // 256, feed_weights, 0)
        pair_fi.send()
        tick()
        sums.combine()
        pair_fo.add()
        work.put(pieces[layer][:n_out])
        tick()
        pair_fi.add()
        work.put(pieces[layer][n_out:n_feed])
        grad_middle = gf[me, :].astype(f32) + norm_back(mid[...], own[...] + sums.result())
        gm[...] = grad_middle
        gb[me, :] = grad_middle.astype(bf16)
        sums.drain()
        gg.drain()

        gbg = Gather(block_of(gb), half, ssem, rsem, base + 12, where)
        gbg.start()
        if layer == 1:
            in_feed = load_feed(0)
        tick()
        for copy in in_gates:
            copy.wait()

        def gating(i, c):
            for n in (1, 2, 3):

                @pl.when(i == n)
                def _(n=n):
                    if n == 1:
                        gbg.forward()
                    tick()
                    gbg.ready(n)

            r = rows_of(partner(t, i), rows)
            b = gb[r, :]
            grad = nt(b, wo[...])
            dots = jnp.sum(b.astype(f32) * branch[r, :].astype(f32), axis=-1, keepdims=True) * (1.0 / D)
            scale = sc[r, 0:1]
            normed = att[r, :] * scale
            gt = gate[r, :]
            gp[r, 3 * WIDTH :] = (grad * normed).astype(bf16)
            prod[r, gated] = (normed * gt).astype(bf16)
            prod[r, gatt] = (scale * (grad * gt - normed * dots)).astype(bf16)
            return c

        lax.fori_loop(0, 4, gating, 0)
        tick()
        if layer == 1:
            in_gates = load_gates(0)
        for copy in in_attn:
            copy.wait()
        if layer == 1:
            for copy in in_tables:
                copy.wait()

        def term(b, c):
            r = rows_of(b, BLOCK)
            for h in range(HEADS_HERE):
                qdec = (q[r, head(h)].astype(f32) * qd[h]).astype(bf16)
                terms[b, h] = tn(qdec, prod[r, gatt_head(h)])
            return c

        lax.fori_loop(0, nb, term, 0)
        for h in range(HEADS_HERE):
            carried = scal[offset + nb - 1] * terms[nb - 1, h]
            for b in reversed(range(nb - 1)):
                carried = scal[offset + b] * (terms[b, h] + scal[offset + nb + 2 + h] * carried)
            zout[layer, h] = carried.astype(bf16)
        z_args = (dp, where, zout.at[layer], zin.at[layer], zs.at[layer], zr.at[layer], False)
        send_states(*z_args)
        tick()

        def unturn(pre, grad, r, h):
            back = grad * turn[0, r, :] - pltpu.roll(grad, HEAD // 2, 1) * turn[1, r, :]
            z = pre[r, head(h)]
            g = sig(z)
            return (back * (g * (1.0 + z * (1.0 - g)))).astype(bf16)

        def inner(b, c):
            r = rows_of(b, BLOCK)
            for h in range(HEADS_HERE):
                qh, kh, vh, gh = q[r, head(h)], k[r, head(h)], v[r, head(h)], prod[r, gatt_head(h)]
                w_t = (nt(kh, qh) * mask_t[h]).astype(bf16)
                dv[r, head(h)] = nn(w_t, gh)
                ds = (nt(gh, vh) * mask[h]).astype(bf16)
                ds_t = (nt(vh, gh) * mask_t[h]).astype(bf16)
                dk[r, head(h)] = nn(ds_t, qh)
                dq = nn(ds, kh) + nt(gh, states[b, h].astype(bf16)) * qd[h]
                gp[r, head(h)] = unturn(zq, dq, r, h)
            return c

        lax.fori_loop(0, nb, inner, 0)
        tick()
        take_states(*z_args, scal, offset + nb + 4 + 2 * dp, run)

        def outer(i, c):
            b = nb - 1 - i
            r = rows_of(b, BLOCK)
            for h in range(HEADS_HERE):
                after = run[h]
                low = after.astype(bf16)
                run[h] = scal[offset + b] * (terms[b, h] + scal[offset + nb + 2 + h] * after)
                kdec = (k[r, head(h)].astype(f32) * kd[h]).astype(bf16)
                dkh = dk[r, head(h)] + nt(v[r, head(h)], low) * kd[h]
                k_cols = slice(WIDTH + h * HEAD, WIDTH + (h + 1) * HEAD)
                v_cols = slice(2 * WIDTH + h * HEAD, 2 * WIDTH + (h + 1) * HEAD)
                gp[r, k_cols] = unturn(zk, dkh, r, h)
                gp[r, v_cols] = (dv[r, head(h)] + nn(kdec, low)).astype(bf16)
            return c

        lax.fori_loop(0, nb, outer, 0)
        tick()
        if layer == 1:
            in_attn = load_attn(0)
        for copy in in_ends:
            copy.wait()
        ins = Scatter(part, got, via, rows, ssem, rsem, base + 18, where)

        def back_in(i, c):
            e = 3 - i
            r = rows_of(partner(t, e), rows)
            o = nt(gp[r, :], wi[...])
            for n in (1, 2, 3):

                @pl.when(e == n)
                def _(n=n):
                    ins.put(n, o)

            @pl.when(e == 0)
            def _():
                own[...] = o

            return c

        lax.fori_loop(0, 4, back_in, 0)
        tick()
        if layer == 0:
            work.until(pieces[1], 2 * LineSum.LAG)

        def in_weights(n, c):
            cols = rows_of(n, 256)
            a = hidden[:, cols]
            gmix[0, cols, :] = tn(a, gp[:, : 2 * WIDTH]).astype(bf16)
            gmix[1, cols, :] = tn(a, gp[:, 2 * WIDTH :]).astype(bf16)
            return c

        lax.fori_loop(0, D // 256, in_weights, 0)
        gmix[0, D:, :] = tn(prod[:, gated], gb[:, : D // 2]).astype(bf16)
        gmix[1, D:, :] = tn(prod[:, gated], gb[:, D // 2 :]).astype(bf16)
        pair_mix.send()
        ins.combine()
        tick()
        pair_mix.add()
        work.put(pieces[layer][n_feed:])
        tick()
        dx = gm[...] + norm_back(xr[...].astype(f32), own[...] + ins.result())
        gr[layer] = dx.astype(bf16)
        ins.drain()
        gbg.drain()
        sent_states(*z_args)
        start, finish = to_owner(
            s == layer, where, gr.at[layer], both_o.at[s], both_o.at[s],
            ol.at[2 * PIECES + layer], os.at[2 * PIECES + layer], or_.at[2 * PIECES + layer],
        )
        start()
        in_out.append(finish)
        if layer == 1:
            gf[me, :] = gr[layer]
            in_ends = load_ends(0)

    work.until(pieces[0], LineSum.END)
    for piece in pieces[0]:
        piece.close()
    for finish in in_out:
        finish()


def layers_backward(cotangent, y0, tokens, turn, scal, weights, saved, dp, ff, uid):
    rows = y0.shape[-2]
    total = 4 * rows
    nb = total // BLOCK
    fp = weights[0][3].shape[0]
    mixed = D + WIDTH
    outs = [
        ((2, rows, D), bf16), ((2, fp, D), bf16), ((2, fp, D // 2), bf16), ((2, mixed, D // 2), bf16)
    ]
    scratch = [
        ((D, 4 * WIDTH), bf16), ((WIDTH, D), bf16), ((2, fp, D), bf16), ((fp, D), bf16),
        ((2, total, HEAD), f32), ((total, D), bf16), ((rows, D), bf16),
    ]
    scratch += [(a.shape, a.dtype) for a in saved[0]]
    scratch += [
        ((HEADS_HERE, BLOCK, BLOCK), f32), ((HEADS_HERE, BLOCK, BLOCK), f32),
        ((HEADS_HERE, BLOCK, HEAD), f32), ((HEADS_HERE, BLOCK, HEAD), f32),
        ((nb, HEADS_HERE, HEAD, HEAD), f32), ((2, HEADS_HERE, HEAD, HEAD), bf16),
        ((2, dp, HEADS_HERE, HEAD, HEAD), bf16), ((HEADS_HERE, HEAD, HEAD), f32),
        ((2, total, fp), bf16), ((total, fp), bf16), ((total, D), bf16), ((rows, D), f32),
        ((total, WIDTH), f32), ((total, WIDTH), f32),
        ((total, 4 * WIDTH), bf16),
        ((3, rows, D), bf16), ((2, rows, D), bf16), ((2, rows // 2, D), bf16), ((rows, D), f32),
        ((2, rows, D), bf16),
        ((2, fp, D), bf16), ((2, fp, D // 2), bf16), ((2, mixed, D // 2), bf16),
        ((fp, D), bf16), ((fp, D // 2), bf16), ((mixed, D // 2), bf16),
        ((ff, D), bf16), ((ff, D // 2), bf16), ((mixed, D // 2), bf16),
        ((ff, D), bf16), ((ff, D // 2), bf16), ((mixed, D // 2), bf16),
    ]
    count = 2 * PIECES
    dma = pltpu.SemaphoreType.DMA
    flops = 8 * total * D * (4 * WIDTH + WIDTH + 3 * fp)
    flat = [w for layer in weights for w in layer]
    kept = [a for layer in saved for a in layer]
    return pl.pallas_call(
        functools.partial(backward_kernel, dp),
        out_shape=tuple(jax.ShapeDtypeStruct(a, b) for a, b in outs),
        in_specs=[ANY] * 4 + [SMEM] + [ANY] * (len(flat) + len(kept)),
        out_specs=(ANY,) * len(outs),
        scratch_shapes=[pltpu.VMEM(a, b) for a, b in scratch]
        + [
            dma((48,)), dma((48,)), dma((48,)), dma((2, dp)), dma((2, dp)), dma((count + 2,)),
            dma((count + 2,)), dma((count + 2,)), dma((6,)), dma((6,)), dma((count, 4)),
            dma((count, 3)), pltpu.SemaphoreType.REGULAR((PIECES,)),
        ],
        compiler_params=pltpu.CompilerParams(
            collective_id=uid, has_side_effects=True, vmem_limit_bytes=VMEM_BYTES
        ),
        cost_estimate=pl.CostEstimate(flops=flops, bytes_accessed=60 << 20, transcendentals=0),
        name="layers_backward",
    )(cotangent, y0, tokens, turn, scal, *flat, *kept)


def widen_kernel(section, fi, fo, mix, mix_out, both0, both1, g_in, g_fi, g_out, g_fo, outputs):
    for n in range(4):
        lanes = slice((n % 2) * WIDTH, (n % 2 + 1) * WIDTH)
        g_in[:, n, :] = mix[n // 2, :, lanes].astype(f32)
    for n in range(2):
        half = slice(n * (D // 2), (n + 1) * (D // 2))
        g_fi[n] = fi[n].astype(f32)
        g_out[:, half] = mix_out[n].astype(f32)
        g_fo[:, half] = fo[n].astype(f32)

    @pl.when(section[0] == 0)
    def _():
        outputs[...] = both0[...]

    @pl.when(section[0] != 0)
    def _():
        outputs[...] = both1[...]


def widen(s, g_fi, g_fo, g_mix, both0, both1, ff):
    cuts = 4
    rows = both0.shape[1]
    n = D // cuts
    ahead = D // (WIDTH // cuts)
    shapes = ((D, 4, WIDTH), (2, ff, D), (WIDTH, D), (ff, D))
    per_row = lambda *shape: pl.BlockSpec(shape, lambda i, _: (i,) + (0,) * (len(shape) - 1))
    halves = lambda *shape: pl.BlockSpec(shape, lambda i, _: (0, i, 0))
    return pl.pallas_call(
        widen_kernel,
        out_shape=tuple(jax.ShapeDtypeStruct(a, f32) for a in shapes)
        + (jax.ShapeDtypeStruct(both0.shape, bf16),),
        grid_spec=pltpu.PrefetchScalarGridSpec(
            num_scalar_prefetch=1,
            grid=(cuts,),
            in_specs=[
                halves(2, ff // cuts, D),
                halves(2, ff // cuts, D // 2),
                halves(2, n, D // 2),
                pl.BlockSpec((2, WIDTH // cuts, D // 2), lambda i, _: (0, ahead + i, 0)),
                halves(2, rows // cuts, D),
                halves(2, rows // cuts, D),
            ],
            out_specs=(
                per_row(n, 4, WIDTH), halves(2, ff // cuts, D), per_row(WIDTH // cuts, D),
                per_row(ff // cuts, D),
                halves(2, rows // cuts, D),
            ),
        ),
        compiler_params=pltpu.CompilerParams(vmem_limit_bytes=VMEM_BYTES),
        cost_estimate=pl.CostEstimate(flops=0, bytes_accessed=24 << 20, transcendentals=0),
        name="widen",
    )(s.reshape(1), g_fi, g_fo, g_mix, g_mix, both0, both1)


def frequencies():
    lane = np.arange(HEAD) % (HEAD // 2)
    row = np.float32(10000.0) ** (-lane.astype(np.float32) / np.float32(HEAD // 2))
    return np.broadcast_to(row.astype(np.float32), (8, HEAD))


def swap(x):
    return lax.ppermute(x, "section", [(0, 1), (1, 0)])


def mine_first(s, a, b):
    return jnp.where(s == 0, a, b)


def shards(tokens, cotangent, mixer_in, mixer_out, feed_in, feed_out, decay_rate, block_starts):
    s = lax.axis_index("section")
    dp = lax.axis_size("dp")
    rows = tokens.shape[1]
    blocks = 4 * rows // BLOCK
    ff = feed_out.shape[1]
    wfi = jnp.transpose(feed_in[0], (1, 2, 0))
    mine = (mixer_in[0], mixer_out[0], wfi, feed_out[0])
    other_rates = swap(decay_rate[0])
    rates = (mine_first(s, decay_rate[0], other_rates), mine_first(s, other_rates, decay_rate[0]))
    starts = lax.dynamic_index_in_dim(block_starts, s, 0, keepdims=False)
    scal = jnp.concatenate([row for r in rates for row in scalar_table(starts, r, dp, blocks)])

    both0, *out0 = layer_forward(0, True, tokens, mine, frequencies(), scal, dp, 1)
    turn, weights0, y0, saved0 = out0[0], out0[1:5], out0[5], out0[6:]
    both1, *out1 = layer_forward(1, False, y0, mine, turn, scal, dp, 2)
    weights1, saved1 = out1[1:5], out1[6:]
    in_grads, g_fi, g_fo, g_mix = layers_backward(
        cotangent, y0, tokens, turn, scal, (weights0, weights1),
        (saved0, saved1), dp, ff, 3,
    )
    g_in, g_feed_in, g_out, g_feed_out, outputs = widen(s, g_fi, g_fo, g_mix, both0, both1, ff)
    g_feed_in = jnp.transpose(g_feed_in, (2, 0, 1))
    return outputs[None], in_grads[None], g_in[None], g_out[None], g_feed_in[None], g_feed_out[None]


def solution(mesh):
    placed = (
        P(None, ("dp", "tensor"), None),
        P(None, ("dp", "tensor"), None),
        P("section", None, None, "tensor"),
        P("section", "tensor", None),
        P("section", None, None, "tensor"),
        P("section", "tensor", None),
        P("section", "tensor"),
        P(),
    )
    return jax.shard_map(
        shards,
        mesh=mesh,
        in_specs=placed,
        out_specs=(
            P("section", None, ("dp", "tensor"), None),
            P("section", None, ("dp", "tensor"), None),
            P("section", None, None, "tensor"),
            P("section", "tensor", None),
            P("section", None, None, "tensor"),
            P("section", "tensor", None),
        ),
        check_vma=False,
    )
```

```python
import functools

import jax
import jax.numpy as jnp
import numpy as np
from jax import lax
from jax.experimental import pallas as pl
from jax.experimental.pallas import tpu as pltpu
from jax.sharding import PartitionSpec as P

D = 1024
HEAD = 128
BLOCK = 256
WIDTH = 256
HEADS_HERE = WIDTH // HEAD
norm_eps = 1e-06
MESH = pl.DeviceIdType.MESH
ANY = pl.BlockSpec(memory_space=pl.ANY)
SMEM = pl.BlockSpec(memory_space=pltpu.SMEM)
bf16, f32 = jnp.bfloat16, jnp.float32
PIECES = 16
VMEM_BYTES = 62 * 1024 * 1024


def place():
    return lax.axis_index("section"), lax.axis_index("dp"), lax.axis_index("tensor")


def partner(t, k):
    return ((t // 2 + k // 2) % 2) * 2 + (t + k) % 2


class Sems:
    def __init__(self, ref):
        self.ref, self.used = ref, 0

    def take(self):
        self.used += 1
        return self.ref.at[self.used - 1]


def remote(src, dst, send, recv, dev):
    return pltpu.make_async_remote_copy(
        src_ref=src, dst_ref=dst, send_sem=send, recv_sem=recv, device_id=dev, device_id_type=MESH
    )


def nn(a, b):
    return lax.dot_general(a, b, (((1,), (0,)), ((), ())), preferred_element_type=f32)


def nt(a, b):
    return lax.dot_general(a, b, (((1,), (1,)), ((), ())), preferred_element_type=f32)


def tn(a, b):
    return lax.dot_general(a, b, (((0,), (0,)), ((), ())), preferred_element_type=f32)


def rms_scale(v):
    return lax.rsqrt(jnp.mean(v * v, axis=-1, keepdims=True) + norm_eps)


def norm_back(v, u):
    q = rms_scale(v)
    n = v * q
    return q * (u - n * jnp.mean(u * n, axis=-1, keepdims=True))


def sig(v):
    return 1.0 / (1.0 + jnp.exp(-v))


def rows_of(p, n):
    return pl.ds(pl.multiple_of(p * n, n), n)


def entry(dp, s, d, t, core=False):
    barrier = pltpu.get_barrier_semaphore()
    count = 3
    for k in (1, 2, 3):
        pl.semaphore_signal(barrier, inc=1, device_id=(s, d, partner(t, k)), device_id_type=MESH)
    if core:
        pl.semaphore_signal(barrier, inc=1, device_id=(1 - s, d, t), device_id_type=MESH)
        count += 1
    if dp > 1:

        def greet(k, c):
            pl.semaphore_signal(
                barrier, inc=1, device_id=(s, (d + k) % dp, t), device_id_type=MESH
            )
            return c

        lax.fori_loop(1, dp, greet, 0)
        count += dp - 1
    pl.semaphore_wait(barrier, count)


class Gather:
    def __init__(self, block_at, half, ssem, rsem, base, where):
        self.at, self.half, self.ssem, self.rsem, self.base = block_at, half, ssem, rsem, base
        self.where = where

    def copy(self, n, peer, half, to):
        s, d, t = self.where
        ref = self.at(partner(t, peer), half)
        k = self.base + n
        return remote(ref, ref, self.ssem.at[k], self.rsem.at[k], (s, d, partner(t, to)))

    def mine(self, n):
        peer, half, to = ((0, 0, 1), (0, 1, 1), (0, 0, 2), (0, 1, 2), (1, 0, 2), (2, 1, 1))[n]
        return self.copy(n, peer, half, to)

    def arriving(self, n):
        s, d, t = self.where
        peer, half = ((1, 0), (1, 1), (2, 0), (2, 1), (3, 0), (3, 1))[n]
        ref = self.at(partner(t, peer), half)
        k = self.base + n
        return remote(ref, ref, self.ssem.at[k], self.rsem.at[k], (s, d, t))

    def start(self):
        self.mine(0).start()
        self.mine(3).start()
        self.mine(1).start()
        self.mine(2).start()

    def forward(self):
        self.arriving(0).wait_recv()
        self.mine(4).start()
        self.arriving(3).wait_recv()
        self.mine(5).start()

    def ready(self, k):
        if k == 1:
            self.arriving(1).wait_recv()
        elif k == 2:
            self.arriving(2).wait_recv()
        else:
            self.arriving(4).wait_recv()
            self.arriving(5).wait_recv()

    def drain(self):
        for n in range(6):
            self.mine(n).wait_send()


class Scatter:
    def __init__(self, part, got, via, rows, ssem, rsem, base, where):
        self.part, self.got, self.via, self.half = part, got, via, rows // 2
        self.ssem, self.rsem, self.base, self.where = ssem, rsem, base, where

    def copy(self, n):
        s, d, t = self.where
        h = self.half
        h0, h1 = pl.ds(0, h), pl.ds(h, h)
        src, dst, to = (
            (self.part.at[2, h0], self.via.at[0], 2),
            (self.part.at[2, h1], self.via.at[1], 1),
            (self.part.at[0, h1], self.got.at[0, h1], 1),
            (self.part.at[1, h0], self.got.at[1, h0], 2),
            (self.part.at[0, h0], self.got.at[0, h0], 1),
            (self.part.at[1, h1], self.got.at[1, h1], 2),
        )[n]
        k = self.base + n
        return remote(src, dst, self.ssem.at[k], self.rsem.at[k], (s, d, partner(t, to)))

    def put(self, k, value):
        self.part[k - 1] = value.astype(bf16)
        self.send(k)

    def send(self, k):
        if k == 3:
            self.copy(0).start()
            self.copy(1).start()
        elif k == 2:
            self.copy(3).start()
        else:
            self.copy(2).start()

    def combine(self):
        h = self.half
        self.copy(0).wait_recv()
        self.part[0, 0:h] = (self.part[0, 0:h].astype(f32) + self.via[0].astype(f32)).astype(bf16)
        self.copy(4).start()
        self.copy(1).wait_recv()
        self.part[1, h:] = (self.part[1, h:].astype(f32) + self.via[1].astype(f32)).astype(bf16)
        self.copy(5).start()

    def result(self):
        for n in (2, 3, 4, 5):
            self.copy(n).wait_recv()
        return self.got[0].astype(f32) + self.got[1].astype(f32)

    def drain(self):
        for n in range(6):
            self.copy(n).wait_send()


def scalar_table(starts, rates, dp, blocks):
    d = lax.axis_index("dp")
    survive = 1.0 - starts.astype(f32).reshape(dp, blocks)
    decay = jnp.exp(-rates * BLOCK)
    factor = jnp.prod(survive, axis=1)[:, None] * (decay**blocks)[None, :]
    at = jnp.arange(dp)
    low, high = jnp.minimum(at, d), jnp.maximum(at, d)
    between = (at[None, :] > low[:, None]) & (at[None, :] < high[:, None])
    through = jnp.prod(jnp.where(between[:, :, None], factor[None], 1.0), axis=1)
    forward = jnp.where((at < d)[:, None], through, 0.0)
    backward = jnp.where((at > d)[:, None], through, 0.0)
    mine = lax.dynamic_index_in_dim(survive, d, 0, keepdims=False)
    index = jnp.arange(starts.shape[0], dtype=jnp.int32)
    begins = jnp.max(
        jnp.where((index[None, :] <= index[:, None]) & (starts > 0)[None, :], index[None, :], 0), axis=1
    )
    offsets = lax.dynamic_slice_in_dim((index - begins) * BLOCK, d * blocks, blocks).astype(f32)
    return [mine, rates, decay, forward.reshape(-1), backward.reshape(-1), offsets]


def decay_fill(scal, base, nb, mask, mask_t, qd, kd):
    for h in range(HEADS_HERE):
        r = scal[base + nb + h]
        i = lax.broadcasted_iota(jnp.int32, (BLOCK, BLOCK), 0).astype(f32)
        j = lax.broadcasted_iota(jnp.int32, (BLOCK, BLOCK), 1).astype(f32)
        gap = i - j
        mask[h] = jnp.where(gap >= 0.0, jnp.exp(-r * jnp.maximum(gap, 0.0)), 0.0)
        if mask_t is not None:
            mask_t[h] = jnp.where(gap <= 0.0, jnp.exp(-r * jnp.maximum(-gap, 0.0)), 0.0)
        i = lax.broadcasted_iota(jnp.int32, (BLOCK, HEAD), 0).astype(f32)
        qd[h] = jnp.exp(-r * (i + 1.0))
        kd[h] = jnp.exp(-r * (BLOCK - 1.0 - i))


def head(h):
    return slice(h * HEAD, (h + 1) * HEAD)


def send_states(dp, where, zout, zin, zs, zr, later):
    s, d, t = where

    def each(k, c):
        to = d + k if later else d - k

        @pl.when((to < dp) if later else (to >= 0))
        def _():
            remote(zout, zin.at[d], zs.at[k], zr.at[d], (s, to, t)).start()

        return c

    lax.fori_loop(1, dp, each, 0)


def sent_states(dp, where, zout, zin, zs, zr, later):
    s, d, t = where

    def each(k, c):
        to = d + k if later else d - k

        @pl.when((to < dp) if later else (to >= 0))
        def _():
            remote(zout, zin.at[d], zs.at[k], zr.at[d], (s, to, t)).wait_send()

        return c

    lax.fori_loop(1, dp, each, 0)


def take_states(dp, where, zout, zin, zs, zr, later, scal, base, run):
    s, d, t = where
    run[...] = jnp.zeros_like(run)

    def each(k, c):
        @pl.when((k < d) if later else (k > d))
        def _():
            remote(zout, zin.at[k], zs.at[0], zr.at[k], (s, d, t)).wait_recv()
            for h in range(HEADS_HERE):
                run[h] += scal[base + 2 * k + h] * zin[k, h].astype(f32)

        return c

    lax.fori_loop(0, dp, each, 0)


def to_owner(owner, where, src, own_dst, far_dst, lsem, ssem, rsem):
    s, d, t = where

    def far():
        return remote(src, far_dst, ssem, rsem, (1 - s, d, t))

    def local():
        return pltpu.make_async_copy(src, own_dst, lsem)

    def start():
        pl.when(owner)(lambda: local().start())
        pl.when(jnp.logical_not(owner))(lambda: far().start())

    def finish():
        @pl.when(owner)
        def _():
            local().wait()
            far().wait_recv()

        pl.when(jnp.logical_not(owner))(lambda: far().wait_send())

    return start, finish


def forward_kernel(
    dp, tok_in, ct_in, my_wi, my_wo, my_wfi, my_wfo, turn_in, scal,
    both0_o, both1_o, turn_o, gf_o, y_out, *refs,
):
    outs = (refs[0:18], refs[18:36])
    (
        raw, wi2, wo2, wfi2, wfo2, turn, gf, xf, hidden, zq, zk, gate, q, k, v, att, sc, states, branch, mid,
        hid2, pair, mask, qd, kd, loc, zout2, zin2, run, u, y, part, got, via, ssq, own, yb2,
        lsem, ssem, rsem, zs2, zr2, wl, ws, wr,
    ) = refs[36:]
    where = s, d, t = place()
    rows = tok_in.shape[-2]
    total = 4 * rows
    nb = total // BLOCK
    local = Sems(lsem)
    me = rows_of(t, rows)

    def load(src, dst):
        copy = pltpu.make_async_copy(src, dst, local.take())
        copy.start()
        return copy

    got_x = load(tok_in.at[s], xf.at[me])
    got_raw = load(my_wi, raw)
    got_turn = load(turn_in, turn.at[0, pl.ds(0, 8)])
    got_ct = load(ct_in.at[s], gf.at[me])
    ff = my_wfo.shape[0]
    pairs = (
        (wi2.at[s], wi2.at[s]), (my_wo, wo2.at[s, rows_of(t, WIDTH)]),
        (my_wfi, wfi2.at[s, :, pl.ds(0, ff)]), (my_wfo, wfo2.at[s, pl.ds(0, ff)]),
    )

    def mine(n):
        return pltpu.make_async_copy(*pairs[n], wl.at[n])

    def over(n):
        return remote(*pairs[n], ws.at[n], wr.at[n], (1 - s, d, t))

    def await_weight(n, owner):
        if n > 0:
            pl.when(owner)(lambda: mine(n).wait())
        pl.when(jnp.logical_not(owner))(lambda: over(n).wait_recv())

    for n in (1, 2, 3):
        mine(n).start()
    wfi2[:, :, ff:, :] = jnp.zeros_like(wfi2[:, :, ff:, :])
    wfo2[:, ff:, :] = jnp.zeros_like(wfo2[:, ff:, :])
    entry(dp, s, d, t, core=True)
    got_x.wait()
    got_ct.wait()
    half = rows // 2

    def block_of(ref):
        return lambda p, h: ref.at[pl.ds(pl.multiple_of(p * rows + h * half, half), half)]

    gg = Gather(block_of(gf), half, ssem, rsem, 42, where)
    quarter = WIDTH // 2
    gw = Gather(
        lambda p, h: wo2.at[s, pl.ds(pl.multiple_of(p * WIDTH + h * quarter, quarter), quarter)],
        quarter, ws, wr, 4, where,
    )

    def wo_over(k, slot):
        ref = wo2.at[slot, rows_of(partner(t, k), WIDTH)]
        return remote(ref, ref, ws.at[10 + k], wr.at[10 + k], (1 - s, d, t))

    stores, finishes = [], []
    for layer in (0, 1):
        (
            wi_o, wo_o, wfi_o, wfo_o, hidden_o, zq_o, zk_o, gate_o, q_o, k_o, v_o, att_o, sc_o, states_o,
            branch_o, mid_o, hid2_o, pair_o,
        ) = outs[layer]
        wi, wo, wfi, wfo = wi2.at[layer], wo2.at[layer], wfi2.at[layer], wfo2.at[layer]
        zout, zin, zs, zr = zout2.at[layer], zin2.at[layer], zs2.at[layer], zr2.at[layer]
        yb = yb2.at[layer]
        both_o = (both0_o, both1_o)[layer]
        owner = s == layer
        at = layer * (2 * nb + 4 + 4 * dp)
        base = 21 * layer
        gx = Gather(block_of(xf), half, ssem, rsem, base, where)
        gx.start()
        if layer == 0:
            for n in (1, 2, 3):
                over(n).start()
            got_raw.wait()

            def chunk(n, c):
                r = rows_of(n, 128)
                wi2[s, r, :] = raw[r].reshape(128, 4 * WIDTH)
                return c

            lax.fori_loop(0, D // 128, chunk, 0)
            over(0).start()
            got_turn.wait()
            frequency = turn[0, 0:1, :]
            sign = jnp.where(lax.broadcasted_iota(jnp.int32, (1, HEAD), 1) < HEAD // 2, -1.0, 1.0)

            def angles(b, c):
                steps_in = lax.broadcasted_iota(jnp.int32, (BLOCK, HEAD), 0).astype(f32)
                angle = (scal[at + nb + 4 + 4 * dp + b] + steps_in) * frequency
                r = rows_of(b, BLOCK)
                turn[0, r, :] = jnp.cos(angle)
                turn[1, r, :] = sign * jnp.sin(angle)
                return c

            lax.fori_loop(0, nb, angles, 0)
            stores.append(load(turn, turn_o))
        decay_fill(scal, at, nb, mask, None, qd, kd)
        await_weight(0, owner)
        if layer == 1:
            for copy in stores:
                copy.wait()
            stores = []

        def project(i, c):
            for n in (1, 2, 3):

                @pl.when(i == n)
                def _(n=n):
                    if n == 1:
                        gx.forward()

                        @pl.when(owner)
                        def _():
                            mine(1).wait()
                            gw.start()

                    gx.ready(n)

            r = rows_of(partner(t, i), rows)
            xv = xf[r, :].astype(f32)
            hid = (xv * rms_scale(xv)).astype(bf16)
            hidden[r, :] = hid
            cs, sn = turn[0, r, :], turn[1, r, :]
            for n, (pre, post) in enumerate(((zq, q), (zk, k))):
                z = nn(hid, wi[:, n * WIDTH : (n + 1) * WIDTH])
                pre[r, :] = z
                a = z * sig(z)
                for h in range(HEADS_HERE):
                    ah = a[:, head(h)]
                    post[r, head(h)] = (ah * cs + pltpu.roll(ah, HEAD // 2, 1) * sn).astype(bf16)
            v[r, :] = nn(hid, wi[:, 2 * WIDTH : 3 * WIDTH]).astype(bf16)
            gate[r, :] = nn(hid, wi[:, 3 * WIDTH :])
            return c

        lax.fori_loop(0, 4, project, 0)

        stores += [load(hidden, hidden_o), load(zq, zq_o), load(zk, zk_o), load(gate, gate_o)]
        stores += [load(q, q_o), load(k, k_o), load(v, v_o)]

        def local_state(b, c):
            r = rows_of(b, BLOCK)
            for h in range(HEADS_HERE):
                kdec = (k[r, head(h)].astype(f32) * kd[h]).astype(bf16)
                loc[b, h] = tn(kdec, v[r, head(h)])
            return c

        lax.fori_loop(0, nb, local_state, 0)
        pl.when(owner)(gw.forward)
        if layer == 1:
            gg.forward()
        for h in range(HEADS_HERE):
            carried = loc[0, h]
            for b in range(1, nb):
                carried = (scal[at + nb + 2 + h] * scal[at + b]) * carried + loc[b, h]
            zout[h] = carried.astype(bf16)
        send_states(dp, where, zout, zin, zs, zr, True)

        def inner(b, c):
            r = rows_of(b, BLOCK)
            for h in range(HEADS_HERE):
                w = (nt(q[r, head(h)], k[r, head(h)]) * mask[h]).astype(bf16)
                att[r, head(h)] = nn(w, v[r, head(h)])
            return c

        lax.fori_loop(0, nb, inner, 0)
        take_states(dp, where, zout, zin, zs, zr, True, scal, at + nb + 4, run)

        def outer(b, c):
            r = rows_of(b, BLOCK)
            for h in range(HEADS_HERE):
                entering = scal[at + b] * run[h]
                states[b, h] = entering
                run[h] = scal[at + nb + 2 + h] * entering + loc[b, h]
                qdec = (q[r, head(h)].astype(f32) * qd[h]).astype(bf16)
                a = att[r, head(h)] + nn(qdec, entering.astype(bf16))
                att[r, head(h)] = a
                u[t, r, head(h)] = (a * gate[r, head(h)]).astype(bf16)
            return c

        lax.fori_loop(0, nb, outer, 0)

        hu = total // 2
        gu = Gather(lambda p, h: u.at[p, pl.ds(h * hu, hu)], hu, ssem, rsem, base + 6, where)
        gu.start()
        for b in range(nb):
            a = att[b * BLOCK : (b + 1) * BLOCK, :]
            ssq[0, :, b * BLOCK : (b + 1) * BLOCK] = lax.dot_general(
                jnp.ones((8, WIDTH), f32), a * a, (((1,), (1,)), ((), ())),
                preferred_element_type=f32, precision=lax.Precision.HIGHEST,
            )
        sums = [
            remote(
                ssq.at[0], ssq.at[n], ssem.at[base + 11 + n], rsem.at[base + 11 + n], (s, d, partner(t, n))
            )
            for n in (1, 2, 3)
        ]
        for copy in sums:
            copy.start()
        stores += [load(att, att_o), load(states, states_o)]

        @pl.when(owner)
        def _():
            for n in (1, 2, 3):
                gw.ready(n)
                wo_over(n, layer).start()

        @pl.when(jnp.logical_not(owner))
        def _():
            over(1).wait_recv()
            for n in (1, 2, 3):
                wo_over(n, layer).wait_recv()

        y[...] = jnp.zeros_like(y)

        def out_project(i, c):
            for n in (1, 2, 3):

                @pl.when(i == n)
                def _(n=n):
                    if n == 1:
                        gu.forward()
                        gg.mine(layer).start()
                        gg.mine(3 - layer).start()
                    gu.ready(n)

            p = partner(t, i)

            def chunk(m, c):
                r = rows_of(m, rows)
                y[r, :] += nn(u[p, r, :], wo[rows_of(p, WIDTH), :])
                return c

            return lax.fori_loop(0, 4, chunk, c)

        lax.fori_loop(0, 4, out_project, 0)
        for copy in sums:
            copy.wait_recv()
        whole = ssq[0] + ssq[1] + ssq[2] + ssq[3]
        sc[...] = jnp.transpose(lax.rsqrt(whole * (1.0 / D) + norm_eps))
        await_weight(2, owner)
        await_weight(3, owner)
        out = Scatter(part, got, via, rows, ssem, rsem, base + 15, where)

        def feed(i, c):
            e = 3 - i
            r = rows_of(partner(t, e), rows)
            br = sc[r, 0:1] * y[r, :]
            m = xf[r, :].astype(f32) + br
            h2 = (m * rms_scale(m)).astype(bf16)
            hid2[r, :] = h2
            p0, p1 = nt(h2, wfi[0]), nt(h2, wfi[1])
            pair[0, r, :] = p0.astype(bf16)
            pair[1, r, :] = p1.astype(bf16)
            o = nn((p0 * p1).astype(bf16), wfo[...])
            for n in (1, 2, 3):

                @pl.when(e == n)
                def _(n=n):
                    out.put(n, o)

            @pl.when(e == 0)
            def _():
                branch[...] = br.astype(bf16)
                mid[...] = m
                own[...] = o + m

            return c

        lax.fori_loop(0, 4, feed, 0)
        stores += [load(sc, sc_o), load(branch, branch_o), load(mid, mid_o), load(hid2, hid2_o)]
        stores += [load(pair, pair_o), load(wi, wi_o), load(wo, wo_o)]
        stores += [load(wfi, wfi_o), load(wfo, wfo_o)]
        gx.drain()
        gu.drain()
        for copy in sums:
            copy.wait_send()
        out.combine()
        yv = (own[...] + out.result()).astype(bf16)
        yb[...] = yv
        out.drain()
        sent_states(dp, where, zout, zin, zs, zr, True)
        start, finish = to_owner(
            owner, where, yb, both_o.at[s], both_o.at[s], wl.at[4 + layer], ws.at[14 + layer],
            wr.at[14 + layer],
        )
        start()
        finishes.append(finish)
        if layer == 0:
            stores.append(load(yb, y_out))
            xf[me, :] = yv


    for n in (1, 2, 3):
        gg.ready(n)
    stores.append(load(gf, gf_o))
    for n in range(4):
        over(n).wait_send()
    for n in (1, 2, 3):
        wo_over(n, s).wait_send()
    gw.drain()
    gg.drain()
    for finish in finishes:
        finish()
    for copy in stores:
        copy.wait()


def layers_forward(tokens, cotangent, weights, frequency, scal, dp, uid):
    rows = tokens.shape[-2]
    total = 4 * rows
    nb = total // BLOCK
    fp = -(-weights[3].shape[0] // 256) * 256
    saved = [
        ((total, D), bf16), ((total, WIDTH), f32), ((total, WIDTH), f32), ((total, WIDTH), f32),
        ((total, WIDTH), bf16), ((total, WIDTH), bf16), ((total, WIDTH), bf16), ((total, WIDTH), f32),
        ((total, 8), f32), ((nb, HEADS_HERE, HEAD, HEAD), f32), ((rows, D), bf16), ((rows, D), f32),
        ((total, D), bf16), ((2, total, fp), bf16),
    ]
    kept = [((D, 4 * WIDTH), bf16), ((D, D), bf16), ((2, fp, D), bf16), ((fp, D), bf16)]
    scratch = [((D, 4, WIDTH), bf16)] + [((2,) + a, b) for a, b in kept]
    scratch += [((2, total, HEAD), f32), ((total, D), bf16), ((total, D), bf16)] + saved
    scratch += [
        ((HEADS_HERE, BLOCK, BLOCK), f32), ((HEADS_HERE, BLOCK, HEAD), f32),
        ((HEADS_HERE, BLOCK, HEAD), f32), ((nb, HEADS_HERE, HEAD, HEAD), f32),
        ((2, HEADS_HERE, HEAD, HEAD), bf16), ((2, dp, HEADS_HERE, HEAD, HEAD), bf16),
        ((HEADS_HERE, HEAD, HEAD), f32), ((4, total, WIDTH), bf16), ((total, D), f32),
        ((3, rows, D), bf16), ((2, rows, D), bf16), ((2, rows // 2, D), bf16),
        ((4, 8, total), f32), ((rows, D), f32), ((2, rows, D), bf16),
    ]
    both = ((2, rows, D), bf16)
    outs = [both, both, ((2, total, HEAD), f32), ((total, D), bf16), ((rows, D), bf16)]
    outs += (kept + saved) * 2
    dma = pltpu.SemaphoreType.DMA
    flops = 4 * total * D * (4 * WIDTH + D + 3 * fp)
    return pl.pallas_call(
        functools.partial(forward_kernel, dp),
        out_shape=tuple(jax.ShapeDtypeStruct(a, b) for a, b in outs),
        in_specs=[ANY] * 7 + [SMEM],
        out_specs=(ANY,) * len(outs),
        scratch_shapes=[pltpu.VMEM(a, b) for a, b in scratch]
        + [
            dma((48,)), dma((48,)), dma((48,)), dma((2, dp)), dma((2, dp)), dma((6,)), dma((16,)),
            dma((16,)),
        ],
        compiler_params=pltpu.CompilerParams(
            collective_id=uid, has_side_effects=True, vmem_limit_bytes=VMEM_BYTES
        ),
        cost_estimate=pl.CostEstimate(flops=flops, bytes_accessed=60 << 20, transcendentals=0),
        name="layers_forward",
    )(tokens, cotangent, *weights, frequency, scal)


class CorePair:
    def __init__(self, where, halves, from_core, ssem, rsem):
        s, d, t = where
        self.s, self.halves, self.landed = s, halves, from_core
        self.copy = lambda: remote(halves.at[1 - s], from_core, ssem, rsem, (1 - s, d, t))

    def send(self):
        self.copy().start()

    def add(self):
        self.copy().wait()
        rows = self.landed.shape[0]
        step = 128

        def chunk(n, c):
            r = rows_of(n, step)
            mine = self.halves[self.s, r, :].astype(f32)
            self.halves[self.s, r, :] = (mine + self.landed[r, :].astype(f32)).astype(bf16)
            return c

        lax.fori_loop(0, rows // step, chunk, 0)


class LineSum:
    LAG = 2
    END = 5 * LAG

    def __init__(self, dp, where, owner, halves, first, size, land, fin, result, sems, before):
        self.dp, self.where, self.owner, self.before = dp, where, owner, before
        self.halves, self.first, self.size, self.land, self.fin = halves, first, size, land, fin
        self.result = result
        self.recv, self.sent, self.free, self.ol, self.os, self.or_ = sems
        self.age = -1
        s, d, t = where
        low = dp // 2 - 1
        self.upward = d <= low
        self.middle = (d == low) | (d == low + 1)
        self.edge = (d == 0) | (d == dp - 1)
        self.inner = (s, jnp.where(self.upward, d + 1, d - 1), t)
        self.outer = (s, jnp.where(self.upward, d - 1, d + 1), t)
        self.mine = jnp.where(self.upward, 0, 1)

    def own(self, h=None):
        return self.halves.at[self.where[0], self.rows(self.first, h)]

    def rows(self, base, h=None):
        if h is None:
            return pl.ds(base, self.size)
        half = self.size // 2
        return pl.ds(pl.multiple_of(base + h * half, 16), half)

    def final(self, h):
        return self.fin.at[self.rows(self.first, h)]

    def inward(self):
        landing = self.land.at[self.rows(self.first)]
        return remote(self.own(), landing, self.sent.at[0], self.recv.at[2], self.inner)

    def swap_part(self):
        h = 1 - self.mine
        return remote(self.own(h), self.final(h), self.sent.at[0], self.recv.at[h], self.inner)

    def swap_sum(self):
        ref = self.final(self.mine)
        return remote(ref, ref, self.sent.at[1], self.recv.at[self.mine], self.inner)

    def outward(self, h):
        ref = self.final(h)
        return remote(ref, ref, self.sent.at[2 + h], self.recv.at[h], self.outer)

    def sweep(self, base, size, fn):
        unit = 32 if size % 32 == 0 else 16

        def chunk(n, c):
            fn(pl.ds(pl.multiple_of(base + n * unit, 16), unit))
            return c

        lax.fori_loop(0, size // unit, chunk, 0)

    def start(self):
        self.age = 0
        before = self.before
        if before is not None:
            assert before.age >= self.END
            before.close()

            @pl.when(self.middle)
            def _():
                pl.semaphore_signal(
                    self.free, inc=1, device_id=self.inner, device_id_type=MESH
                )

        if self.dp > 2:
            pl.when(self.edge)(lambda: self.inward().start())

    def tick(self):
        self.age += 1
        if self.dp == 1:
            if self.age == self.END:
                self.fin[...] = self.halves[0]
            return
        s = self.where[0]
        inside = jnp.logical_not(self.edge)
        if self.age == self.LAG:

            @pl.when(inside)
            def _():
                self.inward().wait_recv()

                def fn(r):
                    total = self.halves[s, r, :].astype(f32) + self.land[r, :].astype(f32)
                    self.halves[s, r, :] = total.astype(bf16)

                self.sweep(self.first, self.size, fn)
                pl.when(jnp.logical_not(self.middle))(lambda: self.inward().start())

            @pl.when(self.middle)
            def _():
                if self.before is not None:
                    pl.semaphore_wait(self.free, 1)
                self.swap_part().start()

        if self.age == 2 * self.LAG:

            @pl.when(self.middle)
            def _():
                h = self.mine
                half = self.size // 2
                self.arrived(h)

                def fn(r):
                    total = self.halves[s, r, :].astype(f32) + self.fin[r, :].astype(f32)
                    self.fin[r, :] = total.astype(bf16)

                self.sweep(self.first + h * half, half, fn)
                self.swap_sum().start()
                pl.when(inside)(lambda: self.outward(h).start())
                self.swap_part().wait_send()

            pl.when(jnp.logical_not(self.middle))(lambda: self.inward().wait_send())

        if self.age == 3 * self.LAG:

            @pl.when(self.middle)
            def _():
                self.arrived(1 - self.mine)
                pl.when(inside)(lambda: self.outward(1 - self.mine).start())

        if self.age == self.END:

            @pl.when(jnp.logical_not(self.middle))
            def _():
                for h in (0, 1):
                    self.arrived(h)
                    pl.when(inside)(lambda h=h: self.outward(h).start())

            pl.when(self.middle)(lambda: self.swap_sum().wait_send())

            @pl.when(inside)
            def _():
                for h in (0, 1):
                    self.outward(h).wait_send()

            self.to_result()[0]()

    def arrived(self, h):
        ref = self.final(h)
        remote(ref, ref, self.sent.at[0], self.recv.at[h], self.where).wait_recv()

    def to_result(self):
        s = self.where[0]
        part = self.rows(self.first)
        target = self.result.at[s, part]
        return to_owner(
            self.owner, self.where, self.fin.at[part], target, target, self.ol, self.os, self.or_
        )

    def close(self):
        self.to_result()[1]()


class Background:
    def __init__(self):
        self.queue, self.active = [], []

    def put(self, pieces):
        self.queue += pieces

    def tick(self):
        for piece in self.active:
            piece.tick()
        self.active = [piece for piece in self.active if piece.age < piece.END]
        if self.queue:
            piece = self.queue.pop(0)
            piece.start()
            self.active.append(piece)

    def until(self, pieces, age):
        while any(piece.age < age for piece in pieces):
            self.tick()


def backward_kernel(
    dp, gf_in, y0_in, tok_in, turn_in, scal,
    wi0, wo0, wfi0, wfo0, wi1, wo1, wfi1, wfo1, *refs,
):
    saved_i = (refs[0:14], refs[14:28])
    both_o, gwfi_o, gwfo_o, gmix_o = refs[28:32]
    (
        wi, wo, wfi, wfo, turn, gf, xr, hidden, zq, zk, gate, q, k, v, att, sc, states, branch, mid,
        hid2, pair, mask, mask_t, qd, kd, terms, zout, zin, run, gpair, prod, gb, gsend, grecv, dots, gm, dv, dk,
        gp, part, got, via, own, gr, gwfi, gwfo, gmix, c_fi, c_fo, c_mix, l_fi, l_fo, l_mix,
        f_fi, f_fo, f_mix, lsem, ssem, rsem, zs, zr, ol, os, or_, core_s, core_r, ls, lr, free,
    ) = refs[32:]
    where = s, d, t = place()
    rows = y0_in.shape[0]
    total = 4 * rows
    nb = total // BLOCK
    fp = wfo.shape[0]
    half = rows // 2
    table = 2 * nb + 4 + 4 * dp
    local = Sems(lsem)
    me = rows_of(t, rows)
    gated, gatt = slice(0, WIDTH), slice(WIDTH, 2 * WIDTH)

    def gatt_head(h):
        return slice(WIDTH + h * HEAD, WIDTH + (h + 1) * HEAD)

    def load(src, dst):
        copy = pltpu.make_async_copy(src, dst, local.take())
        copy.start()
        return copy

    def block_of(ref):
        return lambda p, h: ref.at[pl.ds(pl.multiple_of(p * rows + h * half, half), half)]

    weights = ((wi0, wo0, wfi0, wfo0), (wi1, wo1, wfi1, wfo1))

    def load_feed(layer):
        keep = saved_i[layer]
        return [
            load(weights[layer][3], wfo), load(keep[13], pair), load(weights[layer][2], wfi),
            load(keep[11], mid), load(keep[12], hid2),
        ]

    def load_gates(layer):
        keep = saved_i[layer]
        return [
            load(weights[layer][1], wo), load(keep[10], branch), load(keep[8], sc), load(keep[7], att),
            load(keep[3], gate),
        ]

    def load_attn(layer):
        keep = saved_i[layer]
        pairs = ((4, q), (5, k), (6, v), (9, states), (1, zq), (2, zk))
        return [load(keep[n], ref) for n, ref in pairs]

    def load_ends(layer):
        x = tok_in.at[s] if layer == 0 else y0_in
        return [load(weights[layer][0], wi), load(saved_i[layer][0], hidden), load(x, xr)]


    ff = l_fo.shape[0]
    pieces, pairs = {}, {}
    for layer in (1, 0):
        cuts = [(gwfo, 256 * n, min(256, ff - 256 * n), l_fo, f_fo, gwfo_o) for n in range(-(-ff // 256))]
        cuts += [(gwfi, 96 * n, min(96, ff - 96 * n), l_fi, f_fi, gwfi_o) for n in range(-(-ff // 96))]
        cuts += [(gmix, 256 * n, 256, l_mix, f_mix, gmix_o) for n in range((D + WIDTH) // 256)]
        made = []
        for n, cut in enumerate(cuts):
            slot = PIECES * layer + n
            sems = [ref.at[slot] for ref in (lr, ls)] + [free.at[n]]
            sems += [ref.at[slot] for ref in (ol, os, or_)]
            before = pieces[1][n] if layer == 0 else None
            made.append(LineSum(dp, where, s == layer, *cut, sems, before))
        pieces[layer] = made
        pairs[layer] = [
            CorePair(where, halves, landed, core_s.at[3 * layer + n], core_r.at[3 * layer + n])
            for n, (halves, landed) in enumerate(((gwfo, c_fo), (gwfi, c_fi), (gmix, c_mix)))
        ]
    n_out, n_feed = -(-ff // 256), -(-ff // 256) + -(-ff // 96)
    work = Background()
    tick = work.tick

    got_g = load(gf_in, gf)
    in_feed, in_tables = load_feed(1), [load(turn_in, turn)]
    in_gates, in_attn, in_ends = load_gates(1), load_attn(1), load_ends(1)
    entry(dp, s, d, t, core=True)
    got_g.wait()
    in_out = []

    for layer in (1, 0):
        offset = table * layer
        pair_fo, pair_fi, pair_mix = pairs[layer]
        base = 30 * layer
        gg = Gather(block_of(gf), half, ssem, rsem, base, where) if layer == 0 else None
        if gg is not None:
            gg.start()
        decay_fill(scal, offset, nb, mask, mask_t, qd, kd)
        tick()
        for copy in in_feed:
            copy.wait()
        sums = Scatter(part, got, via, rows, ssem, rsem, base + 6, where)

        def feed(i, c):
            for n in (1, 2, 3) if gg is not None else ():

                @pl.when(i == n)
                def _(n=n):
                    if n == 1:
                        gg.forward()
                    tick()
                    gg.ready(n)

            r = rows_of(partner(t, i), rows)
            grad = nt(gf[r, :], wfo[...])
            p0, p1 = pair[0, r, :].astype(f32), pair[1, r, :].astype(f32)
            prod[r, :] = (p0 * p1).astype(bf16)
            g0, g1 = (grad * p1).astype(bf16), (grad * p0).astype(bf16)
            gpair[0, r, :] = g0
            gpair[1, r, :] = g1
            o = nn(g0, wfi[0]) + nn(g1, wfi[1])
            for n in (1, 2, 3):

                @pl.when(i == n)
                def _(n=n):
                    sums.put(n, o)

            @pl.when(i == 0)
            def _():
                own[...] = o

            return c

        lax.fori_loop(0, 4, feed, 0)
        tick()

        def feed_weights(n, c):
            cols = rows_of(n, 256)
            for part_of in (0, 1):
                gwfi[part_of, cols, :] = tn(gpair[part_of, :, cols], hid2[...]).astype(bf16)
            return c

        def out_weights(n, c):
            cols = rows_of(n, 256)
            a = prod[:, cols]
            gwfo[0, cols, :] = tn(a, gf[:, : D // 2]).astype(bf16)
            gwfo[1, cols, :] = tn(a, gf[:, D // 2 :]).astype(bf16)
            return c

        if layer == 0:
            work.until(pieces[1][:n_feed], 2 * LineSum.LAG)
        lax.fori_loop(0, fp // 256, out_weights, 0)
        pair_fo.send()
        lax.fori_loop(0, fp // 256, feed_weights, 0)
        pair_fi.send()
        tick()
        sums.combine()
        pair_fo.add()
        work.put(pieces[layer][:n_out])
        tick()
        pair_fi.add()
        work.put(pieces[layer][n_out:n_feed])
        grad_middle = gf[me, :].astype(f32) + norm_back(mid[...], own[...] + sums.result())
        gm[...] = grad_middle
        gb[me, :] = grad_middle.astype(bf16)
        sums.drain()
        if gg is not None:
            gg.drain()

        for copy in in_gates:
            copy.wait()
        mine = gb[me, :]
        for p in range(4):
            gsend[p] = nt(mine, wo[p * WIDTH : (p + 1) * WIDTH, :]).astype(bf16)
        grecv[t] = gsend[t]
        dots[t, :, 0:rows] = lax.dot_general(
            jnp.ones((8, D), f32), mine.astype(f32) * branch[...].astype(f32), (((1,), (1,)), ((), ())),
            preferred_element_type=f32, precision=lax.Precision.HIGHEST,
        ) * (1.0 / D)

        def turned(k, into):
            dev = (s, d, partner(t, k))
            slot = partner(t, k) if into else t
            n = base + 24 + 2 * k
            return (
                remote(gsend.at[partner(t, k)], grecv.at[slot], ssem.at[n - 2], rsem.at[n - 2], dev),
                remote(dots.at[t], dots.at[slot], ssem.at[n - 1], rsem.at[n - 1], dev),
            )

        for n in (3, 1, 2):
            for copy in turned(n, False):
                copy.start()
        gbg = Gather(block_of(gb), half, ssem, rsem, base + 12, where)
        gbg.start()
        if layer == 1:
            in_feed = load_feed(0)
        tick()

        def gating(i, c):
            for n in (1, 2, 3):

                @pl.when(i == n)
                def _(n=n):
                    for copy in turned(n, True):
                        copy.wait_recv()

            p = partner(t, i)
            r = rows_of(p, rows)
            grad = grecv[p].astype(f32)
            inner_sum = jnp.transpose(dots[p])[0:rows, 0:1]
            scale = sc[r, 0:1]
            normed = att[r, :] * scale
            gt = gate[r, :]
            gp[r, 3 * WIDTH :] = (grad * normed).astype(bf16)
            prod[r, gated] = (normed * gt).astype(bf16)
            prod[r, gatt] = (scale * (grad * gt - normed * inner_sum)).astype(bf16)
            return c

        lax.fori_loop(0, 4, gating, 0)
        tick()
        if layer == 1:
            in_gates = load_gates(0)
        for copy in in_attn:
            copy.wait()
        if layer == 1:
            for copy in in_tables:
                copy.wait()

        def term(b, c):
            r = rows_of(b, BLOCK)
            for h in range(HEADS_HERE):
                qdec = (q[r, head(h)].astype(f32) * qd[h]).astype(bf16)
                terms[b, h] = tn(qdec, prod[r, gatt_head(h)])
            return c

        lax.fori_loop(0, nb, term, 0)
        for h in range(HEADS_HERE):
            carried = scal[offset + nb - 1] * terms[nb - 1, h]
            for b in reversed(range(nb - 1)):
                carried = scal[offset + b] * (terms[b, h] + scal[offset + nb + 2 + h] * carried)
            zout[layer, h] = carried.astype(bf16)
        z_args = (dp, where, zout.at[layer], zin.at[layer], zs.at[layer], zr.at[layer], False)
        send_states(*z_args)
        tick()
        gbg.forward()

        def unturn(pre, grad, r, h):
            back = grad * turn[0, r, :] - pltpu.roll(grad, HEAD // 2, 1) * turn[1, r, :]
            z = pre[r, head(h)]
            g = sig(z)
            return (back * (g * (1.0 + z * (1.0 - g)))).astype(bf16)

        def inner(b, c):
            r = rows_of(b, BLOCK)
            for h in range(HEADS_HERE):
                qh, kh, vh, gh = q[r, head(h)], k[r, head(h)], v[r, head(h)], prod[r, gatt_head(h)]
                w_t = (nt(kh, qh) * mask_t[h]).astype(bf16)
                dv[r, head(h)] = nn(w_t, gh)
                ds = (nt(gh, vh) * mask[h]).astype(bf16)
                ds_t = (nt(vh, gh) * mask_t[h]).astype(bf16)
                dk[r, head(h)] = nn(ds_t, qh)
                dq = nn(ds, kh) + nt(gh, states[b, h].astype(bf16)) * qd[h]
                gp[r, head(h)] = unturn(zq, dq, r, h)
            return c

        lax.fori_loop(0, nb, inner, 0)
        tick()
        take_states(*z_args, scal, offset + nb + 4 + 2 * dp, run)

        def outer(i, c):
            b = nb - 1 - i
            r = rows_of(b, BLOCK)
            for h in range(HEADS_HERE):
                after = run[h]
                low = after.astype(bf16)
                run[h] = scal[offset + b] * (terms[b, h] + scal[offset + nb + 2 + h] * after)
                kdec = (k[r, head(h)].astype(f32) * kd[h]).astype(bf16)
                dkh = dk[r, head(h)] + nt(v[r, head(h)], low) * kd[h]
                k_cols = slice(WIDTH + h * HEAD, WIDTH + (h + 1) * HEAD)
                v_cols = slice(2 * WIDTH + h * HEAD, 2 * WIDTH + (h + 1) * HEAD)
                gp[r, k_cols] = unturn(zk, dkh, r, h)
                gp[r, v_cols] = (dv[r, head(h)] + nn(kdec, low)).astype(bf16)
            return c

        lax.fori_loop(0, nb, outer, 0)
        tick()
        if layer == 1:
            in_attn = load_attn(0)
        for copy in in_ends:
            copy.wait()
        ins = Scatter(part, got, via, rows, ssem, rsem, base + 18, where)

        def back_in(i, c):
            e = 3 - i
            r = rows_of(partner(t, e), rows)
            o = nt(gp[r, :], wi[...])
            for n in (1, 2, 3):

                @pl.when(e == n)
                def _(n=n):
                    ins.put(n, o)

            @pl.when(e == 0)
            def _():
                own[...] = o

            return c

        lax.fori_loop(0, 4, back_in, 0)
        tick()
        if layer == 0:
            work.until(pieces[1], 2 * LineSum.LAG)

        def in_weights(n, c):
            cols = rows_of(n, 256)
            a = hidden[:, cols]
            gmix[0, cols, :] = tn(a, gp[:, : 2 * WIDTH]).astype(bf16)
            gmix[1, cols, :] = tn(a, gp[:, 2 * WIDTH :]).astype(bf16)
            return c

        lax.fori_loop(0, D // 256, in_weights, 0)
        for n in (1, 2, 3):
            gbg.ready(n)
        gmix[0, D:, :] = tn(prod[:, gated], gb[:, : D // 2]).astype(bf16)
        gmix[1, D:, :] = tn(prod[:, gated], gb[:, D // 2 :]).astype(bf16)
        pair_mix.send()
        ins.combine()
        tick()
        pair_mix.add()
        work.put(pieces[layer][n_feed:])
        tick()
        dx = gm[...] + norm_back(xr[...].astype(f32), own[...] + ins.result())
        gr[layer] = dx.astype(bf16)
        ins.drain()
        gbg.drain()
        for n in (1, 2, 3):
            for copy in turned(n, False):
                copy.wait_send()
        sent_states(*z_args)
        start, finish = to_owner(
            s == layer, where, gr.at[layer], both_o.at[s], both_o.at[s],
            ol.at[2 * PIECES + layer], os.at[2 * PIECES + layer], or_.at[2 * PIECES + layer],
        )
        start()
        in_out.append(finish)
        if layer == 1:
            gf[me, :] = gr[layer]
            in_ends = load_ends(0)

    work.until(pieces[0], LineSum.END)
    for piece in pieces[0]:
        piece.close()
    for finish in in_out:
        finish()


def layers_backward(gathered, y0, tokens, turn, scal, weights, saved, dp, ff, uid):
    rows = y0.shape[-2]
    total = 4 * rows
    nb = total // BLOCK
    fp = weights[0][3].shape[0]
    mixed = D + WIDTH
    outs = [
        ((2, rows, D), bf16), ((2, fp, D), bf16), ((2, fp, D // 2), bf16), ((2, mixed, D // 2), bf16)
    ]
    scratch = [
        ((D, 4 * WIDTH), bf16), ((D, D), bf16), ((2, fp, D), bf16), ((fp, D), bf16),
        ((2, total, HEAD), f32), ((total, D), bf16), ((rows, D), bf16),
    ]
    scratch += [(a.shape, a.dtype) for a in saved[0]]
    scratch += [
        ((HEADS_HERE, BLOCK, BLOCK), f32), ((HEADS_HERE, BLOCK, BLOCK), f32),
        ((HEADS_HERE, BLOCK, HEAD), f32), ((HEADS_HERE, BLOCK, HEAD), f32),
        ((nb, HEADS_HERE, HEAD, HEAD), f32), ((2, HEADS_HERE, HEAD, HEAD), bf16),
        ((2, dp, HEADS_HERE, HEAD, HEAD), bf16), ((HEADS_HERE, HEAD, HEAD), f32),
        ((2, total, fp), bf16), ((total, fp), bf16), ((total, D), bf16), ((4, rows, WIDTH), bf16),
        ((4, rows, WIDTH), bf16), ((4, 8, -(-rows // 128) * 128), f32), ((rows, D), f32),
        ((total, WIDTH), f32), ((total, WIDTH), f32),
        ((total, 4 * WIDTH), bf16),
        ((3, rows, D), bf16), ((2, rows, D), bf16), ((2, rows // 2, D), bf16), ((rows, D), f32),
        ((2, rows, D), bf16),
        ((2, fp, D), bf16), ((2, fp, D // 2), bf16), ((2, mixed, D // 2), bf16),
        ((fp, D), bf16), ((fp, D // 2), bf16), ((mixed, D // 2), bf16),
        ((ff, D), bf16), ((ff, D // 2), bf16), ((mixed, D // 2), bf16),
        ((ff, D), bf16), ((ff, D // 2), bf16), ((mixed, D // 2), bf16),
    ]
    count = 2 * PIECES
    dma = pltpu.SemaphoreType.DMA
    flops = 8 * total * D * (4 * WIDTH + WIDTH + 3 * fp)
    flat = [w for layer in weights for w in layer]
    kept = [a for layer in saved for a in layer]
    return pl.pallas_call(
        functools.partial(backward_kernel, dp),
        out_shape=tuple(jax.ShapeDtypeStruct(a, b) for a, b in outs),
        in_specs=[ANY] * 4 + [SMEM] + [ANY] * (len(flat) + len(kept)),
        out_specs=(ANY,) * len(outs),
        scratch_shapes=[pltpu.VMEM(a, b) for a, b in scratch]
        + [
            dma((48,)), dma((60,)), dma((60,)), dma((2, dp)), dma((2, dp)), dma((count + 2,)),
            dma((count + 2,)), dma((count + 2,)), dma((6,)), dma((6,)), dma((count, 4)),
            dma((count, 3)), pltpu.SemaphoreType.REGULAR((PIECES,)),
        ],
        compiler_params=pltpu.CompilerParams(
            collective_id=uid, has_side_effects=True, vmem_limit_bytes=VMEM_BYTES
        ),
        cost_estimate=pl.CostEstimate(flops=flops, bytes_accessed=60 << 20, transcendentals=0),
        name="layers_backward",
    )(gathered, y0, tokens, turn, scal, *flat, *kept)


def widen_kernel(section, fi, fo, mix, mix_out, both0, both1, g_in, g_fi, g_out, g_fo, outputs):
    for n in range(4):
        lanes = slice((n % 2) * WIDTH, (n % 2 + 1) * WIDTH)
        g_in[:, n, :] = mix[n // 2, :, lanes].astype(f32)
    for n in range(2):
        half = slice(n * (D // 2), (n + 1) * (D // 2))
        g_fi[n] = fi[n].astype(f32)
        g_out[:, half] = mix_out[n].astype(f32)
        g_fo[:, half] = fo[n].astype(f32)

    @pl.when(section[0] == 0)
    def _():
        outputs[...] = both0[...]

    @pl.when(section[0] != 0)
    def _():
        outputs[...] = both1[...]


def widen(s, g_fi, g_fo, g_mix, both0, both1, ff):
    cuts = 4
    rows = both0.shape[1]
    n = D // cuts
    ahead = D // (WIDTH // cuts)
    shapes = ((D, 4, WIDTH), (2, ff, D), (WIDTH, D), (ff, D))
    per_row = lambda *shape: pl.BlockSpec(shape, lambda i, _: (i,) + (0,) * (len(shape) - 1))
    halves = lambda *shape: pl.BlockSpec(shape, lambda i, _: (0, i, 0))
    return pl.pallas_call(
        widen_kernel,
        out_shape=tuple(jax.ShapeDtypeStruct(a, f32) for a in shapes)
        + (jax.ShapeDtypeStruct(both0.shape, bf16),),
        grid_spec=pltpu.PrefetchScalarGridSpec(
            num_scalar_prefetch=1,
            grid=(cuts,),
            in_specs=[
                halves(2, ff // cuts, D),
                halves(2, ff // cuts, D // 2),
                halves(2, n, D // 2),
                pl.BlockSpec((2, WIDTH // cuts, D // 2), lambda i, _: (0, ahead + i, 0)),
                halves(2, rows // cuts, D),
                halves(2, rows // cuts, D),
            ],
            out_specs=(
                per_row(n, 4, WIDTH), halves(2, ff // cuts, D), per_row(WIDTH // cuts, D),
                per_row(ff // cuts, D),
                halves(2, rows // cuts, D),
            ),
        ),
        compiler_params=pltpu.CompilerParams(vmem_limit_bytes=VMEM_BYTES),
        cost_estimate=pl.CostEstimate(flops=0, bytes_accessed=24 << 20, transcendentals=0),
        name="widen",
    )(s.reshape(1), g_fi, g_fo, g_mix, g_mix, both0, both1)


def frequencies():
    lane = np.arange(HEAD) % (HEAD // 2)
    row = np.float32(10000.0) ** (-lane.astype(np.float32) / np.float32(HEAD // 2))
    return np.broadcast_to(row.astype(np.float32), (8, HEAD))


def swap(x):
    return lax.ppermute(x, "section", [(0, 1), (1, 0)])


def mine_first(s, a, b):
    return jnp.where(s == 0, a, b)


def shards(tokens, cotangent, mixer_in, mixer_out, feed_in, feed_out, decay_rate, block_starts):
    s = lax.axis_index("section")
    dp = lax.axis_size("dp")
    rows = tokens.shape[1]
    blocks = 4 * rows // BLOCK
    ff = feed_out.shape[1]
    wfi = jnp.transpose(feed_in[0], (1, 2, 0))
    mine = (mixer_in[0], mixer_out[0], wfi, feed_out[0])
    other_rates = swap(decay_rate[0])
    rates = (mine_first(s, decay_rate[0], other_rates), mine_first(s, other_rates, decay_rate[0]))
    starts = lax.dynamic_index_in_dim(block_starts, s, 0, keepdims=False)
    scal = jnp.concatenate([row for r in rates for row in scalar_table(starts, r, dp, blocks)])

    both0, both1, turn, gf, y0, *kept = layers_forward(
        tokens, cotangent, mine, frequencies(), scal, dp, 1
    )
    weights0, saved0, weights1, saved1 = kept[:4], kept[4:18], kept[18:22], kept[22:]
    in_grads, g_fi, g_fo, g_mix = layers_backward(
        gf, y0, tokens, turn, scal, (weights0, weights1),
        (saved0, saved1), dp, ff, 2,
    )
    g_in, g_feed_in, g_out, g_feed_out, outputs = widen(s, g_fi, g_fo, g_mix, both0, both1, ff)
    g_feed_in = jnp.transpose(g_feed_in, (2, 0, 1))
    return outputs[None], in_grads[None], g_in[None], g_out[None], g_feed_in[None], g_feed_out[None]


def solution(mesh):
    placed = (
        P(None, ("dp", "tensor"), None),
        P(None, ("dp", "tensor"), None),
        P("section", None, None, "tensor"),
        P("section", "tensor", None),
        P("section", None, None, "tensor"),
        P("section", "tensor", None),
        P("section", "tensor"),
        P(),
    )
    return jax.shard_map(
        shards,
        mesh=mesh,
        in_specs=placed,
        out_specs=(
            P("section", None, ("dp", "tensor"), None),
            P("section", None, ("dp", "tensor"), None),
            P("section", None, None, "tensor"),
            P("section", "tensor", None),
            P("section", None, None, "tensor"),
            P("section", "tensor", None),
        ),
        check_vma=False,
    )
```

```python
import functools

import jax
import jax.numpy as jnp
import numpy as np
from jax import lax
from jax.experimental import pallas as pl
from jax.experimental.pallas import tpu as pltpu
from jax.sharding import PartitionSpec as P

D = 1024
HEAD = 128
BLOCK = 256
WIDTH = 256
HEADS_HERE = WIDTH // HEAD
norm_eps = 1e-06
MESH = pl.DeviceIdType.MESH
ANY = pl.BlockSpec(memory_space=pl.ANY)
SMEM = pl.BlockSpec(memory_space=pltpu.SMEM)
bf16, f32 = jnp.bfloat16, jnp.float32
PIECES = 16
VMEM_BYTES = 62 * 1024 * 1024


def place():
    return lax.axis_index("section"), lax.axis_index("dp"), lax.axis_index("tensor")


def partner(t, k):
    return ((t // 2 + k // 2) % 2) * 2 + (t + k) % 2


class Sems:
    def __init__(self, ref):
        self.ref, self.used = ref, 0

    def take(self):
        self.used += 1
        return self.ref.at[self.used - 1]


def remote(src, dst, send, recv, dev):
    return pltpu.make_async_remote_copy(
        src_ref=src, dst_ref=dst, send_sem=send, recv_sem=recv, device_id=dev, device_id_type=MESH
    )


def nn(a, b):
    return lax.dot_general(a, b, (((1,), (0,)), ((), ())), preferred_element_type=f32)


def nt(a, b):
    return lax.dot_general(a, b, (((1,), (1,)), ((), ())), preferred_element_type=f32)


def tn(a, b):
    return lax.dot_general(a, b, (((0,), (0,)), ((), ())), preferred_element_type=f32)


def rms_scale(v):
    return lax.rsqrt(jnp.mean(v * v, axis=-1, keepdims=True) + norm_eps)


def norm_back(v, u):
    q = rms_scale(v)
    n = v * q
    return q * (u - n * jnp.mean(u * n, axis=-1, keepdims=True))


def sig(v):
    return 1.0 / (1.0 + jnp.exp(-v))


def rows_of(p, n):
    return pl.ds(pl.multiple_of(p * n, n), n)


def entry(dp, s, d, t, core=False):
    barrier = pltpu.get_barrier_semaphore()
    count = 3
    for k in (1, 2, 3):
        pl.semaphore_signal(barrier, inc=1, device_id=(s, d, partner(t, k)), device_id_type=MESH)
    if core:
        pl.semaphore_signal(barrier, inc=1, device_id=(1 - s, d, t), device_id_type=MESH)
        count += 1
    if dp > 1:

        def greet(k, c):
            pl.semaphore_signal(
                barrier, inc=1, device_id=(s, (d + k) % dp, t), device_id_type=MESH
            )
            return c

        lax.fori_loop(1, dp, greet, 0)
        count += dp - 1
    pl.semaphore_wait(barrier, count)


class Gather:
    def __init__(self, block_at, half, ssem, rsem, base, where):
        self.at, self.half, self.ssem, self.rsem, self.base = block_at, half, ssem, rsem, base
        self.where = where

    def copy(self, n, peer, half, to):
        s, d, t = self.where
        ref = self.at(partner(t, peer), half)
        k = self.base + n
        return remote(ref, ref, self.ssem.at[k], self.rsem.at[k], (s, d, partner(t, to)))

    def mine(self, n):
        peer, half, to = ((0, 0, 1), (0, 1, 1), (0, 0, 2), (0, 1, 2), (1, 0, 2), (2, 1, 1))[n]
        return self.copy(n, peer, half, to)

    def arriving(self, n):
        s, d, t = self.where
        peer, half = ((1, 0), (1, 1), (2, 0), (2, 1), (3, 0), (3, 1))[n]
        ref = self.at(partner(t, peer), half)
        k = self.base + n
        return remote(ref, ref, self.ssem.at[k], self.rsem.at[k], (s, d, t))

    def start(self):
        self.mine(0).start()
        self.mine(3).start()
        self.mine(1).start()
        self.mine(2).start()

    def forward(self):
        self.arriving(0).wait_recv()
        self.mine(4).start()
        self.arriving(3).wait_recv()
        self.mine(5).start()

    def ready(self, k):
        if k == 1:
            self.arriving(1).wait_recv()
        elif k == 2:
            self.arriving(2).wait_recv()
        else:
            self.arriving(4).wait_recv()
            self.arriving(5).wait_recv()

    def drain(self):
        for n in range(6):
            self.mine(n).wait_send()


class Scatter:
    def __init__(self, part, got, via, rows, ssem, rsem, base, where):
        self.part, self.got, self.via, self.half = part, got, via, rows // 2
        self.ssem, self.rsem, self.base, self.where = ssem, rsem, base, where

    def copy(self, n):
        s, d, t = self.where
        h = self.half
        h0, h1 = pl.ds(0, h), pl.ds(h, h)
        src, dst, to = (
            (self.part.at[2, h0], self.via.at[0], 2),
            (self.part.at[2, h1], self.via.at[1], 1),
            (self.part.at[0, h1], self.got.at[0, h1], 1),
            (self.part.at[1, h0], self.got.at[1, h0], 2),
            (self.part.at[0, h0], self.got.at[0, h0], 1),
            (self.part.at[1, h1], self.got.at[1, h1], 2),
        )[n]
        k = self.base + n
        return remote(src, dst, self.ssem.at[k], self.rsem.at[k], (s, d, partner(t, to)))

    def put(self, k, value):
        self.part[k - 1] = value.astype(bf16)
        self.send(k)

    def send(self, k):
        if k == 3:
            self.copy(0).start()
            self.copy(1).start()
        elif k == 2:
            self.copy(3).start()
        else:
            self.copy(2).start()

    def combine(self):
        h = self.half
        self.copy(0).wait_recv()
        self.part[0, 0:h] = (self.part[0, 0:h].astype(f32) + self.via[0].astype(f32)).astype(bf16)
        self.copy(4).start()
        self.copy(1).wait_recv()
        self.part[1, h:] = (self.part[1, h:].astype(f32) + self.via[1].astype(f32)).astype(bf16)
        self.copy(5).start()

    def result(self):
        for n in (2, 3, 4, 5):
            self.copy(n).wait_recv()
        return self.got[0].astype(f32) + self.got[1].astype(f32)

    def drain(self):
        for n in range(6):
            self.copy(n).wait_send()


def scalar_table(starts, rates, dp, blocks):
    d = lax.axis_index("dp")
    survive = 1.0 - starts.astype(f32).reshape(dp, blocks)
    decay = jnp.exp(-rates * BLOCK)
    factor = jnp.prod(survive, axis=1)[:, None] * (decay**blocks)[None, :]
    at = jnp.arange(dp)
    low, high = jnp.minimum(at, d), jnp.maximum(at, d)
    between = (at[None, :] > low[:, None]) & (at[None, :] < high[:, None])
    through = jnp.prod(jnp.where(between[:, :, None], factor[None], 1.0), axis=1)
    forward = jnp.where((at < d)[:, None], through, 0.0)
    backward = jnp.where((at > d)[:, None], through, 0.0)
    mine = lax.dynamic_index_in_dim(survive, d, 0, keepdims=False)
    index = jnp.arange(starts.shape[0], dtype=jnp.int32)
    begins = jnp.max(
        jnp.where((index[None, :] <= index[:, None]) & (starts > 0)[None, :], index[None, :], 0), axis=1
    )
    offsets = lax.dynamic_slice_in_dim((index - begins) * BLOCK, d * blocks, blocks).astype(f32)
    return [mine, rates, decay, forward.reshape(-1), backward.reshape(-1), offsets]


def decay_fill(scal, base, nb, mask, mask_t, qd, kd):
    for h in range(HEADS_HERE):
        r = scal[base + nb + h]
        i = lax.broadcasted_iota(jnp.int32, (BLOCK, BLOCK), 0).astype(f32)
        j = lax.broadcasted_iota(jnp.int32, (BLOCK, BLOCK), 1).astype(f32)
        gap = i - j
        mask[h] = jnp.where(gap >= 0.0, jnp.exp(-r * jnp.maximum(gap, 0.0)), 0.0)
        if mask_t is not None:
            mask_t[h] = jnp.where(gap <= 0.0, jnp.exp(-r * jnp.maximum(-gap, 0.0)), 0.0)
        i = lax.broadcasted_iota(jnp.int32, (BLOCK, HEAD), 0).astype(f32)
        qd[h] = jnp.exp(-r * (i + 1.0))
        kd[h] = jnp.exp(-r * (BLOCK - 1.0 - i))


def head(h):
    return slice(h * HEAD, (h + 1) * HEAD)


def send_states(dp, where, zout, zin, zs, zr, later):
    s, d, t = where

    def each(k, c):
        to = d + k if later else d - k

        @pl.when((to < dp) if later else (to >= 0))
        def _():
            remote(zout, zin.at[d], zs.at[k], zr.at[d], (s, to, t)).start()

        return c

    lax.fori_loop(1, dp, each, 0)


def sent_states(dp, where, zout, zin, zs, zr, later):
    s, d, t = where

    def each(k, c):
        to = d + k if later else d - k

        @pl.when((to < dp) if later else (to >= 0))
        def _():
            remote(zout, zin.at[d], zs.at[k], zr.at[d], (s, to, t)).wait_send()

        return c

    lax.fori_loop(1, dp, each, 0)


def take_states(dp, where, zout, zin, zs, zr, later, scal, base, run):
    s, d, t = where
    run[...] = jnp.zeros_like(run)

    def each(k, c):
        @pl.when((k < d) if later else (k > d))
        def _():
            remote(zout, zin.at[k], zs.at[0], zr.at[k], (s, d, t)).wait_recv()
            for h in range(HEADS_HERE):
                run[h] += scal[base + 2 * k + h] * zin[k, h].astype(f32)

        return c

    lax.fori_loop(0, dp, each, 0)


def to_owner(owner, where, src, own_dst, far_dst, lsem, ssem, rsem):
    s, d, t = where

    def far():
        return remote(src, far_dst, ssem, rsem, (1 - s, d, t))

    def local():
        return pltpu.make_async_copy(src, own_dst, lsem)

    def start():
        pl.when(owner)(lambda: local().start())
        pl.when(jnp.logical_not(owner))(lambda: far().start())

    def finish():
        @pl.when(owner)
        def _():
            local().wait()
            far().wait_recv()

        pl.when(jnp.logical_not(owner))(lambda: far().wait_send())

    return start, finish


def forward_kernel(
    dp, tok_in, ct_in, my_wi, my_wo, my_wfi, my_wfo, turn_in, scal,
    both0_o, both1_o, turn_o, gf_o, y_out, *refs,
):
    outs = (refs[0:18], refs[18:36])
    (
        raw, wi2, wo2, wfi2, wfo2, turn, gf, xf, hidden, zq, zk, gate, q, k, v, att, sc, states, branch, mid,
        hid2, pair, mask, qd, kd, loc, zout2, zin2, run, u, y, part, got, via, ssq, own, yb2,
        lsem, ssem, rsem, zs2, zr2, wl, ws, wr,
    ) = refs[36:]
    where = s, d, t = place()
    rows = tok_in.shape[-2]
    total = 4 * rows
    nb = total // BLOCK
    local = Sems(lsem)
    me = rows_of(t, rows)

    def load(src, dst):
        copy = pltpu.make_async_copy(src, dst, local.take())
        copy.start()
        return copy

    got_x = load(tok_in.at[s], xf.at[me])
    got_raw = load(my_wi, raw)
    got_turn = load(turn_in, turn.at[0, pl.ds(0, 8)])
    got_ct = load(ct_in.at[s], gf.at[me])
    ff = my_wfo.shape[0]
    pairs = (
        (wi2.at[s], wi2.at[s]), (my_wo, wo2.at[s, rows_of(t, WIDTH)]),
        (my_wfi, wfi2.at[s, :, pl.ds(0, ff)]), (my_wfo, wfo2.at[s, pl.ds(0, ff)]),
    )

    def mine(n):
        return pltpu.make_async_copy(*pairs[n], wl.at[n])

    def over(n):
        return remote(*pairs[n], ws.at[n], wr.at[n], (1 - s, d, t))

    def await_weight(n, owner):
        if n > 0:
            pl.when(owner)(lambda: mine(n).wait())
        pl.when(jnp.logical_not(owner))(lambda: over(n).wait_recv())

    for n in (1, 2, 3):
        mine(n).start()
    wfi2[:, :, ff:, :] = jnp.zeros_like(wfi2[:, :, ff:, :])
    wfo2[:, ff:, :] = jnp.zeros_like(wfo2[:, ff:, :])
    entry(dp, s, d, t, core=True)
    got_x.wait()
    got_ct.wait()
    half = rows // 2

    def block_of(ref):
        return lambda p, h: ref.at[pl.ds(pl.multiple_of(p * rows + h * half, half), half)]

    gg = Gather(block_of(gf), half, ssem, rsem, 42, where)
    quarter = WIDTH // 2
    gw = Gather(
        lambda p, h: wo2.at[s, pl.ds(pl.multiple_of(p * WIDTH + h * quarter, quarter), quarter)],
        quarter, ws, wr, 4, where,
    )

    def wo_over(k, slot):
        ref = wo2.at[slot, rows_of(partner(t, k), WIDTH)]
        return remote(ref, ref, ws.at[10 + k], wr.at[10 + k], (1 - s, d, t))

    stores, finishes = [], []
    for layer in (0, 1):
        (
            wi_o, wo_o, wfi_o, wfo_o, hidden_o, zq_o, zk_o, gate_o, q_o, k_o, v_o, att_o, sc_o, states_o,
            branch_o, mid_o, hid2_o, pair_o,
        ) = outs[layer]
        wi, wo, wfi, wfo = wi2.at[layer], wo2.at[layer], wfi2.at[layer], wfo2.at[layer]
        zout, zin, zs, zr = zout2.at[layer], zin2.at[layer], zs2.at[layer], zr2.at[layer]
        yb = yb2.at[layer]
        both_o = (both0_o, both1_o)[layer]
        owner = s == layer
        at = layer * (2 * nb + 4 + 4 * dp)
        base = 21 * layer
        gx = Gather(block_of(xf), half, ssem, rsem, base, where)
        gx.start()
        if layer == 0:
            for n in (1, 2, 3):
                over(n).start()
            got_raw.wait()

            def chunk(n, c):
                r = rows_of(n, 128)
                wi2[s, r, :] = raw[r].reshape(128, 4 * WIDTH)
                return c

            lax.fori_loop(0, D // 128, chunk, 0)
            over(0).start()
            got_turn.wait()
            frequency = turn[0, 0:1, :]
            sign = jnp.where(lax.broadcasted_iota(jnp.int32, (1, HEAD), 1) < HEAD // 2, -1.0, 1.0)

            def angles(b, c):
                steps_in = lax.broadcasted_iota(jnp.int32, (BLOCK, HEAD), 0).astype(f32)
                angle = (scal[at + nb + 4 + 4 * dp + b] + steps_in) * frequency
                r = rows_of(b, BLOCK)
                turn[0, r, :] = jnp.cos(angle)
                turn[1, r, :] = sign * jnp.sin(angle)
                return c

            lax.fori_loop(0, nb, angles, 0)
            stores.append(load(turn, turn_o))
        decay_fill(scal, at, nb, mask, None, qd, kd)
        await_weight(0, owner)
        if layer == 1:
            for copy in stores:
                copy.wait()
            stores = []

        def project(i, c):
            for n in (1, 2, 3):

                @pl.when(i == n)
                def _(n=n):
                    if n == 1:
                        gx.forward()

                        @pl.when(owner)
                        def _():
                            mine(1).wait()
                            gw.start()

                    gx.ready(n)

            r = rows_of(partner(t, i), rows)
            xv = xf[r, :].astype(f32)
            hid = (xv * rms_scale(xv)).astype(bf16)
            hidden[r, :] = hid
            cs, sn = turn[0, r, :], turn[1, r, :]
            for n, (pre, post) in enumerate(((zq, q), (zk, k))):
                z = nn(hid, wi[:, n * WIDTH : (n + 1) * WIDTH])
                pre[r, :] = z
                a = z * sig(z)
                for h in range(HEADS_HERE):
                    ah = a[:, head(h)]
                    post[r, head(h)] = (ah * cs + pltpu.roll(ah, HEAD // 2, 1) * sn).astype(bf16)
            v[r, :] = nn(hid, wi[:, 2 * WIDTH : 3 * WIDTH]).astype(bf16)
            gate[r, :] = nn(hid, wi[:, 3 * WIDTH :])
            return c

        lax.fori_loop(0, 4, project, 0)

        stores += [load(hidden, hidden_o), load(zq, zq_o), load(zk, zk_o), load(gate, gate_o)]
        stores += [load(q, q_o), load(k, k_o), load(v, v_o)]

        def local_state(b, c):
            r = rows_of(b, BLOCK)
            for h in range(HEADS_HERE):
                kdec = (k[r, head(h)].astype(f32) * kd[h]).astype(bf16)
                loc[b, h] = tn(kdec, v[r, head(h)])
            return c

        lax.fori_loop(0, nb, local_state, 0)
        pl.when(owner)(gw.forward)
        if layer == 1:
            gg.forward()
        for h in range(HEADS_HERE):
            carried = loc[0, h]
            for b in range(1, nb):
                carried = (scal[at + nb + 2 + h] * scal[at + b]) * carried + loc[b, h]
            zout[h] = carried.astype(bf16)
        send_states(dp, where, zout, zin, zs, zr, True)

        def inner(b, c):
            r = rows_of(b, BLOCK)
            for h in range(HEADS_HERE):
                w = (nt(q[r, head(h)], k[r, head(h)]) * mask[h]).astype(bf16)
                att[r, head(h)] = nn(w, v[r, head(h)])
            return c

        lax.fori_loop(0, nb, inner, 0)
        take_states(dp, where, zout, zin, zs, zr, True, scal, at + nb + 4, run)

        def outer(b, c):
            r = rows_of(b, BLOCK)
            for h in range(HEADS_HERE):
                entering = scal[at + b] * run[h]
                states[b, h] = entering
                run[h] = scal[at + nb + 2 + h] * entering + loc[b, h]
                qdec = (q[r, head(h)].astype(f32) * qd[h]).astype(bf16)
                a = att[r, head(h)] + nn(qdec, entering.astype(bf16))
                att[r, head(h)] = a
                u[t, r, head(h)] = (a * gate[r, head(h)]).astype(bf16)
            return c

        lax.fori_loop(0, nb, outer, 0)

        hu = total // 2
        gu = Gather(lambda p, h: u.at[p, pl.ds(h * hu, hu)], hu, ssem, rsem, base + 6, where)
        gu.start()
        for b in range(nb):
            a = att[b * BLOCK : (b + 1) * BLOCK, :]
            ssq[0, :, b * BLOCK : (b + 1) * BLOCK] = lax.dot_general(
                jnp.ones((8, WIDTH), f32), a * a, (((1,), (1,)), ((), ())),
                preferred_element_type=f32, precision=lax.Precision.HIGHEST,
            )
        sums = [
            remote(
                ssq.at[0], ssq.at[n], ssem.at[base + 11 + n], rsem.at[base + 11 + n], (s, d, partner(t, n))
            )
            for n in (1, 2, 3)
        ]
        for copy in sums:
            copy.start()
        stores += [load(att, att_o), load(states, states_o)]

        @pl.when(owner)
        def _():
            for n in (1, 2, 3):
                gw.ready(n)
                wo_over(n, layer).start()

        @pl.when(jnp.logical_not(owner))
        def _():
            over(1).wait_recv()
            for n in (1, 2, 3):
                wo_over(n, layer).wait_recv()

        y[...] = jnp.zeros_like(y)

        def out_project(i, c):
            for n in (1, 2, 3):

                @pl.when(i == n)
                def _(n=n):
                    if n == 1:
                        gu.forward()
                        gg.mine(layer).start()
                        gg.mine(3 - layer).start()
                    gu.ready(n)

            p = partner(t, i)

            def chunk(m, c):
                r = rows_of(m, rows)
                y[r, :] += nn(u[p, r, :], wo[rows_of(p, WIDTH), :])
                return c

            return lax.fori_loop(0, 4, chunk, c)

        lax.fori_loop(0, 4, out_project, 0)
        for copy in sums:
            copy.wait_recv()
        whole = ssq[0] + ssq[1] + ssq[2] + ssq[3]
        sc[...] = jnp.transpose(lax.rsqrt(whole * (1.0 / D) + norm_eps))
        await_weight(2, owner)
        await_weight(3, owner)
        out = Scatter(part, got, via, rows, ssem, rsem, base + 15, where)

        def feed(i, c):
            e = 3 - i
            r = rows_of(partner(t, e), rows)
            br = sc[r, 0:1] * y[r, :]
            m = xf[r, :].astype(f32) + br
            h2 = (m * rms_scale(m)).astype(bf16)
            hid2[r, :] = h2
            p0, p1 = nt(h2, wfi[0]), nt(h2, wfi[1])
            pair[0, r, :] = p0.astype(bf16)
            pair[1, r, :] = p1.astype(bf16)
            o = nn((p0 * p1).astype(bf16), wfo[...])
            for n in (1, 2, 3):

                @pl.when(e == n)
                def _(n=n):
                    out.put(n, o)

            @pl.when(e == 0)
            def _():
                branch[...] = br.astype(bf16)
                mid[...] = m
                own[...] = o + m

            return c

        lax.fori_loop(0, 4, feed, 0)
        stores += [load(sc, sc_o), load(branch, branch_o), load(mid, mid_o), load(hid2, hid2_o)]
        stores += [load(pair, pair_o), load(wi, wi_o), load(wo, wo_o)]
        stores += [load(wfi, wfi_o), load(wfo, wfo_o)]
        gx.drain()
        gu.drain()
        for copy in sums:
            copy.wait_send()
        out.combine()
        yv = (own[...] + out.result()).astype(bf16)
        yb[...] = yv
        out.drain()
        sent_states(dp, where, zout, zin, zs, zr, True)
        start, finish = to_owner(
            owner, where, yb, both_o.at[s], both_o.at[s], wl.at[4 + layer], ws.at[14 + layer],
            wr.at[14 + layer],
        )
        start()
        finishes.append(finish)
        if layer == 0:
            stores.append(load(yb, y_out))
            xf[me, :] = yv


    for n in (1, 2, 3):
        gg.ready(n)
    stores.append(load(gf, gf_o))
    for n in range(4):
        over(n).wait_send()
    for n in (1, 2, 3):
        wo_over(n, s).wait_send()
    gw.drain()
    gg.drain()
    for finish in finishes:
        finish()
    for copy in stores:
        copy.wait()


def layers_forward(tokens, cotangent, weights, frequency, scal, dp, uid):
    rows = tokens.shape[-2]
    total = 4 * rows
    nb = total // BLOCK
    fp = -(-weights[3].shape[0] // 256) * 256
    saved = [
        ((total, D), bf16), ((total, WIDTH), f32), ((total, WIDTH), f32), ((total, WIDTH), f32),
        ((total, WIDTH), bf16), ((total, WIDTH), bf16), ((total, WIDTH), bf16), ((total, WIDTH), f32),
        ((total, 8), f32), ((nb, HEADS_HERE, HEAD, HEAD), f32), ((rows, D), bf16), ((rows, D), f32),
        ((total, D), bf16), ((2, total, fp), bf16),
    ]
    kept = [((D, 4 * WIDTH), bf16), ((D, D), bf16), ((2, fp, D), bf16), ((fp, D), bf16)]
    scratch = [((D, 4, WIDTH), bf16)] + [((2,) + a, b) for a, b in kept]
    scratch += [((2, total, HEAD), f32), ((total, D), bf16), ((total, D), bf16)] + saved
    scratch += [
        ((HEADS_HERE, BLOCK, BLOCK), f32), ((HEADS_HERE, BLOCK, HEAD), f32),
        ((HEADS_HERE, BLOCK, HEAD), f32), ((nb, HEADS_HERE, HEAD, HEAD), f32),
        ((2, HEADS_HERE, HEAD, HEAD), bf16), ((2, dp, HEADS_HERE, HEAD, HEAD), bf16),
        ((HEADS_HERE, HEAD, HEAD), f32), ((4, total, WIDTH), bf16), ((total, D), f32),
        ((3, rows, D), bf16), ((2, rows, D), bf16), ((2, rows // 2, D), bf16),
        ((4, 8, total), f32), ((rows, D), f32), ((2, rows, D), bf16),
    ]
    both = ((2, rows, D), bf16)
    outs = [both, both, ((2, total, HEAD), f32), ((total, D), bf16), ((rows, D), bf16)]
    outs += (kept + saved) * 2
    dma = pltpu.SemaphoreType.DMA
    flops = 4 * total * D * (4 * WIDTH + D + 3 * fp)
    return pl.pallas_call(
        functools.partial(forward_kernel, dp),
        out_shape=tuple(jax.ShapeDtypeStruct(a, b) for a, b in outs),
        in_specs=[ANY] * 7 + [SMEM],
        out_specs=(ANY,) * len(outs),
        scratch_shapes=[pltpu.VMEM(a, b) for a, b in scratch]
        + [
            dma((48,)), dma((48,)), dma((48,)), dma((2, dp)), dma((2, dp)), dma((6,)), dma((16,)),
            dma((16,)),
        ],
        compiler_params=pltpu.CompilerParams(
            collective_id=uid, has_side_effects=True, vmem_limit_bytes=VMEM_BYTES
        ),
        cost_estimate=pl.CostEstimate(flops=flops, bytes_accessed=60 << 20, transcendentals=0),
        name="layers_forward",
    )(tokens, cotangent, *weights, frequency, scal)


class CorePair:
    def __init__(self, where, halves, from_core, ssem, rsem):
        s, d, t = where
        self.s, self.halves, self.landed = s, halves, from_core
        self.copy = lambda: remote(halves.at[1 - s], from_core, ssem, rsem, (1 - s, d, t))

    def send(self):
        self.copy().start()

    def add(self):
        self.copy().wait()
        rows = self.landed.shape[0]
        step = 128

        def chunk(n, c):
            r = rows_of(n, step)
            mine = self.halves[self.s, r, :].astype(f32)
            self.halves[self.s, r, :] = (mine + self.landed[r, :].astype(f32)).astype(bf16)
            return c

        lax.fori_loop(0, rows // step, chunk, 0)


class LineSum:
    LAG = 2
    END = 5 * LAG

    def __init__(self, dp, where, owner, halves, first, size, land, fin, result, sems, before):
        self.dp, self.where, self.owner, self.before = dp, where, owner, before
        self.halves, self.first, self.size, self.land, self.fin = halves, first, size, land, fin
        self.result = result
        self.recv, self.sent, self.free, self.ol, self.os, self.or_ = sems
        self.age = -1
        s, d, t = where
        low = dp // 2 - 1
        self.upward = d <= low
        self.middle = (d == low) | (d == low + 1)
        self.edge = (d == 0) | (d == dp - 1)
        self.inner = (s, jnp.where(self.upward, d + 1, d - 1), t)
        self.outer = (s, jnp.where(self.upward, d - 1, d + 1), t)
        self.mine = jnp.where(self.upward, 0, 1)

    def own(self, h=None):
        return self.halves.at[self.where[0], self.rows(self.first, h)]

    def rows(self, base, h=None):
        if h is None:
            return pl.ds(base, self.size)
        half = self.size // 2
        return pl.ds(pl.multiple_of(base + h * half, 16), half)

    def final(self, h):
        return self.fin.at[self.rows(self.first, h)]

    def inward(self):
        landing = self.land.at[self.rows(self.first)]
        return remote(self.own(), landing, self.sent.at[0], self.recv.at[2], self.inner)

    def swap_part(self):
        h = 1 - self.mine
        return remote(self.own(h), self.final(h), self.sent.at[0], self.recv.at[h], self.inner)

    def swap_sum(self):
        ref = self.final(self.mine)
        return remote(ref, ref, self.sent.at[1], self.recv.at[self.mine], self.inner)

    def outward(self, h):
        ref = self.final(h)
        return remote(ref, ref, self.sent.at[2 + h], self.recv.at[h], self.outer)

    def sweep(self, base, size, fn):
        unit = 32 if size % 32 == 0 else 16

        def chunk(n, c):
            fn(pl.ds(pl.multiple_of(base + n * unit, 16), unit))
            return c

        lax.fori_loop(0, size // unit, chunk, 0)

    def start(self):
        self.age = 0
        before = self.before
        if before is not None:
            assert before.age >= self.END
            before.close()

            @pl.when(self.middle)
            def _():
                pl.semaphore_signal(
                    self.free, inc=1, device_id=self.inner, device_id_type=MESH
                )

        if self.dp > 2:
            pl.when(self.edge)(lambda: self.inward().start())

    def tick(self):
        self.age += 1
        if self.dp == 1:
            if self.age == self.END:
                self.fin[...] = self.halves[0]
            return
        s = self.where[0]
        inside = jnp.logical_not(self.edge)
        if self.age == self.LAG:

            @pl.when(inside)
            def _():
                self.inward().wait_recv()

                def fn(r):
                    total = self.halves[s, r, :].astype(f32) + self.land[r, :].astype(f32)
                    self.halves[s, r, :] = total.astype(bf16)

                self.sweep(self.first, self.size, fn)
                pl.when(jnp.logical_not(self.middle))(lambda: self.inward().start())

            @pl.when(self.middle)
            def _():
                if self.before is not None:
                    pl.semaphore_wait(self.free, 1)
                self.swap_part().start()

        if self.age == 2 * self.LAG:

            @pl.when(self.middle)
            def _():
                h = self.mine
                half = self.size // 2
                self.arrived(h)

                def fn(r):
                    total = self.halves[s, r, :].astype(f32) + self.fin[r, :].astype(f32)
                    self.fin[r, :] = total.astype(bf16)

                self.sweep(self.first + h * half, half, fn)
                self.swap_sum().start()
                pl.when(inside)(lambda: self.outward(h).start())
                self.swap_part().wait_send()

            pl.when(jnp.logical_not(self.middle))(lambda: self.inward().wait_send())

        if self.age == 3 * self.LAG:

            @pl.when(self.middle)
            def _():
                self.arrived(1 - self.mine)
                pl.when(inside)(lambda: self.outward(1 - self.mine).start())

        if self.age == self.END:

            @pl.when(jnp.logical_not(self.middle))
            def _():
                for h in (0, 1):
                    self.arrived(h)
                    pl.when(inside)(lambda h=h: self.outward(h).start())

            pl.when(self.middle)(lambda: self.swap_sum().wait_send())

            @pl.when(inside)
            def _():
                for h in (0, 1):
                    self.outward(h).wait_send()

            self.to_result()[0]()

    def arrived(self, h):
        ref = self.final(h)
        remote(ref, ref, self.sent.at[0], self.recv.at[h], self.where).wait_recv()

    def to_result(self):
        s = self.where[0]
        part = self.rows(self.first)
        target = self.result.at[s, part]
        return to_owner(
            self.owner, self.where, self.fin.at[part], target, target, self.ol, self.os, self.or_
        )

    def close(self):
        self.to_result()[1]()


class Background:
    def __init__(self):
        self.queue, self.active = [], []

    def put(self, pieces):
        self.queue += pieces

    def tick(self):
        for piece in self.active:
            piece.tick()
        self.active = [piece for piece in self.active if piece.age < piece.END]
        if self.queue:
            piece = self.queue.pop(0)
            piece.start()
            self.active.append(piece)

    def until(self, pieces, age):
        while any(piece.age < age for piece in pieces):
            self.tick()


def backward_kernel(
    dp, gf_in, y0_in, tok_in, turn_in, scal,
    wi0, wo0, wfi0, wfo0, wi1, wo1, wfi1, wfo1, *refs,
):
    saved_i = (refs[0:14], refs[14:28])
    both_o, gwfi_o, gwfo_o, gmix_o = refs[28:32]
    (
        wi, wo, wfi, wfo, turn, gf, xr, hidden, zq, zk, gate, q, k, v, att, sc, states, branch, mid,
        hid2, pair, mask, mask_t, qd, kd, terms, zout, zin, run, gpair, prod, gb, gsend, grecv, dots, gm, dv, dk,
        gp, part, got, via, own, gr, gwfi, gwfo, gmix, c_fi, c_fo, c_mix, l_fi, l_fo, l_mix,
        f_fi, f_fo, f_mix, lsem, ssem, rsem, zs, zr, ol, os, or_, core_s, core_r, ls, lr, free,
    ) = refs[32:]
    where = s, d, t = place()
    rows = y0_in.shape[0]
    total = 4 * rows
    nb = total // BLOCK
    fp = wfo.shape[0]
    half = rows // 2
    table = 2 * nb + 4 + 4 * dp
    local = Sems(lsem)
    me = rows_of(t, rows)
    gated, gatt = slice(0, WIDTH), slice(WIDTH, 2 * WIDTH)

    def gatt_head(h):
        return slice(WIDTH + h * HEAD, WIDTH + (h + 1) * HEAD)

    def load(src, dst):
        copy = pltpu.make_async_copy(src, dst, local.take())
        copy.start()
        return copy

    def block_of(ref):
        return lambda p, h: ref.at[pl.ds(pl.multiple_of(p * rows + h * half, half), half)]

    weights = ((wi0, wo0, wfi0, wfo0), (wi1, wo1, wfi1, wfo1))

    def load_feed(layer):
        keep = saved_i[layer]
        return [
            load(weights[layer][3], wfo), load(keep[13], pair), load(weights[layer][2], wfi),
            load(keep[11], mid), load(keep[12], hid2),
        ]

    def load_gates(layer):
        keep = saved_i[layer]
        return [
            load(weights[layer][1], wo), load(keep[10], branch), load(keep[8], sc), load(keep[7], att),
            load(keep[3], gate),
        ]

    def load_attn(layer):
        keep = saved_i[layer]
        pairs = ((4, q), (5, k), (6, v), (9, states), (1, zq), (2, zk))
        return [load(keep[n], ref) for n, ref in pairs]

    def load_ends(layer):
        x = tok_in.at[s] if layer == 0 else y0_in
        return [load(weights[layer][0], wi), load(saved_i[layer][0], hidden), load(x, xr)]


    ff = l_fo.shape[0]
    pieces, pairs = {}, {}
    for layer in (1, 0):
        cuts = [(gwfo, 256 * n, min(256, ff - 256 * n), l_fo, f_fo, gwfo_o) for n in range(-(-ff // 256))]
        cuts += [(gwfi, 96 * n, min(96, ff - 96 * n), l_fi, f_fi, gwfi_o) for n in range(-(-ff // 96))]
        cuts += [(gmix, 256 * n, 256, l_mix, f_mix, gmix_o) for n in range((D + WIDTH) // 256)]
        made = []
        for n, cut in enumerate(cuts):
            slot = PIECES * layer + n
            sems = [ref.at[slot] for ref in (lr, ls)] + [free.at[n]]
            sems += [ref.at[slot] for ref in (ol, os, or_)]
            before = pieces[1][n] if layer == 0 else None
            made.append(LineSum(dp, where, s == layer, *cut, sems, before))
        pieces[layer] = made
        pairs[layer] = [
            CorePair(where, halves, landed, core_s.at[3 * layer + n], core_r.at[3 * layer + n])
            for n, (halves, landed) in enumerate(((gwfo, c_fo), (gwfi, c_fi), (gmix, c_mix)))
        ]
    n_out, n_feed = -(-ff // 256), -(-ff // 256) + -(-ff // 96)
    work = Background()
    tick = work.tick

    got_g = load(gf_in, gf)
    in_feed, in_tables = load_feed(1), [load(turn_in, turn)]
    in_gates, in_attn, in_ends = load_gates(1), load_attn(1), load_ends(1)
    entry(dp, s, d, t, core=True)
    got_g.wait()
    in_out = []

    for layer in (1, 0):
        offset = table * layer
        pair_fo, pair_fi, pair_mix = pairs[layer]
        base = 30 * layer
        gg = Gather(block_of(gf), half, ssem, rsem, base, where) if layer == 0 else None
        if gg is not None:
            gg.start()
        decay_fill(scal, offset, nb, mask, mask_t, qd, kd)
        tick()
        for copy in in_feed:
            copy.wait()
        sums = Scatter(part, got, via, rows, ssem, rsem, base + 6, where)

        def out_weights(n, c):
            cols = rows_of(n, 256)
            a = prod[:, cols]
            gwfo[0, cols, :] = tn(a, gf[:, : D // 2]).astype(bf16)
            gwfo[1, cols, :] = tn(a, gf[:, D // 2 :]).astype(bf16)
            return c

        if layer == 1:

            def products(i, c):
                r = rows_of(i, rows)
                prod[r, :] = (pair[0, r, :].astype(f32) * pair[1, r, :].astype(f32)).astype(bf16)
                return c

            lax.fori_loop(0, 4, products, 0)
            lax.fori_loop(0, fp // 256, out_weights, 0)
            pair_fo.send()

        def feed(i, c):
            for n in (1, 2, 3) if layer == 1 else ():

                @pl.when(i == n)
                def _(n=n):
                    if n == 1:
                        pair_fo.add()
                        work.put(pieces[layer][:n_out])
                    tick()

            for n in (1, 2, 3) if gg is not None else ():

                @pl.when(i == n)
                def _(n=n):
                    if n == 1:
                        gg.forward()
                    tick()
                    gg.ready(n)

            r = rows_of(partner(t, i), rows)
            grad = nt(gf[r, :], wfo[...])
            p0, p1 = pair[0, r, :].astype(f32), pair[1, r, :].astype(f32)
            if layer == 0:
                prod[r, :] = (p0 * p1).astype(bf16)
            g0, g1 = (grad * p1).astype(bf16), (grad * p0).astype(bf16)
            gpair[0, r, :] = g0
            gpair[1, r, :] = g1
            o = nn(g0, wfi[0]) + nn(g1, wfi[1])
            for n in (1, 2, 3):

                @pl.when(i == n)
                def _(n=n):
                    sums.put(n, o)

            @pl.when(i == 0)
            def _():
                own[...] = o

            return c

        lax.fori_loop(0, 4, feed, 0)
        tick()

        def feed_weights(n, c):
            cols = rows_of(n, 256)
            for part_of in (0, 1):
                gwfi[part_of, cols, :] = tn(gpair[part_of, :, cols], hid2[...]).astype(bf16)
            return c

        if layer == 0:
            work.until(pieces[1][:n_feed], 2 * LineSum.LAG)
            lax.fori_loop(0, fp // 256, out_weights, 0)
            pair_fo.send()
        lax.fori_loop(0, fp // 256, feed_weights, 0)
        pair_fi.send()
        tick()
        sums.combine()
        if layer == 0:
            pair_fo.add()
            work.put(pieces[layer][:n_out])
        tick()
        pair_fi.add()
        work.put(pieces[layer][n_out:n_feed])
        tick()
        grad_middle = gf[me, :].astype(f32) + norm_back(mid[...], own[...] + sums.result())
        gm[...] = grad_middle
        gb[me, :] = grad_middle.astype(bf16)
        tick()
        sums.drain()
        if gg is not None:
            gg.drain()

        for copy in in_gates:
            copy.wait()
        mine = gb[me, :]
        for p in range(4):
            gsend[p] = nt(mine, wo[p * WIDTH : (p + 1) * WIDTH, :]).astype(bf16)
        grecv[t] = gsend[t]
        dots[t, :, 0:rows] = lax.dot_general(
            jnp.ones((8, D), f32), mine.astype(f32) * branch[...].astype(f32), (((1,), (1,)), ((), ())),
            preferred_element_type=f32, precision=lax.Precision.HIGHEST,
        ) * (1.0 / D)

        def turned(k, into):
            dev = (s, d, partner(t, k))
            slot = partner(t, k) if into else t
            n = base + 24 + 2 * k
            return (
                remote(gsend.at[partner(t, k)], grecv.at[slot], ssem.at[n - 2], rsem.at[n - 2], dev),
                remote(dots.at[t], dots.at[slot], ssem.at[n - 1], rsem.at[n - 1], dev),
            )

        for n in (3, 1, 2):
            for copy in turned(n, False):
                copy.start()
        gbg = Gather(block_of(gb), half, ssem, rsem, base + 12, where)
        gbg.start()
        if layer == 1:
            in_feed = load_feed(0)
        tick()

        def gating(i, c):
            for n in (1, 2, 3):

                @pl.when(i == n)
                def _(n=n):
                    for copy in turned(n, True):
                        copy.wait_recv()

            p = partner(t, i)
            r = rows_of(p, rows)
            grad = grecv[p].astype(f32)
            inner_sum = jnp.transpose(dots[p])[0:rows, 0:1]
            scale = sc[r, 0:1]
            normed = att[r, :] * scale
            gt = gate[r, :]
            gp[r, 3 * WIDTH :] = (grad * normed).astype(bf16)
            prod[r, gated] = (normed * gt).astype(bf16)
            prod[r, gatt] = (scale * (grad * gt - normed * inner_sum)).astype(bf16)
            return c

        lax.fori_loop(0, 4, gating, 0)
        tick()
        if layer == 1:
            in_gates = load_gates(0)
        for copy in in_attn:
            copy.wait()
        if layer == 1:
            for copy in in_tables:
                copy.wait()

        def term(b, c):
            r = rows_of(b, BLOCK)
            for h in range(HEADS_HERE):
                qdec = (q[r, head(h)].astype(f32) * qd[h]).astype(bf16)
                terms[b, h] = tn(qdec, prod[r, gatt_head(h)])
            return c

        lax.fori_loop(0, nb, term, 0)
        for h in range(HEADS_HERE):
            carried = scal[offset + nb - 1] * terms[nb - 1, h]
            for b in reversed(range(nb - 1)):
                carried = scal[offset + b] * (terms[b, h] + scal[offset + nb + 2 + h] * carried)
            zout[layer, h] = carried.astype(bf16)
        z_args = (dp, where, zout.at[layer], zin.at[layer], zs.at[layer], zr.at[layer], False)
        send_states(*z_args)
        tick()
        gbg.forward()

        def unturn(pre, grad, r, h):
            back = grad * turn[0, r, :] - pltpu.roll(grad, HEAD // 2, 1) * turn[1, r, :]
            z = pre[r, head(h)]
            g = sig(z)
            return (back * (g * (1.0 + z * (1.0 - g)))).astype(bf16)

        def inner(b, c):
            r = rows_of(b, BLOCK)
            for h in range(HEADS_HERE):
                qh, kh, vh, gh = q[r, head(h)], k[r, head(h)], v[r, head(h)], prod[r, gatt_head(h)]
                w_t = (nt(kh, qh) * mask_t[h]).astype(bf16)
                dv[r, head(h)] = nn(w_t, gh)
                ds = (nt(gh, vh) * mask[h]).astype(bf16)
                ds_t = (nt(vh, gh) * mask_t[h]).astype(bf16)
                dk[r, head(h)] = nn(ds_t, qh)
                dq = nn(ds, kh) + nt(gh, states[b, h].astype(bf16)) * qd[h]
                gp[r, head(h)] = unturn(zq, dq, r, h)
            return c

        lax.fori_loop(0, nb, inner, 0)
        tick()
        take_states(*z_args, scal, offset + nb + 4 + 2 * dp, run)

        def outer(i, c):
            b = nb - 1 - i
            r = rows_of(b, BLOCK)
            for h in range(HEADS_HERE):
                after = run[h]
                low = after.astype(bf16)
                run[h] = scal[offset + b] * (terms[b, h] + scal[offset + nb + 2 + h] * after)
                kdec = (k[r, head(h)].astype(f32) * kd[h]).astype(bf16)
                dkh = dk[r, head(h)] + nt(v[r, head(h)], low) * kd[h]
                k_cols = slice(WIDTH + h * HEAD, WIDTH + (h + 1) * HEAD)
                v_cols = slice(2 * WIDTH + h * HEAD, 2 * WIDTH + (h + 1) * HEAD)
                gp[r, k_cols] = unturn(zk, dkh, r, h)
                gp[r, v_cols] = (dv[r, head(h)] + nn(kdec, low)).astype(bf16)
            return c

        lax.fori_loop(0, nb, outer, 0)
        tick()
        if layer == 1:
            in_attn = load_attn(0)
        for copy in in_ends:
            copy.wait()
        ins = Scatter(part, got, via, rows, ssem, rsem, base + 18, where)

        def back_in(i, c):
            e = 3 - i
            r = rows_of(partner(t, e), rows)
            o = nt(gp[r, :], wi[...])
            for n in (1, 2, 3):

                @pl.when(e == n)
                def _(n=n):
                    ins.put(n, o)

            @pl.when(e == 0)
            def _():
                own[...] = o

            return c

        lax.fori_loop(0, 4, back_in, 0)
        tick()
        if layer == 0:
            work.until(pieces[1], 2 * LineSum.LAG)

        def in_weights(n, c):
            cols = rows_of(n, 256)
            a = hidden[:, cols]
            gmix[0, cols, :] = tn(a, gp[:, : 2 * WIDTH]).astype(bf16)
            gmix[1, cols, :] = tn(a, gp[:, 2 * WIDTH :]).astype(bf16)
            return c

        lax.fori_loop(0, D // 256, in_weights, 0)
        for n in (1, 2, 3):
            gbg.ready(n)
        gmix[0, D:, :] = tn(prod[:, gated], gb[:, : D // 2]).astype(bf16)
        gmix[1, D:, :] = tn(prod[:, gated], gb[:, D // 2 :]).astype(bf16)
        pair_mix.send()
        ins.combine()
        tick()
        pair_mix.add()
        work.put(pieces[layer][n_feed:])
        tick()
        dx = gm[...] + norm_back(xr[...].astype(f32), own[...] + ins.result())
        gr[layer] = dx.astype(bf16)
        ins.drain()
        gbg.drain()
        for n in (1, 2, 3):
            for copy in turned(n, False):
                copy.wait_send()
        sent_states(*z_args)
        start, finish = to_owner(
            s == layer, where, gr.at[layer], both_o.at[s], both_o.at[s],
            ol.at[2 * PIECES + layer], os.at[2 * PIECES + layer], or_.at[2 * PIECES + layer],
        )
        start()
        in_out.append(finish)
        if layer == 1:
            gf[me, :] = gr[layer]
            in_ends = load_ends(0)

    work.until(pieces[0], LineSum.END)
    for piece in pieces[0]:
        piece.close()
    for finish in in_out:
        finish()


def layers_backward(gathered, y0, tokens, turn, scal, weights, saved, dp, ff, uid):
    rows = y0.shape[-2]
    total = 4 * rows
    nb = total // BLOCK
    fp = weights[0][3].shape[0]
    mixed = D + WIDTH
    outs = [
        ((2, rows, D), bf16), ((2, fp, D), bf16), ((2, fp, D // 2), bf16), ((2, mixed, D // 2), bf16)
    ]
    scratch = [
        ((D, 4 * WIDTH), bf16), ((D, D), bf16), ((2, fp, D), bf16), ((fp, D), bf16),
        ((2, total, HEAD), f32), ((total, D), bf16), ((rows, D), bf16),
    ]
    scratch += [(a.shape, a.dtype) for a in saved[0]]
    scratch += [
        ((HEADS_HERE, BLOCK, BLOCK), f32), ((HEADS_HERE, BLOCK, BLOCK), f32),
        ((HEADS_HERE, BLOCK, HEAD), f32), ((HEADS_HERE, BLOCK, HEAD), f32),
        ((nb, HEADS_HERE, HEAD, HEAD), f32), ((2, HEADS_HERE, HEAD, HEAD), bf16),
        ((2, dp, HEADS_HERE, HEAD, HEAD), bf16), ((HEADS_HERE, HEAD, HEAD), f32),
        ((2, total, fp), bf16), ((total, fp), bf16), ((total, D), bf16), ((4, rows, WIDTH), bf16),
        ((4, rows, WIDTH), bf16), ((4, 8, -(-rows // 128) * 128), f32), ((rows, D), f32),
        ((total, WIDTH), f32), ((total, WIDTH), f32),
        ((total, 4 * WIDTH), bf16),
        ((3, rows, D), bf16), ((2, rows, D), bf16), ((2, rows // 2, D), bf16), ((rows, D), f32),
        ((2, rows, D), bf16),
        ((2, fp, D), bf16), ((2, fp, D // 2), bf16), ((2, mixed, D // 2), bf16),
        ((fp, D), bf16), ((fp, D // 2), bf16), ((mixed, D // 2), bf16),
        ((ff, D), bf16), ((ff, D // 2), bf16), ((mixed, D // 2), bf16),
        ((ff, D), bf16), ((ff, D // 2), bf16), ((mixed, D // 2), bf16),
    ]
    count = 2 * PIECES
    dma = pltpu.SemaphoreType.DMA
    flops = 8 * total * D * (4 * WIDTH + WIDTH + 3 * fp)
    flat = [w for layer in weights for w in layer]
    kept = [a for layer in saved for a in layer]
    return pl.pallas_call(
        functools.partial(backward_kernel, dp),
        out_shape=tuple(jax.ShapeDtypeStruct(a, b) for a, b in outs),
        in_specs=[ANY] * 4 + [SMEM] + [ANY] * (len(flat) + len(kept)),
        out_specs=(ANY,) * len(outs),
        scratch_shapes=[pltpu.VMEM(a, b) for a, b in scratch]
        + [
            dma((48,)), dma((60,)), dma((60,)), dma((2, dp)), dma((2, dp)), dma((count + 2,)),
            dma((count + 2,)), dma((count + 2,)), dma((6,)), dma((6,)), dma((count, 4)),
            dma((count, 3)), pltpu.SemaphoreType.REGULAR((PIECES,)),
        ],
        compiler_params=pltpu.CompilerParams(
            collective_id=uid, has_side_effects=True, vmem_limit_bytes=VMEM_BYTES
        ),
        cost_estimate=pl.CostEstimate(flops=flops, bytes_accessed=60 << 20, transcendentals=0),
        name="layers_backward",
    )(gathered, y0, tokens, turn, scal, *flat, *kept)


def widen_kernel(section, fi, fo, mix, mix_out, both0, both1, g_in, g_fi, g_out, g_fo, outputs):
    for n in range(4):
        lanes = slice((n % 2) * WIDTH, (n % 2 + 1) * WIDTH)
        g_in[:, n, :] = mix[n // 2, :, lanes].astype(f32)
    for n in range(2):
        half = slice(n * (D // 2), (n + 1) * (D // 2))
        g_fi[n] = fi[n].astype(f32)
        g_out[:, half] = mix_out[n].astype(f32)
        g_fo[:, half] = fo[n].astype(f32)

    @pl.when(section[0] == 0)
    def _():
        outputs[...] = both0[...]

    @pl.when(section[0] != 0)
    def _():
        outputs[...] = both1[...]


def widen(s, g_fi, g_fo, g_mix, both0, both1, ff):
    cuts = 4
    rows = both0.shape[1]
    n = D // cuts
    ahead = D // (WIDTH // cuts)
    shapes = ((D, 4, WIDTH), (2, ff, D), (WIDTH, D), (ff, D))
    per_row = lambda *shape: pl.BlockSpec(shape, lambda i, _: (i,) + (0,) * (len(shape) - 1))
    halves = lambda *shape: pl.BlockSpec(shape, lambda i, _: (0, i, 0))
    return pl.pallas_call(
        widen_kernel,
        out_shape=tuple(jax.ShapeDtypeStruct(a, f32) for a in shapes)
        + (jax.ShapeDtypeStruct(both0.shape, bf16),),
        grid_spec=pltpu.PrefetchScalarGridSpec(
            num_scalar_prefetch=1,
            grid=(cuts,),
            in_specs=[
                halves(2, ff // cuts, D),
                halves(2, ff // cuts, D // 2),
                halves(2, n, D // 2),
                pl.BlockSpec((2, WIDTH // cuts, D // 2), lambda i, _: (0, ahead + i, 0)),
                halves(2, rows // cuts, D),
                halves(2, rows // cuts, D),
            ],
            out_specs=(
                per_row(n, 4, WIDTH), halves(2, ff // cuts, D), per_row(WIDTH // cuts, D),
                per_row(ff // cuts, D),
                halves(2, rows // cuts, D),
            ),
        ),
        compiler_params=pltpu.CompilerParams(vmem_limit_bytes=VMEM_BYTES),
        cost_estimate=pl.CostEstimate(flops=0, bytes_accessed=24 << 20, transcendentals=0),
        name="widen",
    )(s.reshape(1), g_fi, g_fo, g_mix, g_mix, both0, both1)


def frequencies():
    lane = np.arange(HEAD) % (HEAD // 2)
    row = np.float32(10000.0) ** (-lane.astype(np.float32) / np.float32(HEAD // 2))
    return np.broadcast_to(row.astype(np.float32), (8, HEAD))


def swap(x):
    return lax.ppermute(x, "section", [(0, 1), (1, 0)])


def mine_first(s, a, b):
    return jnp.where(s == 0, a, b)


def shards(tokens, cotangent, mixer_in, mixer_out, feed_in, feed_out, decay_rate, block_starts):
    s = lax.axis_index("section")
    dp = lax.axis_size("dp")
    rows = tokens.shape[1]
    blocks = 4 * rows // BLOCK
    ff = feed_out.shape[1]
    wfi = jnp.transpose(feed_in[0], (1, 2, 0))
    mine = (mixer_in[0], mixer_out[0], wfi, feed_out[0])
    other_rates = swap(decay_rate[0])
    rates = (mine_first(s, decay_rate[0], other_rates), mine_first(s, other_rates, decay_rate[0]))
    starts = lax.dynamic_index_in_dim(block_starts, s, 0, keepdims=False)
    scal = jnp.concatenate([row for r in rates for row in scalar_table(starts, r, dp, blocks)])

    both0, both1, turn, gf, y0, *kept = layers_forward(
        tokens, cotangent, mine, frequencies(), scal, dp, 1
    )
    weights0, saved0, weights1, saved1 = kept[:4], kept[4:18], kept[18:22], kept[22:]
    in_grads, g_fi, g_fo, g_mix = layers_backward(
        gf, y0, tokens, turn, scal, (weights0, weights1),
        (saved0, saved1), dp, ff, 2,
    )
    g_in, g_feed_in, g_out, g_feed_out, outputs = widen(s, g_fi, g_fo, g_mix, both0, both1, ff)
    g_feed_in = jnp.transpose(g_feed_in, (2, 0, 1))
    return outputs[None], in_grads[None], g_in[None], g_out[None], g_feed_in[None], g_feed_out[None]


def solution(mesh):
    placed = (
        P(None, ("dp", "tensor"), None),
        P(None, ("dp", "tensor"), None),
        P("section", None, None, "tensor"),
        P("section", "tensor", None),
        P("section", None, None, "tensor"),
        P("section", "tensor", None),
        P("section", "tensor"),
        P(),
    )
    return jax.shard_map(
        shards,
        mesh=mesh,
        in_specs=placed,
        out_specs=(
            P("section", None, ("dp", "tensor"), None),
            P("section", None, ("dp", "tensor"), None),
            P("section", None, None, "tensor"),
            P("section", "tensor", None),
            P("section", None, None, "tensor"),
            P("section", "tensor", None),
        ),
        check_vma=False,
    )
```

```python
import functools

import jax
import jax.numpy as jnp
import numpy as np
from jax import lax
from jax.experimental import pallas as pl
from jax.experimental.pallas import tpu as pltpu
from jax.sharding import PartitionSpec as P

D = 1024
HEAD = 128
BLOCK = 256
WIDTH = 256
HEADS_HERE = WIDTH // HEAD
norm_eps = 1e-06
MESH = pl.DeviceIdType.MESH
ANY = pl.BlockSpec(memory_space=pl.ANY)
SMEM = pl.BlockSpec(memory_space=pltpu.SMEM)
bf16, f32 = jnp.bfloat16, jnp.float32
PIECES = 16
VMEM_BYTES = 62 * 1024 * 1024


def place():
    return lax.axis_index("section"), lax.axis_index("dp"), lax.axis_index("tensor")


def partner(t, k):
    return ((t // 2 + k // 2) % 2) * 2 + (t + k) % 2


class Sems:
    def __init__(self, ref):
        self.ref, self.used = ref, 0

    def take(self):
        self.used += 1
        return self.ref.at[self.used - 1]


def remote(src, dst, send, recv, dev):
    return pltpu.make_async_remote_copy(
        src_ref=src, dst_ref=dst, send_sem=send, recv_sem=recv, device_id=dev, device_id_type=MESH
    )


def nn(a, b):
    return lax.dot_general(a, b, (((1,), (0,)), ((), ())), preferred_element_type=f32)


def nt(a, b):
    return lax.dot_general(a, b, (((1,), (1,)), ((), ())), preferred_element_type=f32)


def tn(a, b):
    return lax.dot_general(a, b, (((0,), (0,)), ((), ())), preferred_element_type=f32)


def rms_scale(v):
    return lax.rsqrt(jnp.mean(v * v, axis=-1, keepdims=True) + norm_eps)


def norm_back(v, u):
    q = rms_scale(v)
    n = v * q
    return q * (u - n * jnp.mean(u * n, axis=-1, keepdims=True))


def sig(v):
    return 1.0 / (1.0 + jnp.exp(-v))


def rows_of(p, n):
    return pl.ds(pl.multiple_of(p * n, n), n)


def entry(dp, s, d, t, core=False):
    barrier = pltpu.get_barrier_semaphore()
    count = 3
    for k in (1, 2, 3):
        pl.semaphore_signal(barrier, inc=1, device_id=(s, d, partner(t, k)), device_id_type=MESH)
    if core:
        pl.semaphore_signal(barrier, inc=1, device_id=(1 - s, d, t), device_id_type=MESH)
        count += 1
    if dp > 1:

        def greet(k, c):
            pl.semaphore_signal(
                barrier, inc=1, device_id=(s, (d + k) % dp, t), device_id_type=MESH
            )
            return c

        lax.fori_loop(1, dp, greet, 0)
        count += dp - 1
    pl.semaphore_wait(barrier, count)


class Gather:
    def __init__(self, block_at, half, ssem, rsem, base, where):
        self.at, self.half, self.ssem, self.rsem, self.base = block_at, half, ssem, rsem, base
        self.where = where

    def copy(self, n, peer, half, to):
        s, d, t = self.where
        ref = self.at(partner(t, peer), half)
        k = self.base + n
        return remote(ref, ref, self.ssem.at[k], self.rsem.at[k], (s, d, partner(t, to)))

    def mine(self, n):
        peer, half, to = ((0, 0, 1), (0, 1, 1), (0, 0, 2), (0, 1, 2), (1, 0, 2), (2, 1, 1))[n]
        return self.copy(n, peer, half, to)

    def arriving(self, n):
        s, d, t = self.where
        peer, half = ((1, 0), (1, 1), (2, 0), (2, 1), (3, 0), (3, 1))[n]
        ref = self.at(partner(t, peer), half)
        k = self.base + n
        return remote(ref, ref, self.ssem.at[k], self.rsem.at[k], (s, d, t))

    def start(self):
        self.mine(0).start()
        self.mine(3).start()
        self.mine(1).start()
        self.mine(2).start()

    def forward(self):
        self.arriving(0).wait_recv()
        self.mine(4).start()
        self.arriving(3).wait_recv()
        self.mine(5).start()

    def ready(self, k):
        if k == 1:
            self.arriving(1).wait_recv()
        elif k == 2:
            self.arriving(2).wait_recv()
        else:
            self.arriving(4).wait_recv()
            self.arriving(5).wait_recv()

    def drain(self):
        for n in range(6):
            self.mine(n).wait_send()


class Scatter:
    def __init__(self, part, got, via, rows, ssem, rsem, base, where):
        self.part, self.got, self.via, self.half = part, got, via, rows // 2
        self.ssem, self.rsem, self.base, self.where = ssem, rsem, base, where

    def copy(self, n):
        s, d, t = self.where
        h = self.half
        h0, h1 = pl.ds(0, h), pl.ds(h, h)
        src, dst, to = (
            (self.part.at[2, h0], self.via.at[0], 2),
            (self.part.at[2, h1], self.via.at[1], 1),
            (self.part.at[0, h1], self.got.at[0, h1], 1),
            (self.part.at[1, h0], self.got.at[1, h0], 2),
            (self.part.at[0, h0], self.got.at[0, h0], 1),
            (self.part.at[1, h1], self.got.at[1, h1], 2),
        )[n]
        k = self.base + n
        return remote(src, dst, self.ssem.at[k], self.rsem.at[k], (s, d, partner(t, to)))

    def put(self, k, value):
        self.part[k - 1] = value.astype(bf16)
        self.send(k)

    def send(self, k):
        if k == 3:
            self.copy(0).start()
            self.copy(1).start()
        elif k == 2:
            self.copy(3).start()
        else:
            self.copy(2).start()

    def combine(self):
        h = self.half
        self.copy(0).wait_recv()
        self.part[0, 0:h] = (self.part[0, 0:h].astype(f32) + self.via[0].astype(f32)).astype(bf16)
        self.copy(4).start()
        self.copy(1).wait_recv()
        self.part[1, h:] = (self.part[1, h:].astype(f32) + self.via[1].astype(f32)).astype(bf16)
        self.copy(5).start()

    def result(self):
        for n in (2, 3, 4, 5):
            self.copy(n).wait_recv()
        return self.got[0].astype(f32) + self.got[1].astype(f32)

    def drain(self):
        for n in range(6):
            self.copy(n).wait_send()


def scalar_table(starts, rates, dp, blocks):
    d = lax.axis_index("dp")
    survive = 1.0 - starts.astype(f32).reshape(dp, blocks)
    decay = jnp.exp(-rates * BLOCK)
    factor = jnp.prod(survive, axis=1)[:, None] * (decay**blocks)[None, :]
    at = jnp.arange(dp)
    low, high = jnp.minimum(at, d), jnp.maximum(at, d)
    between = (at[None, :] > low[:, None]) & (at[None, :] < high[:, None])
    through = jnp.prod(jnp.where(between[:, :, None], factor[None], 1.0), axis=1)
    forward = jnp.where((at < d)[:, None], through, 0.0)
    backward = jnp.where((at > d)[:, None], through, 0.0)
    mine = lax.dynamic_index_in_dim(survive, d, 0, keepdims=False)
    index = jnp.arange(starts.shape[0], dtype=jnp.int32)
    begins = jnp.max(
        jnp.where((index[None, :] <= index[:, None]) & (starts > 0)[None, :], index[None, :], 0), axis=1
    )
    offsets = lax.dynamic_slice_in_dim((index - begins) * BLOCK, d * blocks, blocks).astype(f32)
    return [mine, rates, decay, forward.reshape(-1), backward.reshape(-1), offsets]


def decay_fill(scal, base, nb, mask, mask_t, qd, kd):
    for h in range(HEADS_HERE):
        r = scal[base + nb + h]
        i = lax.broadcasted_iota(jnp.int32, (BLOCK, BLOCK), 0).astype(f32)
        j = lax.broadcasted_iota(jnp.int32, (BLOCK, BLOCK), 1).astype(f32)
        gap = i - j
        mask[h] = jnp.where(gap >= 0.0, jnp.exp(-r * jnp.maximum(gap, 0.0)), 0.0)
        if mask_t is not None:
            mask_t[h] = jnp.where(gap <= 0.0, jnp.exp(-r * jnp.maximum(-gap, 0.0)), 0.0)
        i = lax.broadcasted_iota(jnp.int32, (BLOCK, HEAD), 0).astype(f32)
        qd[h] = jnp.exp(-r * (i + 1.0))
        kd[h] = jnp.exp(-r * (BLOCK - 1.0 - i))


def head(h):
    return slice(h * HEAD, (h + 1) * HEAD)


def send_states(dp, where, zout, zin, zs, zr, later):
    s, d, t = where

    def each(k, c):
        to = d + k if later else d - k

        @pl.when((to < dp) if later else (to >= 0))
        def _():
            remote(zout, zin.at[d], zs.at[k], zr.at[d], (s, to, t)).start()

        return c

    lax.fori_loop(1, dp, each, 0)


def sent_states(dp, where, zout, zin, zs, zr, later):
    s, d, t = where

    def each(k, c):
        to = d + k if later else d - k

        @pl.when((to < dp) if later else (to >= 0))
        def _():
            remote(zout, zin.at[d], zs.at[k], zr.at[d], (s, to, t)).wait_send()

        return c

    lax.fori_loop(1, dp, each, 0)


def take_states(dp, where, zout, zin, zs, zr, later, scal, base, run):
    s, d, t = where
    run[...] = jnp.zeros_like(run)

    def each(k, c):
        @pl.when((k < d) if later else (k > d))
        def _():
            remote(zout, zin.at[k], zs.at[0], zr.at[k], (s, d, t)).wait_recv()
            for h in range(HEADS_HERE):
                run[h] += scal[base + 2 * k + h] * zin[k, h].astype(f32)

        return c

    lax.fori_loop(0, dp, each, 0)


def to_owner(owner, where, src, own_dst, far_dst, lsem, ssem, rsem):
    s, d, t = where

    def far():
        return remote(src, far_dst, ssem, rsem, (1 - s, d, t))

    def local():
        return pltpu.make_async_copy(src, own_dst, lsem)

    def start():
        pl.when(owner)(lambda: local().start())
        pl.when(jnp.logical_not(owner))(lambda: far().start())

    def finish():
        @pl.when(owner)
        def _():
            local().wait()
            far().wait_recv()

        pl.when(jnp.logical_not(owner))(lambda: far().wait_send())

    return start, finish


def forward_kernel(
    dp, tok_in, ct_in, my_wi, my_wo, my_wfi, my_wfo, scal,
    both0_o, both1_o, turn_o, gf_o, y_out, *refs,
):
    outs = (refs[0:18], refs[18:36])
    (
        raw, wi2, wo2, wfi2, wfo2, turn, gf, xf, hidden, zq, zk, gate, q, k, v, att, sc, states, branch, mid,
        hid2, pair, mask, qd, kd, loc, zout2, zin2, run, u, y, part, got, via, ssq, own, yb2,
        lsem, ssem, rsem, zs2, zr2, wl, ws, wr,
    ) = refs[36:]
    where = s, d, t = place()
    rows = tok_in.shape[-2]
    total = 4 * rows
    nb = total // BLOCK
    local = Sems(lsem)
    me = rows_of(t, rows)

    def load(src, dst):
        copy = pltpu.make_async_copy(src, dst, local.take())
        copy.start()
        return copy

    got_x = load(tok_in.at[s], xf.at[me])
    got_raw = load(my_wi, raw)
    got_ct = load(ct_in.at[s], gf.at[me])
    ff = my_wfo.shape[0]
    pairs = (
        (wi2.at[s], wi2.at[s]), (my_wo, wo2.at[s, rows_of(t, WIDTH)]),
        (my_wfi, wfi2.at[s, :, pl.ds(0, ff)]), (my_wfo, wfo2.at[s, pl.ds(0, ff)]),
    )

    def mine(n):
        return pltpu.make_async_copy(*pairs[n], wl.at[n])

    def over(n):
        return remote(*pairs[n], ws.at[n], wr.at[n], (1 - s, d, t))

    def await_weight(n, owner):
        if n > 0:
            pl.when(owner)(lambda: mine(n).wait())
        pl.when(jnp.logical_not(owner))(lambda: over(n).wait_recv())

    for n in (1, 2, 3):
        mine(n).start()
    wfi2[:, :, ff:, :] = jnp.zeros_like(wfi2[:, :, ff:, :])
    wfo2[:, ff:, :] = jnp.zeros_like(wfo2[:, ff:, :])
    entry(dp, s, d, t, core=True)
    got_x.wait()
    got_ct.wait()
    half = rows // 2

    def block_of(ref):
        return lambda p, h: ref.at[pl.ds(pl.multiple_of(p * rows + h * half, half), half)]

    gg = Gather(block_of(gf), half, ssem, rsem, 42, where)
    quarter = WIDTH // 2
    gw = Gather(
        lambda p, h: wo2.at[s, pl.ds(pl.multiple_of(p * WIDTH + h * quarter, quarter), quarter)],
        quarter, ws, wr, 4, where,
    )

    def wo_over(k, slot):
        ref = wo2.at[slot, rows_of(partner(t, k), WIDTH)]
        return remote(ref, ref, ws.at[10 + k], wr.at[10 + k], (1 - s, d, t))

    stores, finishes = [], []
    for layer in (0, 1):
        (
            wi_o, wo_o, wfi_o, wfo_o, hidden_o, zq_o, zk_o, gate_o, q_o, k_o, v_o, att_o, sc_o, states_o,
            branch_o, mid_o, hid2_o, pair_o,
        ) = outs[layer]
        wi, wo, wfi, wfo = wi2.at[layer], wo2.at[layer], wfi2.at[layer], wfo2.at[layer]
        zout, zin, zs, zr = zout2.at[layer], zin2.at[layer], zs2.at[layer], zr2.at[layer]
        yb = yb2.at[layer]
        both_o = (both0_o, both1_o)[layer]
        owner = s == layer
        at = layer * (2 * nb + 4 + 4 * dp)
        base = 21 * layer
        gx = Gather(block_of(xf), half, ssem, rsem, base, where)
        gx.start()
        if layer == 0:
            for n in (1, 2, 3):
                over(n).start()
            got_raw.wait()

            def chunk(n, c):
                r = rows_of(n, 128)
                wi2[s, r, :] = raw[r].reshape(128, 4 * WIDTH)
                return c

            lax.fori_loop(0, D // 128, chunk, 0)
            over(0).start()
            lane = lax.broadcasted_iota(jnp.int32, (1, HEAD), 1)
            sign = jnp.where(lane < HEAD // 2, -1.0, 1.0)
            frequency = jnp.zeros((1, HEAD), f32)
            for n in range(HEAD // 2):
                value = scal[2 * (2 * nb + 4 + 4 * dp) + n]
                frequency = jnp.where(lax.rem(lane, HEAD // 2) == n, value, frequency)

            def angles(b, c):
                steps_in = lax.broadcasted_iota(jnp.int32, (BLOCK, HEAD), 0).astype(f32)
                angle = (scal[at + nb + 4 + 4 * dp + b] + steps_in) * frequency
                r = rows_of(b, BLOCK)
                turn[0, r, :] = jnp.cos(angle)
                turn[1, r, :] = sign * jnp.sin(angle)
                return c

            lax.fori_loop(0, nb, angles, 0)
            stores.append(load(turn, turn_o))
        decay_fill(scal, at, nb, mask, None, qd, kd)
        await_weight(0, owner)
        if layer == 1:
            for copy in stores:
                copy.wait()
            stores = []

        def project(i, c):
            for n in (1, 2, 3):

                @pl.when(i == n)
                def _(n=n):
                    if n == 1:
                        gx.forward()

                        @pl.when(owner)
                        def _():
                            mine(1).wait()
                            gw.start()

                    gx.ready(n)

            r = rows_of(partner(t, i), rows)
            xv = xf[r, :].astype(f32)
            hid = (xv * rms_scale(xv)).astype(bf16)
            hidden[r, :] = hid
            cs, sn = turn[0, r, :], turn[1, r, :]
            for n, (pre, post) in enumerate(((zq, q), (zk, k))):
                z = nn(hid, wi[:, n * WIDTH : (n + 1) * WIDTH])
                pre[r, :] = z
                a = z * sig(z)
                for h in range(HEADS_HERE):
                    ah = a[:, head(h)]
                    post[r, head(h)] = (ah * cs + pltpu.roll(ah, HEAD // 2, 1) * sn).astype(bf16)
            v[r, :] = nn(hid, wi[:, 2 * WIDTH : 3 * WIDTH]).astype(bf16)
            gate[r, :] = nn(hid, wi[:, 3 * WIDTH :])
            return c

        lax.fori_loop(0, 4, project, 0)

        stores += [load(hidden, hidden_o), load(zq, zq_o), load(zk, zk_o), load(gate, gate_o)]
        stores += [load(q, q_o), load(k, k_o), load(v, v_o)]

        def local_state(b, c):
            r = rows_of(b, BLOCK)
            for h in range(HEADS_HERE):
                kdec = (k[r, head(h)].astype(f32) * kd[h]).astype(bf16)
                loc[b, h] = tn(kdec, v[r, head(h)])
            return c

        lax.fori_loop(0, nb, local_state, 0)
        pl.when(owner)(gw.forward)
        if layer == 1:
            gg.forward()
        for h in range(HEADS_HERE):
            carried = loc[0, h]
            for b in range(1, nb):
                carried = (scal[at + nb + 2 + h] * scal[at + b]) * carried + loc[b, h]
            zout[h] = carried.astype(bf16)
        send_states(dp, where, zout, zin, zs, zr, True)

        def inner(b, c):
            r = rows_of(b, BLOCK)
            for h in range(HEADS_HERE):
                w = (nt(q[r, head(h)], k[r, head(h)]) * mask[h]).astype(bf16)
                att[r, head(h)] = nn(w, v[r, head(h)])
            return c

        lax.fori_loop(0, nb, inner, 0)
        take_states(dp, where, zout, zin, zs, zr, True, scal, at + nb + 4, run)

        def outer(b, c):
            r = rows_of(b, BLOCK)
            for h in range(HEADS_HERE):
                entering = scal[at + b] * run[h]
                states[b, h] = entering
                run[h] = scal[at + nb + 2 + h] * entering + loc[b, h]
                qdec = (q[r, head(h)].astype(f32) * qd[h]).astype(bf16)
                a = att[r, head(h)] + nn(qdec, entering.astype(bf16))
                att[r, head(h)] = a
                u[t, r, head(h)] = (a * gate[r, head(h)]).astype(bf16)
            return c

        lax.fori_loop(0, nb, outer, 0)

        hu = total // 2
        gu = Gather(lambda p, h: u.at[p, pl.ds(h * hu, hu)], hu, ssem, rsem, base + 6, where)
        gu.start()
        for b in range(nb):
            a = att[b * BLOCK : (b + 1) * BLOCK, :]
            ssq[0, :, b * BLOCK : (b + 1) * BLOCK] = lax.dot_general(
                jnp.ones((8, WIDTH), f32), a * a, (((1,), (1,)), ((), ())),
                preferred_element_type=f32, precision=lax.Precision.HIGHEST,
            )
        sums = [
            remote(
                ssq.at[0], ssq.at[n], ssem.at[base + 11 + n], rsem.at[base + 11 + n], (s, d, partner(t, n))
            )
            for n in (1, 2, 3)
        ]
        for copy in sums:
            copy.start()
        stores += [load(att, att_o), load(states, states_o)]

        @pl.when(owner)
        def _():
            for n in (1, 2, 3):
                gw.ready(n)
                wo_over(n, layer).start()

        @pl.when(jnp.logical_not(owner))
        def _():
            over(1).wait_recv()
            for n in (1, 2, 3):
                wo_over(n, layer).wait_recv()

        y[...] = jnp.zeros_like(y)

        def out_project(i, c):
            for n in (1, 2, 3):

                @pl.when(i == n)
                def _(n=n):
                    if n == 1:
                        gu.forward()
                        gg.mine(layer).start()
                        gg.mine(3 - layer).start()
                    gu.ready(n)

            p = partner(t, i)

            def chunk(m, c):
                r = rows_of(m, rows)
                y[r, :] += nn(u[p, r, :], wo[rows_of(p, WIDTH), :])
                return c

            return lax.fori_loop(0, 4, chunk, c)

        lax.fori_loop(0, 4, out_project, 0)
        for copy in sums:
            copy.wait_recv()
        whole = ssq[0] + ssq[1] + ssq[2] + ssq[3]
        sc[...] = jnp.transpose(lax.rsqrt(whole * (1.0 / D) + norm_eps))
        await_weight(2, owner)
        await_weight(3, owner)
        out = Scatter(part, got, via, rows, ssem, rsem, base + 15, where)

        def feed(i, c):
            e = 3 - i
            r = rows_of(partner(t, e), rows)
            br = sc[r, 0:1] * y[r, :]
            m = xf[r, :].astype(f32) + br
            h2 = (m * rms_scale(m)).astype(bf16)
            hid2[r, :] = h2
            p0, p1 = nt(h2, wfi[0]), nt(h2, wfi[1])
            pair[0, r, :] = p0.astype(bf16)
            pair[1, r, :] = p1.astype(bf16)
            o = nn((p0 * p1).astype(bf16), wfo[...])
            for n in (1, 2, 3):

                @pl.when(e == n)
                def _(n=n):
                    out.put(n, o)

            @pl.when(e == 0)
            def _():
                branch[...] = br.astype(bf16)
                mid[...] = m
                own[...] = o + m

            return c

        lax.fori_loop(0, 4, feed, 0)
        stores += [load(sc, sc_o), load(branch, branch_o), load(mid, mid_o), load(hid2, hid2_o)]
        stores += [load(pair, pair_o), load(wi, wi_o), load(wo, wo_o)]
        stores += [load(wfi, wfi_o), load(wfo, wfo_o)]
        gx.drain()
        gu.drain()
        for copy in sums:
            copy.wait_send()
        out.combine()
        yv = (own[...] + out.result()).astype(bf16)
        yb[...] = yv
        out.drain()
        sent_states(dp, where, zout, zin, zs, zr, True)
        start, finish = to_owner(
            owner, where, yb, both_o.at[s], both_o.at[s], wl.at[4 + layer], ws.at[14 + layer],
            wr.at[14 + layer],
        )
        start()
        finishes.append(finish)
        if layer == 0:
            stores.append(load(yb, y_out))
            xf[me, :] = yv


    for n in (1, 2, 3):
        gg.ready(n)
    stores.append(load(gf, gf_o))
    for n in range(4):
        over(n).wait_send()
    for n in (1, 2, 3):
        wo_over(n, s).wait_send()
    gw.drain()
    gg.drain()
    for finish in finishes:
        finish()
    for copy in stores:
        copy.wait()


def layers_forward(tokens, cotangent, weights, scal, dp, uid):
    rows = tokens.shape[-2]
    total = 4 * rows
    nb = total // BLOCK
    fp = -(-weights[3].shape[0] // 256) * 256
    saved = [
        ((total, D), bf16), ((total, WIDTH), f32), ((total, WIDTH), f32), ((total, WIDTH), f32),
        ((total, WIDTH), bf16), ((total, WIDTH), bf16), ((total, WIDTH), bf16), ((total, WIDTH), f32),
        ((total, 8), f32), ((nb, HEADS_HERE, HEAD, HEAD), f32), ((rows, D), bf16), ((rows, D), f32),
        ((total, D), bf16), ((2, total, fp), bf16),
    ]
    kept = [((D, 4 * WIDTH), bf16), ((D, D), bf16), ((2, fp, D), bf16), ((fp, D), bf16)]
    scratch = [((D, 4, WIDTH), bf16)] + [((2,) + a, b) for a, b in kept]
    scratch += [((2, total, HEAD), f32), ((total, D), bf16), ((total, D), bf16)] + saved
    scratch += [
        ((HEADS_HERE, BLOCK, BLOCK), f32), ((HEADS_HERE, BLOCK, HEAD), f32),
        ((HEADS_HERE, BLOCK, HEAD), f32), ((nb, HEADS_HERE, HEAD, HEAD), f32),
        ((2, HEADS_HERE, HEAD, HEAD), bf16), ((2, dp, HEADS_HERE, HEAD, HEAD), bf16),
        ((HEADS_HERE, HEAD, HEAD), f32), ((4, total, WIDTH), bf16), ((total, D), f32),
        ((3, rows, D), bf16), ((2, rows, D), bf16), ((2, rows // 2, D), bf16),
        ((4, 8, total), f32), ((rows, D), f32), ((2, rows, D), bf16),
    ]
    both = ((2, rows, D), bf16)
    outs = [both, both, ((2, total, HEAD), f32), ((total, D), bf16), ((rows, D), bf16)]
    outs += (kept + saved) * 2
    dma = pltpu.SemaphoreType.DMA
    flops = 4 * total * D * (4 * WIDTH + D + 3 * fp)
    return pl.pallas_call(
        functools.partial(forward_kernel, dp),
        out_shape=tuple(jax.ShapeDtypeStruct(a, b) for a, b in outs),
        in_specs=[ANY] * 6 + [SMEM],
        out_specs=(ANY,) * len(outs),
        scratch_shapes=[pltpu.VMEM(a, b) for a, b in scratch]
        + [
            dma((48,)), dma((48,)), dma((48,)), dma((2, dp)), dma((2, dp)), dma((6,)), dma((16,)),
            dma((16,)),
        ],
        compiler_params=pltpu.CompilerParams(
            collective_id=uid, has_side_effects=True, vmem_limit_bytes=VMEM_BYTES
        ),
        cost_estimate=pl.CostEstimate(flops=flops, bytes_accessed=60 << 20, transcendentals=0),
        name="layers_forward",
    )(tokens, cotangent, *weights, scal)


class CorePair:
    def __init__(self, where, halves, from_core, ssem, rsem):
        s, d, t = where
        self.s, self.halves, self.landed = s, halves, from_core
        self.copy = lambda: remote(halves.at[1 - s], from_core, ssem, rsem, (1 - s, d, t))

    def send(self):
        self.copy().start()

    def add(self):
        self.copy().wait()
        rows = self.landed.shape[0]
        step = 128

        def chunk(n, c):
            r = rows_of(n, step)
            mine = self.halves[self.s, r, :].astype(f32)
            self.halves[self.s, r, :] = (mine + self.landed[r, :].astype(f32)).astype(bf16)
            return c

        lax.fori_loop(0, rows // step, chunk, 0)


class LineSum:
    LAG = 2
    END = 5 * LAG

    def __init__(self, dp, where, owner, halves, first, size, land, fin, result, sems, before):
        self.dp, self.where, self.owner, self.before = dp, where, owner, before
        self.halves, self.first, self.size, self.land, self.fin = halves, first, size, land, fin
        self.result = result
        self.recv, self.sent, self.free, self.ol, self.os, self.or_ = sems
        self.age = -1
        s, d, t = where
        low = dp // 2 - 1
        self.upward = d <= low
        self.middle = (d == low) | (d == low + 1)
        self.edge = (d == 0) | (d == dp - 1)
        self.inner = (s, jnp.where(self.upward, d + 1, d - 1), t)
        self.outer = (s, jnp.where(self.upward, d - 1, d + 1), t)
        self.mine = jnp.where(self.upward, 0, 1)

    def own(self, h=None):
        return self.halves.at[self.where[0], self.rows(self.first, h)]

    def rows(self, base, h=None):
        if h is None:
            return pl.ds(base, self.size)
        half = self.size // 2
        return pl.ds(pl.multiple_of(base + h * half, 16), half)

    def final(self, h):
        return self.fin.at[self.rows(self.first, h)]

    def inward(self):
        landing = self.land.at[self.rows(self.first)]
        return remote(self.own(), landing, self.sent.at[0], self.recv.at[2], self.inner)

    def swap_part(self):
        h = 1 - self.mine
        return remote(self.own(h), self.final(h), self.sent.at[0], self.recv.at[h], self.inner)

    def swap_sum(self):
        ref = self.final(self.mine)
        return remote(ref, ref, self.sent.at[1], self.recv.at[self.mine], self.inner)

    def outward(self, h):
        ref = self.final(h)
        return remote(ref, ref, self.sent.at[2 + h], self.recv.at[h], self.outer)

    def sweep(self, base, size, fn):
        unit = 32 if size % 32 == 0 else 16

        def chunk(n, c):
            fn(pl.ds(pl.multiple_of(base + n * unit, 16), unit))
            return c

        lax.fori_loop(0, size // unit, chunk, 0)

    def start(self):
        self.age = 0
        before = self.before
        if before is not None:
            assert before.age >= self.END
            before.close()

            @pl.when(self.middle)
            def _():
                pl.semaphore_signal(
                    self.free, inc=1, device_id=self.inner, device_id_type=MESH
                )

        if self.dp > 2:
            pl.when(self.edge)(lambda: self.inward().start())

    def tick(self):
        self.age += 1
        if self.dp == 1:
            if self.age == self.END:
                self.fin[...] = self.halves[0]
            return
        s = self.where[0]
        inside = jnp.logical_not(self.edge)
        if self.age == self.LAG:

            @pl.when(inside)
            def _():
                self.inward().wait_recv()

                def fn(r):
                    total = self.halves[s, r, :].astype(f32) + self.land[r, :].astype(f32)
                    self.halves[s, r, :] = total.astype(bf16)

                self.sweep(self.first, self.size, fn)
                pl.when(jnp.logical_not(self.middle))(lambda: self.inward().start())

            @pl.when(self.middle)
            def _():
                if self.before is not None:
                    pl.semaphore_wait(self.free, 1)
                self.swap_part().start()

        if self.age == 2 * self.LAG:

            @pl.when(self.middle)
            def _():
                h = self.mine
                half = self.size // 2
                self.arrived(h)

                def fn(r):
                    total = self.halves[s, r, :].astype(f32) + self.fin[r, :].astype(f32)
                    self.fin[r, :] = total.astype(bf16)

                self.sweep(self.first + h * half, half, fn)
                self.swap_sum().start()
                pl.when(inside)(lambda: self.outward(h).start())
                self.swap_part().wait_send()

            pl.when(jnp.logical_not(self.middle))(lambda: self.inward().wait_send())

        if self.age == 3 * self.LAG:

            @pl.when(self.middle)
            def _():
                self.arrived(1 - self.mine)
                pl.when(inside)(lambda: self.outward(1 - self.mine).start())

        if self.age == self.END:

            @pl.when(jnp.logical_not(self.middle))
            def _():
                for h in (0, 1):
                    self.arrived(h)
                    pl.when(inside)(lambda h=h: self.outward(h).start())

            pl.when(self.middle)(lambda: self.swap_sum().wait_send())

            @pl.when(inside)
            def _():
                for h in (0, 1):
                    self.outward(h).wait_send()

            self.to_result()[0]()

    def arrived(self, h):
        ref = self.final(h)
        remote(ref, ref, self.sent.at[0], self.recv.at[h], self.where).wait_recv()

    def to_result(self):
        s = self.where[0]
        part = self.rows(self.first)
        target = self.result.at[s, part]
        return to_owner(
            self.owner, self.where, self.fin.at[part], target, target, self.ol, self.os, self.or_
        )

    def close(self):
        self.to_result()[1]()


class Background:
    def __init__(self):
        self.queue, self.active = [], []

    def put(self, pieces):
        self.queue += pieces

    def tick(self):
        for piece in self.active:
            piece.tick()
        self.active = [piece for piece in self.active if piece.age < piece.END]
        if self.queue:
            piece = self.queue.pop(0)
            piece.start()
            self.active.append(piece)

    def until(self, pieces, age):
        while any(piece.age < age for piece in pieces):
            self.tick()


def backward_kernel(
    dp, gf_in, y0_in, tok_in, turn_in, scal,
    wi0, wo0, wfi0, wfo0, wi1, wo1, wfi1, wfo1, *refs,
):
    saved_i = (refs[0:14], refs[14:28])
    both_o, gwfi_o, gwfo_o, gmix_o = refs[28:32]
    (
        wi, wo, wfi, wfo, turn, gf, xr, hidden, zq, zk, gate, q, k, v, att, sc, states, branch, mid,
        hid2, pair, mask, mask_t, qd, kd, terms, zout, zin, run, gpair, prod, gb, gsend, grecv, dots, gm, dv, dk,
        gp, part, got, via, own, gr, gwfi, gwfo, gmix, c_fi, c_fo, c_mix, l_fi, l_fo, l_mix,
        f_fi, f_fo, f_mix, lsem, ssem, rsem, zs, zr, ol, os, or_, core_s, core_r, ls, lr, free,
    ) = refs[32:]
    where = s, d, t = place()
    rows = y0_in.shape[0]
    total = 4 * rows
    nb = total // BLOCK
    fp = wfo.shape[0]
    half = rows // 2
    table = 2 * nb + 4 + 4 * dp
    local = Sems(lsem)
    me = rows_of(t, rows)
    gated, gatt = slice(0, WIDTH), slice(WIDTH, 2 * WIDTH)

    def gatt_head(h):
        return slice(WIDTH + h * HEAD, WIDTH + (h + 1) * HEAD)

    def load(src, dst):
        copy = pltpu.make_async_copy(src, dst, local.take())
        copy.start()
        return copy

    def block_of(ref):
        return lambda p, h: ref.at[pl.ds(pl.multiple_of(p * rows + h * half, half), half)]

    weights = ((wi0, wo0, wfi0, wfo0), (wi1, wo1, wfi1, wfo1))

    def load_feed(layer):
        keep = saved_i[layer]
        return [
            load(weights[layer][3], wfo), load(keep[13], pair), load(weights[layer][2], wfi),
            load(keep[11], mid), load(keep[12], hid2),
        ]

    def load_gates(layer):
        keep = saved_i[layer]
        return [
            load(weights[layer][1], wo), load(keep[10], branch), load(keep[8], sc), load(keep[7], att),
            load(keep[3], gate),
        ]

    def load_attn(layer):
        keep = saved_i[layer]
        pairs = ((4, q), (5, k), (6, v), (9, states), (1, zq), (2, zk))
        return [load(keep[n], ref) for n, ref in pairs]

    def load_ends(layer):
        x = tok_in.at[s] if layer == 0 else y0_in
        return [load(weights[layer][0], wi), load(saved_i[layer][0], hidden), load(x, xr)]


    ff = l_fo.shape[0]
    pieces, pairs = {}, {}
    for layer in (1, 0):
        cuts = [(gwfo, 256 * n, min(256, ff - 256 * n), l_fo, f_fo, gwfo_o) for n in range(-(-ff // 256))]
        cuts += [(gwfi, 96 * n, min(96, ff - 96 * n), l_fi, f_fi, gwfi_o) for n in range(-(-ff // 96))]
        cuts += [(gmix, 256 * n, 256, l_mix, f_mix, gmix_o) for n in range((D + WIDTH) // 256)]
        made = []
        for n, cut in enumerate(cuts):
            slot = PIECES * layer + n
            sems = [ref.at[slot] for ref in (lr, ls)] + [free.at[n]]
            sems += [ref.at[slot] for ref in (ol, os, or_)]
            before = pieces[1][n] if layer == 0 else None
            made.append(LineSum(dp, where, s == layer, *cut, sems, before))
        pieces[layer] = made
        pairs[layer] = [
            CorePair(where, halves, landed, core_s.at[3 * layer + n], core_r.at[3 * layer + n])
            for n, (halves, landed) in enumerate(((gwfo, c_fo), (gwfi, c_fi), (gmix, c_mix)))
        ]
    n_out, n_feed = -(-ff // 256), -(-ff // 256) + -(-ff // 96)
    work = Background()
    tick = work.tick

    got_g = load(gf_in, gf)
    in_feed, in_tables = load_feed(1), [load(turn_in, turn)]
    in_gates, in_attn, in_ends = load_gates(1), load_attn(1), load_ends(1)
    entry(dp, s, d, t, core=True)
    got_g.wait()
    in_out = []

    for layer in (1, 0):
        offset = table * layer
        pair_fo, pair_fi, pair_mix = pairs[layer]
        base = 30 * layer
        gg = Gather(block_of(gf), half, ssem, rsem, base, where) if layer == 0 else None
        if gg is not None:
            gg.start()
        decay_fill(scal, offset, nb, mask, mask_t, qd, kd)
        tick()
        for copy in in_feed:
            copy.wait()
        sums = Scatter(part, got, via, rows, ssem, rsem, base + 6, where)

        def out_weights(n, c):
            cols = rows_of(n, 256)
            a = prod[:, cols]
            gwfo[0, cols, :] = tn(a, gf[:, : D // 2]).astype(bf16)
            gwfo[1, cols, :] = tn(a, gf[:, D // 2 :]).astype(bf16)
            return c

        if layer == 1:

            def products(i, c):
                r = rows_of(i, rows)
                prod[r, :] = (pair[0, r, :].astype(f32) * pair[1, r, :].astype(f32)).astype(bf16)
                return c

            lax.fori_loop(0, 4, products, 0)
            lax.fori_loop(0, fp // 256, out_weights, 0)
            pair_fo.send()

        def feed(i, c):
            for n in (1, 2, 3) if layer == 1 else ():

                @pl.when(i == n)
                def _(n=n):
                    if n == 1:
                        pair_fo.add()
                        work.put(pieces[layer][:n_out])
                    tick()

            for n in (1, 2, 3) if gg is not None else ():

                @pl.when(i == n)
                def _(n=n):
                    if n == 1:
                        gg.forward()
                    tick()
                    gg.ready(n)

            r = rows_of(partner(t, i), rows)
            grad = nt(gf[r, :], wfo[...])
            p0, p1 = pair[0, r, :].astype(f32), pair[1, r, :].astype(f32)
            if layer == 0:
                prod[r, :] = (p0 * p1).astype(bf16)
            g0, g1 = (grad * p1).astype(bf16), (grad * p0).astype(bf16)
            gpair[0, r, :] = g0
            gpair[1, r, :] = g1
            o = nn(g0, wfi[0]) + nn(g1, wfi[1])
            for n in (1, 2, 3):

                @pl.when(i == n)
                def _(n=n):
                    sums.put(n, o)

            @pl.when(i == 0)
            def _():
                own[...] = o

            return c

        lax.fori_loop(0, 4, feed, 0)
        tick()

        def feed_weights(n, c):
            cols = rows_of(n, 256)
            for part_of in (0, 1):
                gwfi[part_of, cols, :] = tn(gpair[part_of, :, cols], hid2[...]).astype(bf16)
            return c

        if layer == 0:
            work.until(pieces[1][:n_feed], 2 * LineSum.LAG)
            lax.fori_loop(0, fp // 256, out_weights, 0)
            pair_fo.send()
        lax.fori_loop(0, fp // 256, feed_weights, 0)
        pair_fi.send()
        tick()
        sums.combine()
        if layer == 0:
            pair_fo.add()
            work.put(pieces[layer][:n_out])
        tick()
        pair_fi.add()
        work.put(pieces[layer][n_out:n_feed])
        tick()
        grad_middle = gf[me, :].astype(f32) + norm_back(mid[...], own[...] + sums.result())
        gm[...] = grad_middle
        gb[me, :] = grad_middle.astype(bf16)
        tick()
        sums.drain()
        if gg is not None:
            gg.drain()

        for copy in in_gates:
            copy.wait()
        mine = gb[me, :]
        for p in range(4):
            gsend[p] = nt(mine, wo[p * WIDTH : (p + 1) * WIDTH, :]).astype(bf16)
        grecv[t] = gsend[t]
        dots[t, :, 0:rows] = lax.dot_general(
            jnp.ones((8, D), f32), mine.astype(f32) * branch[...].astype(f32), (((1,), (1,)), ((), ())),
            preferred_element_type=f32, precision=lax.Precision.HIGHEST,
        ) * (1.0 / D)

        def turned(k, into):
            dev = (s, d, partner(t, k))
            slot = partner(t, k) if into else t
            n = base + 24 + 2 * k
            return (
                remote(gsend.at[partner(t, k)], grecv.at[slot], ssem.at[n - 2], rsem.at[n - 2], dev),
                remote(dots.at[t], dots.at[slot], ssem.at[n - 1], rsem.at[n - 1], dev),
            )

        for n in (3, 1, 2):
            for copy in turned(n, False):
                copy.start()
        gbg = Gather(block_of(gb), half, ssem, rsem, base + 12, where)
        gbg.start()
        if layer == 1:
            in_feed = load_feed(0)
        tick()

        def gating(i, c):
            for n in (1, 2, 3):

                @pl.when(i == n)
                def _(n=n):
                    for copy in turned(n, True):
                        copy.wait_recv()

            p = partner(t, i)
            r = rows_of(p, rows)
            grad = grecv[p].astype(f32)
            inner_sum = jnp.transpose(dots[p])[0:rows, 0:1]
            scale = sc[r, 0:1]
            normed = att[r, :] * scale
            gt = gate[r, :]
            gp[r, 3 * WIDTH :] = (grad * normed).astype(bf16)
            prod[r, gated] = (normed * gt).astype(bf16)
            prod[r, gatt] = (scale * (grad * gt - normed * inner_sum)).astype(bf16)
            return c

        lax.fori_loop(0, 4, gating, 0)
        tick()
        if layer == 1:
            in_gates = load_gates(0)
        for copy in in_attn:
            copy.wait()
        if layer == 1:
            for copy in in_tables:
                copy.wait()

        def term(b, c):
            r = rows_of(b, BLOCK)
            for h in range(HEADS_HERE):
                qdec = (q[r, head(h)].astype(f32) * qd[h]).astype(bf16)
                terms[b, h] = tn(qdec, prod[r, gatt_head(h)])
            return c

        lax.fori_loop(0, nb, term, 0)
        for h in range(HEADS_HERE):
            carried = scal[offset + nb - 1] * terms[nb - 1, h]
            for b in reversed(range(nb - 1)):
                carried = scal[offset + b] * (terms[b, h] + scal[offset + nb + 2 + h] * carried)
            zout[layer, h] = carried.astype(bf16)
        z_args = (dp, where, zout.at[layer], zin.at[layer], zs.at[layer], zr.at[layer], False)
        send_states(*z_args)
        tick()
        gbg.forward()

        def unturn(pre, grad, r, h):
            back = grad * turn[0, r, :] - pltpu.roll(grad, HEAD // 2, 1) * turn[1, r, :]
            z = pre[r, head(h)]
            g = sig(z)
            return (back * (g * (1.0 + z * (1.0 - g)))).astype(bf16)

        def inner(b, c):
            r = rows_of(b, BLOCK)
            for h in range(HEADS_HERE):
                qh, kh, vh, gh = q[r, head(h)], k[r, head(h)], v[r, head(h)], prod[r, gatt_head(h)]
                w_t = (nt(kh, qh) * mask_t[h]).astype(bf16)
                dv[r, head(h)] = nn(w_t, gh)
                ds = (nt(gh, vh) * mask[h]).astype(bf16)
                ds_t = (nt(vh, gh) * mask_t[h]).astype(bf16)
                dk[r, head(h)] = nn(ds_t, qh)
                dq = nn(ds, kh) + nt(gh, states[b, h].astype(bf16)) * qd[h]
                gp[r, head(h)] = unturn(zq, dq, r, h)
            return c

        lax.fori_loop(0, nb, inner, 0)
        tick()
        take_states(*z_args, scal, offset + nb + 4 + 2 * dp, run)

        def outer(i, c):
            b = nb - 1 - i
            r = rows_of(b, BLOCK)
            for h in range(HEADS_HERE):
                after = run[h]
                low = after.astype(bf16)
                run[h] = scal[offset + b] * (terms[b, h] + scal[offset + nb + 2 + h] * after)
                kdec = (k[r, head(h)].astype(f32) * kd[h]).astype(bf16)
                dkh = dk[r, head(h)] + nt(v[r, head(h)], low) * kd[h]
                k_cols = slice(WIDTH + h * HEAD, WIDTH + (h + 1) * HEAD)
                v_cols = slice(2 * WIDTH + h * HEAD, 2 * WIDTH + (h + 1) * HEAD)
                gp[r, k_cols] = unturn(zk, dkh, r, h)
                gp[r, v_cols] = (dv[r, head(h)] + nn(kdec, low)).astype(bf16)
            return c

        lax.fori_loop(0, nb, outer, 0)
        tick()
        if layer == 1:
            in_attn = load_attn(0)
        for copy in in_ends:
            copy.wait()
        ins = Scatter(part, got, via, rows, ssem, rsem, base + 18, where)

        def back_in(i, c):
            e = 3 - i
            r = rows_of(partner(t, e), rows)
            o = nt(gp[r, :], wi[...])
            for n in (1, 2, 3):

                @pl.when(e == n)
                def _(n=n):
                    ins.put(n, o)

            @pl.when(e == 0)
            def _():
                own[...] = o

            return c

        lax.fori_loop(0, 4, back_in, 0)
        tick()
        if layer == 0:
            work.until(pieces[1], 2 * LineSum.LAG)

        def in_weights(n, c):
            cols = rows_of(n, 256)
            a = hidden[:, cols]
            gmix[0, cols, :] = tn(a, gp[:, : 2 * WIDTH]).astype(bf16)
            gmix[1, cols, :] = tn(a, gp[:, 2 * WIDTH :]).astype(bf16)
            return c

        lax.fori_loop(0, D // 256, in_weights, 0)
        for n in (1, 2, 3):
            gbg.ready(n)
        gmix[0, D:, :] = tn(prod[:, gated], gb[:, : D // 2]).astype(bf16)
        gmix[1, D:, :] = tn(prod[:, gated], gb[:, D // 2 :]).astype(bf16)
        pair_mix.send()
        ins.combine()
        tick()
        pair_mix.add()
        work.put(pieces[layer][n_feed:])
        tick()
        dx = gm[...] + norm_back(xr[...].astype(f32), own[...] + ins.result())
        gr[layer] = dx.astype(bf16)
        ins.drain()
        gbg.drain()
        for n in (1, 2, 3):
            for copy in turned(n, False):
                copy.wait_send()
        sent_states(*z_args)
        start, finish = to_owner(
            s == layer, where, gr.at[layer], both_o.at[s], both_o.at[s],
            ol.at[2 * PIECES + layer], os.at[2 * PIECES + layer], or_.at[2 * PIECES + layer],
        )
        start()
        in_out.append(finish)
        if layer == 1:
            gf[me, :] = gr[layer]
            in_ends = load_ends(0)

    work.until(pieces[0], LineSum.END)
    for piece in pieces[0]:
        piece.close()
    for finish in in_out:
        finish()


def layers_backward(gathered, y0, tokens, turn, scal, weights, saved, dp, ff, uid):
    rows = y0.shape[-2]
    total = 4 * rows
    nb = total // BLOCK
    fp = weights[0][3].shape[0]
    mixed = D + WIDTH
    outs = [
        ((2, rows, D), bf16), ((2, fp, D), bf16), ((2, fp, D // 2), bf16), ((2, mixed, D // 2), bf16)
    ]
    scratch = [
        ((D, 4 * WIDTH), bf16), ((D, D), bf16), ((2, fp, D), bf16), ((fp, D), bf16),
        ((2, total, HEAD), f32), ((total, D), bf16), ((rows, D), bf16),
    ]
    scratch += [(a.shape, a.dtype) for a in saved[0]]
    scratch += [
        ((HEADS_HERE, BLOCK, BLOCK), f32), ((HEADS_HERE, BLOCK, BLOCK), f32),
        ((HEADS_HERE, BLOCK, HEAD), f32), ((HEADS_HERE, BLOCK, HEAD), f32),
        ((nb, HEADS_HERE, HEAD, HEAD), f32), ((2, HEADS_HERE, HEAD, HEAD), bf16),
        ((2, dp, HEADS_HERE, HEAD, HEAD), bf16), ((HEADS_HERE, HEAD, HEAD), f32),
        ((2, total, fp), bf16), ((total, fp), bf16), ((total, D), bf16), ((4, rows, WIDTH), bf16),
        ((4, rows, WIDTH), bf16), ((4, 8, -(-rows // 128) * 128), f32), ((rows, D), f32),
        ((total, WIDTH), f32), ((total, WIDTH), f32),
        ((total, 4 * WIDTH), bf16),
        ((3, rows, D), bf16), ((2, rows, D), bf16), ((2, rows // 2, D), bf16), ((rows, D), f32),
        ((2, rows, D), bf16),
        ((2, fp, D), bf16), ((2, fp, D // 2), bf16), ((2, mixed, D // 2), bf16),
        ((fp, D), bf16), ((fp, D // 2), bf16), ((mixed, D // 2), bf16),
        ((ff, D), bf16), ((ff, D // 2), bf16), ((mixed, D // 2), bf16),
        ((ff, D), bf16), ((ff, D // 2), bf16), ((mixed, D // 2), bf16),
    ]
    count = 2 * PIECES
    dma = pltpu.SemaphoreType.DMA
    flops = 8 * total * D * (4 * WIDTH + WIDTH + 3 * fp)
    flat = [w for layer in weights for w in layer]
    kept = [a for layer in saved for a in layer]
    return pl.pallas_call(
        functools.partial(backward_kernel, dp),
        out_shape=tuple(jax.ShapeDtypeStruct(a, b) for a, b in outs),
        in_specs=[ANY] * 4 + [SMEM] + [ANY] * (len(flat) + len(kept)),
        out_specs=(ANY,) * len(outs),
        scratch_shapes=[pltpu.VMEM(a, b) for a, b in scratch]
        + [
            dma((48,)), dma((60,)), dma((60,)), dma((2, dp)), dma((2, dp)), dma((count + 2,)),
            dma((count + 2,)), dma((count + 2,)), dma((6,)), dma((6,)), dma((count, 4)),
            dma((count, 3)), pltpu.SemaphoreType.REGULAR((PIECES,)),
        ],
        compiler_params=pltpu.CompilerParams(
            collective_id=uid, has_side_effects=True, vmem_limit_bytes=VMEM_BYTES
        ),
        cost_estimate=pl.CostEstimate(flops=flops, bytes_accessed=60 << 20, transcendentals=0),
        name="layers_backward",
    )(gathered, y0, tokens, turn, scal, *flat, *kept)


def widen_kernel(section, fi, fo, mix, mix_out, both0, both1, g_in, g_fi, g_out, g_fo, outputs):
    for n in range(4):
        lanes = slice((n % 2) * WIDTH, (n % 2 + 1) * WIDTH)
        g_in[:, n, :] = mix[n // 2, :, lanes].astype(f32)
    for n in range(2):
        half = slice(n * (D // 2), (n + 1) * (D // 2))
        g_fi[n] = fi[n].astype(f32)
        g_out[:, half] = mix_out[n].astype(f32)
        g_fo[:, half] = fo[n].astype(f32)

    @pl.when(section[0] == 0)
    def _():
        outputs[...] = both0[...]

    @pl.when(section[0] != 0)
    def _():
        outputs[...] = both1[...]


def widen(s, g_fi, g_fo, g_mix, both0, both1, ff):
    cuts = 2
    rows = both0.shape[1]
    n = D // cuts
    ahead = D // (WIDTH // cuts)
    shapes = ((D, 4, WIDTH), (2, ff, D), (WIDTH, D), (ff, D))
    per_row = lambda *shape: pl.BlockSpec(shape, lambda i, _: (i,) + (0,) * (len(shape) - 1))
    halves = lambda *shape: pl.BlockSpec(shape, lambda i, _: (0, i, 0))
    return pl.pallas_call(
        widen_kernel,
        out_shape=tuple(jax.ShapeDtypeStruct(a, f32) for a in shapes)
        + (jax.ShapeDtypeStruct(both0.shape, bf16),),
        grid_spec=pltpu.PrefetchScalarGridSpec(
            num_scalar_prefetch=1,
            grid=(cuts,),
            in_specs=[
                halves(2, ff // cuts, D),
                halves(2, ff // cuts, D // 2),
                halves(2, n, D // 2),
                pl.BlockSpec((2, WIDTH // cuts, D // 2), lambda i, _: (0, ahead + i, 0)),
                halves(2, rows // cuts, D),
                halves(2, rows // cuts, D),
            ],
            out_specs=(
                per_row(n, 4, WIDTH), halves(2, ff // cuts, D), per_row(WIDTH // cuts, D),
                per_row(ff // cuts, D),
                halves(2, rows // cuts, D),
            ),
        ),
        compiler_params=pltpu.CompilerParams(vmem_limit_bytes=VMEM_BYTES),
        cost_estimate=pl.CostEstimate(flops=0, bytes_accessed=24 << 20, transcendentals=0),
        name="widen",
    )(s.reshape(1), g_fi, g_fo, g_mix, g_mix, both0, both1)


def frequencies():
    lane = np.arange(HEAD) % (HEAD // 2)
    row = np.float32(10000.0) ** (-lane.astype(np.float32) / np.float32(HEAD // 2))
    return row[: HEAD // 2].astype(np.float32)


def swap(x):
    return lax.ppermute(x, "section", [(0, 1), (1, 0)])


def mine_first(s, a, b):
    return jnp.where(s == 0, a, b)


def shards(tokens, cotangent, mixer_in, mixer_out, feed_in, feed_out, decay_rate, block_starts):
    s = lax.axis_index("section")
    dp = lax.axis_size("dp")
    rows = tokens.shape[1]
    blocks = 4 * rows // BLOCK
    ff = feed_out.shape[1]
    wfi = jnp.transpose(feed_in[0], (1, 2, 0))
    mine = (mixer_in[0], mixer_out[0], wfi, feed_out[0])
    other_rates = swap(decay_rate[0])
    rates = (mine_first(s, decay_rate[0], other_rates), mine_first(s, other_rates, decay_rate[0]))
    starts = lax.dynamic_index_in_dim(block_starts, s, 0, keepdims=False)
    scal = jnp.concatenate([row for r in rates for row in scalar_table(starts, r, dp, blocks)] + [frequencies()])

    both0, both1, turn, gf, y0, *kept = layers_forward(
        tokens, cotangent, mine, scal, dp, 1
    )
    weights0, saved0, weights1, saved1 = kept[:4], kept[4:18], kept[18:22], kept[22:]
    in_grads, g_fi, g_fo, g_mix = layers_backward(
        gf, y0, tokens, turn, scal, (weights0, weights1),
        (saved0, saved1), dp, ff, 2,
    )
    g_in, g_feed_in, g_out, g_feed_out, outputs = widen(s, g_fi, g_fo, g_mix, both0, both1, ff)
    g_feed_in = jnp.transpose(g_feed_in, (2, 0, 1))
    return outputs[None], in_grads[None], g_in[None], g_out[None], g_feed_in[None], g_feed_out[None]


def solution(mesh):
    placed = (
        P(None, ("dp", "tensor"), None),
        P(None, ("dp", "tensor"), None),
        P("section", None, None, "tensor"),
        P("section", "tensor", None),
        P("section", None, None, "tensor"),
        P("section", "tensor", None),
        P("section", "tensor"),
        P(),
    )
    return jax.shard_map(
        shards,
        mesh=mesh,
        in_specs=placed,
        out_specs=(
            P("section", None, ("dp", "tensor"), None),
            P("section", None, ("dp", "tensor"), None),
            P("section", None, None, "tensor"),
            P("section", "tensor", None),
            P("section", None, None, "tensor"),
            P("section", "tensor", None),
        ),
        check_vma=False,
    )
```

```python
import functools

import jax
import jax.numpy as jnp
import numpy as np
from jax import lax
from jax.experimental import pallas as pl
from jax.experimental.pallas import tpu as pltpu
from jax.sharding import PartitionSpec as P

D = 1024
HEAD = 128
BLOCK = 256
WIDTH = 256
HEADS_HERE = WIDTH // HEAD
norm_eps = 1e-06
MESH = pl.DeviceIdType.MESH
ANY = pl.BlockSpec(memory_space=pl.ANY)
SMEM = pl.BlockSpec(memory_space=pltpu.SMEM)
bf16, f32 = jnp.bfloat16, jnp.float32
PIECES = 16
VMEM_BYTES = 62 * 1024 * 1024


def place():
    return lax.axis_index("section"), lax.axis_index("dp"), lax.axis_index("tensor")


def partner(t, k):
    return ((t // 2 + k // 2) % 2) * 2 + (t + k) % 2


class Sems:
    def __init__(self, ref):
        self.ref, self.used = ref, 0

    def take(self):
        self.used += 1
        return self.ref.at[self.used - 1]


def remote(src, dst, send, recv, dev):
    return pltpu.make_async_remote_copy(
        src_ref=src, dst_ref=dst, send_sem=send, recv_sem=recv, device_id=dev, device_id_type=MESH
    )


def nn(a, b):
    return lax.dot_general(a, b, (((1,), (0,)), ((), ())), preferred_element_type=f32)


def nt(a, b):
    return lax.dot_general(a, b, (((1,), (1,)), ((), ())), preferred_element_type=f32)


def tn(a, b):
    return lax.dot_general(a, b, (((0,), (0,)), ((), ())), preferred_element_type=f32)


def rms_scale(v):
    return lax.rsqrt(jnp.mean(v * v, axis=-1, keepdims=True) + norm_eps)


def norm_back(v, u):
    q = rms_scale(v)
    n = v * q
    return q * (u - n * jnp.mean(u * n, axis=-1, keepdims=True))


def sig(v):
    return 1.0 / (1.0 + jnp.exp(-v))


def rows_of(p, n):
    return pl.ds(pl.multiple_of(p * n, n), n)


def entry(dp, s, d, t, core=False):
    barrier = pltpu.get_barrier_semaphore()
    count = 3
    for k in (1, 2, 3):
        pl.semaphore_signal(barrier, inc=1, device_id=(s, d, partner(t, k)), device_id_type=MESH)
    if core:
        pl.semaphore_signal(barrier, inc=1, device_id=(1 - s, d, t), device_id_type=MESH)
        count += 1
    if dp > 1:

        def greet(k, c):
            pl.semaphore_signal(
                barrier, inc=1, device_id=(s, (d + k) % dp, t), device_id_type=MESH
            )
            return c

        lax.fori_loop(1, dp, greet, 0)
        count += dp - 1
    pl.semaphore_wait(barrier, count)


class Gather:
    def __init__(self, block_at, half, ssem, rsem, base, where):
        self.at, self.half, self.ssem, self.rsem, self.base = block_at, half, ssem, rsem, base
        self.where = where

    def copy(self, n, peer, half, to):
        s, d, t = self.where
        ref = self.at(partner(t, peer), half)
        k = self.base + n
        return remote(ref, ref, self.ssem.at[k], self.rsem.at[k], (s, d, partner(t, to)))

    def mine(self, n):
        peer, half, to = ((0, 0, 1), (0, 1, 1), (0, 0, 2), (0, 1, 2), (1, 0, 2), (2, 1, 1))[n]
        return self.copy(n, peer, half, to)

    def arriving(self, n):
        s, d, t = self.where
        peer, half = ((1, 0), (1, 1), (2, 0), (2, 1), (3, 0), (3, 1))[n]
        ref = self.at(partner(t, peer), half)
        k = self.base + n
        return remote(ref, ref, self.ssem.at[k], self.rsem.at[k], (s, d, t))

    def start(self):
        self.mine(0).start()
        self.mine(3).start()
        self.mine(1).start()
        self.mine(2).start()

    def forward(self):
        self.arriving(0).wait_recv()
        self.mine(4).start()
        self.arriving(3).wait_recv()
        self.mine(5).start()

    def ready(self, k):
        if k == 1:
            self.arriving(1).wait_recv()
        elif k == 2:
            self.arriving(2).wait_recv()
        else:
            self.arriving(4).wait_recv()
            self.arriving(5).wait_recv()

    def drain(self):
        for n in range(6):
            self.mine(n).wait_send()


class Scatter:
    def __init__(self, part, got, via, rows, ssem, rsem, base, where):
        self.part, self.got, self.via, self.half = part, got, via, rows // 2
        self.ssem, self.rsem, self.base, self.where = ssem, rsem, base, where

    def copy(self, n):
        s, d, t = self.where
        h = self.half
        h0, h1 = pl.ds(0, h), pl.ds(h, h)
        src, dst, to = (
            (self.part.at[2, h0], self.via.at[0], 2),
            (self.part.at[2, h1], self.via.at[1], 1),
            (self.part.at[0, h1], self.got.at[0, h1], 1),
            (self.part.at[1, h0], self.got.at[1, h0], 2),
            (self.part.at[0, h0], self.got.at[0, h0], 1),
            (self.part.at[1, h1], self.got.at[1, h1], 2),
        )[n]
        k = self.base + n
        return remote(src, dst, self.ssem.at[k], self.rsem.at[k], (s, d, partner(t, to)))

    def put(self, k, value):
        self.part[k - 1] = value.astype(bf16)
        self.send(k)

    def send(self, k):
        if k == 3:
            self.copy(0).start()
            self.copy(1).start()
        elif k == 2:
            self.copy(3).start()
        else:
            self.copy(2).start()

    def combine(self):
        h = self.half
        self.copy(0).wait_recv()
        self.part[0, 0:h] = (self.part[0, 0:h].astype(f32) + self.via[0].astype(f32)).astype(bf16)
        self.copy(4).start()
        self.copy(1).wait_recv()
        self.part[1, h:] = (self.part[1, h:].astype(f32) + self.via[1].astype(f32)).astype(bf16)
        self.copy(5).start()

    def result(self):
        for n in (2, 3, 4, 5):
            self.copy(n).wait_recv()
        return self.got[0].astype(f32) + self.got[1].astype(f32)

    def drain(self):
        for n in range(6):
            self.copy(n).wait_send()


def scalar_table(starts, rates, dp, blocks):
    d = lax.axis_index("dp")
    survive = 1.0 - starts.astype(f32).reshape(dp, blocks)
    decay = jnp.exp(-rates * BLOCK)
    factor = jnp.prod(survive, axis=1)[:, None] * (decay**blocks)[None, :]
    at = jnp.arange(dp)
    low, high = jnp.minimum(at, d), jnp.maximum(at, d)
    between = (at[None, :] > low[:, None]) & (at[None, :] < high[:, None])
    through = jnp.prod(jnp.where(between[:, :, None], factor[None], 1.0), axis=1)
    forward = jnp.where((at < d)[:, None], through, 0.0)
    backward = jnp.where((at > d)[:, None], through, 0.0)
    mine = lax.dynamic_index_in_dim(survive, d, 0, keepdims=False)
    index = jnp.arange(starts.shape[0], dtype=jnp.int32)
    begins = jnp.max(
        jnp.where((index[None, :] <= index[:, None]) & (starts > 0)[None, :], index[None, :], 0), axis=1
    )
    offsets = lax.dynamic_slice_in_dim((index - begins) * BLOCK, d * blocks, blocks).astype(f32)
    return [mine, rates, decay, forward.reshape(-1), backward.reshape(-1), offsets]


def decay_fill(scal, base, nb, mask, mask_t, qd, kd):
    for h in range(HEADS_HERE):
        r = scal[base + nb + h]
        i = lax.broadcasted_iota(jnp.int32, (BLOCK, BLOCK), 0).astype(f32)
        j = lax.broadcasted_iota(jnp.int32, (BLOCK, BLOCK), 1).astype(f32)
        gap = i - j
        mask[h] = jnp.where(gap >= 0.0, jnp.exp(-r * jnp.maximum(gap, 0.0)), 0.0)
        if mask_t is not None:
            mask_t[h] = jnp.where(gap <= 0.0, jnp.exp(-r * jnp.maximum(-gap, 0.0)), 0.0)
        i = lax.broadcasted_iota(jnp.int32, (BLOCK, HEAD), 0).astype(f32)
        qd[h] = jnp.exp(-r * (i + 1.0))
        kd[h] = jnp.exp(-r * (BLOCK - 1.0 - i))


def head(h):
    return slice(h * HEAD, (h + 1) * HEAD)


def send_states(dp, where, zout, zin, zs, zr, later):
    s, d, t = where

    def each(k, c):
        to = d + k if later else d - k

        @pl.when((to < dp) if later else (to >= 0))
        def _():
            remote(zout, zin.at[d], zs.at[k], zr.at[d], (s, to, t)).start()

        return c

    lax.fori_loop(1, dp, each, 0)


def sent_states(dp, where, zout, zin, zs, zr, later):
    s, d, t = where

    def each(k, c):
        to = d + k if later else d - k

        @pl.when((to < dp) if later else (to >= 0))
        def _():
            remote(zout, zin.at[d], zs.at[k], zr.at[d], (s, to, t)).wait_send()

        return c

    lax.fori_loop(1, dp, each, 0)


def take_states(dp, where, zout, zin, zs, zr, later, scal, base, run):
    s, d, t = where
    run[...] = jnp.zeros_like(run)

    def each(k, c):
        @pl.when((k < d) if later else (k > d))
        def _():
            remote(zout, zin.at[k], zs.at[0], zr.at[k], (s, d, t)).wait_recv()
            for h in range(HEADS_HERE):
                run[h] += scal[base + 2 * k + h] * zin[k, h].astype(f32)

        return c

    lax.fori_loop(0, dp, each, 0)


def to_owner(owner, where, src, own_dst, far_dst, lsem, ssem, rsem):
    s, d, t = where

    def far():
        return remote(src, far_dst, ssem, rsem, (1 - s, d, t))

    def local():
        return pltpu.make_async_copy(src, own_dst, lsem)

    def start():
        pl.when(owner)(lambda: local().start())
        pl.when(jnp.logical_not(owner))(lambda: far().start())

    def finish():
        @pl.when(owner)
        def _():
            local().wait()
            far().wait_recv()

        pl.when(jnp.logical_not(owner))(lambda: far().wait_send())

    return start, finish


def forward_kernel(
    dp, tok_in, ct_in, my_wi, my_wo, my_wfi, my_wfo, scal,
    both0_o, both1_o, turn_o, gf_o, y_out, *refs,
):
    outs = (refs[0:18], refs[18:36])
    (
        raw, wi2, wo2, wfi2, wfo2, turn, gf, xf, hidden, zq, zk, gate, q, k, v, att, sc, states, branch, mid,
        hid2, pair, mask, qd, kd, loc, zout2, zin2, run, u, y, part, got, via, ssq, own, yb2,
        lsem, ssem, rsem, zs2, zr2, wl, ws, wr,
    ) = refs[36:]
    where = s, d, t = place()
    rows = tok_in.shape[-2]
    total = 4 * rows
    nb = total // BLOCK
    local = Sems(lsem)
    me = rows_of(t, rows)

    def load(src, dst):
        copy = pltpu.make_async_copy(src, dst, local.take())
        copy.start()
        return copy

    got_x = load(tok_in.at[s], xf.at[me])
    got_raw = load(my_wi, raw)
    got_ct = load(ct_in.at[s], gf.at[me])
    ff = my_wfo.shape[0]
    pairs = (
        (wi2.at[s], wi2.at[s]), (my_wo, wo2.at[s, rows_of(t, WIDTH)]),
        (my_wfi, wfi2.at[s, :, pl.ds(0, ff)]), (my_wfo, wfo2.at[s, pl.ds(0, ff)]),
    )

    def mine(n):
        return pltpu.make_async_copy(*pairs[n], wl.at[n])

    def over(n):
        return remote(*pairs[n], ws.at[n], wr.at[n], (1 - s, d, t))

    def await_weight(n, owner):
        if n > 0:
            pl.when(owner)(lambda: mine(n).wait())
        pl.when(jnp.logical_not(owner))(lambda: over(n).wait_recv())

    for n in (1, 2, 3):
        mine(n).start()
    wfi2[:, :, ff:, :] = jnp.zeros_like(wfi2[:, :, ff:, :])
    wfo2[:, ff:, :] = jnp.zeros_like(wfo2[:, ff:, :])
    entry(dp, s, d, t, core=True)
    got_x.wait()
    got_ct.wait()
    half = rows // 2

    def block_of(ref):
        return lambda p, h: ref.at[pl.ds(pl.multiple_of(p * rows + h * half, half), half)]

    gg = Gather(block_of(gf), half, ssem, rsem, 42, where)
    quarter = WIDTH // 2
    gw = Gather(
        lambda p, h: wo2.at[s, pl.ds(pl.multiple_of(p * WIDTH + h * quarter, quarter), quarter)],
        quarter, ws, wr, 4, where,
    )

    def wo_over(k, slot):
        ref = wo2.at[slot, rows_of(partner(t, k), WIDTH)]
        return remote(ref, ref, ws.at[10 + k], wr.at[10 + k], (1 - s, d, t))

    stores, finishes = [], []
    for layer in (0, 1):
        (
            wi_o, wo_o, wfi_o, wfo_o, hidden_o, zq_o, zk_o, gate_o, q_o, k_o, v_o, att_o, sc_o, states_o,
            branch_o, mid_o, hid2_o, pair_o,
        ) = outs[layer]
        wi, wo, wfi, wfo = wi2.at[layer], wo2.at[layer], wfi2.at[layer], wfo2.at[layer]
        zout, zin, zs, zr = zout2.at[layer], zin2.at[layer], zs2.at[layer], zr2.at[layer]
        yb = yb2.at[layer]
        both_o = (both0_o, both1_o)[layer]
        owner = s == layer
        at = layer * (2 * nb + 4 + 4 * dp)
        base = 21 * layer
        gx = Gather(block_of(xf), half, ssem, rsem, base, where)
        gx.start()
        if layer == 0:
            for n in (1, 2, 3):
                over(n).start()
            got_raw.wait()

            def chunk(n, c):
                r = rows_of(n, 128)
                wi2[s, r, :] = raw[r].reshape(128, 4 * WIDTH)
                return c

            lax.fori_loop(0, D // 128, chunk, 0)
            over(0).start()
            lane = lax.broadcasted_iota(jnp.int32, (1, HEAD), 1)
            sign = jnp.where(lane < HEAD // 2, -1.0, 1.0)
            frequency = jnp.zeros((1, HEAD), f32)
            for n in range(HEAD // 2):
                value = scal[2 * (2 * nb + 4 + 4 * dp) + n]
                frequency = jnp.where(lax.rem(lane, HEAD // 2) == n, value, frequency)

            def angles(b, c):
                steps_in = lax.broadcasted_iota(jnp.int32, (BLOCK, HEAD), 0).astype(f32)
                angle = (scal[at + nb + 4 + 4 * dp + b] + steps_in) * frequency
                r = rows_of(b, BLOCK)
                turn[0, r, :] = jnp.cos(angle)
                turn[1, r, :] = sign * jnp.sin(angle)
                return c

            lax.fori_loop(0, nb, angles, 0)
            stores.append(load(turn, turn_o))
        decay_fill(scal, at, nb, mask, None, qd, kd)
        await_weight(0, owner)
        if layer == 1:
            for copy in stores:
                copy.wait()
            stores = []

        def project(i, c):
            for n in (1, 2, 3):

                @pl.when(i == n)
                def _(n=n):
                    if n == 1:
                        gx.forward()

                        @pl.when(owner)
                        def _():
                            mine(1).wait()
                            gw.start()

                    gx.ready(n)

            r = rows_of(partner(t, i), rows)
            xv = xf[r, :].astype(f32)
            hid = (xv * rms_scale(xv)).astype(bf16)
            hidden[r, :] = hid
            cs, sn = turn[0, r, :], turn[1, r, :]
            for n, (pre, post) in enumerate(((zq, q), (zk, k))):
                z = nn(hid, wi[:, n * WIDTH : (n + 1) * WIDTH])
                pre[r, :] = z
                a = z * sig(z)
                for h in range(HEADS_HERE):
                    ah = a[:, head(h)]
                    post[r, head(h)] = (ah * cs + pltpu.roll(ah, HEAD // 2, 1) * sn).astype(bf16)
            v[r, :] = nn(hid, wi[:, 2 * WIDTH : 3 * WIDTH]).astype(bf16)
            gate[r, :] = nn(hid, wi[:, 3 * WIDTH :])
            return c

        lax.fori_loop(0, 4, project, 0)

        stores += [load(hidden, hidden_o), load(zq, zq_o), load(zk, zk_o), load(gate, gate_o)]
        stores += [load(q, q_o), load(k, k_o), load(v, v_o)]

        def local_state(b, c):
            r = rows_of(b, BLOCK)
            for h in range(HEADS_HERE):
                kdec = (k[r, head(h)].astype(f32) * kd[h]).astype(bf16)
                loc[b, h] = tn(kdec, v[r, head(h)])
            return c

        lax.fori_loop(0, nb, local_state, 0)
        pl.when(owner)(gw.forward)
        if layer == 1:
            gg.forward()
        for h in range(HEADS_HERE):
            carried = loc[0, h]
            for b in range(1, nb):
                carried = (scal[at + nb + 2 + h] * scal[at + b]) * carried + loc[b, h]
            zout[h] = carried.astype(bf16)
        send_states(dp, where, zout, zin, zs, zr, True)

        def inner(b, c):
            r = rows_of(b, BLOCK)
            for h in range(HEADS_HERE):
                w = (nt(q[r, head(h)], k[r, head(h)]) * mask[h]).astype(bf16)
                att[r, head(h)] = nn(w, v[r, head(h)])
            return c

        lax.fori_loop(0, nb, inner, 0)
        take_states(dp, where, zout, zin, zs, zr, True, scal, at + nb + 4, run)

        def outer(b, c):
            r = rows_of(b, BLOCK)
            for h in range(HEADS_HERE):
                entering = scal[at + b] * run[h]
                states[b, h] = entering
                run[h] = scal[at + nb + 2 + h] * entering + loc[b, h]
                qdec = (q[r, head(h)].astype(f32) * qd[h]).astype(bf16)
                a = att[r, head(h)] + nn(qdec, entering.astype(bf16))
                att[r, head(h)] = a
                u[t, r, head(h)] = (a * gate[r, head(h)]).astype(bf16)
            return c

        lax.fori_loop(0, nb, outer, 0)

        hu = total // 2
        gu = Gather(lambda p, h: u.at[p, pl.ds(h * hu, hu)], hu, ssem, rsem, base + 6, where)
        gu.start()
        for b in range(nb):
            a = att[b * BLOCK : (b + 1) * BLOCK, :]
            ssq[0, :, b * BLOCK : (b + 1) * BLOCK] = lax.dot_general(
                jnp.ones((8, WIDTH), f32), a * a, (((1,), (1,)), ((), ())),
                preferred_element_type=f32, precision=lax.Precision.HIGHEST,
            )
        sums = [
            remote(
                ssq.at[0], ssq.at[n], ssem.at[base + 11 + n], rsem.at[base + 11 + n], (s, d, partner(t, n))
            )
            for n in (1, 2, 3)
        ]
        for copy in sums:
            copy.start()
        stores += [load(att, att_o), load(states, states_o)]

        @pl.when(owner)
        def _():
            for n in (1, 2, 3):
                gw.ready(n)
                wo_over(n, layer).start()

        @pl.when(jnp.logical_not(owner))
        def _():
            over(1).wait_recv()
            for n in (1, 2, 3):
                wo_over(n, layer).wait_recv()

        y[...] = jnp.zeros_like(y)

        def out_project(i, c):
            for n in (1, 2, 3):

                @pl.when(i == n)
                def _(n=n):
                    if n == 1:
                        gu.forward()
                        gg.mine(layer).start()
                        gg.mine(3 - layer).start()
                    gu.ready(n)

            p = partner(t, i)

            def chunk(m, c):
                r = rows_of(m, rows)
                y[r, :] += nn(u[p, r, :], wo[rows_of(p, WIDTH), :])
                return c

            return lax.fori_loop(0, 4, chunk, c)

        lax.fori_loop(0, 4, out_project, 0)
        for copy in sums:
            copy.wait_recv()
        whole = ssq[0] + ssq[1] + ssq[2] + ssq[3]
        sc[...] = jnp.transpose(lax.rsqrt(whole * (1.0 / D) + norm_eps))
        await_weight(2, owner)
        await_weight(3, owner)
        out = Scatter(part, got, via, rows, ssem, rsem, base + 15, where)

        def feed(i, c):
            e = 3 - i
            r = rows_of(partner(t, e), rows)
            br = sc[r, 0:1] * y[r, :]
            m = xf[r, :].astype(f32) + br
            h2 = (m * rms_scale(m)).astype(bf16)
            hid2[r, :] = h2
            p0, p1 = nt(h2, wfi[0]), nt(h2, wfi[1])
            pair[0, r, :] = p0.astype(bf16)
            pair[1, r, :] = p1.astype(bf16)
            o = nn((p0 * p1).astype(bf16), wfo[...])
            for n in (1, 2, 3):

                @pl.when(e == n)
                def _(n=n):
                    out.put(n, o)

            @pl.when(e == 0)
            def _():
                branch[...] = br.astype(bf16)
                mid[...] = m
                own[...] = o + m

            return c

        lax.fori_loop(0, 4, feed, 0)
        stores += [load(sc, sc_o), load(branch, branch_o), load(mid, mid_o), load(hid2, hid2_o)]
        stores += [load(pair, pair_o), load(wi, wi_o), load(wo, wo_o)]
        stores += [load(wfi, wfi_o), load(wfo, wfo_o)]
        gx.drain()
        gu.drain()
        for copy in sums:
            copy.wait_send()
        out.combine()
        yv = (own[...] + out.result()).astype(bf16)
        yb[...] = yv
        out.drain()
        sent_states(dp, where, zout, zin, zs, zr, True)
        start, finish = to_owner(
            owner, where, yb, both_o.at[s], both_o.at[s], wl.at[4 + layer], ws.at[14 + layer],
            wr.at[14 + layer],
        )
        start()
        finishes.append(finish)
        if layer == 0:
            stores.append(load(yb, y_out))
            xf[me, :] = yv


    for n in (1, 2, 3):
        gg.ready(n)
    stores.append(load(gf, gf_o))
    for n in range(4):
        over(n).wait_send()
    for n in (1, 2, 3):
        wo_over(n, s).wait_send()
    gw.drain()
    gg.drain()
    for finish in finishes:
        finish()
    for copy in stores:
        copy.wait()


def layers_forward(tokens, cotangent, weights, scal, dp, uid):
    rows = tokens.shape[-2]
    total = 4 * rows
    nb = total // BLOCK
    fp = -(-weights[3].shape[0] // 256) * 256
    saved = [
        ((total, D), bf16), ((total, WIDTH), f32), ((total, WIDTH), f32), ((total, WIDTH), f32),
        ((total, WIDTH), bf16), ((total, WIDTH), bf16), ((total, WIDTH), bf16), ((total, WIDTH), f32),
        ((total, 8), f32), ((nb, HEADS_HERE, HEAD, HEAD), f32), ((rows, D), bf16), ((rows, D), f32),
        ((total, D), bf16), ((2, total, fp), bf16),
    ]
    kept = [((D, 4 * WIDTH), bf16), ((D, D), bf16), ((2, fp, D), bf16), ((fp, D), bf16)]
    scratch = [((D, 4, WIDTH), bf16)] + [((2,) + a, b) for a, b in kept]
    scratch += [((2, total, HEAD), f32), ((total, D), bf16), ((total, D), bf16)] + saved
    scratch += [
        ((HEADS_HERE, BLOCK, BLOCK), f32), ((HEADS_HERE, BLOCK, HEAD), f32),
        ((HEADS_HERE, BLOCK, HEAD), f32), ((nb, HEADS_HERE, HEAD, HEAD), f32),
        ((2, HEADS_HERE, HEAD, HEAD), bf16), ((2, dp, HEADS_HERE, HEAD, HEAD), bf16),
        ((HEADS_HERE, HEAD, HEAD), f32), ((4, total, WIDTH), bf16), ((total, D), f32),
        ((3, rows, D), bf16), ((2, rows, D), bf16), ((2, rows // 2, D), bf16),
        ((4, 8, total), f32), ((rows, D), f32), ((2, rows, D), bf16),
    ]
    both = ((2, rows, D), bf16)
    outs = [both, both, ((2, total, HEAD), f32), ((total, D), bf16), ((rows, D), bf16)]
    outs += (kept + saved) * 2
    dma = pltpu.SemaphoreType.DMA
    flops = 4 * total * D * (4 * WIDTH + D + 3 * fp)
    return pl.pallas_call(
        functools.partial(forward_kernel, dp),
        out_shape=tuple(jax.ShapeDtypeStruct(a, b) for a, b in outs),
        in_specs=[ANY] * 6 + [SMEM],
        out_specs=(ANY,) * len(outs),
        scratch_shapes=[pltpu.VMEM(a, b) for a, b in scratch]
        + [
            dma((48,)), dma((48,)), dma((48,)), dma((2, dp)), dma((2, dp)), dma((6,)), dma((16,)),
            dma((16,)),
        ],
        compiler_params=pltpu.CompilerParams(
            collective_id=uid, has_side_effects=True, vmem_limit_bytes=VMEM_BYTES
        ),
        cost_estimate=pl.CostEstimate(flops=flops, bytes_accessed=60 << 20, transcendentals=0),
        name="layers_forward",
    )(tokens, cotangent, *weights, scal)


class CorePair:
    def __init__(self, where, halves, from_core, ssem, rsem):
        s, d, t = where
        self.s, self.halves, self.landed = s, halves, from_core
        self.copy = lambda: remote(halves.at[1 - s], from_core, ssem, rsem, (1 - s, d, t))

    def send(self):
        self.copy().start()

    def add(self):
        self.copy().wait()
        rows = self.landed.shape[0]
        step = 128

        def chunk(n, c):
            r = rows_of(n, step)
            mine = self.halves[self.s, r, :].astype(f32)
            self.halves[self.s, r, :] = (mine + self.landed[r, :].astype(f32)).astype(bf16)
            return c

        lax.fori_loop(0, rows // step, chunk, 0)


class LineSum:
    LAG = 2
    END = 5 * LAG

    def __init__(self, dp, where, owner, halves, first, size, land, fin, result, sems, before):
        self.dp, self.where, self.owner, self.before = dp, where, owner, before
        self.halves, self.first, self.size, self.land, self.fin = halves, first, size, land, fin
        self.result = result
        self.recv, self.sent, self.free, self.ol, self.os, self.or_ = sems
        self.age = -1
        s, d, t = where
        low = dp // 2 - 1
        self.upward = d <= low
        self.middle = (d == low) | (d == low + 1)
        self.edge = (d == 0) | (d == dp - 1)
        self.inner = (s, jnp.where(self.upward, d + 1, d - 1), t)
        self.outer = (s, jnp.where(self.upward, d - 1, d + 1), t)
        self.mine = jnp.where(self.upward, 0, 1)

    def own(self, h=None):
        return self.halves.at[self.where[0], self.rows(self.first, h)]

    def rows(self, base, h=None):
        if h is None:
            return pl.ds(base, self.size)
        half = self.size // 2
        return pl.ds(pl.multiple_of(base + h * half, 16), half)

    def final(self, h):
        return self.fin.at[self.rows(self.first, h)]

    def inward(self):
        landing = self.land.at[self.rows(self.first)]
        return remote(self.own(), landing, self.sent.at[0], self.recv.at[2], self.inner)

    def swap_part(self):
        h = 1 - self.mine
        return remote(self.own(h), self.final(h), self.sent.at[0], self.recv.at[h], self.inner)

    def swap_sum(self):
        ref = self.final(self.mine)
        return remote(ref, ref, self.sent.at[1], self.recv.at[self.mine], self.inner)

    def outward(self, h):
        ref = self.final(h)
        return remote(ref, ref, self.sent.at[2 + h], self.recv.at[h], self.outer)

    def sweep(self, base, size, fn):
        unit = 32 if size % 32 == 0 else 16

        def chunk(n, c):
            fn(pl.ds(pl.multiple_of(base + n * unit, 16), unit))
            return c

        lax.fori_loop(0, size // unit, chunk, 0)

    def start(self):
        self.age = 0
        before = self.before
        if before is not None:
            assert before.age >= self.END
            before.close()

            @pl.when(self.middle)
            def _():
                pl.semaphore_signal(
                    self.free, inc=1, device_id=self.inner, device_id_type=MESH
                )

        if self.dp > 2:
            pl.when(self.edge)(lambda: self.inward().start())

    def tick(self):
        self.age += 1
        if self.dp == 1:
            if self.age == self.END:
                self.fin[...] = self.halves[0]
            return
        s = self.where[0]
        inside = jnp.logical_not(self.edge)
        if self.age == self.LAG:

            @pl.when(inside)
            def _():
                self.inward().wait_recv()

                def fn(r):
                    total = self.halves[s, r, :].astype(f32) + self.land[r, :].astype(f32)
                    self.halves[s, r, :] = total.astype(bf16)

                self.sweep(self.first, self.size, fn)
                pl.when(jnp.logical_not(self.middle))(lambda: self.inward().start())

            @pl.when(self.middle)
            def _():
                if self.before is not None:
                    pl.semaphore_wait(self.free, 1)
                self.swap_part().start()

        if self.age == 2 * self.LAG:

            @pl.when(self.middle)
            def _():
                h = self.mine
                half = self.size // 2
                self.arrived(h)

                def fn(r):
                    total = self.halves[s, r, :].astype(f32) + self.fin[r, :].astype(f32)
                    self.fin[r, :] = total.astype(bf16)

                self.sweep(self.first + h * half, half, fn)
                self.swap_sum().start()
                pl.when(inside)(lambda: self.outward(h).start())
                self.swap_part().wait_send()

            pl.when(jnp.logical_not(self.middle))(lambda: self.inward().wait_send())

        if self.age == 3 * self.LAG:

            @pl.when(self.middle)
            def _():
                self.arrived(1 - self.mine)
                pl.when(inside)(lambda: self.outward(1 - self.mine).start())

        if self.age == self.END:

            @pl.when(jnp.logical_not(self.middle))
            def _():
                for h in (0, 1):
                    self.arrived(h)
                    pl.when(inside)(lambda h=h: self.outward(h).start())

            pl.when(self.middle)(lambda: self.swap_sum().wait_send())

            @pl.when(inside)
            def _():
                for h in (0, 1):
                    self.outward(h).wait_send()

            self.to_result()[0]()

    def arrived(self, h):
        ref = self.final(h)
        remote(ref, ref, self.sent.at[0], self.recv.at[h], self.where).wait_recv()

    def to_result(self):
        s = self.where[0]
        part = self.rows(self.first)
        target = self.result.at[s, part]
        return to_owner(
            self.owner, self.where, self.fin.at[part], target, target, self.ol, self.os, self.or_
        )

    def close(self):
        self.to_result()[1]()


class Background:
    def __init__(self):
        self.queue, self.active = [], []

    def put(self, pieces):
        self.queue += pieces

    def tick(self):
        for piece in self.active:
            piece.tick()
        self.active = [piece for piece in self.active if piece.age < piece.END]
        if self.queue:
            piece = self.queue.pop(0)
            piece.start()
            self.active.append(piece)

    def until(self, pieces, age):
        while any(piece.age < age for piece in pieces):
            self.tick()


def backward_kernel(
    dp, gf_in, y0_in, tok_in, turn_in, scal,
    wi0, wo0, wfi0, wfo0, wi1, wo1, wfi1, wfo1, *refs,
):
    saved_i = (refs[0:14], refs[14:28])
    both_o, gwfi_o, gwfo_o, gmix_o = refs[28:32]
    (
        wi, wo, wfi, wfo, turn, gf, xr, hidden, zq, zk, gate, q, k, v, att, sc, states, branch, mid,
        hid2, pair, mask, mask_t, qd, kd, terms, zout, zin, run, gpair, prod, gb, gsend, grecv, dots, gm, dv, dk,
        gp, part, got, via, own, gr, gwfi, gwfo, gmix, c_fi, c_fo, c_mix, l_fi, l_fo, l_mix,
        f_fi, f_fo, f_mix, lsem, ssem, rsem, zs, zr, ol, os, or_, core_s, core_r, ls, lr, free,
    ) = refs[32:]
    where = s, d, t = place()
    rows = y0_in.shape[0]
    total = 4 * rows
    nb = total // BLOCK
    fp = wfo.shape[0]
    half = rows // 2
    table = 2 * nb + 4 + 4 * dp
    local = Sems(lsem)
    me = rows_of(t, rows)
    gated, gatt = slice(0, WIDTH), slice(WIDTH, 2 * WIDTH)

    def gatt_head(h):
        return slice(WIDTH + h * HEAD, WIDTH + (h + 1) * HEAD)

    def load(src, dst):
        copy = pltpu.make_async_copy(src, dst, local.take())
        copy.start()
        return copy

    def block_of(ref):
        return lambda p, h: ref.at[pl.ds(pl.multiple_of(p * rows + h * half, half), half)]

    weights = ((wi0, wo0, wfi0, wfo0), (wi1, wo1, wfi1, wfo1))

    def load_feed(layer):
        keep = saved_i[layer]
        return [
            load(weights[layer][3], wfo), load(keep[13], pair), load(weights[layer][2], wfi),
            load(keep[11], mid), load(keep[12], hid2),
        ]

    def load_gates(layer):
        keep = saved_i[layer]
        return [
            load(weights[layer][1], wo), load(keep[10], branch), load(keep[8], sc), load(keep[7], att),
            load(keep[3], gate),
        ]

    def load_attn(layer):
        keep = saved_i[layer]
        pairs = ((4, q), (5, k), (6, v), (9, states), (1, zq), (2, zk))
        return [load(keep[n], ref) for n, ref in pairs]

    def load_ends(layer):
        x = tok_in.at[s] if layer == 0 else y0_in
        return [load(weights[layer][0], wi), load(saved_i[layer][0], hidden), load(x, xr)]


    ff = l_fo.shape[0]
    pieces, pairs = {}, {}
    for layer in (1, 0):
        cuts = [(gwfo, 256 * n, min(256, ff - 256 * n), l_fo, f_fo, gwfo_o) for n in range(-(-ff // 256))]
        cuts += [(gwfi, 96 * n, min(96, ff - 96 * n), l_fi, f_fi, gwfi_o) for n in range(-(-ff // 96))]
        cuts += [(gmix, 256 * n, 256, l_mix, f_mix, gmix_o) for n in range((D + WIDTH) // 256)]
        made = []
        for n, cut in enumerate(cuts):
            slot = PIECES * layer + n
            sems = [ref.at[slot] for ref in (lr, ls)] + [free.at[n]]
            sems += [ref.at[slot] for ref in (ol, os, or_)]
            before = pieces[1][n] if layer == 0 else None
            made.append(LineSum(dp, where, s == layer, *cut, sems, before))
        pieces[layer] = made
        pairs[layer] = [
            CorePair(where, halves, landed, core_s.at[3 * layer + n], core_r.at[3 * layer + n])
            for n, (halves, landed) in enumerate(((gwfo, c_fo), (gwfi, c_fi), (gmix, c_mix)))
        ]
    n_out, n_feed = -(-ff // 256), -(-ff // 256) + -(-ff // 96)
    work = Background()
    tick = work.tick

    got_g = load(gf_in, gf)
    in_feed, in_tables = load_feed(1), [load(turn_in, turn)]
    in_gates, in_attn, in_ends = load_gates(1), load_attn(1), load_ends(1)
    entry(dp, s, d, t, core=True)
    got_g.wait()
    in_out = []

    for layer in (1, 0):
        offset = table * layer
        pair_fo, pair_fi, pair_mix = pairs[layer]
        base = 30 * layer
        gg = Gather(block_of(gf), half, ssem, rsem, base, where) if layer == 0 else None
        if gg is not None:
            gg.start()
        decay_fill(scal, offset, nb, mask, mask_t, qd, kd)
        tick()
        for copy in in_feed:
            copy.wait()
        sums = Scatter(part, got, via, rows, ssem, rsem, base + 6, where)

        def out_weights(n, c):
            cols = rows_of(n, 256)
            a = prod[:, cols]
            gwfo[0, cols, :] = tn(a, gf[:, : D // 2]).astype(bf16)
            gwfo[1, cols, :] = tn(a, gf[:, D // 2 :]).astype(bf16)
            return c

        if layer == 1:

            def products(i, c):
                r = rows_of(i, rows)
                prod[r, :] = (pair[0, r, :].astype(f32) * pair[1, r, :].astype(f32)).astype(bf16)
                return c

            lax.fori_loop(0, 4, products, 0)
            lax.fori_loop(0, fp // 256, out_weights, 0)
            pair_fo.send()

        def feed(i, c):
            for n in (1, 2, 3) if layer == 1 else ():

                @pl.when(i == n)
                def _(n=n):
                    if n == 1:
                        pair_fo.add()
                        work.put(pieces[layer][:n_out])
                    tick()

            for n in (1, 2, 3) if gg is not None else ():

                @pl.when(i == n)
                def _(n=n):
                    if n == 1:
                        gg.forward()
                    tick()
                    gg.ready(n)

            r = rows_of(partner(t, i), rows)
            grad = nt(gf[r, :], wfo[...])
            p0, p1 = pair[0, r, :].astype(f32), pair[1, r, :].astype(f32)
            if layer == 0:
                prod[r, :] = (p0 * p1).astype(bf16)
            g0, g1 = (grad * p1).astype(bf16), (grad * p0).astype(bf16)
            gpair[0, r, :] = g0
            gpair[1, r, :] = g1
            o = nn(g0, wfi[0]) + nn(g1, wfi[1])
            for n in (1, 2, 3):

                @pl.when(i == n)
                def _(n=n):
                    sums.put(n, o)

            @pl.when(i == 0)
            def _():
                own[...] = o

            return c

        lax.fori_loop(0, 4, feed, 0)
        tick()

        def feed_weights(n, c):
            cols = rows_of(n, 256)
            for part_of in (0, 1):
                gwfi[part_of, cols, :] = tn(gpair[part_of, :, cols], hid2[...]).astype(bf16)
            return c

        if layer == 0:
            work.until(pieces[1][:n_feed], 2 * LineSum.LAG)
            lax.fori_loop(0, fp // 256, out_weights, 0)
            pair_fo.send()
        lax.fori_loop(0, fp // 256, feed_weights, 0)
        pair_fi.send()
        tick()
        sums.combine()
        if layer == 0:
            pair_fo.add()
            work.put(pieces[layer][:n_out])
        tick()
        pair_fi.add()
        work.put(pieces[layer][n_out:n_feed])
        tick()
        grad_middle = gf[me, :].astype(f32) + norm_back(mid[...], own[...] + sums.result())
        gm[...] = grad_middle
        gb[me, :] = grad_middle.astype(bf16)
        tick()
        sums.drain()
        if gg is not None:
            gg.drain()

        for copy in in_gates:
            copy.wait()
        mine = gb[me, :]
        for p in range(4):
            gsend[p] = nt(mine, wo[p * WIDTH : (p + 1) * WIDTH, :]).astype(bf16)
        grecv[t] = gsend[t]
        dots[t, :, 0:rows] = lax.dot_general(
            jnp.ones((8, D), f32), mine.astype(f32) * branch[...].astype(f32), (((1,), (1,)), ((), ())),
            preferred_element_type=f32, precision=lax.Precision.HIGHEST,
        ) * (1.0 / D)

        def turned(k, into):
            dev = (s, d, partner(t, k))
            slot = partner(t, k) if into else t
            n = base + 24 + 2 * k
            return (
                remote(gsend.at[partner(t, k)], grecv.at[slot], ssem.at[n - 2], rsem.at[n - 2], dev),
                remote(dots.at[t], dots.at[slot], ssem.at[n - 1], rsem.at[n - 1], dev),
            )

        for n in (3, 1, 2):
            for copy in turned(n, False):
                copy.start()
        gbg = Gather(block_of(gb), half, ssem, rsem, base + 12, where)
        gbg.start()
        if layer == 1:
            in_feed = load_feed(0)
        tick()

        def gating(i, c):
            for n in (1, 2, 3):

                @pl.when(i == n)
                def _(n=n):
                    for copy in turned(n, True):
                        copy.wait_recv()

            p = partner(t, i)
            r = rows_of(p, rows)
            grad = grecv[p].astype(f32)
            inner_sum = jnp.transpose(dots[p])[0:rows, 0:1]
            scale = sc[r, 0:1]
            normed = att[r, :] * scale
            gt = gate[r, :]
            gp[r, 3 * WIDTH :] = (grad * normed).astype(bf16)
            prod[r, gated] = (normed * gt).astype(bf16)
            prod[r, gatt] = (scale * (grad * gt - normed * inner_sum)).astype(bf16)
            return c

        lax.fori_loop(0, 4, gating, 0)
        tick()
        if layer == 1:
            in_gates = load_gates(0)
        for copy in in_attn:
            copy.wait()
        if layer == 1:
            for copy in in_tables:
                copy.wait()

        def term(b, c):
            r = rows_of(b, BLOCK)
            for h in range(HEADS_HERE):
                qdec = (q[r, head(h)].astype(f32) * qd[h]).astype(bf16)
                terms[b, h] = tn(qdec, prod[r, gatt_head(h)])
            return c

        lax.fori_loop(0, nb, term, 0)
        for h in range(HEADS_HERE):
            carried = scal[offset + nb - 1] * terms[nb - 1, h]
            for b in reversed(range(nb - 1)):
                carried = scal[offset + b] * (terms[b, h] + scal[offset + nb + 2 + h] * carried)
            zout[layer, h] = carried.astype(bf16)
        z_args = (dp, where, zout.at[layer], zin.at[layer], zs.at[layer], zr.at[layer], False)
        send_states(*z_args)
        tick()
        gbg.forward()

        def unturn(pre, grad, r, h):
            back = grad * turn[0, r, :] - pltpu.roll(grad, HEAD // 2, 1) * turn[1, r, :]
            z = pre[r, head(h)]
            g = sig(z)
            return (back * (g * (1.0 + z * (1.0 - g)))).astype(bf16)

        def inner(b, c):
            r = rows_of(b, BLOCK)
            for h in range(HEADS_HERE):
                qh, kh, vh, gh = q[r, head(h)], k[r, head(h)], v[r, head(h)], prod[r, gatt_head(h)]
                w_t = (nt(kh, qh) * mask_t[h]).astype(bf16)
                dv[r, head(h)] = nn(w_t, gh)
                ds = (nt(gh, vh) * mask[h]).astype(bf16)
                ds_t = (nt(vh, gh) * mask_t[h]).astype(bf16)
                dk[r, head(h)] = nn(ds_t, qh)
                dq = nn(ds, kh) + nt(gh, states[b, h].astype(bf16)) * qd[h]
                gp[r, head(h)] = unturn(zq, dq, r, h)
            return c

        lax.fori_loop(0, nb, inner, 0)
        tick()
        take_states(*z_args, scal, offset + nb + 4 + 2 * dp, run)

        def outer(i, c):
            b = nb - 1 - i
            r = rows_of(b, BLOCK)
            for h in range(HEADS_HERE):
                after = run[h]
                low = after.astype(bf16)
                run[h] = scal[offset + b] * (terms[b, h] + scal[offset + nb + 2 + h] * after)
                kdec = (k[r, head(h)].astype(f32) * kd[h]).astype(bf16)
                dkh = dk[r, head(h)] + nt(v[r, head(h)], low) * kd[h]
                k_cols = slice(WIDTH + h * HEAD, WIDTH + (h + 1) * HEAD)
                v_cols = slice(2 * WIDTH + h * HEAD, 2 * WIDTH + (h + 1) * HEAD)
                gp[r, k_cols] = unturn(zk, dkh, r, h)
                gp[r, v_cols] = (dv[r, head(h)] + nn(kdec, low)).astype(bf16)
            return c

        lax.fori_loop(0, nb, outer, 0)
        tick()
        if layer == 1:
            in_attn = load_attn(0)
        for copy in in_ends:
            copy.wait()
        ins = Scatter(part, got, via, rows, ssem, rsem, base + 18, where)

        def back_in(i, c):
            e = 3 - i
            r = rows_of(partner(t, e), rows)
            o = nt(gp[r, :], wi[...])
            for n in (1, 2, 3):

                @pl.when(e == n)
                def _(n=n):
                    ins.put(n, o)

            @pl.when(e == 0)
            def _():
                own[...] = o

            return c

        lax.fori_loop(0, 4, back_in, 0)
        tick()
        if layer == 0:
            work.until(pieces[1], 2 * LineSum.LAG)

        def in_weights(n, c):
            cols = rows_of(n, 256)
            a = hidden[:, cols]
            gmix[0, cols, :] = tn(a, gp[:, : 2 * WIDTH]).astype(bf16)
            gmix[1, cols, :] = tn(a, gp[:, 2 * WIDTH :]).astype(bf16)
            return c

        lax.fori_loop(0, D // 256, in_weights, 0)
        for n in (1, 2, 3):
            gbg.ready(n)
        gmix[0, D:, :] = tn(prod[:, gated], gb[:, : D // 2]).astype(bf16)
        gmix[1, D:, :] = tn(prod[:, gated], gb[:, D // 2 :]).astype(bf16)
        pair_mix.send()
        ins.combine()
        tick()
        pair_mix.add()
        work.put(pieces[layer][n_feed:])
        tick()
        dx = gm[...] + norm_back(xr[...].astype(f32), own[...] + ins.result())
        gr[layer] = dx.astype(bf16)
        ins.drain()
        gbg.drain()
        for n in (1, 2, 3):
            for copy in turned(n, False):
                copy.wait_send()
        sent_states(*z_args)
        start, finish = to_owner(
            s == layer, where, gr.at[layer], both_o.at[s], both_o.at[s],
            ol.at[2 * PIECES + layer], os.at[2 * PIECES + layer], or_.at[2 * PIECES + layer],
        )
        start()
        in_out.append(finish)
        if layer == 1:
            gf[me, :] = gr[layer]
            in_ends = load_ends(0)

    work.until(pieces[0], LineSum.END)
    for piece in pieces[0]:
        piece.close()
    for finish in in_out:
        finish()


def layers_backward(gathered, y0, tokens, turn, scal, weights, saved, dp, ff, uid):
    rows = y0.shape[-2]
    total = 4 * rows
    nb = total // BLOCK
    fp = weights[0][3].shape[0]
    mixed = D + WIDTH
    outs = [
        ((2, rows, D), bf16), ((2, fp, D), bf16), ((2, fp, D // 2), bf16), ((2, mixed, D // 2), bf16)
    ]
    scratch = [
        ((D, 4 * WIDTH), bf16), ((D, D), bf16), ((2, fp, D), bf16), ((fp, D), bf16),
        ((2, total, HEAD), f32), ((total, D), bf16), ((rows, D), bf16),
    ]
    scratch += [(a.shape, a.dtype) for a in saved[0]]
    scratch += [
        ((HEADS_HERE, BLOCK, BLOCK), f32), ((HEADS_HERE, BLOCK, BLOCK), f32),
        ((HEADS_HERE, BLOCK, HEAD), f32), ((HEADS_HERE, BLOCK, HEAD), f32),
        ((nb, HEADS_HERE, HEAD, HEAD), f32), ((2, HEADS_HERE, HEAD, HEAD), bf16),
        ((2, dp, HEADS_HERE, HEAD, HEAD), bf16), ((HEADS_HERE, HEAD, HEAD), f32),
        ((2, total, fp), bf16), ((total, fp), bf16), ((total, D), bf16), ((4, rows, WIDTH), bf16),
        ((4, rows, WIDTH), bf16), ((4, 8, -(-rows // 128) * 128), f32), ((rows, D), f32),
        ((total, WIDTH), f32), ((total, WIDTH), f32),
        ((total, 4 * WIDTH), bf16),
        ((3, rows, D), bf16), ((2, rows, D), bf16), ((2, rows // 2, D), bf16), ((rows, D), f32),
        ((2, rows, D), bf16),
        ((2, fp, D), bf16), ((2, fp, D // 2), bf16), ((2, mixed, D // 2), bf16),
        ((fp, D), bf16), ((fp, D // 2), bf16), ((mixed, D // 2), bf16),
        ((ff, D), bf16), ((ff, D // 2), bf16), ((mixed, D // 2), bf16),
        ((ff, D), bf16), ((ff, D // 2), bf16), ((mixed, D // 2), bf16),
    ]
    count = 2 * PIECES
    dma = pltpu.SemaphoreType.DMA
    flops = 8 * total * D * (4 * WIDTH + WIDTH + 3 * fp)
    flat = [w for layer in weights for w in layer]
    kept = [a for layer in saved for a in layer]
    return pl.pallas_call(
        functools.partial(backward_kernel, dp),
        out_shape=tuple(jax.ShapeDtypeStruct(a, b) for a, b in outs),
        in_specs=[ANY] * 4 + [SMEM] + [ANY] * (len(flat) + len(kept)),
        out_specs=(ANY,) * len(outs),
        scratch_shapes=[pltpu.VMEM(a, b) for a, b in scratch]
        + [
            dma((48,)), dma((60,)), dma((60,)), dma((2, dp)), dma((2, dp)), dma((count + 2,)),
            dma((count + 2,)), dma((count + 2,)), dma((6,)), dma((6,)), dma((count, 4)),
            dma((count, 3)), pltpu.SemaphoreType.REGULAR((PIECES,)),
        ],
        compiler_params=pltpu.CompilerParams(
            collective_id=uid, has_side_effects=True, vmem_limit_bytes=VMEM_BYTES
        ),
        cost_estimate=pl.CostEstimate(flops=flops, bytes_accessed=60 << 20, transcendentals=0),
        name="layers_backward",
    )(gathered, y0, tokens, turn, scal, *flat, *kept)


def widen_kernel(
    section, fi, fo, mix, mix_out, both0, both1, grads, g_in, g_fi, g_out, g_fo, outputs, in_grads
):
    in_grads[...] = grads[...]
    for n in range(4):
        lanes = slice((n % 2) * WIDTH, (n % 2 + 1) * WIDTH)
        g_in[:, n, :] = mix[n // 2, :, lanes].astype(f32)
    for n in range(2):
        half = slice(n * (D // 2), (n + 1) * (D // 2))
        g_fi[n] = fi[n].astype(f32)
        g_out[:, half] = mix_out[n].astype(f32)
        g_fo[:, half] = fo[n].astype(f32)

    @pl.when(section[0] == 0)
    def _():
        outputs[...] = both0[...]

    @pl.when(section[0] != 0)
    def _():
        outputs[...] = both1[...]


def widen(s, g_fi, g_fo, g_mix, both0, both1, grads, ff):
    cuts = 2
    rows = both0.shape[1]
    n = D // cuts
    ahead = D // (WIDTH // cuts)
    shapes = ((D, 4, WIDTH), (2, ff, D), (WIDTH, D), (ff, D))
    per_row = lambda *shape: pl.BlockSpec(shape, lambda i, _: (i,) + (0,) * (len(shape) - 1))
    halves = lambda *shape: pl.BlockSpec(shape, lambda i, _: (0, i, 0))
    return pl.pallas_call(
        widen_kernel,
        out_shape=tuple(jax.ShapeDtypeStruct(a, f32) for a in shapes)
        + (jax.ShapeDtypeStruct(both0.shape, bf16),) * 2,
        grid_spec=pltpu.PrefetchScalarGridSpec(
            num_scalar_prefetch=1,
            grid=(cuts,),
            in_specs=[
                halves(2, ff // cuts, D),
                halves(2, ff // cuts, D // 2),
                halves(2, n, D // 2),
                pl.BlockSpec((2, WIDTH // cuts, D // 2), lambda i, _: (0, ahead + i, 0)),
                halves(2, rows // cuts, D),
                halves(2, rows // cuts, D),
                halves(2, rows // cuts, D),
            ],
            out_specs=(
                per_row(n, 4, WIDTH), halves(2, ff // cuts, D), per_row(WIDTH // cuts, D),
                per_row(ff // cuts, D),
                halves(2, rows // cuts, D),
                halves(2, rows // cuts, D),
            ),
        ),
        compiler_params=pltpu.CompilerParams(vmem_limit_bytes=VMEM_BYTES),
        cost_estimate=pl.CostEstimate(flops=0, bytes_accessed=24 << 20, transcendentals=0),
        name="widen",
    )(s.reshape(1), g_fi, g_fo, g_mix, g_mix, both0, both1, grads)


def frequencies():
    lane = np.arange(HEAD) % (HEAD // 2)
    row = np.float32(10000.0) ** (-lane.astype(np.float32) / np.float32(HEAD // 2))
    return row[: HEAD // 2].astype(np.float32)


def swap(x):
    return lax.ppermute(x, "section", [(0, 1), (1, 0)])


def mine_first(s, a, b):
    return jnp.where(s == 0, a, b)


def shards(tokens, cotangent, mixer_in, mixer_out, feed_in, feed_out, decay_rate, block_starts):
    s = lax.axis_index("section")
    dp = lax.axis_size("dp")
    rows = tokens.shape[1]
    blocks = 4 * rows // BLOCK
    ff = feed_out.shape[1]
    wfi = jnp.transpose(feed_in[0], (1, 2, 0))
    mine = (mixer_in[0], mixer_out[0], wfi, feed_out[0])
    other_rates = swap(decay_rate[0])
    rates = (mine_first(s, decay_rate[0], other_rates), mine_first(s, other_rates, decay_rate[0]))
    starts = lax.dynamic_index_in_dim(block_starts, s, 0, keepdims=False)
    scal = jnp.concatenate([row for r in rates for row in scalar_table(starts, r, dp, blocks)] + [frequencies()])

    both0, both1, turn, gf, y0, *kept = layers_forward(
        tokens, cotangent, mine, scal, dp, 1
    )
    weights0, saved0, weights1, saved1 = kept[:4], kept[4:18], kept[18:22], kept[22:]
    in_grads, g_fi, g_fo, g_mix = layers_backward(
        gf, y0, tokens, turn, scal, (weights0, weights1),
        (saved0, saved1), dp, ff, 2,
    )
    g_in, g_feed_in, g_out, g_feed_out, outputs, in_grads = widen(
        s, g_fi, g_fo, g_mix, both0, both1, in_grads, ff
    )
    g_feed_in = jnp.transpose(g_feed_in, (2, 0, 1))
    return outputs[None], in_grads[None], g_in[None], g_out[None], g_feed_in[None], g_feed_out[None]


def solution(mesh):
    placed = (
        P(None, ("dp", "tensor"), None),
        P(None, ("dp", "tensor"), None),
        P("section", None, None, "tensor"),
        P("section", "tensor", None),
        P("section", None, None, "tensor"),
        P("section", "tensor", None),
        P("section", "tensor"),
        P(),
    )
    return jax.shard_map(
        shards,
        mesh=mesh,
        in_specs=placed,
        out_specs=(
            P("section", None, ("dp", "tensor"), None),
            P("section", None, ("dp", "tensor"), None),
            P("section", None, None, "tensor"),
            P("section", "tensor", None),
            P("section", None, None, "tensor"),
            P("section", "tensor", None),
        ),
        check_vma=False,
    )
```
